32 devices in a mesh: wide: 8 (over y, x, core), narrow: 4 (over z).
Axes of the slice: x: 2, y: 2, z: 4, core: 2. Of those that a mesh axis runs over, the one named last changes fastest.
Arguments:
- series: float32 [512, 640], P(('wide', 'narrow'))
- pad_mask: int32 [512, 640], P(('wide', 'narrow')), may hold values from 0 to 1, as said below
- freq_class: int32 [512], P(('wide', 'narrow')), may hold values from 0 to 2, as said below
- owner: int32 [322], replicated, may hold values from 0 to 511, as said below
- step: int32 [1], replicated, may hold values from 1 to 20
- master: float32 [512, 64, 1280], P(('wide', 'narrow')), may hold values from -0.15625 to 0.15625
- moment1: float32 [512, 64, 1280], P(('wide', 'narrow')), may hold values from -3.0517578e-05 to 3.0517578e-05
- moment2: float32 [512, 64, 1280], P(('wide', 'narrow')), may hold values from 3.7893486e-12 to 1.5157394e-11
- small_master: float32 [11520], replicated
- small_m1: float32 [11520], replicated, may hold values from -0.00012207031 to 0.00012207031
- small_m2: float32 [11520], replicated, may hold values from 6.062958e-11 to 2.425183e-10
Outputs:
- loss: float32 [], replicated
- grad_norm: float32 [], replicated
- new_master: float32 [512, 64, 1280], P(('wide', 'narrow'))
- new_moment1: float32 [512, 64, 1280], P(('wide', 'narrow'))
- new_moment2: float32 [512, 64, 1280], P(('wide', 'narrow'))
- weight_copy: bfloat16 [512, 64, 1280], P(('wide', 'narrow'))
- small_new: float32 [11520], replicated
- small_new_m1: float32 [11520], replicated
- small_new_m2: float32 [11520], replicated
The draws below stay inside these ranges and needn't reach their ends.
Inputs may be any that keep to these rules, and one draw needn't show every extreme that they name: `pad_mask`: 1 marks padding; in each series the padding is a prefix shorter than 512 points. `freq_class`: every class occurs. `owner`: distinct slots; slot s lies on the device of index s // 16 along wide+narrow; some device holds 16 blocks, others fewer.
All inputs are finite; a program needn't handle non-finite values.
Results may differ from the reference program's by a relative error of at most 0.0056.
The reference program's roundings to bfloat16 on the way (of `blocks`, `feat` and `qkv`) count: a program that leaves them out, or rounds other values in their place, can miss the bound.
Values may be sent and summed in bfloat16 or wider, within the bound.
A program may use at most 512 MiB of HBM per device.

```python
import math
import jax
import jax.numpy as jnp
from jax import lax

D = 1280
HEADS = 16
HDIM = 80
FF = 5120
PATCH = 32
HORIZON = 128
NQ = 9
NPATCH = 16
NCLASS = 3
BR = 64
TOTAL_SLOTS = 512
CTX = 512
SERLEN = 640
OUTW = 1280
SERIES = 512
ROWS = 20608
NBLK = 322
SMALLN = 11520
DEVICES = 32


def draw_series(key, part):
    key_scale, key_base = jax.random.split(key, 2)
    index = jnp.arange(SERIES, dtype=jnp.float32)
    scale = jnp.power(3.0, index / max(SERIES - 1, 1)) * jax.random.uniform(key_scale, (SERIES,), jnp.float32, 0.7, 1.4)
    base = jax.random.normal(key_base, (SERIES, SERLEN), jnp.float32)
    return base * scale[:, None]


def draw_pad_mask(key, part):
    index = jnp.arange(SERIES, dtype=jnp.int32)
    reach = (CTX - PATCH) * (SERIES - 1 - index) // max(SERIES - 1, 1)
    jitter = jax.random.randint(key, (SERIES,), 0, PATCH)
    length = jnp.maximum(reach - jitter, 0)
    length = length.at[0].set(CTX - PATCH)
    moment = jnp.arange(SERLEN, dtype=jnp.int32)[None, :]
    return (moment < length[:, None]).astype(jnp.int32)


def draw_freq_class(key, part):
    return (jax.random.permutation(key, SERIES) % NCLASS).astype(jnp.int32)


def draw_owner(key, part):
    key_full, key_score, key_order = jax.random.split(key, 3)
    per_device = TOTAL_SLOTS // DEVICES
    full = jax.random.randint(key_full, (), 0, DEVICES)
    score = jax.random.randint(key_score, (TOTAL_SLOTS,), 0, 1 << 20)
    slot_id = jnp.arange(TOTAL_SLOTS, dtype=jnp.int32)
    forced = (slot_id // per_device == full) | (slot_id == TOTAL_SLOTS - 1)
    score = jnp.where(forced, -1, score)
    chosen = jnp.argsort(score, stable=True)[:NBLK]
    return chosen[jax.random.permutation(key_order, NBLK)].astype(jnp.int32)


def draw_small_master(key, part):
    index = jnp.arange(SMALLN, dtype=jnp.int32)
    gains = (index >= (NCLASS + 2) * D) & (index < (NCLASS + 4) * D)
    noise = jax.random.normal(key, (SMALLN,), jnp.float32)
    return jnp.where(gains, 1.0 + 0.1 * noise, 0.3 * noise)


def block_scale(rng, shape, cuts, low, largest):
    level = 1.0
    for position, blocks in cuts:
        draws = jax.random.uniform(jax.random.fold_in(jax.random.fold_in(rng, 6), position), (blocks,), jnp.float32, low / len(cuts), largest / len(cuts))
        level = level * jnp.repeat(jnp.exp(draws), shape[position] // blocks).reshape((-1,) + (1,) * (len(shape) - 1 - position))
    return level


def normal_values(own_key, dims, deviation, bound, cuts=(), kind=jnp.bfloat16):
    values = deviation * jax.random.normal(own_key, dims, jnp.float32)
    if cuts:
        values = values * block_scale(own_key, dims, cuts, -0.22, 0.18)
    return jnp.clip(values, -bound, bound).astype(kind)


def setup_inputs(seed: int = 0) -> dict:
    key_list = jax.random.split(jax.random.key(seed), 12)
    series = draw_series(jax.random.fold_in(key_list[11], 71), 0)
    pad_mask = draw_pad_mask(jax.random.fold_in(key_list[11], 71), 0)
    freq_class = draw_freq_class(jax.random.fold_in(key_list[11], 71), 0)
    owner = draw_owner(jax.random.fold_in(key_list[11], 71), 0)
    step = jax.random.randint(key_list[4], (1,), 1, 21).astype(jnp.int32)
    master = normal_values(key_list[5], (TOTAL_SLOTS, BR, D), D ** -0.5, 0.15625, ((0, 32),), jnp.float32)
    moment1 = normal_values(key_list[6], (TOTAL_SLOTS, BR, D), (0.01 / (ROWS * D + SMALLN) ** 0.5), 3.0517578125e-05, ((0, 32),), jnp.float32)
    moment2 = jnp.clip(jnp.exp(math.log(1.5157394436804417e-11) - 1.3862944 * jax.random.uniform(key_list[7], (TOTAL_SLOTS, BR, D), jnp.float32) ** block_scale(key_list[7], (TOTAL_SLOTS, BR, D), ((0, 32),), -0.2, 0.2)), 3.789348609201104e-12, 1.5157394436804417e-11)
    small_master = draw_small_master(jax.random.fold_in(key_list[11], 71), 0)
    small_m1 = normal_values(key_list[9], (SMALLN,), (0.04 / (ROWS * D + SMALLN) ** 0.5), 0.00012207031, (), jnp.float32)
    small_m2 = jnp.clip(jnp.exp(jax.random.uniform(key_list[10], (SMALLN,), jnp.float32, math.log(6.062957774721767e-11), math.log(2.4251831098887067e-10))), 6.062957774721767e-11, 2.4251831098887067e-10)
    return dict(series=series, pad_mask=pad_mask, freq_class=freq_class, owner=owner, step=step, master=master, moment1=moment1, moment2=moment2, small_master=small_master, small_m1=small_m1, small_m2=small_m2)


HIGH = lax.Precision.HIGHEST
CLIP = 0.01
RATE = 0.03
DECAY = 0.1
BETA = 0.5
EPSILON = 1e-08

@jax.custom_vjp
def low(v):
    return lax.optimization_barrier(v.astype(jnp.bfloat16)).astype(jnp.float32)

@jax.custom_vjp
def low_back(v):
    return v

def low_keep(v):
    return (low(v), None)

def low_pass(kept, grad):
    return (grad,)

def back_keep(v):
    return (v, None)

def back_low(kept, grad):
    return (low(grad),)
low.defvjp(low_keep, low_pass)
low_back.defvjp(back_keep, back_low)

def silu(value):
    return value / (1.0 + jnp.exp(-value))

def rms_norm(hidden, gain):
    return hidden * lax.rsqrt(lax.optimization_barrier(jnp.mean(hidden * hidden, axis=-1, keepdims=True)) + 1e-06) * gain

def tables():
    half = HDIM // 2
    inverse = jnp.power(10000.0, -2.0 * jnp.arange(half, dtype=jnp.float32) / HDIM)
    angle = jnp.arange(NPATCH, dtype=jnp.float32)[:, None] * inverse[None, :]
    return (jnp.cos(angle)[None, :, None, :], jnp.sin(angle)[None, :, None, :])

def rotate(value, cosine, sine):
    half = HDIM // 2
    first = value[..., :half]
    second = value[..., half:]
    return jnp.concatenate([first * cosine - second * sine, first * sine + second * cosine], axis=-1)

def split_rows(flat_rows):
    shapes = ((2 * PATCH, 2 * D), (D, D), (D, 3 * D), (D, D), (D, FF), (FF, D), (D, D + OUTW), (D, OUTW))
    pieces = []
    start = 0
    for first, second in shapes:
        number = first * second // D
        pieces.append(flat_rows[start:start + number].reshape(first, second))
        start += number
    return tuple(pieces)

def split_small(small):
    freq = small[:NCLASS * D].reshape(NCLASS, D)
    rest = small[NCLASS * D:]
    return (freq, rest[0:D], rest[D:2 * D], rest[2 * D:3 * D], rest[3 * D:4 * D], rest[4 * D:5 * D], rest[5 * D:5 * D + OUTW])

def prepare(series, pad_mask):
    valid = (1 - pad_mask).astype(jnp.float32)
    count_series = series.shape[0]
    context = (series[:, :CTX] * valid[:, :CTX]).reshape(count_series, NPATCH, PATCH)
    marks = pad_mask[:, :CTX].astype(jnp.float32).reshape(count_series, NPATCH, PATCH)
    feat = jnp.concatenate([context, marks], axis=-1)
    index = (jnp.arange(NPATCH, dtype=jnp.int32)[:, None] + 1) * PATCH + jnp.arange(HORIZON, dtype=jnp.int32)[None, :]
    return (feat, series[:, index], valid[:, index])

def class_sums(out, target, tmask, onehot):
    pred = out.reshape(onehot.shape[0], NPATCH, HORIZON, NQ + 1)
    error = pred[..., 0] - target
    square = lax.optimization_barrier(jnp.sum(error * error * tmask, axis=(1, 2)))
    levels = (jnp.arange(NQ, dtype=jnp.float32) + 1.0) / (NQ + 1)
    diff = target[..., None] - pred[..., 1:]
    pinball = lax.optimization_barrier(jnp.sum(jnp.maximum(levels * diff, (levels - 1.0) * diff), axis=-1))
    quant = lax.optimization_barrier(jnp.sum(pinball * tmask, axis=(1, 2)))
    return jnp.stack([lax.optimization_barrier(jnp.sum(onehot * square[:, None], 0)), lax.optimization_barrier(jnp.sum(onehot * quant[:, None], 0))])

def forward(mats, small, feat, onehot, target, tmask, class_weight):
    tok_in, tok_out, w_qkv, w_out, w_up, w_down, head_in, head_out = mats
    freq, bias_one, bias_two, gain_one, gain_two, head_bias, out_bias = split_small(small)
    count_series = feat.shape[0]
    tokens = count_series * NPATCH
    patch_in = low(feat.reshape(tokens, 2 * PATCH))
    tok_pre = low_back(jnp.dot(patch_in, tok_in, precision=HIGH))
    hidden = low(silu(tok_pre[:, :D] + bias_one))
    tok_prod = low_back(jnp.dot(hidden, tok_out, precision=HIGH))
    class_rows = jnp.repeat(jnp.dot(onehot, freq, precision=HIGH), NPATCH, axis=0)
    state_zero = tok_prod + bias_two + tok_pre[:, D:] + class_rows
    normed_one = low(rms_norm(state_zero, gain_one))
    qkv = low_back(jnp.dot(normed_one, w_qkv, precision=HIGH)).reshape(count_series, NPATCH, 3, HEADS, HDIM)
    cosine, sine = tables()
    queries = low(rotate(qkv[:, :, 0], cosine, sine) * HDIM ** (-0.5))
    key_rot = low(rotate(qkv[:, :, 1], cosine, sine))
    value_all = low(qkv[:, :, 2])
    scores = low_back(jnp.einsum('sqhd,skhd->shqk', queries, key_rot, precision=HIGH))
    causal = jnp.arange(NPATCH)[:, None] >= jnp.arange(NPATCH)[None, :]
    scores = jnp.where(causal, scores, -1e+30)
    expo = jnp.exp(scores - lax.optimization_barrier(jnp.max(scores, axis=-1, keepdims=True)))
    attend = expo / lax.optimization_barrier(jnp.sum(expo, axis=-1, keepdims=True))
    mixed = jnp.einsum('shqk,skhd->sqhd', low(attend), value_all, precision=HIGH)
    mixed = low_back(low(mixed)).reshape(tokens, D)
    state_one = state_zero + low_back(jnp.dot(mixed, w_out, precision=HIGH))
    normed_two = low(rms_norm(state_one, gain_two))
    up_pre = low_back(jnp.dot(normed_two, w_up, precision=HIGH))
    state_two = state_one + low_back(jnp.dot(low(silu(up_pre)), w_down, precision=HIGH))
    head_pre = low_back(jnp.dot(low(state_two), head_in, precision=HIGH))
    head_hidden = low(silu(head_pre[:, :D] + head_bias))
    out = low_back(jnp.dot(head_hidden, head_out, precision=HIGH) + out_bias + head_pre[:, D:])
    sums = class_sums(out, target, tmask, onehot)
    return (jnp.sum((sums[0] + sums[1] / NQ) * class_weight), sums)

def adamw(weight, first, second, grad, step):
    power = step[0].astype(jnp.float32)
    first = BETA * first + (1.0 - BETA) * grad
    second = BETA * second + (1.0 - BETA) * grad * grad
    fix_one = 1.0 - jnp.power(BETA, power)
    fix_two = 1.0 - jnp.power(BETA, power)
    new = weight - RATE * (first / fix_one / (jnp.sqrt(second / fix_two) + EPSILON) + DECAY * weight)
    return (new, first, second)

def reference(series, pad_mask, freq_class, owner, step, master, moment1, moment2, small_master, small_m1, small_m2):
    rounded = master.astype(jnp.bfloat16).astype(jnp.float32)
    mats = split_rows(rounded[owner].reshape(ROWS, D))
    feat, target, tmask = prepare(series, pad_mask)
    onehot = (freq_class[:, None] == jnp.arange(NCLASS, dtype=jnp.int32)[None, :]).astype(jnp.float32)
    counts = lax.optimization_barrier(jnp.sum(onehot * lax.optimization_barrier(jnp.sum(tmask, axis=(1, 2)))[:, None], 0))
    class_weight = 1.0 / (counts * NCLASS)
    group = math.gcd(SERIES, max(1, 4096 // NPATCH))

    def one_group(carry, index):
        grads, small_grad, sums = carry
        start = (index * group).astype(jnp.int32)

        def part(array):
            return lax.dynamic_slice_in_dim(array, start, group, 0)

        def run(mat_args, small_args):
            return forward(mat_args, small_args, part(feat), part(onehot), part(target), part(tmask), class_weight)
        value, pull, part_sums = jax.vjp(run, mats, small_master, has_aux=True)
        grad_mats, grad_small = pull(jnp.ones_like(value))
        grads = jax.tree.map(lambda left, right: left + right, grads, grad_mats)
        return ((grads, small_grad + grad_small, sums + part_sums), None)
    start_carry = (jax.tree.map(jnp.zeros_like, mats), jnp.zeros_like(small_master), jnp.zeros((2, NCLASS), jnp.float32))
    (grads, small_grad, sums), _ = lax.scan(one_group, start_carry, jnp.arange(SERIES // group, dtype=jnp.int32))
    loss = jnp.sum((sums[0] + sums[1] / NQ) * class_weight)
    flat = jnp.concatenate([grad.reshape(-1, D) for grad in grads], axis=0).reshape(NBLK, BR, D)
    slot_grad = jnp.zeros((TOTAL_SLOTS, BR, D), jnp.float32).at[owner].set(flat)
    grad_norm = jnp.sqrt(jnp.sum(slot_grad * slot_grad) + jnp.sum(small_grad * small_grad))
    scale = jnp.minimum(1.0, CLIP / grad_norm)
    new_master, new_m1, new_m2 = adamw(master, moment1, moment2, slot_grad * scale, step)
    small_new, small_new_m1, small_new_m2 = adamw(small_master, small_m1, small_m2, small_grad * scale, step)
    return (loss, grad_norm, new_master, new_m1, new_m2, new_master.astype(jnp.bfloat16), small_new, small_new_m1, small_new_m2)
```

```python
import jax
import jax.numpy as jnp
from jax import lax
from jax.sharding import PartitionSpec as P

D = 1280
HEADS = 16
HDIM = 80
FF = 5120
PATCH = 32
HORIZON = 128
NQ = 9
NPATCH = 16
NCLASS = 3
BR = 64
TOTAL_SLOTS = 512
CTX = 512
OUTW = 1280
ROWS = 20608
NBLK = 322


CLIP = 0.01
RATE = 0.03
DECAY = 0.1
BETA = 0.5
EPSILON = 1e-08


def matmul(left, right):
    return jnp.dot(left, right, preferred_element_type=jnp.float32)


def tmatmul(left, right):
    return lax.dot_general(
        left, right, (((0,), (0,)), ((), ())), preferred_element_type=jnp.float32
    )


def backmul(left, right):
    return lax.dot_general(
        left, right, (((1,), (1,)), ((), ())), preferred_element_type=jnp.float32
    )


def silu(value):
    return value / (1.0 + jnp.exp(-value))


def silu_slope(value):
    sigmoid = 1.0 / (1.0 + jnp.exp(-value))
    return sigmoid * (1.0 + value * (1.0 - sigmoid))


def rms_norm(hidden, gain):
    return hidden * lax.rsqrt(jnp.mean(hidden * hidden, axis=-1, keepdims=True) + 1e-06) * gain


def tables():
    half = HDIM // 2
    inverse = jnp.power(10000.0, -2.0 * jnp.arange(half, dtype=jnp.float32) / HDIM)
    angle = jnp.arange(NPATCH, dtype=jnp.float32)[:, None] * inverse[None, :]
    return (jnp.cos(angle)[None, :, None, :], jnp.sin(angle)[None, :, None, :])


def rotate(value, cosine, sine):
    half = HDIM // 2
    first = value[..., :half]
    second = value[..., half:]
    return jnp.concatenate(
        [first * cosine - second * sine, first * sine + second * cosine], axis=-1
    )


def split_rows(flat_rows):
    shapes = (
        (2 * PATCH, 2 * D),
        (D, D),
        (D, 3 * D),
        (D, D),
        (D, FF),
        (FF, D),
        (D, D + OUTW),
        (D, OUTW),
    )
    pieces = []
    start = 0
    for first, second in shapes:
        number = first * second // D
        pieces.append(flat_rows[start : start + number].reshape(first, second))
        start += number
    return tuple(pieces)


def split_small(small):
    freq = small[: NCLASS * D].reshape(NCLASS, D)
    rest = small[NCLASS * D :]
    return (
        freq,
        rest[0:D],
        rest[D : 2 * D],
        rest[2 * D : 3 * D],
        rest[3 * D : 4 * D],
        rest[4 * D : 5 * D],
        rest[5 * D : 5 * D + OUTW],
    )


def prepare(series, pad_mask):
    valid = (1 - pad_mask).astype(jnp.float32)
    count_series = series.shape[0]
    context = (series[:, :CTX] * valid[:, :CTX]).reshape(count_series, NPATCH, PATCH)
    marks = pad_mask[:, :CTX].astype(jnp.float32).reshape(count_series, NPATCH, PATCH)
    feat = jnp.concatenate([context, marks], axis=-1)
    index = (jnp.arange(NPATCH, dtype=jnp.int32)[:, None] + 1) * PATCH + jnp.arange(
        HORIZON, dtype=jnp.int32
    )[None, :]
    return (feat, series[:, index], valid[:, index])


def class_sums(out, target, tmask, onehot):
    pred = out.reshape(onehot.shape[0], NPATCH, HORIZON, NQ + 1)
    error = pred[..., 0] - target
    square = jnp.sum(error * error * tmask, axis=(1, 2))
    levels = (jnp.arange(NQ, dtype=jnp.float32) + 1.0) / (NQ + 1)
    diff = target[..., None] - pred[..., 1:]
    pinball = jnp.sum(jnp.maximum(levels * diff, (levels - 1.0) * diff), axis=-1)
    quant = jnp.sum(pinball * tmask, axis=(1, 2))
    return jnp.stack([jnp.sum(onehot * square[:, None], 0), jnp.sum(onehot * quant[:, None], 0)])


def layer_forward(state_zero, mats, parts, cosine, sine, causal):
    w_qkv, w_out, w_up, w_down = (mats[2], mats[3], mats[4], mats[5])
    gain_one, gain_two = (parts[3], parts[4])
    count_series = state_zero.shape[0] // NPATCH
    normed_one = rms_norm(state_zero, gain_one).astype(jnp.bfloat16)
    qkv = matmul(normed_one, w_qkv).reshape(count_series, NPATCH, 3, HEADS, HDIM)
    queries = (rotate(qkv[:, :, 0], cosine, sine) * HDIM ** (-0.5)).astype(jnp.bfloat16)
    key_rot = rotate(qkv[:, :, 1], cosine, sine).astype(jnp.bfloat16)
    value_all = qkv[:, :, 2].astype(jnp.bfloat16)
    scores = jnp.einsum("sqhd,skhd->shqk", queries, key_rot, preferred_element_type=jnp.float32)
    scores = jnp.where(causal, scores, -1e30)
    peak = jnp.max(scores, axis=-1, keepdims=True)
    expo = jnp.exp(scores - peak)
    total = jnp.sum(expo, axis=-1, keepdims=True)
    log_total = peak + jnp.log(total)
    attend = (expo / total).astype(jnp.bfloat16)
    mixed = jnp.einsum("shqk,skhd->sqhd", attend, value_all, preferred_element_type=jnp.float32)
    mixed = mixed.astype(jnp.bfloat16).reshape(state_zero.shape[0], D)
    state_one = state_zero + matmul(mixed, w_out)
    normed_two = rms_norm(state_one, gain_two).astype(jnp.bfloat16)
    up_pre = matmul(normed_two, w_up)
    activ = silu(up_pre).astype(jnp.bfloat16)
    state_two = state_one + matmul(activ, w_down)
    return (
        state_two,
        (
            normed_one,
            queries,
            key_rot,
            value_all,
            log_total,
            mixed,
            state_one,
            normed_two,
            up_pre,
            activ,
        ),
    )


def layer_backward(grad_two, state_zero, kept, mats, parts, cosine, sine, causal):
    (
        normed_one,
        queries,
        key_rot,
        value_all,
        log_total,
        mixed,
        state_one,
        normed_two,
        up_pre,
        activ,
    ) = kept
    w_qkv, w_out, w_up, w_down = (mats[2], mats[3], mats[4], mats[5])
    gain_one, gain_two = (parts[3], parts[4])
    tokens = state_zero.shape[0]
    count_series = tokens // NPATCH
    grad_mlp = grad_two.astype(jnp.bfloat16)
    grad_down = tmatmul(activ, grad_mlp)
    grad_act = backmul(grad_mlp, w_down)
    grad_up_pre = (grad_act * silu_slope(up_pre)).astype(jnp.bfloat16)
    grad_up = tmatmul(normed_two, grad_up_pre)
    grad_normed = backmul(grad_up_pre, w_up)
    _, pull = jax.vjp(rms_norm, state_one, gain_two)
    grad_norm_in, grad_gain_two = pull(grad_normed)
    grad_one = grad_two + grad_norm_in
    grad_proj = grad_one.astype(jnp.bfloat16)
    grad_wout = tmatmul(mixed, grad_proj)
    grad_mixed = (
        backmul(grad_proj, w_out).astype(jnp.bfloat16).reshape(count_series, NPATCH, HEADS, HDIM)
    )
    scores = jnp.einsum("sqhd,skhd->shqk", queries, key_rot, preferred_element_type=jnp.float32)
    attend = jnp.where(causal, jnp.exp(scores - log_total), 0.0)
    grad_attend = jnp.einsum(
        "sqhd,skhd->shqk", grad_mixed, value_all, preferred_element_type=jnp.float32
    )
    grad_scores = (
        attend * (grad_attend - jnp.sum(grad_attend * attend, axis=-1, keepdims=True))
    ).astype(jnp.bfloat16)
    grad_query = jnp.einsum(
        "shqk,skhd->sqhd", grad_scores, key_rot, preferred_element_type=jnp.float32
    )
    grad_key = jnp.einsum(
        "shqk,sqhd->skhd", grad_scores, queries, preferred_element_type=jnp.float32
    )
    grad_value = jnp.einsum(
        "shqk,sqhd->skhd",
        attend.astype(jnp.bfloat16),
        grad_mixed,
        preferred_element_type=jnp.float32,
    )
    grad_qkv = jnp.stack(
        [
            rotate(grad_query, cosine, -sine) * HDIM ** (-0.5),
            rotate(grad_key, cosine, -sine),
            grad_value,
        ],
        axis=2,
    )
    grad_qkv = grad_qkv.reshape(tokens, 3 * D).astype(jnp.bfloat16)
    grad_wqkv = tmatmul(normed_one, grad_qkv)
    grad_normed_one = backmul(grad_qkv, w_qkv)
    _, pull = jax.vjp(rms_norm, state_zero, gain_one)
    grad_zero_in, grad_gain_one = pull(grad_normed_one)
    return (
        grad_one + grad_zero_in,
        (grad_wqkv, grad_wout, grad_up, grad_down),
        grad_gain_one,
        grad_gain_two,
    )


def adamw(weight, first, second, grad, step):
    power = step[0].astype(jnp.float32)
    first = BETA * first + (1.0 - BETA) * grad
    second = BETA * second + (1.0 - BETA) * grad * grad
    fix_one = 1.0 - jnp.power(BETA, power)
    fix_two = 1.0 - jnp.power(BETA, power)
    new = weight - RATE * (
        first / fix_one / (jnp.sqrt(second / fix_two) + EPSILON) + DECAY * weight
    )
    return (new, first, second)


def on_device(
    series,
    pad_mask,
    freq_class,
    owner,
    step,
    master,
    moment1,
    moment2,
    small_master,
    small_m1,
    small_m2,
):
    slot_count = master.shape[0]
    gathered = lax.all_gather(master.astype(jnp.bfloat16), ("wide", "narrow"), axis=0, tiled=True)
    mats = split_rows(gathered[owner].reshape(ROWS, D))
    tok_in, tok_out, head_in, head_out = (mats[0], mats[1], mats[6], mats[7])
    parts = split_small(small_master)
    freq, bias_one, bias_two, head_bias, out_bias = (
        parts[0],
        parts[1],
        parts[2],
        parts[5],
        parts[6],
    )
    feat, target, tmask = prepare(series, pad_mask)
    count_series = series.shape[0]
    tokens = count_series * NPATCH
    onehot = (freq_class[:, None] == jnp.arange(NCLASS, dtype=jnp.int32)[None, :]).astype(
        jnp.float32
    )
    local_counts = jnp.sum(onehot * jnp.sum(tmask, axis=(1, 2))[:, None], 0)
    counts = lax.psum(local_counts, ("wide", "narrow"))
    class_weight = 1.0 / (counts * NCLASS)
    cosine, sine = tables()
    causal = jnp.arange(NPATCH)[:, None] >= jnp.arange(NPATCH)[None, :]
    patch_in = feat.reshape(tokens, 2 * PATCH).astype(jnp.bfloat16)
    tok_pre = matmul(patch_in, tok_in)
    hidden = silu(tok_pre[:, :D] + bias_one).astype(jnp.bfloat16)
    class_rows = jnp.repeat(jnp.dot(onehot, freq, precision=lax.Precision.HIGHEST), NPATCH, axis=0)
    state_zero = matmul(hidden, tok_out) + bias_two + tok_pre[:, D:] + class_rows
    state_two, _ = layer_forward(state_zero, mats, parts, cosine, sine, causal)
    state_low = state_two.astype(jnp.bfloat16)
    head_pre = matmul(state_low, head_in)
    head_hidden = silu(head_pre[:, :D] + head_bias).astype(jnp.bfloat16)
    out = matmul(head_hidden, head_out) + out_bias + head_pre[:, D:]

    def loss_of(value):
        sums_here = class_sums(value, target, tmask, onehot)
        return (jnp.sum((sums_here[0] + sums_here[1] / NQ) * class_weight), sums_here)

    _, pull, local_sums = jax.vjp(loss_of, out, has_aux=True)
    (grad_out,) = pull(jnp.ones((), jnp.float32))
    sums = lax.psum(local_sums, ("wide", "narrow"))
    grad_out = grad_out.astype(jnp.bfloat16)
    grad_out_bias = jnp.sum(grad_out.astype(jnp.float32), axis=0)
    grad_head_out = tmatmul(head_hidden, grad_out)
    grad_head_first = backmul(grad_out, head_out) * silu_slope(head_pre[:, :D] + head_bias)
    grad_head_bias = jnp.sum(grad_head_first, axis=0)
    grad_head_pre = jnp.concatenate([grad_head_first, grad_out.astype(jnp.float32)], axis=1).astype(
        jnp.bfloat16
    )
    grad_head_in = tmatmul(state_low, grad_head_pre)
    grad_two = backmul(grad_head_pre, head_in)
    _, kept = layer_forward(state_zero, mats, parts, cosine, sine, causal)
    grad_zero, layer_grads, grad_gain_one, grad_gain_two = layer_backward(
        grad_two, state_zero, kept, mats, parts, cosine, sine, causal
    )
    grad_prod = grad_zero.astype(jnp.bfloat16)
    grad_tok_out = tmatmul(hidden, grad_prod)
    grad_first = backmul(grad_prod, tok_out) * silu_slope(tok_pre[:, :D] + bias_one)
    grad_tok_pre = jnp.concatenate([grad_first, grad_zero], axis=1).astype(jnp.bfloat16)
    grad_tok_in = tmatmul(patch_in, grad_tok_pre)
    grad_freq = jnp.dot(
        onehot.T,
        grad_zero.reshape(count_series, NPATCH, D).sum(axis=1),
        precision=lax.Precision.HIGHEST,
    )
    small_local = jnp.concatenate(
        [
            grad_freq.reshape(-1),
            jnp.sum(grad_first, axis=0),
            jnp.sum(grad_zero, axis=0),
            grad_gain_one,
            grad_gain_two,
            grad_head_bias,
            grad_out_bias,
        ]
    )
    small_grad = lax.psum(small_local, ("wide", "narrow"))
    grad_list = (grad_tok_in, grad_tok_out) + tuple(layer_grads) + (grad_head_in, grad_head_out)
    grad_blocks = jnp.concatenate(
        [piece.astype(jnp.bfloat16).reshape(-1, D) for piece in grad_list], axis=0
    ).reshape(NBLK, BR, D)
    inverse = (
        jnp.full((TOTAL_SLOTS,), NBLK, jnp.int32).at[owner].set(jnp.arange(NBLK, dtype=jnp.int32))
    )
    picked = grad_blocks[jnp.minimum(inverse, NBLK - 1)]
    slot_buffer = jnp.where((inverse < NBLK)[:, None, None], picked, 0.0).astype(jnp.bfloat16)
    partial_value = lax.psum_scatter(slot_buffer, "wide", scatter_dimension=0, tiled=True)
    owned = lax.psum_scatter(
        partial_value.astype(jnp.float32), "narrow", scatter_dimension=0, tiled=True
    )
    local_square = jnp.sum(owned * owned)
    square_total = lax.psum(local_square, ("wide", "narrow"))
    grad_norm = jnp.sqrt(square_total + jnp.sum(small_grad * small_grad))
    scale = jnp.minimum(1.0, CLIP / grad_norm)
    loss = jnp.sum((sums[0] + sums[1] / NQ) * class_weight)
    new_master, new_m1, new_m2 = adamw(master, moment1, moment2, owned * scale, step)
    small_new, small_new_m1, small_new_m2 = adamw(
        small_master, small_m1, small_m2, small_grad * scale, step
    )
    return (
        loss,
        grad_norm,
        new_master,
        new_m1,
        new_m2,
        new_master.astype(jnp.bfloat16),
        small_new,
        small_new_m1,
        small_new_m2,
    )


def solution(mesh):
    return jax.shard_map(
        on_device,
        mesh=mesh,
        in_specs=(
            P(("wide", "narrow"), None),
            P(("wide", "narrow"), None),
            P(("wide", "narrow")),
            P(),
            P(),
            P(("wide", "narrow"), None, None),
            P(("wide", "narrow"), None, None),
            P(("wide", "narrow"), None, None),
            P(),
            P(),
            P(),
        ),
        out_specs=(
            P(),
            P(),
            P(("wide", "narrow"), None, None),
            P(("wide", "narrow"), None, None),
            P(("wide", "narrow"), None, None),
            P(("wide", "narrow"), None, None),
            P(),
            P(),
            P(),
        ),
        check_vma=False,
    )
```

```python
import functools

import jax
import jax.numpy as jnp
from jax import lax
from jax.experimental import pallas as pl
from jax.experimental.pallas import tpu as pltpu
from jax.sharding import PartitionSpec as P

D = 1280
HEADS = 16
HDIM = 80
FF = 5120
PATCH = 32
HORIZON = 128
NQ = 9
NPATCH = 16
NCLASS = 3
BR = 64
TOTAL_SLOTS = 512
CTX = 512
OUTW = 1280
ROWS = 20608
NBLK = 322


CLIP = 0.01
RATE = 0.03
DECAY = 0.1
BETA = 0.5
EPSILON = 1e-08


def matmul(left, right):
    return jnp.dot(left, right, preferred_element_type=jnp.float32)


def tmatmul(left, right):
    return lax.dot_general(
        left, right, (((0,), (0,)), ((), ())), preferred_element_type=jnp.float32
    )


def backmul(left, right):
    return lax.dot_general(
        left, right, (((1,), (1,)), ((), ())), preferred_element_type=jnp.float32
    )


def silu(value):
    return value / (1.0 + jnp.exp(-value))


def silu_slope(value):
    sigmoid = 1.0 / (1.0 + jnp.exp(-value))
    return sigmoid * (1.0 + value * (1.0 - sigmoid))


def rms_norm(hidden, gain):
    return hidden * lax.rsqrt(jnp.mean(hidden * hidden, axis=-1, keepdims=True) + 1e-06) * gain


def tables():
    half = HDIM // 2
    inverse = jnp.power(10000.0, -2.0 * jnp.arange(half, dtype=jnp.float32) / HDIM)
    angle = jnp.arange(NPATCH, dtype=jnp.float32)[:, None] * inverse[None, :]
    return (jnp.cos(angle)[None, :, None, :], jnp.sin(angle)[None, :, None, :])


def rotate(value, cosine, sine):
    half = HDIM // 2
    first = value[..., :half]
    second = value[..., half:]
    return jnp.concatenate(
        [first * cosine - second * sine, first * sine + second * cosine], axis=-1
    )


MATS = (
    (2 * PATCH, 2, 2),
    (D, 1, 4),
    (D, 3, 6),
    (D, 1, 4),
    (D, FF // D, 8),
    (FF, 1, 8),
    (D, (D + OUTW) // D, 4),
    (D, 1, 4),
)
BASES = tuple(sum(r * g for r, g, _ in MATS[:i]) // BR for i in range(len(MATS)))
LANES = 128
VMEM_LIMIT = 56 * 1024 * 1024


def unpack_kernel(groups, count, owner_ref, *refs):
    out_ref = refs[count]
    if groups == 1:
        for b in range(count):
            out_ref[b * BR : (b + 1) * BR, :] = refs[b][...]
        return
    wide_ref = refs[count + 1]
    for b in range(count):
        for c in range(D // LANES):
            wide_ref[c, b * BR : (b + 1) * BR, :] = refs[b][
                :, c * LANES : (c + 1) * LANES
            ].astype(jnp.float32)
    rows = count * BR // groups
    for j in range(groups):
        for c in range(D // LANES):
            at = j * D + c * LANES
            out_ref[:, at : at + LANES] = wide_ref[c, pl.ds(j, rows, stride=groups), :].astype(
                jnp.bfloat16
            )


def unpack(gathered, owner, which):
    total, groups, count = MATS[which]
    base = BASES[which]
    rows = count * BR // groups

    def spec(b):
        return pl.BlockSpec(
            (None, BR, D), lambda i, own, b=b: (own[base + i * count + b], 0, 0)
        )

    return pl.pallas_call(
        functools.partial(unpack_kernel, groups, count),
        out_shape=jax.ShapeDtypeStruct((total, groups * D), jnp.bfloat16),
        grid_spec=pltpu.PrefetchScalarGridSpec(
            num_scalar_prefetch=1,
            grid=(total // rows,),
            in_specs=[spec(b) for b in range(count)],
            out_specs=pl.BlockSpec((rows, groups * D), lambda i, own: (i, 0)),
            scratch_shapes=[]
            if groups == 1
            else [pltpu.VMEM((D // LANES, count * BR, LANES), jnp.float32)],
        ),
        compiler_params=pltpu.CompilerParams(vmem_limit_bytes=VMEM_LIMIT),
        cost_estimate=pl.CostEstimate(
            flops=0, bytes_accessed=4 * total * groups * D, transcendentals=0
        ),
        name=f"unpack_{which}",
    )(owner, *([gathered] * count))


def grad_kernel(groups, count, base, steps, owner_ref, left_ref, right_ref, *refs):
    out_ref, stage_ref, sems = refs[-3 - (groups > 1)], refs[-2 - (groups > 1)], refs[-1 - (groups > 1)]
    step = pl.program_id(0)
    slot = lax.rem(step, 2)
    rows = count * BR // groups

    def copy(at, b, when):
        return pltpu.make_async_copy(
            stage_ref.at[at, pl.ds(b * BR, BR), :],
            out_ref.at[owner_ref[base + when * count + b]],
            sems.at[at, b],
        )

    @pl.when(step >= 2)
    def _():
        for b in range(count):
            copy(slot, b, step - 2).wait()

    left = left_ref[...]
    for j in range(groups):
        part = tmatmul(left, right_ref[:, j * D : (j + 1) * D])
        if groups == 1:
            stage_ref[slot] = part.astype(jnp.bfloat16)
        else:
            for c in range(D // LANES):
                refs[-1][c, pl.ds(j, rows, stride=groups), :] = part[
                    :, c * LANES : (c + 1) * LANES
                ]
    if groups > 1:
        for c in range(D // LANES):
            stage_ref[slot, :, c * LANES : (c + 1) * LANES] = refs[-1][c].astype(jnp.bfloat16)
    for b in range(count):
        copy(slot, b, step).start()

    @pl.when(step == steps - 1)
    def _():
        for b in range(count):
            copy(slot, b, step).wait()

    if steps > 1:

        @pl.when(step == steps - 1)
        def _():
            for b in range(count):
                copy(1 - slot, b, step - 1).wait()


def grad_blocks(left, right, owner, which, slots):
    total, groups, count = MATS[which]
    rows = count * BR // groups
    steps = total // rows
    tokens = left.shape[0]
    scratch = [
        pltpu.VMEM((2, count * BR, D), jnp.bfloat16),
        pltpu.SemaphoreType.DMA((2, count)),
    ]
    if groups > 1:
        scratch.append(pltpu.VMEM((D // LANES, count * BR, LANES), jnp.float32))
    held = [] if slots is None else [slots]
    return pl.pallas_call(
        functools.partial(grad_kernel, groups, count, BASES[which], steps),
        out_shape=jax.ShapeDtypeStruct((TOTAL_SLOTS, BR, D), jnp.bfloat16),
        grid_spec=pltpu.PrefetchScalarGridSpec(
            num_scalar_prefetch=1,
            grid=(steps,),
            in_specs=[
                pl.BlockSpec((tokens, rows), lambda i, own: (0, i)),
                pl.BlockSpec((tokens, groups * D), lambda i, own: (0, 0)),
            ]
            + [pl.BlockSpec(memory_space=pl.ANY)] * len(held),
            out_specs=pl.BlockSpec(memory_space=pl.ANY),
            scratch_shapes=scratch,
        ),
        input_output_aliases={3: 0} if held else {},
        compiler_params=pltpu.CompilerParams(vmem_limit_bytes=VMEM_LIMIT),
        cost_estimate=pl.CostEstimate(
            flops=2 * tokens * total * groups * D,
            bytes_accessed=2 * total * groups * D,
            transcendentals=0,
        ),
        name=f"grad_{which}",
    )(owner, left, right, *held)


def split_small(small):
    freq = small[: NCLASS * D].reshape(NCLASS, D)
    rest = small[NCLASS * D :]
    return (
        freq,
        rest[0:D],
        rest[D : 2 * D],
        rest[2 * D : 3 * D],
        rest[3 * D : 4 * D],
        rest[4 * D : 5 * D],
        rest[5 * D : 5 * D + OUTW],
    )


def prepare(series, pad_mask):
    valid = (1 - pad_mask).astype(jnp.float32)
    count_series = series.shape[0]
    context = (series[:, :CTX] * valid[:, :CTX]).reshape(count_series, NPATCH, PATCH)
    marks = pad_mask[:, :CTX].astype(jnp.float32).reshape(count_series, NPATCH, PATCH)
    feat = jnp.concatenate([context, marks], axis=-1)
    index = (jnp.arange(NPATCH, dtype=jnp.int32)[:, None] + 1) * PATCH + jnp.arange(
        HORIZON, dtype=jnp.int32
    )[None, :]
    return (feat, series[:, index], valid[:, index])


def class_sums(out, target, tmask, onehot):
    pred = out.reshape(onehot.shape[0], NPATCH, HORIZON, NQ + 1)
    error = pred[..., 0] - target
    square = jnp.sum(error * error * tmask, axis=(1, 2))
    levels = (jnp.arange(NQ, dtype=jnp.float32) + 1.0) / (NQ + 1)
    diff = target[..., None] - pred[..., 1:]
    pinball = jnp.sum(jnp.maximum(levels * diff, (levels - 1.0) * diff), axis=-1)
    quant = jnp.sum(pinball * tmask, axis=(1, 2))
    return jnp.stack([jnp.sum(onehot * square[:, None], 0), jnp.sum(onehot * quant[:, None], 0)])


def layer_forward(state_zero, mats, parts, cosine, sine, causal):
    w_qkv, w_out, w_up, w_down = (mats[2], mats[3], mats[4], mats[5])
    gain_one, gain_two = (parts[3], parts[4])
    count_series = state_zero.shape[0] // NPATCH
    normed_one = rms_norm(state_zero, gain_one).astype(jnp.bfloat16)
    qkv = matmul(normed_one, w_qkv).reshape(count_series, NPATCH, 3, HEADS, HDIM)
    queries = (rotate(qkv[:, :, 0], cosine, sine) * HDIM ** (-0.5)).astype(jnp.bfloat16)
    key_rot = rotate(qkv[:, :, 1], cosine, sine).astype(jnp.bfloat16)
    value_all = qkv[:, :, 2].astype(jnp.bfloat16)
    scores = jnp.einsum("sqhd,skhd->shqk", queries, key_rot, preferred_element_type=jnp.float32)
    scores = jnp.where(causal, scores, -1e30)
    peak = jnp.max(scores, axis=-1, keepdims=True)
    expo = jnp.exp(scores - peak)
    total = jnp.sum(expo, axis=-1, keepdims=True)
    log_total = peak + jnp.log(total)
    attend = (expo / total).astype(jnp.bfloat16)
    mixed = jnp.einsum("shqk,skhd->sqhd", attend, value_all, preferred_element_type=jnp.float32)
    mixed = mixed.astype(jnp.bfloat16).reshape(state_zero.shape[0], D)
    state_one = state_zero + matmul(mixed, w_out)
    normed_two = rms_norm(state_one, gain_two).astype(jnp.bfloat16)
    up_pre = matmul(normed_two, w_up)
    activ = silu(up_pre).astype(jnp.bfloat16)
    state_two = state_one + matmul(activ, w_down)
    return (
        state_two,
        (
            normed_one,
            queries,
            key_rot,
            value_all,
            log_total,
            mixed,
            state_one,
            normed_two,
            up_pre,
            activ,
        ),
    )


def layer_backward(
    grad_two, state_zero, kept, mats, parts, cosine, sine, causal, owner, slots
):
    (
        normed_one,
        queries,
        key_rot,
        value_all,
        log_total,
        mixed,
        state_one,
        normed_two,
        up_pre,
        activ,
    ) = kept
    w_qkv, w_out, w_up, w_down = (mats[2], mats[3], mats[4], mats[5])
    gain_one, gain_two = (parts[3], parts[4])
    tokens = state_zero.shape[0]
    count_series = tokens // NPATCH
    grad_mlp = grad_two.astype(jnp.bfloat16)
    slots = grad_blocks(activ, grad_mlp, owner, 5, slots)
    grad_act = backmul(grad_mlp, w_down)
    grad_up_pre = (grad_act * silu_slope(up_pre)).astype(jnp.bfloat16)
    slots = grad_blocks(normed_two, grad_up_pre, owner, 4, slots)
    grad_normed = backmul(grad_up_pre, w_up)
    _, pull = jax.vjp(rms_norm, state_one, gain_two)
    grad_norm_in, grad_gain_two = pull(grad_normed)
    grad_one = grad_two + grad_norm_in
    grad_proj = grad_one.astype(jnp.bfloat16)
    slots = grad_blocks(mixed, grad_proj, owner, 3, slots)
    grad_mixed = (
        backmul(grad_proj, w_out).astype(jnp.bfloat16).reshape(count_series, NPATCH, HEADS, HDIM)
    )
    scores = jnp.einsum("sqhd,skhd->shqk", queries, key_rot, preferred_element_type=jnp.float32)
    attend = jnp.where(causal, jnp.exp(scores - log_total), 0.0)
    grad_attend = jnp.einsum(
        "sqhd,skhd->shqk", grad_mixed, value_all, preferred_element_type=jnp.float32
    )
    grad_scores = (
        attend * (grad_attend - jnp.sum(grad_attend * attend, axis=-1, keepdims=True))
    ).astype(jnp.bfloat16)
    grad_query = jnp.einsum(
        "shqk,skhd->sqhd", grad_scores, key_rot, preferred_element_type=jnp.float32
    )
    grad_key = jnp.einsum(
        "shqk,sqhd->skhd", grad_scores, queries, preferred_element_type=jnp.float32
    )
    grad_value = jnp.einsum(
        "shqk,sqhd->skhd",
        attend.astype(jnp.bfloat16),
        grad_mixed,
        preferred_element_type=jnp.float32,
    )
    grad_qkv = jnp.stack(
        [
            rotate(grad_query, cosine, -sine) * HDIM ** (-0.5),
            rotate(grad_key, cosine, -sine),
            grad_value,
        ],
        axis=2,
    )
    grad_qkv = grad_qkv.reshape(tokens, 3 * D).astype(jnp.bfloat16)
    slots = grad_blocks(normed_one, grad_qkv, owner, 2, slots)
    grad_normed_one = backmul(grad_qkv, w_qkv)
    _, pull = jax.vjp(rms_norm, state_zero, gain_one)
    grad_zero_in, grad_gain_one = pull(grad_normed_one)
    return (
        grad_one + grad_zero_in,
        slots,
        grad_gain_one,
        grad_gain_two,
    )


def adamw(weight, first, second, grad, step):
    power = step[0].astype(jnp.float32)
    first = BETA * first + (1.0 - BETA) * grad
    second = BETA * second + (1.0 - BETA) * grad * grad
    fix_one = 1.0 - jnp.power(BETA, power)
    fix_two = 1.0 - jnp.power(BETA, power)
    new = weight - RATE * (
        first / fix_one / (jnp.sqrt(second / fix_two) + EPSILON) + DECAY * weight
    )
    return (new, first, second)


def on_device(
    series,
    pad_mask,
    freq_class,
    owner,
    step,
    master,
    moment1,
    moment2,
    small_master,
    small_m1,
    small_m2,
):
    slot_count = master.shape[0]
    gathered = lax.all_gather(master.astype(jnp.bfloat16), ("wide", "narrow"), axis=0, tiled=True)
    mats = tuple(unpack(gathered, owner, which) for which in range(len(MATS)))
    tok_in, tok_out, head_in, head_out = (mats[0], mats[1], mats[6], mats[7])
    parts = split_small(small_master)
    freq, bias_one, bias_two, head_bias, out_bias = (
        parts[0],
        parts[1],
        parts[2],
        parts[5],
        parts[6],
    )
    feat, target, tmask = prepare(series, pad_mask)
    count_series = series.shape[0]
    tokens = count_series * NPATCH
    onehot = (freq_class[:, None] == jnp.arange(NCLASS, dtype=jnp.int32)[None, :]).astype(
        jnp.float32
    )
    local_counts = jnp.sum(onehot * jnp.sum(tmask, axis=(1, 2))[:, None], 0)
    counts = lax.psum(local_counts, ("wide", "narrow"))
    class_weight = 1.0 / (counts * NCLASS)
    cosine, sine = tables()
    causal = jnp.arange(NPATCH)[:, None] >= jnp.arange(NPATCH)[None, :]
    patch_in = feat.reshape(tokens, 2 * PATCH).astype(jnp.bfloat16)
    tok_pre = matmul(patch_in, tok_in)
    hidden = silu(tok_pre[:, :D] + bias_one).astype(jnp.bfloat16)
    class_rows = jnp.repeat(jnp.dot(onehot, freq, precision=lax.Precision.HIGHEST), NPATCH, axis=0)
    state_zero = matmul(hidden, tok_out) + bias_two + tok_pre[:, D:] + class_rows
    state_two, _ = layer_forward(state_zero, mats, parts, cosine, sine, causal)
    state_low = state_two.astype(jnp.bfloat16)
    head_pre = matmul(state_low, head_in)
    head_hidden = silu(head_pre[:, :D] + head_bias).astype(jnp.bfloat16)
    out = matmul(head_hidden, head_out) + out_bias + head_pre[:, D:]

    def loss_of(value):
        sums_here = class_sums(value, target, tmask, onehot)
        return (jnp.sum((sums_here[0] + sums_here[1] / NQ) * class_weight), sums_here)

    _, pull, local_sums = jax.vjp(loss_of, out, has_aux=True)
    (grad_out,) = pull(jnp.ones((), jnp.float32))
    sums = lax.psum(local_sums, ("wide", "narrow"))
    grad_out = grad_out.astype(jnp.bfloat16)
    grad_out_bias = jnp.sum(grad_out.astype(jnp.float32), axis=0)
    slots = grad_blocks(head_hidden, grad_out, owner, 7, None)
    grad_head_first = backmul(grad_out, head_out) * silu_slope(head_pre[:, :D] + head_bias)
    grad_head_bias = jnp.sum(grad_head_first, axis=0)
    grad_head_pre = jnp.concatenate([grad_head_first, grad_out.astype(jnp.float32)], axis=1).astype(
        jnp.bfloat16
    )
    slots = grad_blocks(state_low, grad_head_pre, owner, 6, slots)
    grad_two = backmul(grad_head_pre, head_in)
    _, kept = layer_forward(state_zero, mats, parts, cosine, sine, causal)
    grad_zero, slots, grad_gain_one, grad_gain_two = layer_backward(
        grad_two, state_zero, kept, mats, parts, cosine, sine, causal, owner, slots
    )
    grad_prod = grad_zero.astype(jnp.bfloat16)
    slots = grad_blocks(hidden, grad_prod, owner, 1, slots)
    grad_first = backmul(grad_prod, tok_out) * silu_slope(tok_pre[:, :D] + bias_one)
    grad_tok_pre = jnp.concatenate([grad_first, grad_zero], axis=1).astype(jnp.bfloat16)
    slots = grad_blocks(patch_in, grad_tok_pre, owner, 0, slots)
    grad_freq = jnp.dot(
        onehot.T,
        grad_zero.reshape(count_series, NPATCH, D).sum(axis=1),
        precision=lax.Precision.HIGHEST,
    )
    small_local = jnp.concatenate(
        [
            grad_freq.reshape(-1),
            jnp.sum(grad_first, axis=0),
            jnp.sum(grad_zero, axis=0),
            grad_gain_one,
            grad_gain_two,
            grad_head_bias,
            grad_out_bias,
        ]
    )
    small_grad = lax.psum(small_local, ("wide", "narrow"))
    partial_value = lax.psum_scatter(slots, "wide", scatter_dimension=0, tiled=True)
    owned = lax.psum_scatter(partial_value, "narrow", scatter_dimension=0, tiled=True)
    rank = lax.axis_index("wide") * lax.axis_size("narrow") + lax.axis_index("narrow")
    mine = rank * slot_count + jnp.arange(slot_count, dtype=jnp.int32)
    filled = jnp.any(owner[:, None] == mine[None, :], axis=0)
    owned = jnp.where(filled[:, None, None], owned.astype(jnp.float32), 0.0)
    local_square = jnp.sum(owned * owned)
    square_total = lax.psum(local_square, ("wide", "narrow"))
    grad_norm = jnp.sqrt(square_total + jnp.sum(small_grad * small_grad))
    scale = jnp.minimum(1.0, CLIP / grad_norm)
    loss = jnp.sum((sums[0] + sums[1] / NQ) * class_weight)
    new_master, new_m1, new_m2 = adamw(master, moment1, moment2, owned * scale, step)
    small_new, small_new_m1, small_new_m2 = adamw(
        small_master, small_m1, small_m2, small_grad * scale, step
    )
    return (
        loss,
        grad_norm,
        new_master,
        new_m1,
        new_m2,
        new_master.astype(jnp.bfloat16),
        small_new,
        small_new_m1,
        small_new_m2,
    )


def solution(mesh):
    return jax.shard_map(
        on_device,
        mesh=mesh,
        in_specs=(
            P(("wide", "narrow"), None),
            P(("wide", "narrow"), None),
            P(("wide", "narrow")),
            P(),
            P(),
            P(("wide", "narrow"), None, None),
            P(("wide", "narrow"), None, None),
            P(("wide", "narrow"), None, None),
            P(),
            P(),
            P(),
        ),
        out_specs=(
            P(),
            P(),
            P(("wide", "narrow"), None, None),
            P(("wide", "narrow"), None, None),
            P(("wide", "narrow"), None, None),
            P(("wide", "narrow"), None, None),
            P(),
            P(),
            P(),
        ),
        check_vma=False,
    )
```

```python
import functools

import jax
import jax.numpy as jnp
from jax import lax
from jax.experimental import pallas as pl
from jax.experimental.pallas import tpu as pltpu
from jax.sharding import PartitionSpec as P

D = 1280
HEADS = 16
HDIM = 80
FF = 5120
PATCH = 32
HORIZON = 128
NQ = 9
NPATCH = 16
NCLASS = 3
BR = 64
TOTAL_SLOTS = 512
CTX = 512
OUTW = 1280
ROWS = 20608
NBLK = 322


CLIP = 0.01
RATE = 0.03
DECAY = 0.1
BETA = 0.5
EPSILON = 1e-08


def matmul(left, right):
    return jnp.dot(left, right, preferred_element_type=jnp.float32)


def tmatmul(left, right):
    return lax.dot_general(
        left, right, (((0,), (0,)), ((), ())), preferred_element_type=jnp.float32
    )


def backmul(left, right):
    return lax.dot_general(
        left, right, (((1,), (1,)), ((), ())), preferred_element_type=jnp.float32
    )


def silu(value):
    return value / (1.0 + jnp.exp(-value))


def silu_slope(value):
    sigmoid = 1.0 / (1.0 + jnp.exp(-value))
    return sigmoid * (1.0 + value * (1.0 - sigmoid))


def rms_norm(hidden, gain):
    return hidden * lax.rsqrt(jnp.mean(hidden * hidden, axis=-1, keepdims=True) + 1e-06) * gain


def tables():
    half = HDIM // 2
    inverse = jnp.power(10000.0, -2.0 * jnp.arange(half, dtype=jnp.float32) / HDIM)
    angle = jnp.arange(NPATCH, dtype=jnp.float32)[:, None] * inverse[None, :]
    return (jnp.cos(angle)[None, :, None, :], jnp.sin(angle)[None, :, None, :])


def rotate(value, cosine, sine):
    half = HDIM // 2
    first = value[..., :half]
    second = value[..., half:]
    return jnp.concatenate(
        [first * cosine - second * sine, first * sine + second * cosine], axis=-1
    )


MATS = (
    (2 * PATCH, 2, 2),
    (D, 1, 4),
    (D, 3, 6),
    (D, 1, 4),
    (D, FF // D, 8),
    (FF, 1, 8),
    (D, (D + OUTW) // D, 4),
    (D, 1, 4),
)
BASES = tuple(sum(r * g for r, g, _ in MATS[:i]) // BR for i in range(len(MATS)))
LANES = 128
VMEM_LIMIT = 56 * 1024 * 1024


def unpack_kernel(groups, count, owner_ref, *refs):
    out_ref = refs[count]
    if groups == 1:
        for b in range(count):
            out_ref[b * BR : (b + 1) * BR, :] = refs[b][...]
        return
    wide_ref = refs[count + 1]
    for b in range(count):
        for c in range(D // LANES):
            wide_ref[c, b * BR : (b + 1) * BR, :] = refs[b][
                :, c * LANES : (c + 1) * LANES
            ].astype(jnp.float32)
    rows = count * BR // groups
    for j in range(groups):
        for c in range(D // LANES):
            at = j * D + c * LANES
            out_ref[:, at : at + LANES] = wide_ref[c, pl.ds(j, rows, stride=groups), :].astype(
                jnp.bfloat16
            )


def unpack(gathered, owner, which):
    total, groups, count = MATS[which]
    base = BASES[which]
    rows = count * BR // groups

    def spec(b):
        return pl.BlockSpec(
            (None, BR, D), lambda i, own, b=b: (own[base + i * count + b], 0, 0)
        )

    return pl.pallas_call(
        functools.partial(unpack_kernel, groups, count),
        out_shape=jax.ShapeDtypeStruct((total, groups * D), jnp.bfloat16),
        grid_spec=pltpu.PrefetchScalarGridSpec(
            num_scalar_prefetch=1,
            grid=(total // rows,),
            in_specs=[spec(b) for b in range(count)],
            out_specs=pl.BlockSpec((rows, groups * D), lambda i, own: (i, 0)),
            scratch_shapes=[]
            if groups == 1
            else [pltpu.VMEM((D // LANES, count * BR, LANES), jnp.float32)],
        ),
        compiler_params=pltpu.CompilerParams(vmem_limit_bytes=VMEM_LIMIT),
        cost_estimate=pl.CostEstimate(
            flops=0, bytes_accessed=4 * total * groups * D, transcendentals=0
        ),
        name=f"unpack_{which}",
    )(owner, *([gathered] * count))


def grad_kernel(groups, count, base, steps, owner_ref, left_ref, right_ref, *refs):
    out_ref, stage_ref, sems = refs[-3 - (groups > 1)], refs[-2 - (groups > 1)], refs[-1 - (groups > 1)]
    step = pl.program_id(0)
    slot = lax.rem(step, 2)
    rows = count * BR // groups

    def copy(at, b, when):
        return pltpu.make_async_copy(
            stage_ref.at[at, pl.ds(b * BR, BR), :],
            out_ref.at[owner_ref[base + when * count + b]],
            sems.at[at, b],
        )

    @pl.when(step >= 2)
    def _():
        for b in range(count):
            copy(slot, b, step - 2).wait()

    left = left_ref[...]
    for j in range(groups):
        part = tmatmul(left, right_ref[:, j * D : (j + 1) * D])
        if groups == 1:
            stage_ref[slot] = part.astype(jnp.bfloat16)
        else:
            for c in range(D // LANES):
                refs[-1][c, pl.ds(j, rows, stride=groups), :] = part[
                    :, c * LANES : (c + 1) * LANES
                ]
    if groups > 1:
        for c in range(D // LANES):
            stage_ref[slot, :, c * LANES : (c + 1) * LANES] = refs[-1][c].astype(jnp.bfloat16)
    for b in range(count):
        copy(slot, b, step).start()

    @pl.when(step == steps - 1)
    def _():
        for b in range(count):
            copy(slot, b, step).wait()

    if steps > 1:

        @pl.when(step == steps - 1)
        def _():
            for b in range(count):
                copy(1 - slot, b, step - 1).wait()


def grad_blocks(left, right, owner, which, slots):
    total, groups, count = MATS[which]
    rows = count * BR // groups
    steps = total // rows
    tokens = left.shape[0]
    scratch = [
        pltpu.VMEM((2, count * BR, D), jnp.bfloat16),
        pltpu.SemaphoreType.DMA((2, count)),
    ]
    if groups > 1:
        scratch.append(pltpu.VMEM((D // LANES, count * BR, LANES), jnp.float32))
    held = [] if slots is None else [slots]
    return pl.pallas_call(
        functools.partial(grad_kernel, groups, count, BASES[which], steps),
        out_shape=jax.ShapeDtypeStruct((TOTAL_SLOTS, BR, D), jnp.bfloat16),
        grid_spec=pltpu.PrefetchScalarGridSpec(
            num_scalar_prefetch=1,
            grid=(steps,),
            in_specs=[
                pl.BlockSpec((tokens, rows), lambda i, own: (0, i)),
                pl.BlockSpec((tokens, groups * D), lambda i, own: (0, 0)),
            ]
            + [pl.BlockSpec(memory_space=pl.ANY)] * len(held),
            out_specs=pl.BlockSpec(memory_space=pl.ANY),
            scratch_shapes=scratch,
        ),
        input_output_aliases={3: 0} if held else {},
        compiler_params=pltpu.CompilerParams(vmem_limit_bytes=VMEM_LIMIT),
        cost_estimate=pl.CostEstimate(
            flops=2 * tokens * total * groups * D,
            bytes_accessed=2 * total * groups * D,
            transcendentals=0,
        ),
        name=f"grad_{which}",
    )(owner, left, right, *held)


CHUNKS = 16
STEPS = CHUNKS + 7
MESH = pl.DeviceIdType.MESH


def total_of(*blocks):
    result = blocks[0].astype(jnp.float32)
    for block in blocks[1:]:
        result = result + block.astype(jnp.float32)
    return result


def scatter_kernel(
    slots_ref,
    out_ref,
    own,
    pair_in,
    pair_sum,
    first_in,
    second_in,
    second_out,
    column,
    up_in,
    down_in,
    up_out,
    down_out,
    result,
    own_sem,
    pair_send,
    pair_recv,
    first_send,
    first_recv,
    second_send,
    second_recv,
    up_send,
    up_recv,
    down_send,
    down_recv,
    result_sem,
):
    wide, z = lax.axis_index("wide"), lax.axis_index("narrow")
    core, here = lax.rem(wide, 2), lax.div(wide, 2)
    x, y = lax.rem(here, 2), lax.div(here, 2)
    far = 3 - here

    def device(place, level):
        return (place * 2 + core, level)

    partner = (here * 2 + 1 - core, z)

    def near(k, which):
        along_y = lax.rem(k + which, 2)
        return (y + along_y - 2 * y * along_y) * 2 + (x + (1 - along_y) - 2 * x * (1 - along_y))

    barrier = pltpu.get_barrier_semaphore()
    pl.semaphore_signal(barrier, inc=1, device_id=partner, device_id_type=MESH)
    for which in range(2):
        pl.semaphore_signal(
            barrier, inc=1, device_id=device(near(0, which), z), device_id_type=MESH
        )

    @pl.when(z > 0)
    def _():
        pl.semaphore_signal(barrier, inc=1, device_id=device(here, z - 1), device_id_type=MESH)

    @pl.when(z < 3)
    def _():
        pl.semaphore_signal(barrier, inc=1, device_id=device(here, z + 1), device_id_type=MESH)

    pl.semaphore_wait(barrier, 3 + jnp.minimum(z, 1) + jnp.minimum(3 - z, 1))

    def own_copy(k):
        at = lax.rem(k, 2)
        return pltpu.make_async_copy(slots_ref.at[:, core, :, k], own.at[at], own_sem.at[at])

    def pair_copy(k):
        at = lax.rem(k, 2)
        return pltpu.make_async_remote_copy(
            src_ref=slots_ref.at[:, 1 - core, :, k],
            dst_ref=pair_in.at[at],
            send_sem=pair_send.at[at],
            recv_sem=pair_recv.at[at],
            device_id=partner,
            device_id_type=MESH,
        )

    def first_copy(k, part):
        place = near(k, 0)
        return pltpu.make_async_remote_copy(
            src_ref=pair_sum.at[lax.rem(k, 3), far if part == 0 else place],
            dst_ref=first_in.at[lax.rem(k, 5), part],
            send_sem=first_send.at[lax.rem(k, 3), part],
            recv_sem=first_recv.at[lax.rem(k, 5), part],
            device_id=device(place, z),
            device_id_type=MESH,
        )

    def second_copy(k):
        return pltpu.make_async_remote_copy(
            src_ref=second_out.at[lax.rem(k, 2)],
            dst_ref=second_in.at[lax.rem(k, 4)],
            send_sem=second_send.at[lax.rem(k, 2)],
            recv_sem=second_recv.at[lax.rem(k, 4)],
            device_id=device(near(k, 1), z),
            device_id_type=MESH,
        )

    def line_copy(k, level, source, target, send, recv, step):
        return pltpu.make_async_remote_copy(
            src_ref=source.at[lax.rem(k, 2), level],
            dst_ref=target.at[lax.rem(k, 6), level],
            send_sem=send.at[lax.rem(k, 2), level],
            recv_sem=recv.at[lax.rem(k, 6), level],
            device_id=device(here, z + step),
            device_id_type=MESH,
        )

    def up_copy(k, level):
        return line_copy(k, level, up_out, up_in, up_send, up_recv, 1)

    def down_copy(k, level):
        return line_copy(k, level, down_out, down_in, down_send, down_recv, -1)

    def result_copy(k):
        at = lax.rem(k, 2)
        return pltpu.make_async_copy(result.at[at], out_ref.at[k], result_sem.at[at])

    def valid(k):
        return jnp.logical_and(k >= 0, k < CHUNKS)

    own_copy(0).start()
    pair_copy(0).start()

    def step(t, carry):
        @pl.when(valid(t - 3))
        def _():
            first_copy(t - 3, 0).wait_send()
            first_copy(t - 3, 1).wait_send()

        @pl.when(valid(t))
        def _():
            own_copy(t).wait()
            pair_copy(t).wait_recv()
            at, ring = lax.rem(t, 2), lax.rem(t, 3)

            def add(i, inner):
                p, n = lax.div(i, 4), lax.rem(i, 4)
                pair_sum[ring, p, n] = total_of(own[at, p, n], pair_in[at, p, n]).astype(
                    jnp.bfloat16
                )
                return inner

            lax.fori_loop(0, 16, add, 0)
            first_copy(t, 0).start()
            first_copy(t, 1).start()

        @pl.when(valid(t - 1))
        def _():
            pair_copy(t - 1).wait_send()

        @pl.when(t + 1 < CHUNKS)
        def _():
            own_copy(t + 1).start()
            pair_copy(t + 1).start()

        @pl.when(valid(t - 3))
        def _():
            second_copy(t - 3).wait_send()

        @pl.when(valid(t - 1))
        def _():
            k = t - 1
            first_copy(k, 0).wait_recv()
            place = near(k, 1)

            def add(n, inner):
                second_out[lax.rem(k, 2), n] = total_of(
                    pair_sum[lax.rem(k, 3), place, n], first_in[lax.rem(k, 5), 0, n]
                ).astype(jnp.bfloat16)
                return inner

            lax.fori_loop(0, 4, add, 0)
            second_copy(k).start()

        @pl.when(valid(t - 2))
        def _():
            k = t - 2
            first_copy(k, 1).wait_recv()
            second_copy(k).wait_recv()

            def add(n, inner):
                column[lax.rem(k, 4), n] = total_of(
                    pair_sum[lax.rem(k, 3), here, n],
                    first_in[lax.rem(k, 5), 1, n],
                    second_in[lax.rem(k, 4), n],
                ).astype(jnp.bfloat16)
                return inner

            lax.fori_loop(0, 4, add, 0)

        for lag, ahead, behind, copy, arrived, leaving in (
            (z, lambda n: n > z, z > 0, up_copy, up_in, up_out),
            (3 - z, lambda n: n < z, z < 3, down_copy, down_in, down_out),
        ):
            k = t - 2 - lag
            for n in range(4):

                @pl.when(jnp.logical_and(valid(k - 2), ahead(n)))
                def _(n=n, k=k, copy=copy):
                    copy(k - 2, n).wait_send()

                @pl.when(
                    jnp.logical_and(
                        jnp.logical_and(valid(k), behind), jnp.logical_or(ahead(n), n == z)
                    )
                )
                def _(n=n, k=k, copy=copy):
                    copy(k, n).wait_recv()

                moving = jnp.logical_and(valid(k), ahead(n))

                @pl.when(jnp.logical_and(moving, behind))
                def _(n=n, k=k, arrived=arrived, leaving=leaving):
                    leaving[lax.rem(k, 2), n] = total_of(
                        column[lax.rem(k, 4), n], arrived[lax.rem(k, 6), n]
                    ).astype(jnp.bfloat16)

                @pl.when(jnp.logical_and(moving, jnp.logical_not(behind)))
                def _(n=n, k=k, leaving=leaving):
                    leaving[lax.rem(k, 2), n] = column[lax.rem(k, 4), n]

                @pl.when(moving)
                def _(n=n, k=k, copy=copy):
                    copy(k, n).start()

        k = t - 5

        @pl.when(valid(k - 2))
        def _():
            result_copy(k - 2).wait()

        @pl.when(valid(k))
        def _():
            result[lax.rem(k, 2)] = column[lax.rem(k, 4), z].astype(jnp.float32)

            @pl.when(z > 0)
            def _():
                result[lax.rem(k, 2)] += up_in[lax.rem(k, 6), z].astype(jnp.float32)

            @pl.when(z < 3)
            def _():
                result[lax.rem(k, 2)] += down_in[lax.rem(k, 6), z].astype(jnp.float32)

            result_copy(k).start()

        return carry

    lax.fori_loop(0, STEPS, step, 0)


def scatter_sum(slots, slot_count):
    wide, narrow = lax.axis_size("wide"), lax.axis_size("narrow")
    if (wide, narrow, slot_count) != (8, 4, CHUNKS):
        part = lax.psum_scatter(slots, "wide", scatter_dimension=0, tiled=True)
        return lax.psum_scatter(
            part.astype(jnp.float32), "narrow", scatter_dimension=0, tiled=True
        )
    low = functools.partial(pltpu.VMEM, dtype=jnp.bfloat16)
    dma = pltpu.SemaphoreType.DMA
    block = (BR, D)
    return pl.pallas_call(
        scatter_kernel,
        out_shape=jax.ShapeDtypeStruct((slot_count,) + block, jnp.float32),
        in_specs=[pl.BlockSpec(memory_space=pl.ANY)],
        out_specs=pl.BlockSpec(memory_space=pl.ANY),
        scratch_shapes=[
            low((2, 4, 4) + block),
            low((2, 4, 4) + block),
            low((3, 4, 4) + block),
            low((5, 2, 4) + block),
            low((4, 4) + block),
            low((2, 4) + block),
            low((4, 4) + block),
            low((6, 4) + block),
            low((6, 4) + block),
            low((2, 4) + block),
            low((2, 4) + block),
            pltpu.VMEM((2,) + block, jnp.float32),
            dma((2,)),
            dma((2,)),
            dma((2,)),
            dma((3, 2)),
            dma((5, 2)),
            dma((2,)),
            dma((4,)),
            dma((2, 4)),
            dma((6, 4)),
            dma((2, 4)),
            dma((6, 4)),
            dma((2,)),
        ],
        compiler_params=pltpu.CompilerParams(
            collective_id=1, has_side_effects=True, vmem_limit_bytes=VMEM_LIMIT
        ),
        name="scatter_sum",
    )(slots.reshape(4, 2, narrow, slot_count, BR, D))


def split_small(small):
    freq = small[: NCLASS * D].reshape(NCLASS, D)
    rest = small[NCLASS * D :]
    return (
        freq,
        rest[0:D],
        rest[D : 2 * D],
        rest[2 * D : 3 * D],
        rest[3 * D : 4 * D],
        rest[4 * D : 5 * D],
        rest[5 * D : 5 * D + OUTW],
    )


def prepare(series, pad_mask):
    valid = (1 - pad_mask).astype(jnp.float32)
    count_series = series.shape[0]
    context = (series[:, :CTX] * valid[:, :CTX]).reshape(count_series, NPATCH, PATCH)
    marks = pad_mask[:, :CTX].astype(jnp.float32).reshape(count_series, NPATCH, PATCH)
    feat = jnp.concatenate([context, marks], axis=-1)
    index = (jnp.arange(NPATCH, dtype=jnp.int32)[:, None] + 1) * PATCH + jnp.arange(
        HORIZON, dtype=jnp.int32
    )[None, :]
    return (feat, series[:, index], valid[:, index])


def class_sums(out, target, tmask, onehot):
    pred = out.reshape(onehot.shape[0], NPATCH, HORIZON, NQ + 1)
    error = pred[..., 0] - target
    square = jnp.sum(error * error * tmask, axis=(1, 2))
    levels = (jnp.arange(NQ, dtype=jnp.float32) + 1.0) / (NQ + 1)
    diff = target[..., None] - pred[..., 1:]
    pinball = jnp.sum(jnp.maximum(levels * diff, (levels - 1.0) * diff), axis=-1)
    quant = jnp.sum(pinball * tmask, axis=(1, 2))
    return jnp.stack([jnp.sum(onehot * square[:, None], 0), jnp.sum(onehot * quant[:, None], 0)])


def layer_forward(state_zero, mats, parts, cosine, sine, causal):
    w_qkv, w_out, w_up, w_down = (mats[2], mats[3], mats[4], mats[5])
    gain_one, gain_two = (parts[3], parts[4])
    count_series = state_zero.shape[0] // NPATCH
    normed_one = rms_norm(state_zero, gain_one).astype(jnp.bfloat16)
    qkv = matmul(normed_one, w_qkv).reshape(count_series, NPATCH, 3, HEADS, HDIM)
    queries = (rotate(qkv[:, :, 0], cosine, sine) * HDIM ** (-0.5)).astype(jnp.bfloat16)
    key_rot = rotate(qkv[:, :, 1], cosine, sine).astype(jnp.bfloat16)
    value_all = qkv[:, :, 2].astype(jnp.bfloat16)
    scores = jnp.einsum("sqhd,skhd->shqk", queries, key_rot, preferred_element_type=jnp.float32)
    scores = jnp.where(causal, scores, -1e30)
    peak = jnp.max(scores, axis=-1, keepdims=True)
    expo = jnp.exp(scores - peak)
    total = jnp.sum(expo, axis=-1, keepdims=True)
    log_total = peak + jnp.log(total)
    attend = (expo / total).astype(jnp.bfloat16)
    mixed = jnp.einsum("shqk,skhd->sqhd", attend, value_all, preferred_element_type=jnp.float32)
    mixed = mixed.astype(jnp.bfloat16).reshape(state_zero.shape[0], D)
    state_one = state_zero + matmul(mixed, w_out)
    normed_two = rms_norm(state_one, gain_two).astype(jnp.bfloat16)
    up_pre = matmul(normed_two, w_up)
    activ = silu(up_pre).astype(jnp.bfloat16)
    state_two = state_one + matmul(activ, w_down)
    return (
        state_two,
        (
            normed_one,
            queries,
            key_rot,
            value_all,
            log_total,
            mixed,
            state_one,
            normed_two,
            up_pre,
            activ,
        ),
    )


def layer_backward(
    grad_two, state_zero, kept, mats, parts, cosine, sine, causal, owner, slots
):
    (
        normed_one,
        queries,
        key_rot,
        value_all,
        log_total,
        mixed,
        state_one,
        normed_two,
        up_pre,
        activ,
    ) = kept
    w_qkv, w_out, w_up, w_down = (mats[2], mats[3], mats[4], mats[5])
    gain_one, gain_two = (parts[3], parts[4])
    tokens = state_zero.shape[0]
    count_series = tokens // NPATCH
    grad_mlp = grad_two.astype(jnp.bfloat16)
    slots = grad_blocks(activ, grad_mlp, owner, 5, slots)
    grad_act = backmul(grad_mlp, w_down)
    grad_up_pre = (grad_act * silu_slope(up_pre)).astype(jnp.bfloat16)
    slots = grad_blocks(normed_two, grad_up_pre, owner, 4, slots)
    grad_normed = backmul(grad_up_pre, w_up)
    _, pull = jax.vjp(rms_norm, state_one, gain_two)
    grad_norm_in, grad_gain_two = pull(grad_normed)
    grad_one = grad_two + grad_norm_in
    grad_proj = grad_one.astype(jnp.bfloat16)
    slots = grad_blocks(mixed, grad_proj, owner, 3, slots)
    grad_mixed = (
        backmul(grad_proj, w_out).astype(jnp.bfloat16).reshape(count_series, NPATCH, HEADS, HDIM)
    )
    scores = jnp.einsum("sqhd,skhd->shqk", queries, key_rot, preferred_element_type=jnp.float32)
    attend = jnp.where(causal, jnp.exp(scores - log_total), 0.0)
    grad_attend = jnp.einsum(
        "sqhd,skhd->shqk", grad_mixed, value_all, preferred_element_type=jnp.float32
    )
    grad_scores = (
        attend * (grad_attend - jnp.sum(grad_attend * attend, axis=-1, keepdims=True))
    ).astype(jnp.bfloat16)
    grad_query = jnp.einsum(
        "shqk,skhd->sqhd", grad_scores, key_rot, preferred_element_type=jnp.float32
    )
    grad_key = jnp.einsum(
        "shqk,sqhd->skhd", grad_scores, queries, preferred_element_type=jnp.float32
    )
    grad_value = jnp.einsum(
        "shqk,sqhd->skhd",
        attend.astype(jnp.bfloat16),
        grad_mixed,
        preferred_element_type=jnp.float32,
    )
    grad_qkv = jnp.stack(
        [
            rotate(grad_query, cosine, -sine) * HDIM ** (-0.5),
            rotate(grad_key, cosine, -sine),
            grad_value,
        ],
        axis=2,
    )
    grad_qkv = grad_qkv.reshape(tokens, 3 * D).astype(jnp.bfloat16)
    slots = grad_blocks(normed_one, grad_qkv, owner, 2, slots)
    grad_normed_one = backmul(grad_qkv, w_qkv)
    _, pull = jax.vjp(rms_norm, state_zero, gain_one)
    grad_zero_in, grad_gain_one = pull(grad_normed_one)
    return (
        grad_one + grad_zero_in,
        slots,
        grad_gain_one,
        grad_gain_two,
    )


def adamw(weight, first, second, grad, step):
    power = step[0].astype(jnp.float32)
    first = BETA * first + (1.0 - BETA) * grad
    second = BETA * second + (1.0 - BETA) * grad * grad
    fix_one = 1.0 - jnp.power(BETA, power)
    fix_two = 1.0 - jnp.power(BETA, power)
    new = weight - RATE * (
        first / fix_one / (jnp.sqrt(second / fix_two) + EPSILON) + DECAY * weight
    )
    return (new, first, second)


def on_device(
    series,
    pad_mask,
    freq_class,
    owner,
    step,
    master,
    moment1,
    moment2,
    small_master,
    small_m1,
    small_m2,
):
    slot_count = master.shape[0]
    gathered = lax.all_gather(master.astype(jnp.bfloat16), ("wide", "narrow"), axis=0, tiled=True)
    mats = tuple(unpack(gathered, owner, which) for which in range(len(MATS)))
    tok_in, tok_out, head_in, head_out = (mats[0], mats[1], mats[6], mats[7])
    parts = split_small(small_master)
    freq, bias_one, bias_two, head_bias, out_bias = (
        parts[0],
        parts[1],
        parts[2],
        parts[5],
        parts[6],
    )
    feat, target, tmask = prepare(series, pad_mask)
    count_series = series.shape[0]
    tokens = count_series * NPATCH
    onehot = (freq_class[:, None] == jnp.arange(NCLASS, dtype=jnp.int32)[None, :]).astype(
        jnp.float32
    )
    local_counts = jnp.sum(onehot * jnp.sum(tmask, axis=(1, 2))[:, None], 0)
    counts = lax.psum(local_counts, ("wide", "narrow"))
    class_weight = 1.0 / (counts * NCLASS)
    cosine, sine = tables()
    causal = jnp.arange(NPATCH)[:, None] >= jnp.arange(NPATCH)[None, :]
    patch_in = feat.reshape(tokens, 2 * PATCH).astype(jnp.bfloat16)
    tok_pre = matmul(patch_in, tok_in)
    hidden = silu(tok_pre[:, :D] + bias_one).astype(jnp.bfloat16)
    class_rows = jnp.repeat(jnp.dot(onehot, freq, precision=lax.Precision.HIGHEST), NPATCH, axis=0)
    state_zero = matmul(hidden, tok_out) + bias_two + tok_pre[:, D:] + class_rows
    state_two, _ = layer_forward(state_zero, mats, parts, cosine, sine, causal)
    state_low = state_two.astype(jnp.bfloat16)
    head_pre = matmul(state_low, head_in)
    head_hidden = silu(head_pre[:, :D] + head_bias).astype(jnp.bfloat16)
    out = matmul(head_hidden, head_out) + out_bias + head_pre[:, D:]

    def loss_of(value):
        sums_here = class_sums(value, target, tmask, onehot)
        return (jnp.sum((sums_here[0] + sums_here[1] / NQ) * class_weight), sums_here)

    _, pull, local_sums = jax.vjp(loss_of, out, has_aux=True)
    (grad_out,) = pull(jnp.ones((), jnp.float32))
    sums = lax.psum(local_sums, ("wide", "narrow"))
    grad_out = grad_out.astype(jnp.bfloat16)
    grad_out_bias = jnp.sum(grad_out.astype(jnp.float32), axis=0)
    slots = grad_blocks(head_hidden, grad_out, owner, 7, None)
    grad_head_first = backmul(grad_out, head_out) * silu_slope(head_pre[:, :D] + head_bias)
    grad_head_bias = jnp.sum(grad_head_first, axis=0)
    grad_head_pre = jnp.concatenate([grad_head_first, grad_out.astype(jnp.float32)], axis=1).astype(
        jnp.bfloat16
    )
    slots = grad_blocks(state_low, grad_head_pre, owner, 6, slots)
    grad_two = backmul(grad_head_pre, head_in)
    _, kept = layer_forward(state_zero, mats, parts, cosine, sine, causal)
    grad_zero, slots, grad_gain_one, grad_gain_two = layer_backward(
        grad_two, state_zero, kept, mats, parts, cosine, sine, causal, owner, slots
    )
    grad_prod = grad_zero.astype(jnp.bfloat16)
    slots = grad_blocks(hidden, grad_prod, owner, 1, slots)
    grad_first = backmul(grad_prod, tok_out) * silu_slope(tok_pre[:, :D] + bias_one)
    grad_tok_pre = jnp.concatenate([grad_first, grad_zero], axis=1).astype(jnp.bfloat16)
    slots = grad_blocks(patch_in, grad_tok_pre, owner, 0, slots)
    grad_freq = jnp.dot(
        onehot.T,
        grad_zero.reshape(count_series, NPATCH, D).sum(axis=1),
        precision=lax.Precision.HIGHEST,
    )
    small_local = jnp.concatenate(
        [
            grad_freq.reshape(-1),
            jnp.sum(grad_first, axis=0),
            jnp.sum(grad_zero, axis=0),
            grad_gain_one,
            grad_gain_two,
            grad_head_bias,
            grad_out_bias,
        ]
    )
    small_grad = lax.psum(small_local, ("wide", "narrow"))
    owned = scatter_sum(slots, slot_count)
    rank = lax.axis_index("wide") * lax.axis_size("narrow") + lax.axis_index("narrow")
    mine = rank * slot_count + jnp.arange(slot_count, dtype=jnp.int32)
    filled = jnp.any(owner[:, None] == mine[None, :], axis=0)
    owned = jnp.where(filled[:, None, None], owned, 0.0)
    local_square = jnp.sum(owned * owned)
    square_total = lax.psum(local_square, ("wide", "narrow"))
    grad_norm = jnp.sqrt(square_total + jnp.sum(small_grad * small_grad))
    scale = jnp.minimum(1.0, CLIP / grad_norm)
    loss = jnp.sum((sums[0] + sums[1] / NQ) * class_weight)
    new_master, new_m1, new_m2 = adamw(master, moment1, moment2, owned * scale, step)
    small_new, small_new_m1, small_new_m2 = adamw(
        small_master, small_m1, small_m2, small_grad * scale, step
    )
    return (
        loss,
        grad_norm,
        new_master,
        new_m1,
        new_m2,
        new_master.astype(jnp.bfloat16),
        small_new,
        small_new_m1,
        small_new_m2,
    )


def solution(mesh):
    return jax.shard_map(
        on_device,
        mesh=mesh,
        in_specs=(
            P(("wide", "narrow"), None),
            P(("wide", "narrow"), None),
            P(("wide", "narrow")),
            P(),
            P(),
            P(("wide", "narrow"), None, None),
            P(("wide", "narrow"), None, None),
            P(("wide", "narrow"), None, None),
            P(),
            P(),
            P(),
        ),
        out_specs=(
            P(),
            P(),
            P(("wide", "narrow"), None, None),
            P(("wide", "narrow"), None, None),
            P(("wide", "narrow"), None, None),
            P(("wide", "narrow"), None, None),
            P(),
            P(),
            P(),
        ),
        check_vma=False,
    )
```

```python
import functools

import jax
import jax.numpy as jnp
from jax import lax
from jax.experimental import pallas as pl
from jax.experimental.pallas import tpu as pltpu
from jax.sharding import PartitionSpec as P

D = 1280
HEADS = 16
HDIM = 80
FF = 5120
PATCH = 32
HORIZON = 128
NQ = 9
NPATCH = 16
NCLASS = 3
BR = 64
TOTAL_SLOTS = 512
CTX = 512
OUTW = 1280
ROWS = 20608
NBLK = 322


CLIP = 0.01
RATE = 0.03
DECAY = 0.1
BETA = 0.5
EPSILON = 1e-08


def matmul(left, right):
    return jnp.dot(left, right, preferred_element_type=jnp.float32)


def tmatmul(left, right):
    return lax.dot_general(
        left, right, (((0,), (0,)), ((), ())), preferred_element_type=jnp.float32
    )


def backmul(left, right):
    return lax.dot_general(
        left, right, (((1,), (1,)), ((), ())), preferred_element_type=jnp.float32
    )


def silu(value):
    return value / (1.0 + jnp.exp(-value))


def silu_slope(value):
    sigmoid = 1.0 / (1.0 + jnp.exp(-value))
    return sigmoid * (1.0 + value * (1.0 - sigmoid))


def rms_norm(hidden, gain):
    return hidden * lax.rsqrt(jnp.mean(hidden * hidden, axis=-1, keepdims=True) + 1e-06) * gain


def tables():
    half = HDIM // 2
    inverse = jnp.power(10000.0, -2.0 * jnp.arange(half, dtype=jnp.float32) / HDIM)
    angle = jnp.arange(NPATCH, dtype=jnp.float32)[:, None] * inverse[None, :]
    return (jnp.cos(angle)[None, :, None, :], jnp.sin(angle)[None, :, None, :])


def rotate(value, cosine, sine):
    half = HDIM // 2
    first = value[..., :half]
    second = value[..., half:]
    return jnp.concatenate(
        [first * cosine - second * sine, first * sine + second * cosine], axis=-1
    )


MATS = (
    (2 * PATCH, 2, 2),
    (D, 1, 4),
    (D, 3, 6),
    (D, 1, 4),
    (D, FF // D, 8),
    (FF, 1, 8),
    (D, (D + OUTW) // D, 4),
    (D, 1, 4),
)
BASES = tuple(sum(r * g for r, g, _ in MATS[:i]) // BR for i in range(len(MATS)))
LANES = 128
VMEM_LIMIT = 56 * 1024 * 1024


def unpack_kernel(groups, count, owner_ref, *refs):
    out_ref = refs[count]
    if groups == 1:
        for b in range(count):
            out_ref[b * BR : (b + 1) * BR, :] = refs[b][...]
        return
    wide_ref = refs[count + 1]
    for b in range(count):
        for c in range(D // LANES):
            wide_ref[c, b * BR : (b + 1) * BR, :] = refs[b][
                :, c * LANES : (c + 1) * LANES
            ].astype(jnp.float32)
    rows = count * BR // groups
    for j in range(groups):
        for c in range(D // LANES):
            at = j * D + c * LANES
            out_ref[:, at : at + LANES] = wide_ref[c, pl.ds(j, rows, stride=groups), :].astype(
                jnp.bfloat16
            )


def unpack(gathered, owner, which):
    total, groups, count = MATS[which]
    base = BASES[which]
    rows = count * BR // groups

    def spec(b):
        return pl.BlockSpec(
            (None, BR, D), lambda i, own, b=b: (own[base + i * count + b], 0, 0)
        )

    return pl.pallas_call(
        functools.partial(unpack_kernel, groups, count),
        out_shape=jax.ShapeDtypeStruct((total, groups * D), jnp.bfloat16),
        grid_spec=pltpu.PrefetchScalarGridSpec(
            num_scalar_prefetch=1,
            grid=(total // rows,),
            in_specs=[spec(b) for b in range(count)],
            out_specs=pl.BlockSpec((rows, groups * D), lambda i, own: (i, 0)),
            scratch_shapes=[]
            if groups == 1
            else [pltpu.VMEM((D // LANES, count * BR, LANES), jnp.float32)],
        ),
        compiler_params=pltpu.CompilerParams(vmem_limit_bytes=VMEM_LIMIT),
        cost_estimate=pl.CostEstimate(
            flops=0, bytes_accessed=4 * total * groups * D, transcendentals=0
        ),
        name=f"unpack_{which}",
    )(owner, *([gathered] * count))


def grad_kernel(groups, count, base, steps, owner_ref, left_ref, right_ref, *refs):
    out_ref, stage_ref, sems = refs[-3 - (groups > 1)], refs[-2 - (groups > 1)], refs[-1 - (groups > 1)]
    step = pl.program_id(0)
    slot = lax.rem(step, 2)
    rows = count * BR // groups

    def copy(at, b, when):
        return pltpu.make_async_copy(
            stage_ref.at[at, pl.ds(b * BR, BR), :],
            out_ref.at[owner_ref[base + when * count + b]],
            sems.at[at, b],
        )

    @pl.when(step >= 2)
    def _():
        for b in range(count):
            copy(slot, b, step - 2).wait()

    left = left_ref[...]
    for j in range(groups):
        part = tmatmul(left, right_ref[:, j * D : (j + 1) * D])
        if groups == 1:
            stage_ref[slot] = part.astype(jnp.bfloat16)
        else:
            for c in range(D // LANES):
                refs[-1][c, pl.ds(j, rows, stride=groups), :] = part[
                    :, c * LANES : (c + 1) * LANES
                ]
    if groups > 1:
        for c in range(D // LANES):
            stage_ref[slot, :, c * LANES : (c + 1) * LANES] = refs[-1][c].astype(jnp.bfloat16)
    for b in range(count):
        copy(slot, b, step).start()

    @pl.when(step == steps - 1)
    def _():
        for b in range(count):
            copy(slot, b, step).wait()

    if steps > 1:

        @pl.when(step == steps - 1)
        def _():
            for b in range(count):
                copy(1 - slot, b, step - 1).wait()


def grad_blocks(left, right, owner, which, slots):
    total, groups, count = MATS[which]
    rows = count * BR // groups
    steps = total // rows
    tokens = left.shape[0]
    scratch = [
        pltpu.VMEM((2, count * BR, D), jnp.bfloat16),
        pltpu.SemaphoreType.DMA((2, count)),
    ]
    if groups > 1:
        scratch.append(pltpu.VMEM((D // LANES, count * BR, LANES), jnp.float32))
    held = [] if slots is None else [slots]
    return pl.pallas_call(
        functools.partial(grad_kernel, groups, count, BASES[which], steps),
        out_shape=jax.ShapeDtypeStruct((TOTAL_SLOTS, BR, D), jnp.bfloat16),
        grid_spec=pltpu.PrefetchScalarGridSpec(
            num_scalar_prefetch=1,
            grid=(steps,),
            in_specs=[
                pl.BlockSpec((tokens, rows), lambda i, own: (0, i)),
                pl.BlockSpec((tokens, groups * D), lambda i, own: (0, 0)),
            ]
            + [pl.BlockSpec(memory_space=pl.ANY)] * len(held),
            out_specs=pl.BlockSpec(memory_space=pl.ANY),
            scratch_shapes=scratch,
        ),
        input_output_aliases={3: 0} if held else {},
        compiler_params=pltpu.CompilerParams(vmem_limit_bytes=VMEM_LIMIT),
        cost_estimate=pl.CostEstimate(
            flops=2 * tokens * total * groups * D,
            bytes_accessed=2 * total * groups * D,
            transcendentals=0,
        ),
        name=f"grad_{which}",
    )(owner, left, right, *held)


CHUNKS = 16
STEPS = CHUNKS + 7
MESH = pl.DeviceIdType.MESH


def total_of(*blocks):
    result = blocks[0].astype(jnp.float32)
    for block in blocks[1:]:
        result = result + block.astype(jnp.float32)
    return result


def scatter_kernel(
    slots_ref,
    out_ref,
    own,
    pair_in,
    pair_sum,
    first_in,
    second_in,
    second_out,
    column,
    up_in,
    down_in,
    up_out,
    down_out,
    result,
    own_sem,
    pair_send,
    pair_recv,
    first_send,
    first_recv,
    second_send,
    second_recv,
    up_send,
    up_recv,
    down_send,
    down_recv,
    result_sem,
):
    wide, z = lax.axis_index("wide"), lax.axis_index("narrow")
    core, here = lax.rem(wide, 2), lax.div(wide, 2)
    x, y = lax.rem(here, 2), lax.div(here, 2)
    far = 3 - here

    def device(place, level):
        return (place * 2 + core, level)

    partner = (here * 2 + 1 - core, z)

    def near(k, which):
        along_y = lax.rem(k + which, 2)
        return (y + along_y - 2 * y * along_y) * 2 + (x + (1 - along_y) - 2 * x * (1 - along_y))

    barrier = pltpu.get_barrier_semaphore()
    pl.semaphore_signal(barrier, inc=1, device_id=partner, device_id_type=MESH)
    for which in range(2):
        pl.semaphore_signal(
            barrier, inc=1, device_id=device(near(0, which), z), device_id_type=MESH
        )

    @pl.when(z > 0)
    def _():
        pl.semaphore_signal(barrier, inc=1, device_id=device(here, z - 1), device_id_type=MESH)

    @pl.when(z < 3)
    def _():
        pl.semaphore_signal(barrier, inc=1, device_id=device(here, z + 1), device_id_type=MESH)

    pl.semaphore_wait(barrier, 3 + jnp.minimum(z, 1) + jnp.minimum(3 - z, 1))

    def own_copy(k):
        at = lax.rem(k, 2)
        return pltpu.make_async_copy(slots_ref.at[:, core, :, k], own.at[at], own_sem.at[at])

    def pair_copy(k):
        at = lax.rem(k, 2)
        return pltpu.make_async_remote_copy(
            src_ref=slots_ref.at[:, 1 - core, :, k],
            dst_ref=pair_in.at[at],
            send_sem=pair_send.at[at],
            recv_sem=pair_recv.at[at],
            device_id=partner,
            device_id_type=MESH,
        )

    def first_copy(k, part):
        place = near(k, 0)
        return pltpu.make_async_remote_copy(
            src_ref=pair_sum.at[lax.rem(k, 3), far if part == 0 else place],
            dst_ref=first_in.at[lax.rem(k, 5), part],
            send_sem=first_send.at[lax.rem(k, 3), part],
            recv_sem=first_recv.at[lax.rem(k, 5), part],
            device_id=device(place, z),
            device_id_type=MESH,
        )

    def second_copy(k):
        return pltpu.make_async_remote_copy(
            src_ref=second_out.at[lax.rem(k, 2)],
            dst_ref=second_in.at[lax.rem(k, 4)],
            send_sem=second_send.at[lax.rem(k, 2)],
            recv_sem=second_recv.at[lax.rem(k, 4)],
            device_id=device(near(k, 1), z),
            device_id_type=MESH,
        )

    def line_copy(k, level, source, target, send, recv, step):
        return pltpu.make_async_remote_copy(
            src_ref=source.at[lax.rem(k, 2), level],
            dst_ref=target.at[lax.rem(k, 6), level],
            send_sem=send.at[lax.rem(k, 2), level],
            recv_sem=recv.at[lax.rem(k, 6), level],
            device_id=device(here, z + step),
            device_id_type=MESH,
        )

    def up_copy(k, level):
        return line_copy(k, level, up_out, up_in, up_send, up_recv, 1)

    def down_copy(k, level):
        return line_copy(k, level, down_out, down_in, down_send, down_recv, -1)

    def result_copy(k):
        at = lax.rem(k, 2)
        return pltpu.make_async_copy(result.at[at], out_ref.at[k], result_sem.at[at])

    def valid(k):
        return jnp.logical_and(k >= 0, k < CHUNKS)

    own_copy(0).start()
    pair_copy(0).start()

    def step(t, carry):
        @pl.when(valid(t - 3))
        def _():
            first_copy(t - 3, 0).wait_send()
            first_copy(t - 3, 1).wait_send()

        @pl.when(valid(t))
        def _():
            own_copy(t).wait()
            pair_copy(t).wait_recv()
            at, ring = lax.rem(t, 2), lax.rem(t, 3)

            def add(i, inner):
                p, n = lax.div(i, 4), lax.rem(i, 4)
                pair_sum[ring, p, n] = total_of(own[at, p, n], pair_in[at, p, n]).astype(
                    jnp.bfloat16
                )
                return inner

            lax.fori_loop(0, 16, add, 0)
            first_copy(t, 0).start()
            first_copy(t, 1).start()

        @pl.when(valid(t - 1))
        def _():
            pair_copy(t - 1).wait_send()

        @pl.when(t + 1 < CHUNKS)
        def _():
            own_copy(t + 1).start()
            pair_copy(t + 1).start()

        @pl.when(valid(t - 3))
        def _():
            second_copy(t - 3).wait_send()

        @pl.when(valid(t - 1))
        def _():
            k = t - 1
            first_copy(k, 0).wait_recv()
            place = near(k, 1)

            def add(n, inner):
                second_out[lax.rem(k, 2), n] = total_of(
                    pair_sum[lax.rem(k, 3), place, n], first_in[lax.rem(k, 5), 0, n]
                ).astype(jnp.bfloat16)
                return inner

            lax.fori_loop(0, 4, add, 0)
            second_copy(k).start()

        @pl.when(valid(t - 2))
        def _():
            k = t - 2
            first_copy(k, 1).wait_recv()
            second_copy(k).wait_recv()

            def add(n, inner):
                column[lax.rem(k, 4), n] = total_of(
                    pair_sum[lax.rem(k, 3), here, n],
                    first_in[lax.rem(k, 5), 1, n],
                    second_in[lax.rem(k, 4), n],
                ).astype(jnp.bfloat16)
                return inner

            lax.fori_loop(0, 4, add, 0)

        for lag, ahead, behind, copy, arrived, leaving in (
            (z, lambda n: n > z, z > 0, up_copy, up_in, up_out),
            (3 - z, lambda n: n < z, z < 3, down_copy, down_in, down_out),
        ):
            k = t - 2 - lag
            for n in range(4):

                @pl.when(jnp.logical_and(valid(k - 2), ahead(n)))
                def _(n=n, k=k, copy=copy):
                    copy(k - 2, n).wait_send()

                @pl.when(
                    jnp.logical_and(
                        jnp.logical_and(valid(k), behind), jnp.logical_or(ahead(n), n == z)
                    )
                )
                def _(n=n, k=k, copy=copy):
                    copy(k, n).wait_recv()

                moving = jnp.logical_and(valid(k), ahead(n))

                @pl.when(jnp.logical_and(moving, behind))
                def _(n=n, k=k, arrived=arrived, leaving=leaving):
                    leaving[lax.rem(k, 2), n] = total_of(
                        column[lax.rem(k, 4), n], arrived[lax.rem(k, 6), n]
                    ).astype(jnp.bfloat16)

                @pl.when(jnp.logical_and(moving, jnp.logical_not(behind)))
                def _(n=n, k=k, leaving=leaving):
                    leaving[lax.rem(k, 2), n] = column[lax.rem(k, 4), n]

                @pl.when(moving)
                def _(n=n, k=k, copy=copy):
                    copy(k, n).start()

        k = t - 5

        @pl.when(valid(k - 2))
        def _():
            result_copy(k - 2).wait()

        @pl.when(valid(k))
        def _():
            result[lax.rem(k, 2)] = column[lax.rem(k, 4), z].astype(jnp.float32)

            @pl.when(z > 0)
            def _():
                result[lax.rem(k, 2)] += up_in[lax.rem(k, 6), z].astype(jnp.float32)

            @pl.when(z < 3)
            def _():
                result[lax.rem(k, 2)] += down_in[lax.rem(k, 6), z].astype(jnp.float32)

            result_copy(k).start()

        return carry

    lax.fori_loop(0, STEPS, step, 0)


def scatter_sum(slots, slot_count):
    wide, narrow = lax.axis_size("wide"), lax.axis_size("narrow")
    if (wide, narrow, slot_count) != (8, 4, CHUNKS):
        part = lax.psum_scatter(slots, "wide", scatter_dimension=0, tiled=True)
        return lax.psum_scatter(
            part.astype(jnp.float32), "narrow", scatter_dimension=0, tiled=True
        )
    low = functools.partial(pltpu.VMEM, dtype=jnp.bfloat16)
    dma = pltpu.SemaphoreType.DMA
    block = (BR, D)
    return pl.pallas_call(
        scatter_kernel,
        out_shape=jax.ShapeDtypeStruct((slot_count,) + block, jnp.float32),
        in_specs=[pl.BlockSpec(memory_space=pl.ANY)],
        out_specs=pl.BlockSpec(memory_space=pl.ANY),
        scratch_shapes=[
            low((2, 4, 4) + block),
            low((2, 4, 4) + block),
            low((3, 4, 4) + block),
            low((5, 2, 4) + block),
            low((4, 4) + block),
            low((2, 4) + block),
            low((4, 4) + block),
            low((6, 4) + block),
            low((6, 4) + block),
            low((2, 4) + block),
            low((2, 4) + block),
            pltpu.VMEM((2,) + block, jnp.float32),
            dma((2,)),
            dma((2,)),
            dma((2,)),
            dma((3, 2)),
            dma((5, 2)),
            dma((2,)),
            dma((4,)),
            dma((2, 4)),
            dma((6, 4)),
            dma((2, 4)),
            dma((6, 4)),
            dma((2,)),
        ],
        compiler_params=pltpu.CompilerParams(
            collective_id=1, has_side_effects=True, vmem_limit_bytes=VMEM_LIMIT
        ),
        name="scatter_sum",
    )(slots.reshape(4, 2, narrow, slot_count, BR, D))


LATE = 4
EARLY = CHUNKS - LATE
COMBOS = 4 * LATE
GATHER_STEPS = EARLY + 5


def gather_kernel(
    own_ref,
    count_ref,
    all_ref,
    counts_ref,
    own_sem,
    recv,
    pair_recv,
    line_send,
    plane_send,
    turn_send,
    late_send,
    pair_send,
    late_pair_send,
    count_send,
    count_recv,
):
    wide, z = lax.axis_index("wide"), lax.axis_index("narrow")
    core, here = lax.rem(wide, 2), lax.div(wide, 2)
    x, y = lax.rem(here, 2), lax.div(here, 2)
    side, front, far = y * 2 + 1 - x, (1 - y) * 2 + x, 3 - here
    places = 8 * 4
    me = wide * 4 + z

    barrier = pltpu.get_barrier_semaphore()

    def greet(i, carry):
        other = lax.rem(me + i, places)
        pl.semaphore_signal(
            barrier,
            inc=1,
            device_id=(lax.div(other, 4), lax.rem(other, 4)),
            device_id_type=MESH,
        )
        return carry

    lax.fori_loop(1, places, greet, 0)
    fill = pltpu.make_async_copy(own_ref, all_ref.at[here, core, z], own_sem)
    fill.start()
    counts_ref[me] = count_ref[...]
    pl.semaphore_wait(barrier, places - 1)
    fill.wait()

    def count_copy(i):
        other = lax.rem(me + i, places)
        return pltpu.make_async_remote_copy(
            src_ref=count_ref,
            dst_ref=counts_ref.at[me],
            send_sem=count_send.at[i],
            recv_sem=count_recv.at[i],
            device_id=(lax.div(other, 4), lax.rem(other, 4)),
            device_id_type=MESH,
        )

    def count_start(i, carry):
        count_copy(i).start()
        return carry

    lax.fori_loop(1, places, count_start, 0)

    def piece(p, n, k, send, to):
        return pltpu.make_async_remote_copy(
            src_ref=all_ref.at[p, core, n, k],
            dst_ref=all_ref.at[p, core, n, k],
            send_sem=send,
            recv_sem=recv.at[p, n, k],
            device_id=to,
            device_id_type=MESH,
        )

    up, down = (wide, z + 1), (wide, z - 1)
    to_side, to_front = (side * 2 + core, z), (front * 2 + core, z)

    def line(n, k, step):
        return piece(here, n, k, line_send.at[step, n, k], (up, down)[step])

    def plane(n, k, which):
        return piece(here, n, k, plane_send.at[which, n, k], (to_side, to_front)[which])

    def turn(n, k, which):
        return piece(
            (side, front)[which], n, k, turn_send.at[n, k], (to_front, to_side)[which]
        )

    def late(c, n, step):
        p, k = lax.rem(here + c, 4), EARLY + lax.div(c, 4)
        return piece(p, n, k, late_send.at[step, c, n], (up, down)[step])

    def pair(p, k, send):
        return pltpu.make_async_remote_copy(
            src_ref=all_ref.at[p, core, :, k],
            dst_ref=all_ref.at[p, core, :, k],
            send_sem=send,
            recv_sem=pair_recv,
            device_id=(here * 2 + 1 - core, z),
            device_id_type=MESH,
        )

    def early_pair(p, k):
        return pair(p, k, pair_send.at[p, k])

    def late_pair(c):
        p, k = lax.rem(here + c, 4), EARLY + lax.div(c, 4)
        return pair(p, k, late_pair_send.at[c])

    def both_lines(make, n, j, start):
        @pl.when(jnp.logical_and(start, z < 3))
        def _():
            if j <= 0:
                make(n, 0)

        @pl.when(jnp.logical_and(start, z > 0))
        def _():
            if j >= 0:
                make(n, 1)

    def early(k):
        return jnp.logical_and(k >= 0, k < EARLY)

    def swap(n, k, go):
        even = lax.rem(n + k, 2) == 0

        @pl.when(jnp.logical_and(go, even))
        def _():
            turn(n, k, 0).start()

        @pl.when(jnp.logical_and(go, jnp.logical_not(even)))
        def _():
            turn(n, k, 1).start()

    for k in range(EARLY, CHUNKS):
        plane(z, k, 0).start()
        plane(z, k, 1).start()

    def step(t, carry):
        @pl.when(early(t))
        def _():
            plane(z, t, 0).start()
            plane(z, t, 1).start()

        both_lines(lambda n, way: line(n, t, way).start(), z, 0, early(t))

        for j in (-1, 1, -2, 2, -3, 3):
            n, k = z + j, t - abs(j)
            there = jnp.logical_and(early(k), jnp.logical_and(n >= 0, n < 4))

            @pl.when(there)
            def _(n=n, k=k, j=j):
                piece(here, n, k, plane_send.at[0, n, k], to_side).wait_recv()

            both_lines(lambda n, way, k=k: line(n, k, way).start(), n, j, there)

            @pl.when(there)
            def _(n=n, k=k):
                plane(n, k, 0).start()
                plane(n, k, 1).start()

        @pl.when(t == 1)
        def _():
            for k in range(EARLY, CHUNKS):
                plane_wait(side, z, k)
                plane_wait(front, z, k)
                swap(z, k, True)

        @pl.when(t == 2)
        def _():
            for k in range(EARLY, CHUNKS):
                plane_wait(far, z, k)

        for j in (0, -1, 1, -2, 2, -3, 3):
            m = t - 2 - abs(j)
            n = z + j
            first = m + lax.div(m + 2, 3)
            for c, more in ((first, True), (first + 1, lax.rem(m, 3) == 0)):
                there = jnp.logical_and(
                    jnp.logical_and(m >= 0, c < COMBOS),
                    jnp.logical_and(jnp.logical_and(n >= 0, n < 4), more),
                )
                if j:

                    @pl.when(there)
                    def _(n=n, c=c):
                        plane_wait(lax.rem(here + c, 4), n, EARLY + lax.div(c, 4))

                both_lines(lambda n, way, c=c: late(c, n, way).start(), n, j, there)

        for n in range(4):
            gap = jnp.abs(z - n)
            k = t - 1 - gap

            @pl.when(early(k))
            def _(n=n, k=k):
                plane_wait(side, n, k)
                plane_wait(front, n, k)

            swap(n, k, early(k))
            k = t - 2 - gap

            @pl.when(early(k))
            def _(n=n, k=k):
                plane_wait(far, n, k)

        for lag, sent in ((3, (here,)), (4, (side, front)), (5, (far,))):
            k = t - lag

            @pl.when(early(k))
            def _(k=k, sent=sent):
                for p in sent:
                    early_pair(p, k).start()

        m = t - 5
        first = m + lax.div(m + 2, 3)
        for c, more in ((first, True), (first + 1, lax.rem(m, 3) == 0)):

            @pl.when(jnp.logical_and(jnp.logical_and(m >= 0, c < COMBOS), more))
            def _(c=c):
                late_pair(c).start()

        return carry

    def plane_wait(p, n, k):
        piece(p, n, k, plane_send.at[0, n, k], to_side).wait_recv()

    lax.fori_loop(0, GATHER_STEPS, step, 0)

    def finish(k, carry):
        for n in range(4):
            plane_used = jnp.logical_or(k < EARLY, n == z)

            @pl.when(plane_used)
            def _(n=n):
                plane(n, k, 0).wait_send()
                plane(n, k, 1).wait_send()
                turn(n, k, 0).wait_send()

            @pl.when(jnp.logical_and(k < EARLY, jnp.logical_and(n <= z, z < 3)))
            def _(n=n):
                line(n, k, 0).wait_send()

            @pl.when(jnp.logical_and(k < EARLY, jnp.logical_and(n >= z, z > 0)))
            def _(n=n):
                line(n, k, 1).wait_send()

            @pl.when(jnp.logical_and(n <= z, z < 3))
            def _(n=n):
                late(k, n, 0).wait_send()

            @pl.when(jnp.logical_and(n >= z, z > 0))
            def _(n=n):
                late(k, n, 1).wait_send()

        @pl.when(k < EARLY)
        def _():
            for p in range(4):
                early_pair(p, k).wait_send()

        late_pair(k).wait_send()
        return carry

    lax.fori_loop(0, CHUNKS, finish, 0)

    def count_wait(i, carry):
        count_copy(i).wait()
        return carry

    lax.fori_loop(1, places, count_wait, 0)
    pltpu.make_async_copy(
        all_ref.at[:, 1 - core], all_ref.at[:, 1 - core], pair_recv
    ).wait()


def gather_all(low, local_counts):
    slot_count = low.shape[0]
    wide, narrow = lax.axis_size("wide"), lax.axis_size("narrow")
    if (wide, narrow, slot_count) != (8, 4, CHUNKS):
        return (
            lax.all_gather(low, ("wide", "narrow"), axis=0, tiled=True),
            lax.psum(local_counts, ("wide", "narrow")),
        )
    dma = pltpu.SemaphoreType.DMA
    tile = jnp.zeros((8, LANES), jnp.float32).at[0, :NCLASS].set(local_counts)
    gathered, tiles = pl.pallas_call(
        gather_kernel,
        out_shape=(
            jax.ShapeDtypeStruct((4, 2, narrow, slot_count, BR, D), jnp.bfloat16),
            jax.ShapeDtypeStruct((wide * narrow, 8, LANES), jnp.float32),
        ),
        in_specs=[
            pl.BlockSpec(memory_space=pltpu.VMEM),
            pl.BlockSpec(memory_space=pltpu.VMEM),
        ],
        out_specs=(
            pl.BlockSpec(memory_space=pl.ANY),
            pl.BlockSpec(memory_space=pltpu.VMEM),
        ),
        scratch_shapes=[
            dma,
            dma((4, 4, CHUNKS)),
            dma,
            dma((2, 4, EARLY)),
            dma((2, 4, CHUNKS)),
            dma((4, CHUNKS)),
            dma((2, COMBOS, 4)),
            dma((4, EARLY)),
            dma((COMBOS,)),
            dma((wide * narrow,)),
            dma((wide * narrow,)),
        ],
        compiler_params=pltpu.CompilerParams(
            collective_id=2, has_side_effects=True, vmem_limit_bytes=VMEM_LIMIT
        ),
        name="gather_all",
    )(low, tile)
    return (
        gathered.reshape(wide * narrow * slot_count, BR, D),
        jnp.sum(tiles[:, 0, :NCLASS], axis=0),
    )


def split_small(small):
    freq = small[: NCLASS * D].reshape(NCLASS, D)
    rest = small[NCLASS * D :]
    return (
        freq,
        rest[0:D],
        rest[D : 2 * D],
        rest[2 * D : 3 * D],
        rest[3 * D : 4 * D],
        rest[4 * D : 5 * D],
        rest[5 * D : 5 * D + OUTW],
    )


def prepare(series, pad_mask):
    valid = (1 - pad_mask).astype(jnp.float32)
    count_series = series.shape[0]
    context = (series[:, :CTX] * valid[:, :CTX]).reshape(count_series, NPATCH, PATCH)
    marks = pad_mask[:, :CTX].astype(jnp.float32).reshape(count_series, NPATCH, PATCH)
    feat = jnp.concatenate([context, marks], axis=-1)
    index = (jnp.arange(NPATCH, dtype=jnp.int32)[:, None] + 1) * PATCH + jnp.arange(
        HORIZON, dtype=jnp.int32
    )[None, :]
    return (feat, series[:, index], valid[:, index])


def class_sums(out, target, tmask, onehot):
    pred = out.reshape(onehot.shape[0], NPATCH, HORIZON, NQ + 1)
    error = pred[..., 0] - target
    square = jnp.sum(error * error * tmask, axis=(1, 2))
    levels = (jnp.arange(NQ, dtype=jnp.float32) + 1.0) / (NQ + 1)
    diff = target[..., None] - pred[..., 1:]
    pinball = jnp.sum(jnp.maximum(levels * diff, (levels - 1.0) * diff), axis=-1)
    quant = jnp.sum(pinball * tmask, axis=(1, 2))
    return jnp.stack([jnp.sum(onehot * square[:, None], 0), jnp.sum(onehot * quant[:, None], 0)])


def layer_forward(state_zero, mats, parts, cosine, sine, causal):
    w_qkv, w_out, w_up, w_down = (mats[2], mats[3], mats[4], mats[5])
    gain_one, gain_two = (parts[3], parts[4])
    count_series = state_zero.shape[0] // NPATCH
    normed_one = rms_norm(state_zero, gain_one).astype(jnp.bfloat16)
    qkv = matmul(normed_one, w_qkv).reshape(count_series, NPATCH, 3, HEADS, HDIM)
    queries = (rotate(qkv[:, :, 0], cosine, sine) * HDIM ** (-0.5)).astype(jnp.bfloat16)
    key_rot = rotate(qkv[:, :, 1], cosine, sine).astype(jnp.bfloat16)
    value_all = qkv[:, :, 2].astype(jnp.bfloat16)
    scores = jnp.einsum("sqhd,skhd->shqk", queries, key_rot, preferred_element_type=jnp.float32)
    scores = jnp.where(causal, scores, -1e30)
    peak = jnp.max(scores, axis=-1, keepdims=True)
    expo = jnp.exp(scores - peak)
    total = jnp.sum(expo, axis=-1, keepdims=True)
    log_total = peak + jnp.log(total)
    attend = (expo / total).astype(jnp.bfloat16)
    mixed = jnp.einsum("shqk,skhd->sqhd", attend, value_all, preferred_element_type=jnp.float32)
    mixed = mixed.astype(jnp.bfloat16).reshape(state_zero.shape[0], D)
    state_one = state_zero + matmul(mixed, w_out)
    normed_two = rms_norm(state_one, gain_two).astype(jnp.bfloat16)
    up_pre = matmul(normed_two, w_up)
    activ = silu(up_pre).astype(jnp.bfloat16)
    state_two = state_one + matmul(activ, w_down)
    return (
        state_two,
        (
            normed_one,
            queries,
            key_rot,
            value_all,
            log_total,
            mixed,
            state_one,
            normed_two,
            up_pre,
            activ,
        ),
    )


def layer_backward(
    grad_two, state_zero, kept, mats, parts, cosine, sine, causal, owner, slots
):
    (
        normed_one,
        queries,
        key_rot,
        value_all,
        log_total,
        mixed,
        state_one,
        normed_two,
        up_pre,
        activ,
    ) = kept
    w_qkv, w_out, w_up, w_down = (mats[2], mats[3], mats[4], mats[5])
    gain_one, gain_two = (parts[3], parts[4])
    tokens = state_zero.shape[0]
    count_series = tokens // NPATCH
    grad_mlp = grad_two.astype(jnp.bfloat16)
    slots = grad_blocks(activ, grad_mlp, owner, 5, slots)
    grad_act = backmul(grad_mlp, w_down)
    grad_up_pre = (grad_act * silu_slope(up_pre)).astype(jnp.bfloat16)
    slots = grad_blocks(normed_two, grad_up_pre, owner, 4, slots)
    grad_normed = backmul(grad_up_pre, w_up)
    _, pull = jax.vjp(rms_norm, state_one, gain_two)
    grad_norm_in, grad_gain_two = pull(grad_normed)
    grad_one = grad_two + grad_norm_in
    grad_proj = grad_one.astype(jnp.bfloat16)
    slots = grad_blocks(mixed, grad_proj, owner, 3, slots)
    grad_mixed = (
        backmul(grad_proj, w_out).astype(jnp.bfloat16).reshape(count_series, NPATCH, HEADS, HDIM)
    )
    scores = jnp.einsum("sqhd,skhd->shqk", queries, key_rot, preferred_element_type=jnp.float32)
    attend = jnp.where(causal, jnp.exp(scores - log_total), 0.0)
    grad_attend = jnp.einsum(
        "sqhd,skhd->shqk", grad_mixed, value_all, preferred_element_type=jnp.float32
    )
    grad_scores = (
        attend * (grad_attend - jnp.sum(grad_attend * attend, axis=-1, keepdims=True))
    ).astype(jnp.bfloat16)
    grad_query = jnp.einsum(
        "shqk,skhd->sqhd", grad_scores, key_rot, preferred_element_type=jnp.float32
    )
    grad_key = jnp.einsum(
        "shqk,sqhd->skhd", grad_scores, queries, preferred_element_type=jnp.float32
    )
    grad_value = jnp.einsum(
        "shqk,sqhd->skhd",
        attend.astype(jnp.bfloat16),
        grad_mixed,
        preferred_element_type=jnp.float32,
    )
    grad_qkv = jnp.stack(
        [
            rotate(grad_query, cosine, -sine) * HDIM ** (-0.5),
            rotate(grad_key, cosine, -sine),
            grad_value,
        ],
        axis=2,
    )
    grad_qkv = grad_qkv.reshape(tokens, 3 * D).astype(jnp.bfloat16)
    slots = grad_blocks(normed_one, grad_qkv, owner, 2, slots)
    grad_normed_one = backmul(grad_qkv, w_qkv)
    _, pull = jax.vjp(rms_norm, state_zero, gain_one)
    grad_zero_in, grad_gain_one = pull(grad_normed_one)
    return (
        grad_one + grad_zero_in,
        slots,
        grad_gain_one,
        grad_gain_two,
    )


def adamw(weight, first, second, grad, step):
    power = step[0].astype(jnp.float32)
    first = BETA * first + (1.0 - BETA) * grad
    second = BETA * second + (1.0 - BETA) * grad * grad
    fix_one = 1.0 - jnp.power(BETA, power)
    fix_two = 1.0 - jnp.power(BETA, power)
    new = weight - RATE * (
        first / fix_one / (jnp.sqrt(second / fix_two) + EPSILON) + DECAY * weight
    )
    return (new, first, second)


def on_device(
    series,
    pad_mask,
    freq_class,
    owner,
    step,
    master,
    moment1,
    moment2,
    small_master,
    small_m1,
    small_m2,
):
    slot_count = master.shape[0]
    parts = split_small(small_master)
    freq, bias_one, bias_two, head_bias, out_bias = (
        parts[0],
        parts[1],
        parts[2],
        parts[5],
        parts[6],
    )
    feat, target, tmask = prepare(series, pad_mask)
    count_series = series.shape[0]
    tokens = count_series * NPATCH
    onehot = (freq_class[:, None] == jnp.arange(NCLASS, dtype=jnp.int32)[None, :]).astype(
        jnp.float32
    )
    local_counts = jnp.sum(onehot * jnp.sum(tmask, axis=(1, 2))[:, None], 0)
    gathered, counts = gather_all(master.astype(jnp.bfloat16), local_counts)
    mats = tuple(unpack(gathered, owner, which) for which in range(len(MATS)))
    tok_in, tok_out, head_in, head_out = (mats[0], mats[1], mats[6], mats[7])
    class_weight = 1.0 / (counts * NCLASS)
    cosine, sine = tables()
    causal = jnp.arange(NPATCH)[:, None] >= jnp.arange(NPATCH)[None, :]
    patch_in = feat.reshape(tokens, 2 * PATCH).astype(jnp.bfloat16)
    tok_pre = matmul(patch_in, tok_in)
    hidden = silu(tok_pre[:, :D] + bias_one).astype(jnp.bfloat16)
    class_rows = jnp.repeat(jnp.dot(onehot, freq, precision=lax.Precision.HIGHEST), NPATCH, axis=0)
    state_zero = matmul(hidden, tok_out) + bias_two + tok_pre[:, D:] + class_rows
    state_two, _ = layer_forward(state_zero, mats, parts, cosine, sine, causal)
    state_low = state_two.astype(jnp.bfloat16)
    head_pre = matmul(state_low, head_in)
    head_hidden = silu(head_pre[:, :D] + head_bias).astype(jnp.bfloat16)
    out = matmul(head_hidden, head_out) + out_bias + head_pre[:, D:]

    def loss_of(value):
        sums_here = class_sums(value, target, tmask, onehot)
        return (jnp.sum((sums_here[0] + sums_here[1] / NQ) * class_weight), sums_here)

    _, pull, local_sums = jax.vjp(loss_of, out, has_aux=True)
    (grad_out,) = pull(jnp.ones((), jnp.float32))
    sums = lax.psum(local_sums, ("wide", "narrow"))
    grad_out = grad_out.astype(jnp.bfloat16)
    grad_out_bias = jnp.sum(grad_out.astype(jnp.float32), axis=0)
    slots = grad_blocks(head_hidden, grad_out, owner, 7, None)
    grad_head_first = backmul(grad_out, head_out) * silu_slope(head_pre[:, :D] + head_bias)
    grad_head_bias = jnp.sum(grad_head_first, axis=0)
    grad_head_pre = jnp.concatenate([grad_head_first, grad_out.astype(jnp.float32)], axis=1).astype(
        jnp.bfloat16
    )
    slots = grad_blocks(state_low, grad_head_pre, owner, 6, slots)
    grad_two = backmul(grad_head_pre, head_in)
    _, kept = layer_forward(state_zero, mats, parts, cosine, sine, causal)
    grad_zero, slots, grad_gain_one, grad_gain_two = layer_backward(
        grad_two, state_zero, kept, mats, parts, cosine, sine, causal, owner, slots
    )
    grad_prod = grad_zero.astype(jnp.bfloat16)
    slots = grad_blocks(hidden, grad_prod, owner, 1, slots)
    grad_first = backmul(grad_prod, tok_out) * silu_slope(tok_pre[:, :D] + bias_one)
    grad_tok_pre = jnp.concatenate([grad_first, grad_zero], axis=1).astype(jnp.bfloat16)
    slots = grad_blocks(patch_in, grad_tok_pre, owner, 0, slots)
    grad_freq = jnp.dot(
        onehot.T,
        grad_zero.reshape(count_series, NPATCH, D).sum(axis=1),
        precision=lax.Precision.HIGHEST,
    )
    small_local = jnp.concatenate(
        [
            grad_freq.reshape(-1),
            jnp.sum(grad_first, axis=0),
            jnp.sum(grad_zero, axis=0),
            grad_gain_one,
            grad_gain_two,
            grad_head_bias,
            grad_out_bias,
        ]
    )
    small_grad = lax.psum(small_local, ("wide", "narrow"))
    owned = scatter_sum(slots, slot_count)
    rank = lax.axis_index("wide") * lax.axis_size("narrow") + lax.axis_index("narrow")
    mine = rank * slot_count + jnp.arange(slot_count, dtype=jnp.int32)
    filled = jnp.any(owner[:, None] == mine[None, :], axis=0)
    owned = jnp.where(filled[:, None, None], owned, 0.0)
    local_square = jnp.sum(owned * owned)
    square_total = lax.psum(local_square, ("wide", "narrow"))
    grad_norm = jnp.sqrt(square_total + jnp.sum(small_grad * small_grad))
    scale = jnp.minimum(1.0, CLIP / grad_norm)
    loss = jnp.sum((sums[0] + sums[1] / NQ) * class_weight)
    new_master, new_m1, new_m2 = adamw(master, moment1, moment2, owned * scale, step)
    small_new, small_new_m1, small_new_m2 = adamw(
        small_master, small_m1, small_m2, small_grad * scale, step
    )
    return (
        loss,
        grad_norm,
        new_master,
        new_m1,
        new_m2,
        new_master.astype(jnp.bfloat16),
        small_new,
        small_new_m1,
        small_new_m2,
    )


def solution(mesh):
    return jax.shard_map(
        on_device,
        mesh=mesh,
        in_specs=(
            P(("wide", "narrow"), None),
            P(("wide", "narrow"), None),
            P(("wide", "narrow")),
            P(),
            P(),
            P(("wide", "narrow"), None, None),
            P(("wide", "narrow"), None, None),
            P(("wide", "narrow"), None, None),
            P(),
            P(),
            P(),
        ),
        out_specs=(
            P(),
            P(),
            P(("wide", "narrow"), None, None),
            P(("wide", "narrow"), None, None),
            P(("wide", "narrow"), None, None),
            P(("wide", "narrow"), None, None),
            P(),
            P(),
            P(),
        ),
        check_vma=False,
    )
```

```python
import functools

import jax
import jax.numpy as jnp
from jax import lax
from jax.experimental import pallas as pl
from jax.experimental.pallas import tpu as pltpu
from jax.sharding import PartitionSpec as P

D = 1280
HEADS = 16
HDIM = 80
FF = 5120
PATCH = 32
HORIZON = 128
NQ = 9
NPATCH = 16
NCLASS = 3
BR = 64
TOTAL_SLOTS = 512
CTX = 512
OUTW = 1280
ROWS = 20608
NBLK = 322


CLIP = 0.01
RATE = 0.03
DECAY = 0.1
BETA = 0.5
EPSILON = 1e-08


def matmul(left, right):
    return jnp.dot(left, right, preferred_element_type=jnp.float32)


def tmatmul(left, right):
    return lax.dot_general(
        left, right, (((0,), (0,)), ((), ())), preferred_element_type=jnp.float32
    )


def backmul(left, right):
    return lax.dot_general(
        left, right, (((1,), (1,)), ((), ())), preferred_element_type=jnp.float32
    )


def silu(value):
    return value / (1.0 + jnp.exp(-value))


def silu_slope(value):
    sigmoid = 1.0 / (1.0 + jnp.exp(-value))
    return sigmoid * (1.0 + value * (1.0 - sigmoid))


def rms_norm(hidden, gain):
    return hidden * lax.rsqrt(jnp.mean(hidden * hidden, axis=-1, keepdims=True) + 1e-06) * gain


def tables():
    half = HDIM // 2
    inverse = jnp.power(10000.0, -2.0 * jnp.arange(half, dtype=jnp.float32) / HDIM)
    angle = jnp.arange(NPATCH, dtype=jnp.float32)[:, None] * inverse[None, :]
    return (jnp.cos(angle)[None, :, None, :], jnp.sin(angle)[None, :, None, :])


def rotate(value, cosine, sine):
    half = HDIM // 2
    first = value[..., :half]
    second = value[..., half:]
    return jnp.concatenate(
        [first * cosine - second * sine, first * sine + second * cosine], axis=-1
    )


MATS = (
    (2 * PATCH, 2, 2),
    (D, 1, 4),
    (D, 3, 6),
    (D, 1, 4),
    (D, FF // D, 8),
    (FF, 1, 8),
    (D, (D + OUTW) // D, 4),
    (D, 1, 4),
)
BASES = tuple(sum(r * g for r, g, _ in MATS[:i]) // BR for i in range(len(MATS)))
LANES = 128
VMEM_LIMIT = 56 * 1024 * 1024


def unpack_kernel(groups, count, owner_ref, *refs):
    out_ref = refs[count]
    if groups == 1:
        for b in range(count):
            out_ref[b * BR : (b + 1) * BR, :] = refs[b][...]
        return
    wide_ref = refs[count + 1]
    for b in range(count):
        for c in range(D // LANES):
            wide_ref[c, b * BR : (b + 1) * BR, :] = refs[b][
                :, c * LANES : (c + 1) * LANES
            ].astype(jnp.float32)
    rows = count * BR // groups
    for j in range(groups):
        for c in range(D // LANES):
            at = j * D + c * LANES
            out_ref[:, at : at + LANES] = wide_ref[c, pl.ds(j, rows, stride=groups), :].astype(
                jnp.bfloat16
            )


def unpack(gathered, owner, which):
    total, groups, count = MATS[which]
    base = BASES[which]
    rows = count * BR // groups

    def spec(b):
        return pl.BlockSpec(
            (None, BR, D), lambda i, own, b=b: (own[base + i * count + b], 0, 0)
        )

    return pl.pallas_call(
        functools.partial(unpack_kernel, groups, count),
        out_shape=jax.ShapeDtypeStruct((total, groups * D), jnp.bfloat16),
        grid_spec=pltpu.PrefetchScalarGridSpec(
            num_scalar_prefetch=1,
            grid=(total // rows,),
            in_specs=[spec(b) for b in range(count)],
            out_specs=pl.BlockSpec((rows, groups * D), lambda i, own: (i, 0)),
            scratch_shapes=[]
            if groups == 1
            else [pltpu.VMEM((D // LANES, count * BR, LANES), jnp.float32)],
        ),
        compiler_params=pltpu.CompilerParams(vmem_limit_bytes=VMEM_LIMIT),
        cost_estimate=pl.CostEstimate(
            flops=0, bytes_accessed=4 * total * groups * D, transcendentals=0
        ),
        name=f"unpack_{which}",
    )(owner, *([gathered] * count))


def grad_kernel(groups, count, base, steps, owner_ref, left_ref, right_ref, *refs):
    out_ref, stage_ref, sems = refs[-3 - (groups > 1)], refs[-2 - (groups > 1)], refs[-1 - (groups > 1)]
    step = pl.program_id(0)
    slot = lax.rem(step, 2)
    rows = count * BR // groups

    def copy(at, b, when):
        return pltpu.make_async_copy(
            stage_ref.at[at, pl.ds(b * BR, BR), :],
            out_ref.at[owner_ref[base + when * count + b]],
            sems.at[at, b],
        )

    @pl.when(step >= 2)
    def _():
        for b in range(count):
            copy(slot, b, step - 2).wait()

    left = left_ref[...]
    for j in range(groups):
        part = tmatmul(left, right_ref[:, j * D : (j + 1) * D])
        if groups == 1:
            stage_ref[slot] = part.astype(jnp.bfloat16)
        else:
            for c in range(D // LANES):
                refs[-1][c, pl.ds(j, rows, stride=groups), :] = part[
                    :, c * LANES : (c + 1) * LANES
                ]
    if groups > 1:
        for c in range(D // LANES):
            stage_ref[slot, :, c * LANES : (c + 1) * LANES] = refs[-1][c].astype(jnp.bfloat16)
    for b in range(count):
        copy(slot, b, step).start()

    @pl.when(step == steps - 1)
    def _():
        for b in range(count):
            copy(slot, b, step).wait()

    if steps > 1:

        @pl.when(step == steps - 1)
        def _():
            for b in range(count):
                copy(1 - slot, b, step - 1).wait()


def grad_blocks(left, right, owner, which, slots):
    total, groups, count = MATS[which]
    rows = count * BR // groups
    steps = total // rows
    tokens = left.shape[0]
    scratch = [
        pltpu.VMEM((2, count * BR, D), jnp.bfloat16),
        pltpu.SemaphoreType.DMA((2, count)),
    ]
    if groups > 1:
        scratch.append(pltpu.VMEM((D // LANES, count * BR, LANES), jnp.float32))
    held = [] if slots is None else [slots]
    return pl.pallas_call(
        functools.partial(grad_kernel, groups, count, BASES[which], steps),
        out_shape=jax.ShapeDtypeStruct((TOTAL_SLOTS, BR, D), jnp.bfloat16),
        grid_spec=pltpu.PrefetchScalarGridSpec(
            num_scalar_prefetch=1,
            grid=(steps,),
            in_specs=[
                pl.BlockSpec((tokens, rows), lambda i, own: (0, i)),
                pl.BlockSpec((tokens, groups * D), lambda i, own: (0, 0)),
            ]
            + [pl.BlockSpec(memory_space=pl.ANY)] * len(held),
            out_specs=pl.BlockSpec(memory_space=pl.ANY),
            scratch_shapes=scratch,
        ),
        input_output_aliases={3: 0} if held else {},
        compiler_params=pltpu.CompilerParams(vmem_limit_bytes=VMEM_LIMIT),
        cost_estimate=pl.CostEstimate(
            flops=2 * tokens * total * groups * D,
            bytes_accessed=2 * total * groups * D,
            transcendentals=0,
        ),
        name=f"grad_{which}",
    )(owner, left, right, *held)


CHUNKS = 16
STEPS = CHUNKS + 7
MESH = pl.DeviceIdType.MESH


def total_of(*blocks):
    result = blocks[0].astype(jnp.float32)
    for block in blocks[1:]:
        result = result + block.astype(jnp.float32)
    return result


def scatter_kernel(
    slots_ref,
    small_ref,
    filled_ref,
    out_ref,
    small_out,
    square_out,
    small_in,
    own,
    pair_in,
    pair_sum,
    first_in,
    second_in,
    second_out,
    column,
    up_in,
    down_in,
    up_out,
    down_out,
    result,
    own_sem,
    pair_send,
    pair_recv,
    first_send,
    first_recv,
    second_send,
    second_recv,
    up_send,
    up_recv,
    down_send,
    down_recv,
    result_sem,
    share_send,
    share_recv,
    spread_send,
    spread_recv,
    square_send,
    square_recv,
):
    wide, z = lax.axis_index("wide"), lax.axis_index("narrow")
    core, here = lax.rem(wide, 2), lax.div(wide, 2)
    x, y = lax.rem(here, 2), lax.div(here, 2)
    far = 3 - here

    def device(place, level):
        return (place * 2 + core, level)

    partner = (here * 2 + 1 - core, z)

    def near(k, which):
        along_y = lax.rem(k + which, 2)
        return (y + along_y - 2 * y * along_y) * 2 + (x + (1 - along_y) - 2 * x * (1 - along_y))

    places = 8 * 4
    me = wide * 4 + z
    barrier = pltpu.get_barrier_semaphore()

    def each(action):
        def body(i, carry):
            other = lax.rem(me + i, places)
            action(i, other, (lax.div(other, 4), lax.rem(other, 4)))
            return carry

        lax.fori_loop(1, places, body, 0)

    def greet(i, other, to):
        pl.semaphore_signal(barrier, inc=1, device_id=to, device_id_type=MESH)

    def share(i, other, to):
        return pltpu.make_async_remote_copy(
            src_ref=small_ref.at[other],
            dst_ref=small_in.at[me],
            send_sem=share_send.at[i],
            recv_sem=share_recv.at[i],
            device_id=to,
            device_id_type=MESH,
        )

    def tell(ref, send, recv):
        def make(i, other, to):
            return pltpu.make_async_remote_copy(
                src_ref=ref.at[me],
                dst_ref=ref.at[me],
                send_sem=send.at[i],
                recv_sem=recv.at[i],
                device_id=to,
                device_id_type=MESH,
            )

        return make

    spread = tell(small_out, spread_send, spread_recv)
    square = tell(square_out, square_send, square_recv)
    each(greet)
    small_in[me] = small_ref[me]
    square_out[me] = jnp.zeros((8, LANES), jnp.float32)
    pl.semaphore_wait(barrier, places - 1)

    def own_copy(k):
        at = lax.rem(k, 2)
        return pltpu.make_async_copy(slots_ref.at[:, core, :, k], own.at[at], own_sem.at[at])

    def pair_copy(k):
        at = lax.rem(k, 2)
        return pltpu.make_async_remote_copy(
            src_ref=slots_ref.at[:, 1 - core, :, k],
            dst_ref=pair_in.at[at],
            send_sem=pair_send.at[at],
            recv_sem=pair_recv.at[at],
            device_id=partner,
            device_id_type=MESH,
        )

    def first_copy(k, part):
        place = near(k, 0)
        return pltpu.make_async_remote_copy(
            src_ref=pair_sum.at[lax.rem(k, 3), far if part == 0 else place],
            dst_ref=first_in.at[lax.rem(k, 5), part],
            send_sem=first_send.at[lax.rem(k, 3), part],
            recv_sem=first_recv.at[lax.rem(k, 5), part],
            device_id=device(place, z),
            device_id_type=MESH,
        )

    def second_copy(k):
        return pltpu.make_async_remote_copy(
            src_ref=second_out.at[lax.rem(k, 2)],
            dst_ref=second_in.at[lax.rem(k, 4)],
            send_sem=second_send.at[lax.rem(k, 2)],
            recv_sem=second_recv.at[lax.rem(k, 4)],
            device_id=device(near(k, 1), z),
            device_id_type=MESH,
        )

    def line_copy(k, level, source, target, send, recv, step):
        return pltpu.make_async_remote_copy(
            src_ref=source.at[lax.rem(k, 2), level],
            dst_ref=target.at[lax.rem(k, 6), level],
            send_sem=send.at[lax.rem(k, 2), level],
            recv_sem=recv.at[lax.rem(k, 6), level],
            device_id=device(here, z + step),
            device_id_type=MESH,
        )

    def up_copy(k, level):
        return line_copy(k, level, up_out, up_in, up_send, up_recv, 1)

    def down_copy(k, level):
        return line_copy(k, level, down_out, down_in, down_send, down_recv, -1)

    def result_copy(k):
        at = lax.rem(k, 2)
        return pltpu.make_async_copy(result.at[at], out_ref.at[k], result_sem.at[at])

    def valid(k):
        return jnp.logical_and(k >= 0, k < CHUNKS)

    own_copy(0).start()
    pair_copy(0).start()
    each(lambda *at: share(*at).start())

    def step(t, carry):
        @pl.when(valid(t - 3))
        def _():
            first_copy(t - 3, 0).wait_send()
            first_copy(t - 3, 1).wait_send()

        @pl.when(valid(t))
        def _():
            own_copy(t).wait()
            pair_copy(t).wait_recv()
            at, ring = lax.rem(t, 2), lax.rem(t, 3)

            def add(i, inner):
                p, n = lax.div(i, 4), lax.rem(i, 4)
                pair_sum[ring, p, n] = total_of(own[at, p, n], pair_in[at, p, n]).astype(
                    jnp.bfloat16
                )
                return inner

            lax.fori_loop(0, 16, add, 0)
            first_copy(t, 0).start()
            first_copy(t, 1).start()

        @pl.when(valid(t - 1))
        def _():
            pair_copy(t - 1).wait_send()

        @pl.when(t + 1 < CHUNKS)
        def _():
            own_copy(t + 1).start()
            pair_copy(t + 1).start()

        @pl.when(valid(t - 3))
        def _():
            second_copy(t - 3).wait_send()

        @pl.when(valid(t - 1))
        def _():
            k = t - 1
            first_copy(k, 0).wait_recv()
            place = near(k, 1)

            def add(n, inner):
                second_out[lax.rem(k, 2), n] = total_of(
                    pair_sum[lax.rem(k, 3), place, n], first_in[lax.rem(k, 5), 0, n]
                ).astype(jnp.bfloat16)
                return inner

            lax.fori_loop(0, 4, add, 0)
            second_copy(k).start()

        @pl.when(valid(t - 2))
        def _():
            k = t - 2
            first_copy(k, 1).wait_recv()
            second_copy(k).wait_recv()

            def add(n, inner):
                column[lax.rem(k, 4), n] = total_of(
                    pair_sum[lax.rem(k, 3), here, n],
                    first_in[lax.rem(k, 5), 1, n],
                    second_in[lax.rem(k, 4), n],
                ).astype(jnp.bfloat16)
                return inner

            lax.fori_loop(0, 4, add, 0)

        for lag, ahead, behind, copy, arrived, leaving in (
            (z, lambda n: n > z, z > 0, up_copy, up_in, up_out),
            (3 - z, lambda n: n < z, z < 3, down_copy, down_in, down_out),
        ):
            k = t - 2 - lag
            for n in range(4):

                @pl.when(jnp.logical_and(valid(k - 2), ahead(n)))
                def _(n=n, k=k, copy=copy):
                    copy(k - 2, n).wait_send()

                @pl.when(
                    jnp.logical_and(
                        jnp.logical_and(valid(k), behind), jnp.logical_or(ahead(n), n == z)
                    )
                )
                def _(n=n, k=k, copy=copy):
                    copy(k, n).wait_recv()

                moving = jnp.logical_and(valid(k), ahead(n))

                @pl.when(jnp.logical_and(moving, behind))
                def _(n=n, k=k, arrived=arrived, leaving=leaving):
                    leaving[lax.rem(k, 2), n] = total_of(
                        column[lax.rem(k, 4), n], arrived[lax.rem(k, 6), n]
                    ).astype(jnp.bfloat16)

                @pl.when(jnp.logical_and(moving, jnp.logical_not(behind)))
                def _(n=n, k=k, leaving=leaving):
                    leaving[lax.rem(k, 2), n] = column[lax.rem(k, 4), n]

                @pl.when(moving)
                def _(n=n, k=k, copy=copy):
                    copy(k, n).start()

        k = t - 5

        @pl.when(valid(k - 2))
        def _():
            result_copy(k - 2).wait()

        @pl.when(valid(k))
        def _():
            result[lax.rem(k, 2)] = column[lax.rem(k, 4), z].astype(jnp.float32)

            @pl.when(z > 0)
            def _():
                result[lax.rem(k, 2)] += up_in[lax.rem(k, 6), z].astype(jnp.float32)

            @pl.when(z < 3)
            def _():
                result[lax.rem(k, 2)] += down_in[lax.rem(k, 6), z].astype(jnp.float32)

            kept = jnp.where(filled_ref[k, 0:1, 0:1] > 0.0, result[lax.rem(k, 2)], 0.0)
            result[lax.rem(k, 2)] = kept
            squares = square_out[me]
            for i in range(BR // 8):
                for j in range(D // LANES):
                    part = kept[i * 8 : (i + 1) * 8, j * LANES : (j + 1) * LANES]
                    squares = squares + part * part
            square_out[me] = squares
            result_copy(k).start()

        @pl.when(t == CHUNKS // 2)
        def _():
            each(lambda *at: share(*at).wait())
            small = small_in[0]
            for i in range(1, places):
                small = small + small_in[i]
            small_out[me] = small
            each(lambda *at: spread(*at).start())

        return carry

    lax.fori_loop(0, STEPS, step, 0)
    each(lambda *at: square(*at).start())
    each(lambda *at: spread(*at).wait())
    each(lambda *at: square(*at).wait())


def scatter_sum(slots, filled, small):
    slot_count = filled.shape[0]
    wide, narrow = lax.axis_size("wide"), lax.axis_size("narrow")
    if (wide, narrow, slot_count) != (8, 4, CHUNKS):
        part = lax.psum_scatter(slots, "wide", scatter_dimension=0, tiled=True)
        owned = lax.psum_scatter(
            part.astype(jnp.float32), "narrow", scatter_dimension=0, tiled=True
        )
        owned = jnp.where(filled[:, None, None], owned, 0.0)
        square = lax.psum(jnp.sum(owned * owned), ("wide", "narrow"))
        return owned, square, lax.psum(small, ("wide", "narrow"))
    tiles = (wide * narrow, 8, LANES)
    room = wide * narrow * 8 * LANES - small.shape[0]
    assert room >= 0
    low = functools.partial(pltpu.VMEM, dtype=jnp.bfloat16)
    dma = pltpu.SemaphoreType.DMA
    block = (BR, D)
    owned, small_tiles, square_tiles = pl.pallas_call(
        scatter_kernel,
        out_shape=(
            jax.ShapeDtypeStruct((slot_count,) + block, jnp.float32),
            jax.ShapeDtypeStruct(tiles, jnp.float32),
            jax.ShapeDtypeStruct(tiles, jnp.float32),
        ),
        in_specs=[
            pl.BlockSpec(memory_space=pl.ANY),
            pl.BlockSpec(memory_space=pltpu.VMEM),
            pl.BlockSpec(memory_space=pltpu.VMEM),
        ],
        out_specs=(
            pl.BlockSpec(memory_space=pl.ANY),
            pl.BlockSpec(memory_space=pltpu.VMEM),
            pl.BlockSpec(memory_space=pltpu.VMEM),
        ),
        scratch_shapes=[
            pltpu.VMEM(tiles, jnp.float32),
            low((2, 4, 4) + block),
            low((2, 4, 4) + block),
            low((3, 4, 4) + block),
            low((5, 2, 4) + block),
            low((4, 4) + block),
            low((2, 4) + block),
            low((4, 4) + block),
            low((6, 4) + block),
            low((6, 4) + block),
            low((2, 4) + block),
            low((2, 4) + block),
            pltpu.VMEM((2,) + block, jnp.float32),
            dma((2,)),
            dma((2,)),
            dma((2,)),
            dma((3, 2)),
            dma((5, 2)),
            dma((2,)),
            dma((4,)),
            dma((2, 4)),
            dma((6, 4)),
            dma((2, 4)),
            dma((6, 4)),
            dma((2,)),
        ]
        + [dma((wide * narrow,))] * 6,
        compiler_params=pltpu.CompilerParams(
            collective_id=1, has_side_effects=True, vmem_limit_bytes=VMEM_LIMIT
        ),
        name="scatter_sum",
    )(
        slots.reshape(4, 2, narrow, slot_count, BR, D),
        jnp.pad(small, (0, room)).reshape(tiles),
        jnp.broadcast_to(
            filled.astype(jnp.float32)[:, None, None], (slot_count, 8, LANES)
        ),
    )
    return owned, jnp.sum(square_tiles), small_tiles.reshape(-1)[: small.shape[0]]


LATE = 4
EARLY = CHUNKS - LATE
COMBOS = 4 * LATE
GATHER_STEPS = EARLY + 5


def gather_kernel(
    own_ref,
    count_ref,
    all_ref,
    counts_ref,
    own_sem,
    recv,
    pair_recv,
    line_send,
    plane_send,
    turn_send,
    late_send,
    pair_send,
    late_pair_send,
    count_send,
    count_recv,
):
    wide, z = lax.axis_index("wide"), lax.axis_index("narrow")
    core, here = lax.rem(wide, 2), lax.div(wide, 2)
    x, y = lax.rem(here, 2), lax.div(here, 2)
    side, front, far = y * 2 + 1 - x, (1 - y) * 2 + x, 3 - here
    places = 8 * 4
    me = wide * 4 + z

    barrier = pltpu.get_barrier_semaphore()

    def greet(i, carry):
        other = lax.rem(me + i, places)
        pl.semaphore_signal(
            barrier,
            inc=1,
            device_id=(lax.div(other, 4), lax.rem(other, 4)),
            device_id_type=MESH,
        )
        return carry

    lax.fori_loop(1, places, greet, 0)
    fill = pltpu.make_async_copy(own_ref, all_ref.at[here, core, z], own_sem)
    fill.start()
    counts_ref[me] = count_ref[...]
    pl.semaphore_wait(barrier, places - 1)
    fill.wait()

    def count_copy(i):
        other = lax.rem(me + i, places)
        return pltpu.make_async_remote_copy(
            src_ref=count_ref,
            dst_ref=counts_ref.at[me],
            send_sem=count_send.at[i],
            recv_sem=count_recv.at[i],
            device_id=(lax.div(other, 4), lax.rem(other, 4)),
            device_id_type=MESH,
        )

    def count_start(i, carry):
        count_copy(i).start()
        return carry

    lax.fori_loop(1, places, count_start, 0)

    def piece(p, n, k, send, to):
        return pltpu.make_async_remote_copy(
            src_ref=all_ref.at[p, core, n, k],
            dst_ref=all_ref.at[p, core, n, k],
            send_sem=send,
            recv_sem=recv.at[p, n, k],
            device_id=to,
            device_id_type=MESH,
        )

    up, down = (wide, z + 1), (wide, z - 1)
    to_side, to_front = (side * 2 + core, z), (front * 2 + core, z)

    def line(n, k, step):
        return piece(here, n, k, line_send.at[step, n, k], (up, down)[step])

    def plane(n, k, which):
        return piece(here, n, k, plane_send.at[which, n, k], (to_side, to_front)[which])

    def turn(n, k, which):
        return piece(
            (side, front)[which], n, k, turn_send.at[n, k], (to_front, to_side)[which]
        )

    def late(c, n, step):
        p, k = lax.rem(here + c, 4), EARLY + lax.div(c, 4)
        return piece(p, n, k, late_send.at[step, c, n], (up, down)[step])

    def pair(p, k, send):
        return pltpu.make_async_remote_copy(
            src_ref=all_ref.at[p, core, :, k],
            dst_ref=all_ref.at[p, core, :, k],
            send_sem=send,
            recv_sem=pair_recv,
            device_id=(here * 2 + 1 - core, z),
            device_id_type=MESH,
        )

    def early_pair(p, k):
        return pair(p, k, pair_send.at[p, k])

    def late_pair(c):
        p, k = lax.rem(here + c, 4), EARLY + lax.div(c, 4)
        return pair(p, k, late_pair_send.at[c])

    def both_lines(make, n, j, start):
        @pl.when(jnp.logical_and(start, z < 3))
        def _():
            if j <= 0:
                make(n, 0)

        @pl.when(jnp.logical_and(start, z > 0))
        def _():
            if j >= 0:
                make(n, 1)

    def early(k):
        return jnp.logical_and(k >= 0, k < EARLY)

    def swap(n, k, go):
        even = lax.rem(n + k, 2) == 0

        @pl.when(jnp.logical_and(go, even))
        def _():
            turn(n, k, 0).start()

        @pl.when(jnp.logical_and(go, jnp.logical_not(even)))
        def _():
            turn(n, k, 1).start()

    for k in range(EARLY, CHUNKS):
        plane(z, k, 0).start()
        plane(z, k, 1).start()

    def step(t, carry):
        @pl.when(early(t))
        def _():
            plane(z, t, 0).start()
            plane(z, t, 1).start()

        both_lines(lambda n, way: line(n, t, way).start(), z, 0, early(t))

        for j in (-1, 1, -2, 2, -3, 3):
            n, k = z + j, t - abs(j)
            there = jnp.logical_and(early(k), jnp.logical_and(n >= 0, n < 4))

            @pl.when(there)
            def _(n=n, k=k, j=j):
                piece(here, n, k, plane_send.at[0, n, k], to_side).wait_recv()

            both_lines(lambda n, way, k=k: line(n, k, way).start(), n, j, there)

            @pl.when(there)
            def _(n=n, k=k):
                plane(n, k, 0).start()
                plane(n, k, 1).start()

        @pl.when(t == 1)
        def _():
            for k in range(EARLY, CHUNKS):
                plane_wait(side, z, k)
                plane_wait(front, z, k)
                swap(z, k, True)

        @pl.when(t == 2)
        def _():
            for k in range(EARLY, CHUNKS):
                plane_wait(far, z, k)

        for j in (0, -1, 1, -2, 2, -3, 3):
            m = t - 2 - abs(j)
            n = z + j
            first = m + lax.div(m + 2, 3)
            for c, more in ((first, True), (first + 1, lax.rem(m, 3) == 0)):
                there = jnp.logical_and(
                    jnp.logical_and(m >= 0, c < COMBOS),
                    jnp.logical_and(jnp.logical_and(n >= 0, n < 4), more),
                )
                if j:

                    @pl.when(there)
                    def _(n=n, c=c):
                        plane_wait(lax.rem(here + c, 4), n, EARLY + lax.div(c, 4))

                both_lines(lambda n, way, c=c: late(c, n, way).start(), n, j, there)

        for n in range(4):
            gap = jnp.abs(z - n)
            k = t - 1 - gap

            @pl.when(early(k))
            def _(n=n, k=k):
                plane_wait(side, n, k)
                plane_wait(front, n, k)

            swap(n, k, early(k))
            k = t - 2 - gap

            @pl.when(early(k))
            def _(n=n, k=k):
                plane_wait(far, n, k)

        for lag, sent in ((3, (here,)), (4, (side, front)), (5, (far,))):
            k = t - lag

            @pl.when(early(k))
            def _(k=k, sent=sent):
                for p in sent:
                    early_pair(p, k).start()

        m = t - 5
        first = m + lax.div(m + 2, 3)
        for c, more in ((first, True), (first + 1, lax.rem(m, 3) == 0)):

            @pl.when(jnp.logical_and(jnp.logical_and(m >= 0, c < COMBOS), more))
            def _(c=c):
                late_pair(c).start()

        return carry

    def plane_wait(p, n, k):
        piece(p, n, k, plane_send.at[0, n, k], to_side).wait_recv()

    lax.fori_loop(0, GATHER_STEPS, step, 0)

    def finish(k, carry):
        for n in range(4):
            plane_used = jnp.logical_or(k < EARLY, n == z)

            @pl.when(plane_used)
            def _(n=n):
                plane(n, k, 0).wait_send()
                plane(n, k, 1).wait_send()
                turn(n, k, 0).wait_send()

            @pl.when(jnp.logical_and(k < EARLY, jnp.logical_and(n <= z, z < 3)))
            def _(n=n):
                line(n, k, 0).wait_send()

            @pl.when(jnp.logical_and(k < EARLY, jnp.logical_and(n >= z, z > 0)))
            def _(n=n):
                line(n, k, 1).wait_send()

            @pl.when(jnp.logical_and(n <= z, z < 3))
            def _(n=n):
                late(k, n, 0).wait_send()

            @pl.when(jnp.logical_and(n >= z, z > 0))
            def _(n=n):
                late(k, n, 1).wait_send()

        @pl.when(k < EARLY)
        def _():
            for p in range(4):
                early_pair(p, k).wait_send()

        late_pair(k).wait_send()
        return carry

    lax.fori_loop(0, CHUNKS, finish, 0)

    def count_wait(i, carry):
        count_copy(i).wait()
        return carry

    lax.fori_loop(1, places, count_wait, 0)
    pltpu.make_async_copy(
        all_ref.at[:, 1 - core], all_ref.at[:, 1 - core], pair_recv
    ).wait()


def gather_all(low, local_counts):
    slot_count = low.shape[0]
    wide, narrow = lax.axis_size("wide"), lax.axis_size("narrow")
    if (wide, narrow, slot_count) != (8, 4, CHUNKS):
        return (
            lax.all_gather(low, ("wide", "narrow"), axis=0, tiled=True),
            lax.psum(local_counts, ("wide", "narrow")),
        )
    dma = pltpu.SemaphoreType.DMA
    tile = jnp.zeros((8, LANES), jnp.float32).at[0, :NCLASS].set(local_counts)
    gathered, tiles = pl.pallas_call(
        gather_kernel,
        out_shape=(
            jax.ShapeDtypeStruct((4, 2, narrow, slot_count, BR, D), jnp.bfloat16),
            jax.ShapeDtypeStruct((wide * narrow, 8, LANES), jnp.float32),
        ),
        in_specs=[
            pl.BlockSpec(memory_space=pltpu.VMEM),
            pl.BlockSpec(memory_space=pltpu.VMEM),
        ],
        out_specs=(
            pl.BlockSpec(memory_space=pl.ANY),
            pl.BlockSpec(memory_space=pltpu.VMEM),
        ),
        scratch_shapes=[
            dma,
            dma((4, 4, CHUNKS)),
            dma,
            dma((2, 4, EARLY)),
            dma((2, 4, CHUNKS)),
            dma((4, CHUNKS)),
            dma((2, COMBOS, 4)),
            dma((4, EARLY)),
            dma((COMBOS,)),
            dma((wide * narrow,)),
            dma((wide * narrow,)),
        ],
        compiler_params=pltpu.CompilerParams(
            collective_id=2, has_side_effects=True, vmem_limit_bytes=VMEM_LIMIT
        ),
        name="gather_all",
    )(low, tile)
    return (
        gathered.reshape(wide * narrow * slot_count, BR, D),
        jnp.sum(tiles[:, 0, :NCLASS], axis=0),
    )


def split_small(small):
    freq = small[: NCLASS * D].reshape(NCLASS, D)
    rest = small[NCLASS * D :]
    return (
        freq,
        rest[0:D],
        rest[D : 2 * D],
        rest[2 * D : 3 * D],
        rest[3 * D : 4 * D],
        rest[4 * D : 5 * D],
        rest[5 * D : 5 * D + OUTW],
    )


def prepare(series, pad_mask):
    valid = (1 - pad_mask).astype(jnp.float32)
    count_series = series.shape[0]
    context = (series[:, :CTX] * valid[:, :CTX]).reshape(count_series, NPATCH, PATCH)
    marks = pad_mask[:, :CTX].astype(jnp.float32).reshape(count_series, NPATCH, PATCH)
    feat = jnp.concatenate([context, marks], axis=-1)
    return (feat, horizons(series), horizons(valid))


def horizons(points):
    count_series = points.shape[0]
    pieces = points.reshape(count_series, -1, PATCH)
    return jnp.concatenate(
        [pieces[:, 1 + j : 1 + j + NPATCH] for j in range(HORIZON // PATCH)], axis=-1
    ).reshape(count_series * NPATCH, HORIZON)


def loss_parts(out, target, tmask, onehot, class_weight):
    column = lax.broadcasted_iota(jnp.int32, (HORIZON, OUTW), 1)
    row = lax.broadcasted_iota(jnp.int32, (HORIZON, OUTW), 0)
    spread = (lax.div(column, NQ + 1) == row).astype(jnp.float32)
    wanted = jnp.dot(target, spread, precision=lax.Precision.HIGHEST)
    mask = matmul(tmask.astype(jnp.bfloat16), spread.astype(jnp.bfloat16))
    kind = lax.rem(lax.broadcasted_iota(jnp.int32, (1, OUTW), 1), NQ + 1)
    level = kind.astype(jnp.float32) / (NQ + 1)
    error = out - wanted
    above, below = level * -error, (level - 1.0) * -error
    slope = jnp.where(above > below, -level, jnp.where(above < below, 1.0 - level, 0.5 - level))
    square = jnp.sum(jnp.where(kind == 0, error * error * mask, 0.0), axis=1)
    quant = jnp.sum(jnp.where(kind == 0, 0.0, jnp.maximum(above, below) * mask), axis=1)
    weight = jnp.repeat(jnp.sum(onehot * class_weight[None, :], axis=1), NPATCH)[:, None]
    grad = weight * mask * jnp.where(kind == 0, 2.0 * error, slope / NQ)
    sums = [
        jnp.sum(onehot * jnp.sum(part.reshape(-1, NPATCH), axis=1)[:, None], 0)
        for part in (square, quant)
    ]
    return jnp.stack(sums), grad.astype(jnp.bfloat16)


def layer_forward(state_zero, mats, parts, cosine, sine, causal):
    w_qkv, w_out, w_up, w_down = (mats[2], mats[3], mats[4], mats[5])
    gain_one, gain_two = (parts[3], parts[4])
    count_series = state_zero.shape[0] // NPATCH
    normed_one = rms_norm(state_zero, gain_one).astype(jnp.bfloat16)
    qkv = matmul(normed_one, w_qkv).reshape(count_series, NPATCH, 3, HEADS, HDIM)
    queries = (rotate(qkv[:, :, 0], cosine, sine) * HDIM ** (-0.5)).astype(jnp.bfloat16)
    key_rot = rotate(qkv[:, :, 1], cosine, sine).astype(jnp.bfloat16)
    value_all = qkv[:, :, 2].astype(jnp.bfloat16)
    scores = jnp.einsum("sqhd,skhd->shqk", queries, key_rot, preferred_element_type=jnp.float32)
    scores = jnp.where(causal, scores, -1e30)
    peak = jnp.max(scores, axis=-1, keepdims=True)
    expo = jnp.exp(scores - peak)
    total = jnp.sum(expo, axis=-1, keepdims=True)
    log_total = peak + jnp.log(total)
    attend = (expo / total).astype(jnp.bfloat16)
    mixed = jnp.einsum("shqk,skhd->sqhd", attend, value_all, preferred_element_type=jnp.float32)
    mixed = mixed.astype(jnp.bfloat16).reshape(state_zero.shape[0], D)
    state_one = state_zero + matmul(mixed, w_out)
    normed_two = rms_norm(state_one, gain_two).astype(jnp.bfloat16)
    up_pre = matmul(normed_two, w_up)
    activ = silu(up_pre).astype(jnp.bfloat16)
    state_two = state_one + matmul(activ, w_down)
    return (
        state_two,
        (
            normed_one,
            queries,
            key_rot,
            value_all,
            log_total,
            mixed,
            state_one,
            normed_two,
            up_pre,
            activ,
        ),
    )


def layer_backward(
    grad_two, state_zero, kept, mats, parts, cosine, sine, causal, owner, slots
):
    (
        normed_one,
        queries,
        key_rot,
        value_all,
        log_total,
        mixed,
        state_one,
        normed_two,
        up_pre,
        activ,
    ) = kept
    w_qkv, w_out, w_up, w_down = (mats[2], mats[3], mats[4], mats[5])
    gain_one, gain_two = (parts[3], parts[4])
    tokens = state_zero.shape[0]
    count_series = tokens // NPATCH
    grad_mlp = grad_two.astype(jnp.bfloat16)
    slots = grad_blocks(activ, grad_mlp, owner, 5, slots)
    grad_act = backmul(grad_mlp, w_down)
    grad_up_pre = (grad_act * silu_slope(up_pre)).astype(jnp.bfloat16)
    slots = grad_blocks(normed_two, grad_up_pre, owner, 4, slots)
    grad_normed = backmul(grad_up_pre, w_up)
    _, pull = jax.vjp(rms_norm, state_one, gain_two)
    grad_norm_in, grad_gain_two = pull(grad_normed)
    grad_one = grad_two + grad_norm_in
    grad_proj = grad_one.astype(jnp.bfloat16)
    slots = grad_blocks(mixed, grad_proj, owner, 3, slots)
    grad_mixed = (
        backmul(grad_proj, w_out).astype(jnp.bfloat16).reshape(count_series, NPATCH, HEADS, HDIM)
    )
    scores = jnp.einsum("sqhd,skhd->shqk", queries, key_rot, preferred_element_type=jnp.float32)
    attend = jnp.where(causal, jnp.exp(scores - log_total), 0.0)
    grad_attend = jnp.einsum(
        "sqhd,skhd->shqk", grad_mixed, value_all, preferred_element_type=jnp.float32
    )
    grad_scores = (
        attend * (grad_attend - jnp.sum(grad_attend * attend, axis=-1, keepdims=True))
    ).astype(jnp.bfloat16)
    grad_query = jnp.einsum(
        "shqk,skhd->sqhd", grad_scores, key_rot, preferred_element_type=jnp.float32
    )
    grad_key = jnp.einsum(
        "shqk,sqhd->skhd", grad_scores, queries, preferred_element_type=jnp.float32
    )
    grad_value = jnp.einsum(
        "shqk,sqhd->skhd",
        attend.astype(jnp.bfloat16),
        grad_mixed,
        preferred_element_type=jnp.float32,
    )
    grad_qkv = jnp.stack(
        [
            rotate(grad_query, cosine, -sine) * HDIM ** (-0.5),
            rotate(grad_key, cosine, -sine),
            grad_value,
        ],
        axis=2,
    )
    grad_qkv = grad_qkv.reshape(tokens, 3 * D).astype(jnp.bfloat16)
    slots = grad_blocks(normed_one, grad_qkv, owner, 2, slots)
    grad_normed_one = backmul(grad_qkv, w_qkv)
    _, pull = jax.vjp(rms_norm, state_zero, gain_one)
    grad_zero_in, grad_gain_one = pull(grad_normed_one)
    return (
        grad_one + grad_zero_in,
        slots,
        grad_gain_one,
        grad_gain_two,
    )


def adamw(weight, first, second, grad, step):
    power = step[0].astype(jnp.float32)
    first = BETA * first + (1.0 - BETA) * grad
    second = BETA * second + (1.0 - BETA) * grad * grad
    fix_one = 1.0 - jnp.power(BETA, power)
    fix_two = 1.0 - jnp.power(BETA, power)
    new = weight - RATE * (
        first / fix_one / (jnp.sqrt(second / fix_two) + EPSILON) + DECAY * weight
    )
    return (new, first, second)


def on_device(
    series,
    pad_mask,
    freq_class,
    owner,
    step,
    master,
    moment1,
    moment2,
    small_master,
    small_m1,
    small_m2,
):
    slot_count = master.shape[0]
    parts = split_small(small_master)
    freq, bias_one, bias_two, head_bias, out_bias = (
        parts[0],
        parts[1],
        parts[2],
        parts[5],
        parts[6],
    )
    feat, target, tmask = prepare(series, pad_mask)
    count_series = series.shape[0]
    tokens = count_series * NPATCH
    onehot = (freq_class[:, None] == jnp.arange(NCLASS, dtype=jnp.int32)[None, :]).astype(
        jnp.float32
    )
    local_counts = jnp.sum(
        onehot * jnp.sum(tmask.reshape(count_series, -1), axis=1)[:, None], 0
    )
    gathered, counts = gather_all(master.astype(jnp.bfloat16), local_counts)
    mats = tuple(unpack(gathered, owner, which) for which in range(len(MATS)))
    tok_in, tok_out, head_in, head_out = (mats[0], mats[1], mats[6], mats[7])
    class_weight = 1.0 / (counts * NCLASS)
    cosine, sine = tables()
    causal = jnp.arange(NPATCH)[:, None] >= jnp.arange(NPATCH)[None, :]
    patch_in = feat.reshape(tokens, 2 * PATCH).astype(jnp.bfloat16)
    tok_pre = matmul(patch_in, tok_in)
    hidden = silu(tok_pre[:, :D] + bias_one).astype(jnp.bfloat16)
    class_rows = jnp.repeat(jnp.dot(onehot, freq, precision=lax.Precision.HIGHEST), NPATCH, axis=0)
    state_zero = matmul(hidden, tok_out) + bias_two + tok_pre[:, D:] + class_rows
    state_two, _ = layer_forward(state_zero, mats, parts, cosine, sine, causal)
    state_low = state_two.astype(jnp.bfloat16)
    head_pre = matmul(state_low, head_in)
    head_hidden = silu(head_pre[:, :D] + head_bias).astype(jnp.bfloat16)
    out = matmul(head_hidden, head_out) + out_bias + head_pre[:, D:]

    local_sums, grad_out = loss_parts(out, target, tmask, onehot, class_weight)
    grad_out_bias = jnp.sum(grad_out.astype(jnp.float32), axis=0)
    slots = grad_blocks(head_hidden, grad_out, owner, 7, None)
    grad_head_first = backmul(grad_out, head_out) * silu_slope(head_pre[:, :D] + head_bias)
    grad_head_bias = jnp.sum(grad_head_first, axis=0)
    grad_head_pre = jnp.concatenate([grad_head_first, grad_out.astype(jnp.float32)], axis=1).astype(
        jnp.bfloat16
    )
    slots = grad_blocks(state_low, grad_head_pre, owner, 6, slots)
    grad_two = backmul(grad_head_pre, head_in)
    _, kept = layer_forward(state_zero, mats, parts, cosine, sine, causal)
    grad_zero, slots, grad_gain_one, grad_gain_two = layer_backward(
        grad_two, state_zero, kept, mats, parts, cosine, sine, causal, owner, slots
    )
    grad_prod = grad_zero.astype(jnp.bfloat16)
    slots = grad_blocks(hidden, grad_prod, owner, 1, slots)
    grad_first = backmul(grad_prod, tok_out) * silu_slope(tok_pre[:, :D] + bias_one)
    grad_tok_pre = jnp.concatenate([grad_first, grad_zero], axis=1).astype(jnp.bfloat16)
    slots = grad_blocks(patch_in, grad_tok_pre, owner, 0, slots)
    grad_freq = jnp.dot(
        onehot.T,
        grad_zero.reshape(count_series, NPATCH, D).sum(axis=1),
        precision=lax.Precision.HIGHEST,
    )
    small_local = jnp.concatenate(
        [
            grad_freq.reshape(-1),
            jnp.sum(grad_first, axis=0),
            jnp.sum(grad_zero, axis=0),
            grad_gain_one,
            grad_gain_two,
            grad_head_bias,
            grad_out_bias,
            local_sums.reshape(-1),
        ]
    )
    rank = lax.axis_index("wide") * lax.axis_size("narrow") + lax.axis_index("narrow")
    mine = rank * slot_count + jnp.arange(slot_count, dtype=jnp.int32)
    filled = jnp.any(owner[:, None] == mine[None, :], axis=0)
    owned, square_total, small_total = scatter_sum(slots, filled, small_local)
    small_grad = small_total[: small_master.shape[0]]
    sums = small_total[small_master.shape[0] :].reshape(2, NCLASS)
    grad_norm = jnp.sqrt(square_total + jnp.sum(small_grad * small_grad))
    scale = jnp.minimum(1.0, CLIP / grad_norm)
    loss = jnp.sum((sums[0] + sums[1] / NQ) * class_weight)
    new_master, new_m1, new_m2 = adamw(master, moment1, moment2, owned * scale, step)
    small_new, small_new_m1, small_new_m2 = adamw(
        small_master, small_m1, small_m2, small_grad * scale, step
    )
    return (
        loss,
        grad_norm,
        new_master,
        new_m1,
        new_m2,
        new_master.astype(jnp.bfloat16),
        small_new,
        small_new_m1,
        small_new_m2,
    )


def solution(mesh):
    return jax.shard_map(
        on_device,
        mesh=mesh,
        in_specs=(
            P(("wide", "narrow"), None),
            P(("wide", "narrow"), None),
            P(("wide", "narrow")),
            P(),
            P(),
            P(("wide", "narrow"), None, None),
            P(("wide", "narrow"), None, None),
            P(("wide", "narrow"), None, None),
            P(),
            P(),
            P(),
        ),
        out_specs=(
            P(),
            P(),
            P(("wide", "narrow"), None, None),
            P(("wide", "narrow"), None, None),
            P(("wide", "narrow"), None, None),
            P(("wide", "narrow"), None, None),
            P(),
            P(),
            P(),
        ),
        check_vma=False,
    )
```

```python
import functools

import jax
import jax.numpy as jnp
from jax import lax
from jax.experimental import pallas as pl
from jax.experimental.pallas import tpu as pltpu
from jax.sharding import PartitionSpec as P

D = 1280
HEADS = 16
HDIM = 80
FF = 5120
PATCH = 32
HORIZON = 128
NQ = 9
NPATCH = 16
NCLASS = 3
BR = 64
TOTAL_SLOTS = 512
CTX = 512
OUTW = 1280
ROWS = 20608
NBLK = 322


CLIP = 0.01
RATE = 0.03
DECAY = 0.1
BETA = 0.5
EPSILON = 1e-08


def matmul(left, right):
    return jnp.dot(left, right, preferred_element_type=jnp.float32)


def tmatmul(left, right):
    return lax.dot_general(
        left, right, (((0,), (0,)), ((), ())), preferred_element_type=jnp.float32
    )


def backmul(left, right):
    return lax.dot_general(
        left, right, (((1,), (1,)), ((), ())), preferred_element_type=jnp.float32
    )


def silu(value):
    return value / (1.0 + jnp.exp(-value))


def silu_slope(value):
    sigmoid = 1.0 / (1.0 + jnp.exp(-value))
    return sigmoid * (1.0 + value * (1.0 - sigmoid))


def rms_norm(hidden, gain):
    return hidden * lax.rsqrt(jnp.mean(hidden * hidden, axis=-1, keepdims=True) + 1e-06) * gain


def tables():
    half = HDIM // 2
    inverse = jnp.power(10000.0, -2.0 * jnp.arange(half, dtype=jnp.float32) / HDIM)
    angle = jnp.arange(NPATCH, dtype=jnp.float32)[:, None] * inverse[None, :]
    return (jnp.cos(angle)[None, :, None, :], jnp.sin(angle)[None, :, None, :])


def rotate(value, cosine, sine):
    half = HDIM // 2
    first = value[..., :half]
    second = value[..., half:]
    return jnp.concatenate(
        [first * cosine - second * sine, first * sine + second * cosine], axis=-1
    )


MATS = (
    (2 * PATCH, 2, 2),
    (D, 1, 4),
    (D, 3, 6),
    (D, 1, 4),
    (D, FF // D, 8),
    (FF, 1, 8),
    (D, (D + OUTW) // D, 8),
    (D, 1, 4),
)
BASES = tuple(sum(r * g for r, g, _ in MATS[:i]) // BR for i in range(len(MATS)))
LANES = 128
VMEM_LIMIT = 56 * 1024 * 1024


RING = 48


def steps_of(which):
    total, groups, count = MATS[which]
    return total * groups // (count * BR)


def stages(kind):
    return [pltpu.VMEM((2,) + kind(*MATS[which]), jnp.bfloat16) for which in range(len(MATS))]


def unpack_kernel(owner_ref, gathered_ref, *refs):
    outs, held = refs[:8], refs[8:16]
    ring, wide_ref, load_sem, store_sem = refs[16:]

    def load(b):
        at = lax.rem(b, RING)
        return pltpu.make_async_copy(
            gathered_ref.at[owner_ref[b]], ring.at[at], load_sem.at[at]
        )

    def first_load(b, carry):
        load(b).start()
        return carry

    lax.fori_loop(0, RING, first_load, 0)

    def store(which, i):
        total, groups, count = MATS[which]
        rows = count * BR // groups
        at = lax.rem(i, 2)
        return pltpu.make_async_copy(
            held[which].at[at],
            outs[which].at[pl.ds(pl.multiple_of(i * rows, rows), rows)],
            store_sem.at[which, at],
        )

    for which, (total, groups, count) in enumerate(MATS):
        rows = count * BR // groups

        def step(i, carry, which=which, groups=groups, count=count, rows=rows):
            first = BASES[which] + i * count
            at = lax.rem(i, 2)

            @pl.when(i >= 2)
            def _():
                store(which, i - 2).wait()

            for b in range(count):
                load(first + b).wait()
            for b in range(count):
                block = ring.at[lax.rem(first + b, RING)]
                span = slice(b * BR, (b + 1) * BR)
                if groups == 1:
                    held[which][at, span, :] = block[...]
                    continue
                for c in range(D // LANES):
                    wide_ref[c, span, :] = block[:, c * LANES : (c + 1) * LANES].astype(
                        jnp.float32
                    )
            if groups > 1:
                for j in range(groups):
                    for c in range(D // LANES):
                        left = j * D + c * LANES
                        held[which][at, :, left : left + LANES] = wide_ref[
                            c, pl.ds(j, rows, stride=groups), :
                        ].astype(jnp.bfloat16)
            store(which, i).start()
            for b in range(count):

                @pl.when(first + b + RING < NBLK)
                def _(b=b):
                    load(first + b + RING).start()

            return carry

        lax.fori_loop(0, steps_of(which), step, 0)

    for which in range(len(MATS)):
        for i in range(max(steps_of(which) - 2, 0), steps_of(which)):
            store(which, i).wait()


def unpack(gathered, owner):
    dma = pltpu.SemaphoreType.DMA
    return pl.pallas_call(
        unpack_kernel,
        out_shape=tuple(
            jax.ShapeDtypeStruct((total, groups * D), jnp.bfloat16) for total, groups, _ in MATS
        ),
        in_specs=[
            pl.BlockSpec(memory_space=pltpu.SMEM),
            pl.BlockSpec(memory_space=pl.ANY),
        ],
        out_specs=tuple(pl.BlockSpec(memory_space=pl.ANY) for _ in MATS),
        scratch_shapes=stages(lambda total, groups, count: (count * BR // groups, groups * D))
        + [
            pltpu.VMEM((RING, BR, D), jnp.bfloat16),
            pltpu.VMEM((D // LANES, 8 * BR, LANES), jnp.float32),
            dma((RING,)),
            dma((len(MATS), 2)),
        ],
        compiler_params=pltpu.CompilerParams(vmem_limit_bytes=VMEM_LIMIT),
        cost_estimate=pl.CostEstimate(
            flops=0, bytes_accessed=4 * ROWS * D, transcendentals=0
        ),
        name="unpack",
    )(owner, gathered)


def grad_kernel(owner_ref, *refs):
    lefts, rights, out_ref = refs[:8], refs[8:16], refs[16]
    left_in, right_in, held = refs[17:25], refs[25:33], refs[33:41]
    wide_ref, load_sem, store_sem = refs[41:]

    def loads(which):
        return (
            pltpu.make_async_copy(lefts[which], left_in[which], load_sem.at[which, 0]),
            pltpu.make_async_copy(rights[which], right_in[which], load_sem.at[which, 1]),
        )

    def store(which, i, b):
        at = lax.rem(i, 2)
        return pltpu.make_async_copy(
            held[which].at[at, pl.ds(b * BR, BR), :],
            out_ref.at[owner_ref[BASES[which] + i * MATS[which][2] + b]],
            store_sem.at[which, at, b],
        )

    order = tuple(reversed(range(len(MATS))))
    for which in order:
        for copy in loads(which):
            copy.start()
    for which in order:
        total, groups, count = MATS[which]
        rows = count * BR // groups
        for copy in loads(which):
            copy.wait()

        def step(i, carry, which=which, groups=groups, count=count, rows=rows):
            at = lax.rem(i, 2)

            @pl.when(i >= 2)
            def _():
                for b in range(count):
                    store(which, i - 2, b).wait()

            if steps_of(which) == 1:
                left = left_in[which][...]
            else:
                left = left_in[which][:, pl.ds(pl.multiple_of(i * rows, rows), rows)]
            for j in range(groups):
                part = tmatmul(left, right_in[which][:, j * D : (j + 1) * D])
                if groups == 1:
                    held[which][at] = part.astype(jnp.bfloat16)
                    continue
                for c in range(D // LANES):
                    wide_ref[c, pl.ds(j, rows, stride=groups), :] = part[
                        :, c * LANES : (c + 1) * LANES
                    ]
            if groups > 1:
                for c in range(D // LANES):
                    held[which][at, :, c * LANES : (c + 1) * LANES] = wide_ref[
                        c, 0 : count * BR, :
                    ].astype(jnp.bfloat16)
            for b in range(count):
                store(which, i, b).start()
            return carry

        lax.fori_loop(0, steps_of(which), step, 0)
    for which in order:
        for i in range(max(steps_of(which) - 2, 0), steps_of(which)):
            for b in range(MATS[which][2]):
                store(which, i, b).wait()


def grad_blocks(pairs, owner):
    lefts, rights = zip(*pairs)
    dma = pltpu.SemaphoreType.DMA
    tokens = lefts[0].shape[0]
    return pl.pallas_call(
        grad_kernel,
        out_shape=jax.ShapeDtypeStruct((TOTAL_SLOTS, BR, D), jnp.bfloat16),
        in_specs=[pl.BlockSpec(memory_space=pltpu.SMEM)]
        + [pl.BlockSpec(memory_space=pl.ANY)] * (2 * len(MATS)),
        out_specs=pl.BlockSpec(memory_space=pl.ANY),
        scratch_shapes=[pltpu.VMEM(left.shape, jnp.bfloat16) for left in lefts]
        + [pltpu.VMEM(right.shape, jnp.bfloat16) for right in rights]
        + stages(lambda total, groups, count: (count * BR, D))
        + [
            pltpu.VMEM((D // LANES, 8 * BR, LANES), jnp.float32),
            dma((len(MATS), 2)),
            dma((len(MATS), 2, 8)),
        ],
        compiler_params=pltpu.CompilerParams(vmem_limit_bytes=VMEM_LIMIT),
        cost_estimate=pl.CostEstimate(
            flops=2 * tokens * ROWS * D, bytes_accessed=2 * ROWS * D, transcendentals=0
        ),
        name="grad_blocks",
    )(owner, *lefts, *rights)


CHUNKS = 16
STEPS = CHUNKS + 7
MESH = pl.DeviceIdType.MESH


def total_of(*blocks):
    result = blocks[0].astype(jnp.float32)
    for block in blocks[1:]:
        result = result + block.astype(jnp.float32)
    return result


def scatter_kernel(
    slots_ref,
    small_ref,
    filled_ref,
    out_ref,
    small_out,
    square_out,
    small_in,
    own,
    pair_in,
    pair_sum,
    first_in,
    second_in,
    second_out,
    column,
    up_in,
    down_in,
    up_out,
    down_out,
    result,
    own_sem,
    pair_send,
    pair_recv,
    first_send,
    first_recv,
    second_send,
    second_recv,
    up_send,
    up_recv,
    down_send,
    down_recv,
    result_sem,
    share_send,
    share_recv,
    spread_send,
    spread_recv,
    square_send,
    square_recv,
):
    wide, z = lax.axis_index("wide"), lax.axis_index("narrow")
    core, here = lax.rem(wide, 2), lax.div(wide, 2)
    x, y = lax.rem(here, 2), lax.div(here, 2)
    far = 3 - here

    def device(place, level):
        return (place * 2 + core, level)

    partner = (here * 2 + 1 - core, z)

    def near(k, which):
        along_y = lax.rem(k + which, 2)
        return (y + along_y - 2 * y * along_y) * 2 + (x + (1 - along_y) - 2 * x * (1 - along_y))

    places = 8 * 4
    me = wide * 4 + z
    barrier = pltpu.get_barrier_semaphore()

    def each(action):
        def body(i, carry):
            other = lax.rem(me + i, places)
            action(i, other, (lax.div(other, 4), lax.rem(other, 4)))
            return carry

        lax.fori_loop(1, places, body, 0)

    def greet(i, other, to):
        pl.semaphore_signal(barrier, inc=1, device_id=to, device_id_type=MESH)

    def share(i, other, to):
        return pltpu.make_async_remote_copy(
            src_ref=small_ref.at[other],
            dst_ref=small_in.at[me],
            send_sem=share_send.at[i],
            recv_sem=share_recv.at[i],
            device_id=to,
            device_id_type=MESH,
        )

    def tell(ref, send, recv):
        def make(i, other, to):
            return pltpu.make_async_remote_copy(
                src_ref=ref.at[me],
                dst_ref=ref.at[me],
                send_sem=send.at[i],
                recv_sem=recv.at[i],
                device_id=to,
                device_id_type=MESH,
            )

        return make

    spread = tell(small_out, spread_send, spread_recv)
    square = tell(square_out, square_send, square_recv)
    each(greet)
    small_in[me] = small_ref[me]
    square_out[me] = jnp.zeros((8, LANES), jnp.float32)
    pl.semaphore_wait(barrier, places - 1)

    def own_copy(k):
        at = lax.rem(k, 2)
        return pltpu.make_async_copy(slots_ref.at[:, core, :, k], own.at[at], own_sem.at[at])

    def pair_copy(k):
        at = lax.rem(k, 2)
        return pltpu.make_async_remote_copy(
            src_ref=slots_ref.at[:, 1 - core, :, k],
            dst_ref=pair_in.at[at],
            send_sem=pair_send.at[at],
            recv_sem=pair_recv.at[at],
            device_id=partner,
            device_id_type=MESH,
        )

    def first_copy(k, part):
        place = near(k, 0)
        return pltpu.make_async_remote_copy(
            src_ref=pair_sum.at[lax.rem(k, 3), far if part == 0 else place],
            dst_ref=first_in.at[lax.rem(k, 5), part],
            send_sem=first_send.at[lax.rem(k, 3), part],
            recv_sem=first_recv.at[lax.rem(k, 5), part],
            device_id=device(place, z),
            device_id_type=MESH,
        )

    def second_copy(k):
        return pltpu.make_async_remote_copy(
            src_ref=second_out.at[lax.rem(k, 2)],
            dst_ref=second_in.at[lax.rem(k, 4)],
            send_sem=second_send.at[lax.rem(k, 2)],
            recv_sem=second_recv.at[lax.rem(k, 4)],
            device_id=device(near(k, 1), z),
            device_id_type=MESH,
        )

    def line_copy(k, level, source, target, send, recv, step):
        return pltpu.make_async_remote_copy(
            src_ref=source.at[lax.rem(k, 2), level],
            dst_ref=target.at[lax.rem(k, 6), level],
            send_sem=send.at[lax.rem(k, 2), level],
            recv_sem=recv.at[lax.rem(k, 6), level],
            device_id=device(here, z + step),
            device_id_type=MESH,
        )

    def up_copy(k, level):
        return line_copy(k, level, up_out, up_in, up_send, up_recv, 1)

    def down_copy(k, level):
        return line_copy(k, level, down_out, down_in, down_send, down_recv, -1)

    def result_copy(k):
        at = lax.rem(k, 2)
        return pltpu.make_async_copy(result.at[at], out_ref.at[k], result_sem.at[at])

    def valid(k):
        return jnp.logical_and(k >= 0, k < CHUNKS)

    own_copy(0).start()
    pair_copy(0).start()
    each(lambda *at: share(*at).start())

    def step(t, carry):
        @pl.when(valid(t - 3))
        def _():
            first_copy(t - 3, 0).wait_send()
            first_copy(t - 3, 1).wait_send()

        @pl.when(valid(t))
        def _():
            own_copy(t).wait()
            pair_copy(t).wait_recv()
            at, ring = lax.rem(t, 2), lax.rem(t, 3)

            def add(i, inner):
                p, n = lax.div(i, 4), lax.rem(i, 4)
                pair_sum[ring, p, n] = total_of(own[at, p, n], pair_in[at, p, n]).astype(
                    jnp.bfloat16
                )
                return inner

            lax.fori_loop(0, 16, add, 0)
            first_copy(t, 0).start()
            first_copy(t, 1).start()

        @pl.when(valid(t - 1))
        def _():
            pair_copy(t - 1).wait_send()

        @pl.when(t + 1 < CHUNKS)
        def _():
            own_copy(t + 1).start()
            pair_copy(t + 1).start()

        @pl.when(valid(t - 3))
        def _():
            second_copy(t - 3).wait_send()

        @pl.when(valid(t - 1))
        def _():
            k = t - 1
            first_copy(k, 0).wait_recv()
            place = near(k, 1)

            def add(n, inner):
                second_out[lax.rem(k, 2), n] = total_of(
                    pair_sum[lax.rem(k, 3), place, n], first_in[lax.rem(k, 5), 0, n]
                ).astype(jnp.bfloat16)
                return inner

            lax.fori_loop(0, 4, add, 0)
            second_copy(k).start()

        @pl.when(valid(t - 2))
        def _():
            k = t - 2
            first_copy(k, 1).wait_recv()
            second_copy(k).wait_recv()

            def add(n, inner):
                column[lax.rem(k, 4), n] = total_of(
                    pair_sum[lax.rem(k, 3), here, n],
                    first_in[lax.rem(k, 5), 1, n],
                    second_in[lax.rem(k, 4), n],
                ).astype(jnp.bfloat16)
                return inner

            lax.fori_loop(0, 4, add, 0)

        for lag, ahead, behind, copy, arrived, leaving in (
            (z, lambda n: n > z, z > 0, up_copy, up_in, up_out),
            (3 - z, lambda n: n < z, z < 3, down_copy, down_in, down_out),
        ):
            k = t - 2 - lag
            for n in range(4):

                @pl.when(jnp.logical_and(valid(k - 2), ahead(n)))
                def _(n=n, k=k, copy=copy):
                    copy(k - 2, n).wait_send()

                @pl.when(
                    jnp.logical_and(
                        jnp.logical_and(valid(k), behind), jnp.logical_or(ahead(n), n == z)
                    )
                )
                def _(n=n, k=k, copy=copy):
                    copy(k, n).wait_recv()

                moving = jnp.logical_and(valid(k), ahead(n))

                @pl.when(jnp.logical_and(moving, behind))
                def _(n=n, k=k, arrived=arrived, leaving=leaving):
                    leaving[lax.rem(k, 2), n] = total_of(
                        column[lax.rem(k, 4), n], arrived[lax.rem(k, 6), n]
                    ).astype(jnp.bfloat16)

                @pl.when(jnp.logical_and(moving, jnp.logical_not(behind)))
                def _(n=n, k=k, leaving=leaving):
                    leaving[lax.rem(k, 2), n] = column[lax.rem(k, 4), n]

                @pl.when(moving)
                def _(n=n, k=k, copy=copy):
                    copy(k, n).start()

        k = t - 5

        @pl.when(valid(k - 2))
        def _():
            result_copy(k - 2).wait()

        @pl.when(valid(k))
        def _():
            result[lax.rem(k, 2)] = column[lax.rem(k, 4), z].astype(jnp.float32)

            @pl.when(z > 0)
            def _():
                result[lax.rem(k, 2)] += up_in[lax.rem(k, 6), z].astype(jnp.float32)

            @pl.when(z < 3)
            def _():
                result[lax.rem(k, 2)] += down_in[lax.rem(k, 6), z].astype(jnp.float32)

            kept = jnp.where(filled_ref[k, 0:1, 0:1] > 0.0, result[lax.rem(k, 2)], 0.0)
            result[lax.rem(k, 2)] = kept
            squares = square_out[me]
            for i in range(BR // 8):
                for j in range(D // LANES):
                    part = kept[i * 8 : (i + 1) * 8, j * LANES : (j + 1) * LANES]
                    squares = squares + part * part
            square_out[me] = squares
            result_copy(k).start()

        @pl.when(t == CHUNKS // 2)
        def _():
            each(lambda *at: share(*at).wait())
            small = small_in[0]
            for i in range(1, places):
                small = small + small_in[i]
            small_out[me] = small
            each(lambda *at: spread(*at).start())

        return carry

    lax.fori_loop(0, STEPS, step, 0)
    each(lambda *at: square(*at).start())
    each(lambda *at: spread(*at).wait())
    each(lambda *at: square(*at).wait())


def scatter_sum(slots, filled, small):
    slot_count = filled.shape[0]
    wide, narrow = lax.axis_size("wide"), lax.axis_size("narrow")
    if (wide, narrow, slot_count) != (8, 4, CHUNKS):
        part = lax.psum_scatter(slots, "wide", scatter_dimension=0, tiled=True)
        owned = lax.psum_scatter(
            part.astype(jnp.float32), "narrow", scatter_dimension=0, tiled=True
        )
        owned = jnp.where(filled[:, None, None], owned, 0.0)
        square = lax.psum(jnp.sum(owned * owned), ("wide", "narrow"))
        return owned, square, lax.psum(small, ("wide", "narrow"))
    tiles = (wide * narrow, 8, LANES)
    room = wide * narrow * 8 * LANES - small.shape[0]
    assert room >= 0
    low = functools.partial(pltpu.VMEM, dtype=jnp.bfloat16)
    dma = pltpu.SemaphoreType.DMA
    block = (BR, D)
    owned, small_tiles, square_tiles = pl.pallas_call(
        scatter_kernel,
        out_shape=(
            jax.ShapeDtypeStruct((slot_count,) + block, jnp.float32),
            jax.ShapeDtypeStruct(tiles, jnp.float32),
            jax.ShapeDtypeStruct(tiles, jnp.float32),
        ),
        in_specs=[
            pl.BlockSpec(memory_space=pl.ANY),
            pl.BlockSpec(memory_space=pltpu.VMEM),
            pl.BlockSpec(memory_space=pltpu.VMEM),
        ],
        out_specs=(
            pl.BlockSpec(memory_space=pl.ANY),
            pl.BlockSpec(memory_space=pltpu.VMEM),
            pl.BlockSpec(memory_space=pltpu.VMEM),
        ),
        scratch_shapes=[
            pltpu.VMEM(tiles, jnp.float32),
            low((2, 4, 4) + block),
            low((2, 4, 4) + block),
            low((3, 4, 4) + block),
            low((5, 2, 4) + block),
            low((4, 4) + block),
            low((2, 4) + block),
            low((4, 4) + block),
            low((6, 4) + block),
            low((6, 4) + block),
            low((2, 4) + block),
            low((2, 4) + block),
            pltpu.VMEM((2,) + block, jnp.float32),
            dma((2,)),
            dma((2,)),
            dma((2,)),
            dma((3, 2)),
            dma((5, 2)),
            dma((2,)),
            dma((4,)),
            dma((2, 4)),
            dma((6, 4)),
            dma((2, 4)),
            dma((6, 4)),
            dma((2,)),
        ]
        + [dma((wide * narrow,))] * 6,
        compiler_params=pltpu.CompilerParams(
            collective_id=1, has_side_effects=True, vmem_limit_bytes=VMEM_LIMIT
        ),
        name="scatter_sum",
    )(
        slots.reshape(4, 2, narrow, slot_count, BR, D),
        jnp.pad(small, (0, room)).reshape(tiles),
        jnp.broadcast_to(
            filled.astype(jnp.float32)[:, None, None], (slot_count, 8, LANES)
        ),
    )
    return owned, jnp.sum(square_tiles), small_tiles.reshape(-1)[: small.shape[0]]


LATE = 4
EARLY = CHUNKS - LATE
COMBOS = 4 * LATE
GATHER_STEPS = EARLY + 5


def gather_kernel(
    own_ref,
    count_ref,
    all_ref,
    counts_ref,
    own_sem,
    recv,
    pair_recv,
    line_send,
    plane_send,
    turn_send,
    late_send,
    pair_send,
    late_pair_send,
    count_send,
    count_recv,
):
    wide, z = lax.axis_index("wide"), lax.axis_index("narrow")
    core, here = lax.rem(wide, 2), lax.div(wide, 2)
    x, y = lax.rem(here, 2), lax.div(here, 2)
    side, front, far = y * 2 + 1 - x, (1 - y) * 2 + x, 3 - here
    places = 8 * 4
    me = wide * 4 + z

    barrier = pltpu.get_barrier_semaphore()

    def greet(i, carry):
        other = lax.rem(me + i, places)
        pl.semaphore_signal(
            barrier,
            inc=1,
            device_id=(lax.div(other, 4), lax.rem(other, 4)),
            device_id_type=MESH,
        )
        return carry

    lax.fori_loop(1, places, greet, 0)
    fill = pltpu.make_async_copy(own_ref, all_ref.at[here, core, z], own_sem)
    fill.start()
    counts_ref[me] = count_ref[...]
    pl.semaphore_wait(barrier, places - 1)
    fill.wait()

    def count_copy(i):
        other = lax.rem(me + i, places)
        return pltpu.make_async_remote_copy(
            src_ref=count_ref,
            dst_ref=counts_ref.at[me],
            send_sem=count_send.at[i],
            recv_sem=count_recv.at[i],
            device_id=(lax.div(other, 4), lax.rem(other, 4)),
            device_id_type=MESH,
        )

    def count_start(i, carry):
        count_copy(i).start()
        return carry

    lax.fori_loop(1, places, count_start, 0)

    def piece(p, n, k, send, to):
        return pltpu.make_async_remote_copy(
            src_ref=all_ref.at[p, core, n, k],
            dst_ref=all_ref.at[p, core, n, k],
            send_sem=send,
            recv_sem=recv.at[p, n, k],
            device_id=to,
            device_id_type=MESH,
        )

    up, down = (wide, z + 1), (wide, z - 1)
    to_side, to_front = (side * 2 + core, z), (front * 2 + core, z)

    def line(n, k, step):
        return piece(here, n, k, line_send.at[step, n, k], (up, down)[step])

    def plane(n, k, which):
        return piece(here, n, k, plane_send.at[which, n, k], (to_side, to_front)[which])

    def turn(n, k, which):
        return piece(
            (side, front)[which], n, k, turn_send.at[n, k], (to_front, to_side)[which]
        )

    def late(c, n, step):
        p, k = lax.rem(here + c, 4), EARLY + lax.div(c, 4)
        return piece(p, n, k, late_send.at[step, c, n], (up, down)[step])

    def pair(p, k, send):
        return pltpu.make_async_remote_copy(
            src_ref=all_ref.at[p, core, :, k],
            dst_ref=all_ref.at[p, core, :, k],
            send_sem=send,
            recv_sem=pair_recv,
            device_id=(here * 2 + 1 - core, z),
            device_id_type=MESH,
        )

    def early_pair(p, k):
        return pair(p, k, pair_send.at[p, k])

    def late_pair(c):
        p, k = lax.rem(here + c, 4), EARLY + lax.div(c, 4)
        return pair(p, k, late_pair_send.at[c])

    def both_lines(make, n, j, start):
        @pl.when(jnp.logical_and(start, z < 3))
        def _():
            if j <= 0:
                make(n, 0)

        @pl.when(jnp.logical_and(start, z > 0))
        def _():
            if j >= 0:
                make(n, 1)

    def early(k):
        return jnp.logical_and(k >= 0, k < EARLY)

    def swap(n, k, go):
        even = lax.rem(n + k, 2) == 0

        @pl.when(jnp.logical_and(go, even))
        def _():
            turn(n, k, 0).start()

        @pl.when(jnp.logical_and(go, jnp.logical_not(even)))
        def _():
            turn(n, k, 1).start()

    for k in range(EARLY, CHUNKS):
        plane(z, k, 0).start()
        plane(z, k, 1).start()

    def step(t, carry):
        @pl.when(early(t))
        def _():
            plane(z, t, 0).start()
            plane(z, t, 1).start()

        both_lines(lambda n, way: line(n, t, way).start(), z, 0, early(t))

        for j in (-1, 1, -2, 2, -3, 3):
            n, k = z + j, t - abs(j)
            there = jnp.logical_and(early(k), jnp.logical_and(n >= 0, n < 4))

            @pl.when(there)
            def _(n=n, k=k, j=j):
                piece(here, n, k, plane_send.at[0, n, k], to_side).wait_recv()

            both_lines(lambda n, way, k=k: line(n, k, way).start(), n, j, there)

            @pl.when(there)
            def _(n=n, k=k):
                plane(n, k, 0).start()
                plane(n, k, 1).start()

        @pl.when(t == 1)
        def _():
            for k in range(EARLY, CHUNKS):
                plane_wait(side, z, k)
                plane_wait(front, z, k)
                swap(z, k, True)

        @pl.when(t == 2)
        def _():
            for k in range(EARLY, CHUNKS):
                plane_wait(far, z, k)

        for j in (0, -1, 1, -2, 2, -3, 3):
            m = t - 2 - abs(j)
            n = z + j
            first = m + lax.div(m + 2, 3)
            for c, more in ((first, True), (first + 1, lax.rem(m, 3) == 0)):
                there = jnp.logical_and(
                    jnp.logical_and(m >= 0, c < COMBOS),
                    jnp.logical_and(jnp.logical_and(n >= 0, n < 4), more),
                )
                if j:

                    @pl.when(there)
                    def _(n=n, c=c):
                        plane_wait(lax.rem(here + c, 4), n, EARLY + lax.div(c, 4))

                both_lines(lambda n, way, c=c: late(c, n, way).start(), n, j, there)

        for n in range(4):
            gap = jnp.abs(z - n)
            k = t - 1 - gap

            @pl.when(early(k))
            def _(n=n, k=k):
                plane_wait(side, n, k)
                plane_wait(front, n, k)

            swap(n, k, early(k))
            k = t - 2 - gap

            @pl.when(early(k))
            def _(n=n, k=k):
                plane_wait(far, n, k)

        for lag, sent in ((3, (here,)), (4, (side, front)), (5, (far,))):
            k = t - lag

            @pl.when(early(k))
            def _(k=k, sent=sent):
                for p in sent:
                    early_pair(p, k).start()

        m = t - 5
        first = m + lax.div(m + 2, 3)
        for c, more in ((first, True), (first + 1, lax.rem(m, 3) == 0)):

            @pl.when(jnp.logical_and(jnp.logical_and(m >= 0, c < COMBOS), more))
            def _(c=c):
                late_pair(c).start()

        return carry

    def plane_wait(p, n, k):
        piece(p, n, k, plane_send.at[0, n, k], to_side).wait_recv()

    lax.fori_loop(0, GATHER_STEPS, step, 0)

    def finish(k, carry):
        for n in range(4):
            plane_used = jnp.logical_or(k < EARLY, n == z)

            @pl.when(plane_used)
            def _(n=n):
                plane(n, k, 0).wait_send()
                plane(n, k, 1).wait_send()
                turn(n, k, 0).wait_send()

            @pl.when(jnp.logical_and(k < EARLY, jnp.logical_and(n <= z, z < 3)))
            def _(n=n):
                line(n, k, 0).wait_send()

            @pl.when(jnp.logical_and(k < EARLY, jnp.logical_and(n >= z, z > 0)))
            def _(n=n):
                line(n, k, 1).wait_send()

            @pl.when(jnp.logical_and(n <= z, z < 3))
            def _(n=n):
                late(k, n, 0).wait_send()

            @pl.when(jnp.logical_and(n >= z, z > 0))
            def _(n=n):
                late(k, n, 1).wait_send()

        @pl.when(k < EARLY)
        def _():
            for p in range(4):
                early_pair(p, k).wait_send()

        late_pair(k).wait_send()
        return carry

    lax.fori_loop(0, CHUNKS, finish, 0)

    def count_wait(i, carry):
        count_copy(i).wait()
        return carry

    lax.fori_loop(1, places, count_wait, 0)
    pltpu.make_async_copy(
        all_ref.at[:, 1 - core], all_ref.at[:, 1 - core], pair_recv
    ).wait()


def gather_all(low, local_counts):
    slot_count = low.shape[0]
    wide, narrow = lax.axis_size("wide"), lax.axis_size("narrow")
    if (wide, narrow, slot_count) != (8, 4, CHUNKS):
        return (
            lax.all_gather(low, ("wide", "narrow"), axis=0, tiled=True),
            lax.psum(local_counts, ("wide", "narrow")),
        )
    dma = pltpu.SemaphoreType.DMA
    tile = jnp.zeros((8, LANES), jnp.float32).at[0, :NCLASS].set(local_counts)
    gathered, tiles = pl.pallas_call(
        gather_kernel,
        out_shape=(
            jax.ShapeDtypeStruct((4, 2, narrow, slot_count, BR, D), jnp.bfloat16),
            jax.ShapeDtypeStruct((wide * narrow, 8, LANES), jnp.float32),
        ),
        in_specs=[
            pl.BlockSpec(memory_space=pltpu.VMEM),
            pl.BlockSpec(memory_space=pltpu.VMEM),
        ],
        out_specs=(
            pl.BlockSpec(memory_space=pl.ANY),
            pl.BlockSpec(memory_space=pltpu.VMEM),
        ),
        scratch_shapes=[
            dma,
            dma((4, 4, CHUNKS)),
            dma,
            dma((2, 4, EARLY)),
            dma((2, 4, CHUNKS)),
            dma((4, CHUNKS)),
            dma((2, COMBOS, 4)),
            dma((4, EARLY)),
            dma((COMBOS,)),
            dma((wide * narrow,)),
            dma((wide * narrow,)),
        ],
        compiler_params=pltpu.CompilerParams(
            collective_id=2, has_side_effects=True, vmem_limit_bytes=VMEM_LIMIT
        ),
        name="gather_all",
    )(low, tile)
    return (
        gathered.reshape(wide * narrow * slot_count, BR, D),
        jnp.sum(tiles[:, 0, :NCLASS], axis=0),
    )


def split_small(small):
    freq = small[: NCLASS * D].reshape(NCLASS, D)
    rest = small[NCLASS * D :]
    return (
        freq,
        rest[0:D],
        rest[D : 2 * D],
        rest[2 * D : 3 * D],
        rest[3 * D : 4 * D],
        rest[4 * D : 5 * D],
        rest[5 * D : 5 * D + OUTW],
    )


def prepare(series, pad_mask):
    valid = (1 - pad_mask).astype(jnp.float32)
    count_series = series.shape[0]
    context = (series[:, :CTX] * valid[:, :CTX]).reshape(count_series, NPATCH, PATCH)
    marks = pad_mask[:, :CTX].astype(jnp.float32).reshape(count_series, NPATCH, PATCH)
    feat = jnp.concatenate([context, marks], axis=-1)
    return (feat, horizons(series), horizons(valid))


def horizons(points):
    count_series = points.shape[0]
    pieces = points.reshape(count_series, -1, PATCH)
    return jnp.concatenate(
        [pieces[:, 1 + j : 1 + j + NPATCH] for j in range(HORIZON // PATCH)], axis=-1
    ).reshape(count_series * NPATCH, HORIZON)


def loss_parts(out, target, tmask, onehot, class_weight):
    column = lax.broadcasted_iota(jnp.int32, (HORIZON, OUTW), 1)
    row = lax.broadcasted_iota(jnp.int32, (HORIZON, OUTW), 0)
    spread = (lax.div(column, NQ + 1) == row).astype(jnp.float32)
    wanted = jnp.dot(target, spread, precision=lax.Precision.HIGHEST)
    mask = matmul(tmask.astype(jnp.bfloat16), spread.astype(jnp.bfloat16))
    kind = lax.rem(lax.broadcasted_iota(jnp.int32, (1, OUTW), 1), NQ + 1)
    level = kind.astype(jnp.float32) / (NQ + 1)
    error = out - wanted
    above, below = level * -error, (level - 1.0) * -error
    slope = jnp.where(above > below, -level, jnp.where(above < below, 1.0 - level, 0.5 - level))
    square = jnp.sum(jnp.where(kind == 0, error * error * mask, 0.0), axis=1)
    quant = jnp.sum(jnp.where(kind == 0, 0.0, jnp.maximum(above, below) * mask), axis=1)
    weight = jnp.repeat(jnp.sum(onehot * class_weight[None, :], axis=1), NPATCH)[:, None]
    grad = weight * mask * jnp.where(kind == 0, 2.0 * error, slope / NQ)
    sums = [
        jnp.sum(onehot * jnp.sum(part.reshape(-1, NPATCH), axis=1)[:, None], 0)
        for part in (square, quant)
    ]
    return jnp.stack(sums), grad.astype(jnp.bfloat16)


def layer_forward(state_zero, mats, parts, cosine, sine, causal):
    w_qkv, w_out, w_up, w_down = (mats[2], mats[3], mats[4], mats[5])
    gain_one, gain_two = (parts[3], parts[4])
    count_series = state_zero.shape[0] // NPATCH
    normed_one = rms_norm(state_zero, gain_one).astype(jnp.bfloat16)
    qkv = matmul(normed_one, w_qkv).reshape(count_series, NPATCH, 3, HEADS, HDIM)
    queries = (rotate(qkv[:, :, 0], cosine, sine) * HDIM ** (-0.5)).astype(jnp.bfloat16)
    key_rot = rotate(qkv[:, :, 1], cosine, sine).astype(jnp.bfloat16)
    value_all = qkv[:, :, 2].astype(jnp.bfloat16)
    scores = jnp.einsum("sqhd,skhd->shqk", queries, key_rot, preferred_element_type=jnp.float32)
    scores = jnp.where(causal, scores, -1e30)
    peak = jnp.max(scores, axis=-1, keepdims=True)
    expo = jnp.exp(scores - peak)
    total = jnp.sum(expo, axis=-1, keepdims=True)
    log_total = peak + jnp.log(total)
    attend = (expo / total).astype(jnp.bfloat16)
    mixed = jnp.einsum("shqk,skhd->sqhd", attend, value_all, preferred_element_type=jnp.float32)
    mixed = mixed.astype(jnp.bfloat16).reshape(state_zero.shape[0], D)
    state_one = state_zero + matmul(mixed, w_out)
    normed_two = rms_norm(state_one, gain_two).astype(jnp.bfloat16)
    up_pre = matmul(normed_two, w_up)
    activ = silu(up_pre).astype(jnp.bfloat16)
    state_two = state_one + matmul(activ, w_down)
    return (
        state_two,
        (
            normed_one,
            queries,
            key_rot,
            value_all,
            log_total,
            mixed,
            state_one,
            normed_two,
            up_pre,
            activ,
        ),
    )


def layer_backward(grad_two, state_zero, kept, mats, parts, cosine, sine, causal):
    (
        normed_one,
        queries,
        key_rot,
        value_all,
        log_total,
        mixed,
        state_one,
        normed_two,
        up_pre,
        activ,
    ) = kept
    w_qkv, w_out, w_up, w_down = (mats[2], mats[3], mats[4], mats[5])
    gain_one, gain_two = (parts[3], parts[4])
    tokens = state_zero.shape[0]
    count_series = tokens // NPATCH
    grad_mlp = grad_two.astype(jnp.bfloat16)
    grad_act = backmul(grad_mlp, w_down)
    grad_up_pre = (grad_act * silu_slope(up_pre)).astype(jnp.bfloat16)
    grad_normed = backmul(grad_up_pre, w_up)
    _, pull = jax.vjp(rms_norm, state_one, gain_two)
    grad_norm_in, grad_gain_two = pull(grad_normed)
    grad_one = grad_two + grad_norm_in
    grad_proj = grad_one.astype(jnp.bfloat16)
    grad_mixed = (
        backmul(grad_proj, w_out).astype(jnp.bfloat16).reshape(count_series, NPATCH, HEADS, HDIM)
    )
    scores = jnp.einsum("sqhd,skhd->shqk", queries, key_rot, preferred_element_type=jnp.float32)
    attend = jnp.where(causal, jnp.exp(scores - log_total), 0.0)
    grad_attend = jnp.einsum(
        "sqhd,skhd->shqk", grad_mixed, value_all, preferred_element_type=jnp.float32
    )
    grad_scores = (
        attend * (grad_attend - jnp.sum(grad_attend * attend, axis=-1, keepdims=True))
    ).astype(jnp.bfloat16)
    grad_query = jnp.einsum(
        "shqk,skhd->sqhd", grad_scores, key_rot, preferred_element_type=jnp.float32
    )
    grad_key = jnp.einsum(
        "shqk,sqhd->skhd", grad_scores, queries, preferred_element_type=jnp.float32
    )
    grad_value = jnp.einsum(
        "shqk,sqhd->skhd",
        attend.astype(jnp.bfloat16),
        grad_mixed,
        preferred_element_type=jnp.float32,
    )
    grad_qkv = jnp.stack(
        [
            rotate(grad_query, cosine, -sine) * HDIM ** (-0.5),
            rotate(grad_key, cosine, -sine),
            grad_value,
        ],
        axis=2,
    )
    grad_qkv = grad_qkv.reshape(tokens, 3 * D).astype(jnp.bfloat16)
    grad_normed_one = backmul(grad_qkv, w_qkv)
    _, pull = jax.vjp(rms_norm, state_zero, gain_one)
    grad_zero_in, grad_gain_one = pull(grad_normed_one)
    return (
        grad_one + grad_zero_in,
        (
            (normed_one, grad_qkv),
            (mixed, grad_proj),
            (normed_two, grad_up_pre),
            (activ, grad_mlp),
        ),
        grad_gain_one,
        grad_gain_two,
    )


def adamw(weight, first, second, grad, step):
    power = step[0].astype(jnp.float32)
    first = BETA * first + (1.0 - BETA) * grad
    second = BETA * second + (1.0 - BETA) * grad * grad
    fix_one = 1.0 - jnp.power(BETA, power)
    fix_two = 1.0 - jnp.power(BETA, power)
    new = weight - RATE * (
        first / fix_one / (jnp.sqrt(second / fix_two) + EPSILON) + DECAY * weight
    )
    return (new, first, second)


def on_device(
    series,
    pad_mask,
    freq_class,
    owner,
    step,
    master,
    moment1,
    moment2,
    small_master,
    small_m1,
    small_m2,
):
    slot_count = master.shape[0]
    parts = split_small(small_master)
    freq, bias_one, bias_two, head_bias, out_bias = (
        parts[0],
        parts[1],
        parts[2],
        parts[5],
        parts[6],
    )
    feat, target, tmask = prepare(series, pad_mask)
    count_series = series.shape[0]
    tokens = count_series * NPATCH
    onehot = (freq_class[:, None] == jnp.arange(NCLASS, dtype=jnp.int32)[None, :]).astype(
        jnp.float32
    )
    local_counts = jnp.sum(
        onehot * jnp.sum(tmask.reshape(count_series, -1), axis=1)[:, None], 0
    )
    gathered, counts = gather_all(master.astype(jnp.bfloat16), local_counts)
    mats = unpack(gathered, owner)
    tok_in, tok_out, head_in, head_out = (mats[0], mats[1], mats[6], mats[7])
    class_weight = 1.0 / (counts * NCLASS)
    cosine, sine = tables()
    causal = jnp.arange(NPATCH)[:, None] >= jnp.arange(NPATCH)[None, :]
    patch_in = feat.reshape(tokens, 2 * PATCH).astype(jnp.bfloat16)
    tok_pre = matmul(patch_in, tok_in)
    hidden = silu(tok_pre[:, :D] + bias_one).astype(jnp.bfloat16)
    class_rows = jnp.repeat(jnp.dot(onehot, freq, precision=lax.Precision.HIGHEST), NPATCH, axis=0)
    state_zero = matmul(hidden, tok_out) + bias_two + tok_pre[:, D:] + class_rows
    state_two, _ = layer_forward(state_zero, mats, parts, cosine, sine, causal)
    state_low = state_two.astype(jnp.bfloat16)
    head_pre = matmul(state_low, head_in)
    head_hidden = silu(head_pre[:, :D] + head_bias).astype(jnp.bfloat16)
    out = matmul(head_hidden, head_out) + out_bias + head_pre[:, D:]

    local_sums, grad_out = loss_parts(out, target, tmask, onehot, class_weight)
    grad_out_bias = jnp.sum(grad_out.astype(jnp.float32), axis=0)
    grad_head_first = backmul(grad_out, head_out) * silu_slope(head_pre[:, :D] + head_bias)
    grad_head_bias = jnp.sum(grad_head_first, axis=0)
    grad_head_pre = jnp.concatenate([grad_head_first, grad_out.astype(jnp.float32)], axis=1).astype(
        jnp.bfloat16
    )
    grad_two = backmul(grad_head_pre, head_in)
    _, kept = layer_forward(state_zero, mats, parts, cosine, sine, causal)
    grad_zero, layer_pairs, grad_gain_one, grad_gain_two = layer_backward(
        grad_two, state_zero, kept, mats, parts, cosine, sine, causal
    )
    grad_prod = grad_zero.astype(jnp.bfloat16)
    grad_first = backmul(grad_prod, tok_out) * silu_slope(tok_pre[:, :D] + bias_one)
    grad_tok_pre = jnp.concatenate([grad_first, grad_zero], axis=1).astype(jnp.bfloat16)
    slots = grad_blocks(
        ((patch_in, grad_tok_pre), (hidden, grad_prod))
        + layer_pairs
        + ((state_low, grad_head_pre), (head_hidden, grad_out)),
        owner,
    )
    grad_freq = jnp.dot(
        onehot.T,
        grad_zero.reshape(count_series, NPATCH, D).sum(axis=1),
        precision=lax.Precision.HIGHEST,
    )
    small_local = jnp.concatenate(
        [
            grad_freq.reshape(-1),
            jnp.sum(grad_first, axis=0),
            jnp.sum(grad_zero, axis=0),
            grad_gain_one,
            grad_gain_two,
            grad_head_bias,
            grad_out_bias,
            local_sums.reshape(-1),
        ]
    )
    rank = lax.axis_index("wide") * lax.axis_size("narrow") + lax.axis_index("narrow")
    mine = rank * slot_count + jnp.arange(slot_count, dtype=jnp.int32)
    filled = jnp.any(owner[:, None] == mine[None, :], axis=0)
    owned, square_total, small_total = scatter_sum(slots, filled, small_local)
    small_grad = small_total[: small_master.shape[0]]
    sums = small_total[small_master.shape[0] :].reshape(2, NCLASS)
    grad_norm = jnp.sqrt(square_total + jnp.sum(small_grad * small_grad))
    scale = jnp.minimum(1.0, CLIP / grad_norm)
    loss = jnp.sum((sums[0] + sums[1] / NQ) * class_weight)
    new_master, new_m1, new_m2 = adamw(master, moment1, moment2, owned * scale, step)
    small_new, small_new_m1, small_new_m2 = adamw(
        small_master, small_m1, small_m2, small_grad * scale, step
    )
    return (
        loss,
        grad_norm,
        new_master,
        new_m1,
        new_m2,
        new_master.astype(jnp.bfloat16),
        small_new,
        small_new_m1,
        small_new_m2,
    )


def solution(mesh):
    return jax.shard_map(
        on_device,
        mesh=mesh,
        in_specs=(
            P(("wide", "narrow"), None),
            P(("wide", "narrow"), None),
            P(("wide", "narrow")),
            P(),
            P(),
            P(("wide", "narrow"), None, None),
            P(("wide", "narrow"), None, None),
            P(("wide", "narrow"), None, None),
            P(),
            P(),
            P(),
        ),
        out_specs=(
            P(),
            P(),
            P(("wide", "narrow"), None, None),
            P(("wide", "narrow"), None, None),
            P(("wide", "narrow"), None, None),
            P(("wide", "narrow"), None, None),
            P(),
            P(),
            P(),
        ),
        check_vma=False,
    )
```

```python
import functools

import jax
import jax.numpy as jnp
from jax import lax
from jax.experimental import pallas as pl
from jax.experimental.pallas import tpu as pltpu
from jax.sharding import PartitionSpec as P

D = 1280
HEADS = 16
HDIM = 80
FF = 5120
PATCH = 32
HORIZON = 128
NQ = 9
NPATCH = 16
NCLASS = 3
BR = 64
TOTAL_SLOTS = 512
CTX = 512
OUTW = 1280
ROWS = 20608
NBLK = 322


CLIP = 0.01
RATE = 0.03
DECAY = 0.1
BETA = 0.5
EPSILON = 1e-08


def matmul(left, right):
    return jnp.dot(left, right, preferred_element_type=jnp.float32)


def tmatmul(left, right):
    return lax.dot_general(
        left, right, (((0,), (0,)), ((), ())), preferred_element_type=jnp.float32
    )


def backmul(left, right):
    return lax.dot_general(
        left, right, (((1,), (1,)), ((), ())), preferred_element_type=jnp.float32
    )


def silu(value):
    return value / (1.0 + jnp.exp(-value))


def silu_slope(value):
    sigmoid = 1.0 / (1.0 + jnp.exp(-value))
    return sigmoid * (1.0 + value * (1.0 - sigmoid))


def rms_norm(hidden, gain):
    return hidden * lax.rsqrt(jnp.mean(hidden * hidden, axis=-1, keepdims=True) + 1e-06) * gain


def tables():
    half = HDIM // 2
    inverse = jnp.power(10000.0, -2.0 * jnp.arange(half, dtype=jnp.float32) / HDIM)
    angle = jnp.arange(NPATCH, dtype=jnp.float32)[:, None] * inverse[None, :]
    return (jnp.cos(angle)[None, :, None, :], jnp.sin(angle)[None, :, None, :])


def rotate(value, cosine, sine):
    half = HDIM // 2
    first = value[..., :half]
    second = value[..., half:]
    return jnp.concatenate(
        [first * cosine - second * sine, first * sine + second * cosine], axis=-1
    )


MATS = (
    (2 * PATCH, 2, 2),
    (D, 1, 4),
    (D, 3, 6),
    (D, 1, 4),
    (D, FF // D, 8),
    (FF, 1, 8),
    (D, (D + OUTW) // D, 8),
    (D, 1, 4),
)
BASES = tuple(sum(r * g for r, g, _ in MATS[:i]) // BR for i in range(len(MATS)))
LANES = 128
VMEM_LIMIT = 56 * 1024 * 1024
SCATTER_VMEM = 61 * 1024 * 1024


RING = 48


def steps_of(which):
    total, groups, count = MATS[which]
    return total * groups // (count * BR)


def stages(kind):
    return [pltpu.VMEM((2,) + kind(*MATS[which]), jnp.bfloat16) for which in range(len(MATS))]


def unpack_kernel(owner_ref, gathered_ref, *refs):
    outs, held = refs[:8], refs[8:16]
    ring, wide_ref, load_sem, store_sem = refs[16:]

    def load(b):
        at = lax.rem(b, RING)
        return pltpu.make_async_copy(
            gathered_ref.at[owner_ref[b]], ring.at[at], load_sem.at[at]
        )

    def first_load(b, carry):
        load(b).start()
        return carry

    lax.fori_loop(0, RING, first_load, 0)

    def store(which, i):
        total, groups, count = MATS[which]
        rows = count * BR // groups
        at = lax.rem(i, 2)
        return pltpu.make_async_copy(
            held[which].at[at],
            outs[which].at[pl.ds(pl.multiple_of(i * rows, rows), rows)],
            store_sem.at[which, at],
        )

    for which, (total, groups, count) in enumerate(MATS):
        rows = count * BR // groups

        def step(i, carry, which=which, groups=groups, count=count, rows=rows):
            first = BASES[which] + i * count
            at = lax.rem(i, 2)

            @pl.when(i >= 2)
            def _():
                store(which, i - 2).wait()

            for b in range(count):
                load(first + b).wait()
            for b in range(count):
                block = ring.at[lax.rem(first + b, RING)]
                span = slice(b * BR, (b + 1) * BR)
                if groups == 1:
                    held[which][at, span, :] = block[...]
                    continue
                for c in range(D // LANES):
                    wide_ref[c, span, :] = block[:, c * LANES : (c + 1) * LANES].astype(
                        jnp.float32
                    )
            if groups > 1:
                for j in range(groups):
                    for c in range(D // LANES):
                        left = j * D + c * LANES
                        held[which][at, :, left : left + LANES] = wide_ref[
                            c, pl.ds(j, rows, stride=groups), :
                        ].astype(jnp.bfloat16)
            store(which, i).start()
            for b in range(count):

                @pl.when(first + b + RING < NBLK)
                def _(b=b):
                    load(first + b + RING).start()

            return carry

        lax.fori_loop(0, steps_of(which), step, 0)

    for which in range(len(MATS)):
        for i in range(max(steps_of(which) - 2, 0), steps_of(which)):
            store(which, i).wait()


def unpack(gathered, owner):
    dma = pltpu.SemaphoreType.DMA
    return pl.pallas_call(
        unpack_kernel,
        out_shape=tuple(
            jax.ShapeDtypeStruct((total, groups * D), jnp.bfloat16) for total, groups, _ in MATS
        ),
        in_specs=[
            pl.BlockSpec(memory_space=pltpu.SMEM),
            pl.BlockSpec(memory_space=pl.ANY),
        ],
        out_specs=tuple(pl.BlockSpec(memory_space=pl.ANY) for _ in MATS),
        scratch_shapes=stages(lambda total, groups, count: (count * BR // groups, groups * D))
        + [
            pltpu.VMEM((RING, BR, D), jnp.bfloat16),
            pltpu.VMEM((D // LANES, 8 * BR, LANES), jnp.float32),
            dma((RING,)),
            dma((len(MATS), 2)),
        ],
        compiler_params=pltpu.CompilerParams(vmem_limit_bytes=VMEM_LIMIT),
        cost_estimate=pl.CostEstimate(
            flops=0, bytes_accessed=4 * ROWS * D, transcendentals=0
        ),
        name="unpack",
    )(owner, gathered)


def grad_kernel(owner_ref, *refs):
    lefts, rights, out_ref = refs[:8], refs[8:16], refs[16]
    left_in, right_in, held = refs[17:25], refs[25:33], refs[33:41]
    wide_ref, load_sem, store_sem = refs[41:]

    def loads(which):
        return (
            pltpu.make_async_copy(lefts[which], left_in[which], load_sem.at[which, 0]),
            pltpu.make_async_copy(rights[which], right_in[which], load_sem.at[which, 1]),
        )

    def store(which, i, b):
        at = lax.rem(i, 2)
        return pltpu.make_async_copy(
            held[which].at[at, pl.ds(b * BR, BR), :],
            out_ref.at[owner_ref[BASES[which] + i * MATS[which][2] + b]],
            store_sem.at[which, at, b],
        )

    order = tuple(reversed(range(len(MATS))))
    for which in order:
        for copy in loads(which):
            copy.start()
    for which in order:
        total, groups, count = MATS[which]
        rows = count * BR // groups
        for copy in loads(which):
            copy.wait()

        def step(i, carry, which=which, groups=groups, count=count, rows=rows):
            at = lax.rem(i, 2)

            @pl.when(i >= 2)
            def _():
                for b in range(count):
                    store(which, i - 2, b).wait()

            if steps_of(which) == 1:
                left = left_in[which][...]
            else:
                left = left_in[which][:, pl.ds(pl.multiple_of(i * rows, rows), rows)]
            for j in range(groups):
                part = tmatmul(left, right_in[which][:, j * D : (j + 1) * D])
                if groups == 1:
                    held[which][at] = part.astype(jnp.bfloat16)
                    continue
                for c in range(D // LANES):
                    wide_ref[c, pl.ds(j, rows, stride=groups), :] = part[
                        :, c * LANES : (c + 1) * LANES
                    ]
            if groups > 1:
                for c in range(D // LANES):
                    held[which][at, :, c * LANES : (c + 1) * LANES] = wide_ref[
                        c, 0 : count * BR, :
                    ].astype(jnp.bfloat16)
            for b in range(count):
                store(which, i, b).start()
            return carry

        lax.fori_loop(0, steps_of(which), step, 0)
    for which in order:
        for i in range(max(steps_of(which) - 2, 0), steps_of(which)):
            for b in range(MATS[which][2]):
                store(which, i, b).wait()


def grad_blocks(pairs, owner):
    lefts, rights = zip(*pairs)
    dma = pltpu.SemaphoreType.DMA
    tokens = lefts[0].shape[0]
    return pl.pallas_call(
        grad_kernel,
        out_shape=jax.ShapeDtypeStruct((TOTAL_SLOTS, BR, D), jnp.bfloat16),
        in_specs=[pl.BlockSpec(memory_space=pltpu.SMEM)]
        + [pl.BlockSpec(memory_space=pl.ANY)] * (2 * len(MATS)),
        out_specs=pl.BlockSpec(memory_space=pl.ANY),
        scratch_shapes=[pltpu.VMEM(left.shape, jnp.bfloat16) for left in lefts]
        + [pltpu.VMEM(right.shape, jnp.bfloat16) for right in rights]
        + stages(lambda total, groups, count: (count * BR, D))
        + [
            pltpu.VMEM((D // LANES, 8 * BR, LANES), jnp.float32),
            dma((len(MATS), 2)),
            dma((len(MATS), 2, 8)),
        ],
        compiler_params=pltpu.CompilerParams(vmem_limit_bytes=VMEM_LIMIT),
        cost_estimate=pl.CostEstimate(
            flops=2 * tokens * ROWS * D, bytes_accessed=2 * ROWS * D, transcendentals=0
        ),
        name="grad_blocks",
    )(owner, *lefts, *rights)


CHUNKS = 16
LATE = 4
EARLY = CHUNKS - LATE
COMBOS = 4 * LATE
STEPS = COMBOS + 5
MESH = pl.DeviceIdType.MESH


def total_of(*blocks):
    result = blocks[0].astype(jnp.float32)
    for block in blocks[1:]:
        result = result + block.astype(jnp.float32)
    return result


def scatter_kernel(
    slots_ref,
    small_ref,
    filled_ref,
    out_ref,
    small_out,
    square_out,
    small_in,
    own,
    pair_in,
    pair_sum,
    first_in,
    second_in,
    second_out,
    column,
    up_in,
    down_in,
    up_out,
    down_out,
    result,
    late_own,
    late_pair_in,
    late_sum,
    late_up_in,
    late_down_in,
    late_up_out,
    late_down_out,
    late_column,
    late_first_in,
    late_second_in,
    late_second_out,
    late_result,
    own_sem,
    pair_send,
    pair_recv,
    first_send,
    first_recv,
    second_send,
    second_recv,
    up_send,
    up_recv,
    down_send,
    down_recv,
    result_sem,
    late_own_sem,
    late_pair_send,
    late_pair_recv,
    late_up_send,
    late_up_recv,
    late_down_send,
    late_down_recv,
    late_first_send,
    late_first_recv,
    late_second_send,
    late_second_recv,
    late_result_sem,
    share_send,
    share_recv,
    spread_send,
    spread_recv,
    square_send,
    square_recv,
):
    wide, z = lax.axis_index("wide"), lax.axis_index("narrow")
    core, here = lax.rem(wide, 2), lax.div(wide, 2)
    x, y = lax.rem(here, 2), lax.div(here, 2)
    far = 3 - here

    def device(place, level):
        return (place * 2 + core, level)

    partner = (here * 2 + 1 - core, z)

    def near(k, which):
        along_y = lax.rem(k + which, 2)
        return (y + along_y - 2 * y * along_y) * 2 + (x + (1 - along_y) - 2 * x * (1 - along_y))

    places = 8 * 4
    me = wide * 4 + z
    barrier = pltpu.get_barrier_semaphore()

    def each(action):
        def body(i, carry):
            other = lax.rem(me + i, places)
            action(i, other, (lax.div(other, 4), lax.rem(other, 4)))
            return carry

        lax.fori_loop(1, places, body, 0)

    def greet(i, other, to):
        pl.semaphore_signal(barrier, inc=1, device_id=to, device_id_type=MESH)

    def share(i, other, to):
        return pltpu.make_async_remote_copy(
            src_ref=small_ref.at[other],
            dst_ref=small_in.at[me],
            send_sem=share_send.at[i],
            recv_sem=share_recv.at[i],
            device_id=to,
            device_id_type=MESH,
        )

    def tell(ref, send, recv):
        def make(i, other, to):
            return pltpu.make_async_remote_copy(
                src_ref=ref.at[me],
                dst_ref=ref.at[me],
                send_sem=send.at[i],
                recv_sem=recv.at[i],
                device_id=to,
                device_id_type=MESH,
            )

        return make

    spread = tell(small_out, spread_send, spread_recv)
    square = tell(square_out, square_send, square_recv)
    each(greet)
    small_in[me] = small_ref[me]
    square_out[me] = jnp.zeros((8, LANES), jnp.float32)
    pl.semaphore_wait(barrier, places - 1)

    def own_copy(k):
        at = lax.rem(k, 2)
        return pltpu.make_async_copy(slots_ref.at[:, core, :, k], own.at[at], own_sem.at[at])

    def pair_copy(k):
        at = lax.rem(k, 2)
        return pltpu.make_async_remote_copy(
            src_ref=slots_ref.at[:, 1 - core, :, k],
            dst_ref=pair_in.at[at],
            send_sem=pair_send.at[at],
            recv_sem=pair_recv.at[at],
            device_id=partner,
            device_id_type=MESH,
        )

    def first_copy(k, part):
        place = near(k, 0)
        return pltpu.make_async_remote_copy(
            src_ref=pair_sum.at[lax.rem(k, 3), far if part == 0 else place],
            dst_ref=first_in.at[lax.rem(k, 5), part],
            send_sem=first_send.at[lax.rem(k, 3), part],
            recv_sem=first_recv.at[lax.rem(k, 5), part],
            device_id=device(place, z),
            device_id_type=MESH,
        )

    def second_copy(k):
        return pltpu.make_async_remote_copy(
            src_ref=second_out.at[lax.rem(k, 2)],
            dst_ref=second_in.at[lax.rem(k, 4)],
            send_sem=second_send.at[lax.rem(k, 2)],
            recv_sem=second_recv.at[lax.rem(k, 4)],
            device_id=device(near(k, 1), z),
            device_id_type=MESH,
        )

    def line_copy(source, target, send, recv, way):
        base = 1 if way > 0 else 0

        def make(k, level):
            return pltpu.make_async_remote_copy(
                src_ref=source.at[lax.rem(k, 2), level - base],
                dst_ref=target.at[lax.rem(k, 6), level - base],
                send_sem=send.at[lax.rem(k, 2), level - base],
                recv_sem=recv.at[lax.rem(k, 6), level - base],
                device_id=device(here, z + way),
                device_id_type=MESH,
            )

        return make

    def late_own_copy(c):
        at = lax.rem(c, 2)
        return pltpu.make_async_copy(
            slots_ref.at[lax.rem(c, 4), core, :, EARLY + lax.div(c, 4)],
            late_own.at[at],
            late_own_sem.at[at],
        )

    def late_pair_copy(c):
        at = lax.rem(c, 2)
        return pltpu.make_async_remote_copy(
            src_ref=slots_ref.at[lax.rem(c, 4), 1 - core, :, EARLY + lax.div(c, 4)],
            dst_ref=late_pair_in.at[at],
            send_sem=late_pair_send.at[at],
            recv_sem=late_pair_recv.at[at],
            device_id=partner,
            device_id_type=MESH,
        )

    def late_first_copy(slot, part):
        place = near(slot, 0)
        return pltpu.make_async_remote_copy(
            src_ref=late_column.at[slot, far if part == 0 else place],
            dst_ref=late_first_in.at[slot, part],
            send_sem=late_first_send.at[slot, part],
            recv_sem=late_first_recv.at[slot, part],
            device_id=device(place, z),
            device_id_type=MESH,
        )

    def late_second_copy(slot):
        return pltpu.make_async_remote_copy(
            src_ref=late_second_out.at[slot],
            dst_ref=late_second_in.at[slot],
            send_sem=late_second_send.at[slot],
            recv_sem=late_second_recv.at[slot],
            device_id=device(near(slot, 1), z),
            device_id_type=MESH,
        )

    def late_result_copy(slot):
        return pltpu.make_async_copy(late_result, out_ref.at[EARLY + slot], late_result_sem)

    def result_copy(k):
        at = lax.rem(k, 2)
        return pltpu.make_async_copy(result.at[at], out_ref.at[k], result_sem.at[at])

    def valid(k):
        return jnp.logical_and(k >= 0, k < EARLY)

    def valid_late(c):
        return jnp.logical_and(c >= 0, c < COMBOS)

    def keep(ref, k):
        kept = jnp.where(filled_ref[k, 0:1, 0:1] > 0.0, ref[...], 0.0)
        ref[...] = kept
        squares = square_out[me]
        for i in range(BR // 8):
            for j in range(D // LANES):
                part = kept[i * 8 : (i + 1) * 8, j * LANES : (j + 1) * LANES]
                squares = squares + part * part
        square_out[me] = squares

    def flows(lags, known, sums, ring, ins, outs, copies):
        for base, lag, behind, copy, arrived, leaving in zip(
            (1, 0), lags, (z > 0, z < 3), copies, ins, outs
        ):
            k = lag
            for n in range(base, base + 3):
                ahead = n > z if base else n < z

                @pl.when(jnp.logical_and(known(k - 2), ahead))
                def _(n=n, k=k, copy=copy):
                    copy(k - 2, n).wait_send()

                @pl.when(
                    jnp.logical_and(
                        jnp.logical_and(known(k), behind), jnp.logical_or(ahead, n == z)
                    )
                )
                def _(n=n, k=k, copy=copy):
                    copy(k, n).wait_recv()

                moving = jnp.logical_and(known(k), ahead)

                @pl.when(jnp.logical_and(moving, behind))
                def _(n=n, k=k, base=base, arrived=arrived, leaving=leaving):
                    leaving[lax.rem(k, 2), n - base] = total_of(
                        sums[lax.rem(k, ring), n], arrived[lax.rem(k, 6), n - base]
                    ).astype(jnp.bfloat16)

                @pl.when(jnp.logical_and(moving, jnp.logical_not(behind)))
                def _(n=n, k=k, base=base, leaving=leaving):
                    leaving[lax.rem(k, 2), n - base] = sums[lax.rem(k, ring), n]

                @pl.when(moving)
                def _(n=n, k=k, copy=copy):
                    copy(k, n).start()

    copies = (
        line_copy(up_out, up_in, up_send, up_recv, 1),
        line_copy(down_out, down_in, down_send, down_recv, -1),
    )
    late_copies = (
        line_copy(late_up_out, late_up_in, late_up_send, late_up_recv, 1),
        line_copy(late_down_out, late_down_in, late_down_send, late_down_recv, -1),
    )

    own_copy(0).start()
    pair_copy(0).start()
    late_own_copy(0).start()
    late_pair_copy(0).start()
    each(lambda *at: share(*at).start())

    def step(t, carry):
        @pl.when(valid(t - 3))
        def _():
            first_copy(t - 3, 0).wait_send()
            first_copy(t - 3, 1).wait_send()

        @pl.when(valid(t))
        def _():
            own_copy(t).wait()
            pair_copy(t).wait_recv()
            at, ring = lax.rem(t, 2), lax.rem(t, 3)

            def add(i, inner):
                p, n = lax.div(i, 4), lax.rem(i, 4)
                pair_sum[ring, p, n] = total_of(own[at, p, n], pair_in[at, p, n]).astype(
                    jnp.bfloat16
                )
                return inner

            lax.fori_loop(0, 16, add, 0)
            first_copy(t, 0).start()
            first_copy(t, 1).start()

        @pl.when(valid(t - 1))
        def _():
            pair_copy(t - 1).wait_send()

        @pl.when(t + 1 < EARLY)
        def _():
            own_copy(t + 1).start()
            pair_copy(t + 1).start()

        @pl.when(valid_late(t))
        def _():
            late_own_copy(t).wait()
            late_pair_copy(t).wait_recv()

            def add(n, inner):
                late_sum[lax.rem(t, 4), n] = total_of(
                    late_own[lax.rem(t, 2), n], late_pair_in[lax.rem(t, 2), n]
                ).astype(jnp.bfloat16)
                return inner

            lax.fori_loop(0, 4, add, 0)

        @pl.when(valid_late(t - 1))
        def _():
            late_pair_copy(t - 1).wait_send()

        @pl.when(t + 1 < COMBOS)
        def _():
            late_own_copy(t + 1).start()
            late_pair_copy(t + 1).start()

        @pl.when(valid(t - 3))
        def _():
            second_copy(t - 3).wait_send()

        @pl.when(valid(t - 1))
        def _():
            k = t - 1
            first_copy(k, 0).wait_recv()
            place = near(k, 1)

            def add(n, inner):
                second_out[lax.rem(k, 2), n] = total_of(
                    pair_sum[lax.rem(k, 3), place, n], first_in[lax.rem(k, 5), 0, n]
                ).astype(jnp.bfloat16)
                return inner

            lax.fori_loop(0, 4, add, 0)
            second_copy(k).start()

        @pl.when(valid(t - 2))
        def _():
            k = t - 2
            first_copy(k, 1).wait_recv()
            second_copy(k).wait_recv()

            def add(n, inner):
                column[lax.rem(k, 4), n] = total_of(
                    pair_sum[lax.rem(k, 3), here, n],
                    first_in[lax.rem(k, 5), 1, n],
                    second_in[lax.rem(k, 4), n],
                ).astype(jnp.bfloat16)
                return inner

            lax.fori_loop(0, 4, add, 0)

        flows(
            (t - 2 - z, t - 5 + z), valid, column, 4, (up_in, down_in), (up_out, down_out), copies
        )
        flows(
            (t - z, t - 3 + z),
            valid_late,
            late_sum,
            4,
            (late_up_in, late_down_in),
            (late_up_out, late_down_out),
            late_copies,
        )
        c = t - 3

        @pl.when(valid_late(c))
        def _():
            slot, p = lax.div(c, 4), lax.rem(c, 4)
            mine = late_sum.at[lax.rem(c, 4), z]
            below = late_up_in.at[lax.rem(c, 6), jnp.maximum(z - 1, 0)]
            above = late_down_in.at[lax.rem(c, 6), jnp.minimum(z, 2)]

            @pl.when(z == 0)
            def _():
                late_column[slot, p] = total_of(mine[...], above[...]).astype(jnp.bfloat16)

            @pl.when(z == 3)
            def _():
                late_column[slot, p] = total_of(mine[...], below[...]).astype(jnp.bfloat16)

            @pl.when(jnp.logical_and(z > 0, z < 3))
            def _():
                late_column[slot, p] = total_of(mine[...], below[...], above[...]).astype(
                    jnp.bfloat16
                )

        for slot in range(LATE):
            place = near(slot, 1)

            @pl.when(t == 4 * slot + 6)
            def _(slot=slot):
                late_first_copy(slot, 0).start()
                late_first_copy(slot, 1).start()

            @pl.when(t == 4 * slot + 7)
            def _(slot=slot, place=place):
                late_first_copy(slot, 0).wait_recv()
                late_second_out[slot] = total_of(
                    late_column[slot, place], late_first_in[slot, 0]
                ).astype(jnp.bfloat16)
                late_second_copy(slot).start()

            @pl.when(t == 4 * slot + 8)
            def _(slot=slot):
                late_first_copy(slot, 1).wait_recv()
                late_second_copy(slot).wait_recv()
                if slot:
                    late_result_copy(slot - 1).wait()
                late_result[...] = total_of(
                    late_column[slot, here], late_first_in[slot, 1], late_second_in[slot]
                )
                keep(late_result, EARLY + slot)
                late_result_copy(slot).start()

        k = t - 5

        @pl.when(valid(k - 2))
        def _():
            result_copy(k - 2).wait()

        @pl.when(valid(k))
        def _():
            result[lax.rem(k, 2)] = column[lax.rem(k, 4), z].astype(jnp.float32)

            @pl.when(z > 0)
            def _():
                result[lax.rem(k, 2)] += up_in[lax.rem(k, 6), z - 1].astype(jnp.float32)

            @pl.when(z < 3)
            def _():
                result[lax.rem(k, 2)] += down_in[lax.rem(k, 6), z].astype(jnp.float32)

            keep(result.at[lax.rem(k, 2)], k)
            result_copy(k).start()

        @pl.when(t == CHUNKS // 2)
        def _():
            each(lambda *at: share(*at).wait())
            small = small_in[0]
            for i in range(1, places):
                small = small + small_in[i]
            small_out[me] = small
            each(lambda *at: spread(*at).start())

        return carry

    lax.fori_loop(0, STEPS, step, 0)
    each(lambda *at: square(*at).start())
    late_result_copy(LATE - 1).wait()
    for slot in range(LATE):
        late_first_copy(slot, 0).wait_send()
        late_first_copy(slot, 1).wait_send()
        late_second_copy(slot).wait_send()
    each(lambda *at: spread(*at).wait())
    each(lambda *at: square(*at).wait())


def scatter_sum(slots, filled, small):
    slot_count = filled.shape[0]
    wide, narrow = lax.axis_size("wide"), lax.axis_size("narrow")
    if (wide, narrow, slot_count) != (8, 4, CHUNKS):
        part = lax.psum_scatter(slots, "wide", scatter_dimension=0, tiled=True)
        owned = lax.psum_scatter(
            part.astype(jnp.float32), "narrow", scatter_dimension=0, tiled=True
        )
        owned = jnp.where(filled[:, None, None], owned, 0.0)
        square = lax.psum(jnp.sum(owned * owned), ("wide", "narrow"))
        return owned, square, lax.psum(small, ("wide", "narrow"))
    tiles = (wide * narrow, 8, LANES)
    room = wide * narrow * 8 * LANES - small.shape[0]
    assert room >= 0
    low = functools.partial(pltpu.VMEM, dtype=jnp.bfloat16)
    dma = pltpu.SemaphoreType.DMA
    block = (BR, D)
    owned, small_tiles, square_tiles = pl.pallas_call(
        scatter_kernel,
        out_shape=(
            jax.ShapeDtypeStruct((slot_count,) + block, jnp.float32),
            jax.ShapeDtypeStruct(tiles, jnp.float32),
            jax.ShapeDtypeStruct(tiles, jnp.float32),
        ),
        in_specs=[
            pl.BlockSpec(memory_space=pl.ANY),
            pl.BlockSpec(memory_space=pltpu.VMEM),
            pl.BlockSpec(memory_space=pltpu.VMEM),
        ],
        out_specs=(
            pl.BlockSpec(memory_space=pl.ANY),
            pl.BlockSpec(memory_space=pltpu.VMEM),
            pl.BlockSpec(memory_space=pltpu.VMEM),
        ),
        scratch_shapes=[
            pltpu.VMEM(tiles, jnp.float32),
            low((2, 4, 4) + block),
            low((2, 4, 4) + block),
            low((3, 4, 4) + block),
            low((5, 2, 4) + block),
            low((4, 4) + block),
            low((2, 4) + block),
            low((4, 4) + block),
            low((6, 3) + block),
            low((6, 3) + block),
            low((2, 3) + block),
            low((2, 3) + block),
            pltpu.VMEM((2,) + block, jnp.float32),
            low((2, 4) + block),
            low((2, 4) + block),
            low((4, 4) + block),
            low((6, 3) + block),
            low((6, 3) + block),
            low((2, 3) + block),
            low((2, 3) + block),
            low((LATE, 4) + block),
            low((LATE, 2) + block),
            low((LATE,) + block),
            low((LATE,) + block),
            pltpu.VMEM(block, jnp.float32),
            dma((2,)),
            dma((2,)),
            dma((2,)),
            dma((3, 2)),
            dma((5, 2)),
            dma((2,)),
            dma((4,)),
            dma((2, 3)),
            dma((6, 3)),
            dma((2, 3)),
            dma((6, 3)),
            dma((2,)),
            dma((2,)),
            dma((2,)),
            dma((2,)),
            dma((2, 3)),
            dma((6, 3)),
            dma((2, 3)),
            dma((6, 3)),
            dma((LATE, 2)),
            dma((LATE, 2)),
            dma((LATE,)),
            dma((LATE,)),
            dma,
        ]
        + [dma((wide * narrow,))] * 6,
        compiler_params=pltpu.CompilerParams(
            collective_id=1, has_side_effects=True, vmem_limit_bytes=SCATTER_VMEM
        ),
        name="scatter_sum",
    )(
        slots.reshape(4, 2, narrow, slot_count, BR, D),
        jnp.pad(small, (0, room)).reshape(tiles),
        jnp.broadcast_to(
            filled.astype(jnp.float32)[:, None, None], (slot_count, 8, LANES)
        ),
    )
    return owned, jnp.sum(square_tiles), small_tiles.reshape(-1)[: small.shape[0]]


GATHER_STEPS = EARLY + 5


def gather_kernel(
    own_ref,
    count_ref,
    all_ref,
    counts_ref,
    own_sem,
    recv,
    pair_recv,
    line_send,
    plane_send,
    turn_send,
    late_send,
    pair_send,
    late_pair_send,
    count_send,
    count_recv,
):
    wide, z = lax.axis_index("wide"), lax.axis_index("narrow")
    core, here = lax.rem(wide, 2), lax.div(wide, 2)
    x, y = lax.rem(here, 2), lax.div(here, 2)
    side, front, far = y * 2 + 1 - x, (1 - y) * 2 + x, 3 - here
    places = 8 * 4
    me = wide * 4 + z

    barrier = pltpu.get_barrier_semaphore()

    def greet(i, carry):
        other = lax.rem(me + i, places)
        pl.semaphore_signal(
            barrier,
            inc=1,
            device_id=(lax.div(other, 4), lax.rem(other, 4)),
            device_id_type=MESH,
        )
        return carry

    lax.fori_loop(1, places, greet, 0)
    fill = pltpu.make_async_copy(own_ref, all_ref.at[here, core, z], own_sem)
    fill.start()
    counts_ref[me] = count_ref[...]
    pl.semaphore_wait(barrier, places - 1)
    fill.wait()

    def count_copy(i):
        other = lax.rem(me + i, places)
        return pltpu.make_async_remote_copy(
            src_ref=count_ref,
            dst_ref=counts_ref.at[me],
            send_sem=count_send.at[i],
            recv_sem=count_recv.at[i],
            device_id=(lax.div(other, 4), lax.rem(other, 4)),
            device_id_type=MESH,
        )

    def count_start(i, carry):
        count_copy(i).start()
        return carry

    lax.fori_loop(1, places, count_start, 0)

    def piece(p, n, k, send, to):
        return pltpu.make_async_remote_copy(
            src_ref=all_ref.at[p, core, n, k],
            dst_ref=all_ref.at[p, core, n, k],
            send_sem=send,
            recv_sem=recv.at[p, n, k],
            device_id=to,
            device_id_type=MESH,
        )

    up, down = (wide, z + 1), (wide, z - 1)
    to_side, to_front = (side * 2 + core, z), (front * 2 + core, z)

    def line(n, k, step):
        return piece(here, n, k, line_send.at[step, n, k], (up, down)[step])

    def plane(n, k, which):
        return piece(here, n, k, plane_send.at[which, n, k], (to_side, to_front)[which])

    def turn(n, k, which):
        return piece(
            (side, front)[which], n, k, turn_send.at[n, k], (to_front, to_side)[which]
        )

    def late(c, n, step):
        p, k = lax.rem(here + c, 4), EARLY + lax.div(c, 4)
        return piece(p, n, k, late_send.at[step, c, n], (up, down)[step])

    def pair(p, k, send):
        return pltpu.make_async_remote_copy(
            src_ref=all_ref.at[p, core, :, k],
            dst_ref=all_ref.at[p, core, :, k],
            send_sem=send,
            recv_sem=pair_recv,
            device_id=(here * 2 + 1 - core, z),
            device_id_type=MESH,
        )

    def early_pair(p, k):
        return pair(p, k, pair_send.at[p, k])

    def late_pair(c):
        p, k = lax.rem(here + c, 4), EARLY + lax.div(c, 4)
        return pair(p, k, late_pair_send.at[c])

    def both_lines(make, n, j, start):
        @pl.when(jnp.logical_and(start, z < 3))
        def _():
            if j <= 0:
                make(n, 0)

        @pl.when(jnp.logical_and(start, z > 0))
        def _():
            if j >= 0:
                make(n, 1)

    def early(k):
        return jnp.logical_and(k >= 0, k < EARLY)

    def swap(n, k, go):
        even = lax.rem(n + k, 2) == 0

        @pl.when(jnp.logical_and(go, even))
        def _():
            turn(n, k, 0).start()

        @pl.when(jnp.logical_and(go, jnp.logical_not(even)))
        def _():
            turn(n, k, 1).start()

    for k in range(EARLY, CHUNKS):
        plane(z, k, 0).start()
        plane(z, k, 1).start()

    def step(t, carry):
        @pl.when(early(t))
        def _():
            plane(z, t, 0).start()
            plane(z, t, 1).start()

        both_lines(lambda n, way: line(n, t, way).start(), z, 0, early(t))

        for j in (-1, 1, -2, 2, -3, 3):
            n, k = z + j, t - abs(j)
            there = jnp.logical_and(early(k), jnp.logical_and(n >= 0, n < 4))

            @pl.when(there)
            def _(n=n, k=k, j=j):
                piece(here, n, k, plane_send.at[0, n, k], to_side).wait_recv()

            both_lines(lambda n, way, k=k: line(n, k, way).start(), n, j, there)

            @pl.when(there)
            def _(n=n, k=k):
                plane(n, k, 0).start()
                plane(n, k, 1).start()

        @pl.when(t == 1)
        def _():
            for k in range(EARLY, CHUNKS):
                plane_wait(side, z, k)
                plane_wait(front, z, k)
                swap(z, k, True)

        @pl.when(t == 2)
        def _():
            for k in range(EARLY, CHUNKS):
                plane_wait(far, z, k)

        for j in (0, -1, 1, -2, 2, -3, 3):
            m = t - 2 - abs(j)
            n = z + j
            first = m + lax.div(m + 2, 3)
            for c, more in ((first, True), (first + 1, lax.rem(m, 3) == 0)):
                there = jnp.logical_and(
                    jnp.logical_and(m >= 0, c < COMBOS),
                    jnp.logical_and(jnp.logical_and(n >= 0, n < 4), more),
                )
                if j:

                    @pl.when(there)
                    def _(n=n, c=c):
                        plane_wait(lax.rem(here + c, 4), n, EARLY + lax.div(c, 4))

                both_lines(lambda n, way, c=c: late(c, n, way).start(), n, j, there)

        for n in range(4):
            gap = jnp.abs(z - n)
            k = t - 1 - gap

            @pl.when(early(k))
            def _(n=n, k=k):
                plane_wait(side, n, k)
                plane_wait(front, n, k)

            swap(n, k, early(k))
            k = t - 2 - gap

            @pl.when(early(k))
            def _(n=n, k=k):
                plane_wait(far, n, k)

        for lag, sent in ((3, (here,)), (4, (side, front)), (5, (far,))):
            k = t - lag

            @pl.when(early(k))
            def _(k=k, sent=sent):
                for p in sent:
                    early_pair(p, k).start()

        m = t - 5
        first = m + lax.div(m + 2, 3)
        for c, more in ((first, True), (first + 1, lax.rem(m, 3) == 0)):

            @pl.when(jnp.logical_and(jnp.logical_and(m >= 0, c < COMBOS), more))
            def _(c=c):
                late_pair(c).start()

        return carry

    def plane_wait(p, n, k):
        piece(p, n, k, plane_send.at[0, n, k], to_side).wait_recv()

    lax.fori_loop(0, GATHER_STEPS, step, 0)

    def finish(k, carry):
        for n in range(4):
            plane_used = jnp.logical_or(k < EARLY, n == z)

            @pl.when(plane_used)
            def _(n=n):
                plane(n, k, 0).wait_send()
                plane(n, k, 1).wait_send()
                turn(n, k, 0).wait_send()

            @pl.when(jnp.logical_and(k < EARLY, jnp.logical_and(n <= z, z < 3)))
            def _(n=n):
                line(n, k, 0).wait_send()

            @pl.when(jnp.logical_and(k < EARLY, jnp.logical_and(n >= z, z > 0)))
            def _(n=n):
                line(n, k, 1).wait_send()

            @pl.when(jnp.logical_and(n <= z, z < 3))
            def _(n=n):
                late(k, n, 0).wait_send()

            @pl.when(jnp.logical_and(n >= z, z > 0))
            def _(n=n):
                late(k, n, 1).wait_send()

        @pl.when(k < EARLY)
        def _():
            for p in range(4):
                early_pair(p, k).wait_send()

        late_pair(k).wait_send()
        return carry

    lax.fori_loop(0, CHUNKS, finish, 0)

    def count_wait(i, carry):
        count_copy(i).wait()
        return carry

    lax.fori_loop(1, places, count_wait, 0)
    pltpu.make_async_copy(
        all_ref.at[:, 1 - core], all_ref.at[:, 1 - core], pair_recv
    ).wait()


def gather_all(low, local_counts):
    slot_count = low.shape[0]
    wide, narrow = lax.axis_size("wide"), lax.axis_size("narrow")
    if (wide, narrow, slot_count) != (8, 4, CHUNKS):
        return (
            lax.all_gather(low, ("wide", "narrow"), axis=0, tiled=True),
            lax.psum(local_counts, ("wide", "narrow")),
        )
    dma = pltpu.SemaphoreType.DMA
    tile = jnp.zeros((8, LANES), jnp.float32).at[0, :NCLASS].set(local_counts)
    gathered, tiles = pl.pallas_call(
        gather_kernel,
        out_shape=(
            jax.ShapeDtypeStruct((4, 2, narrow, slot_count, BR, D), jnp.bfloat16),
            jax.ShapeDtypeStruct((wide * narrow, 8, LANES), jnp.float32),
        ),
        in_specs=[
            pl.BlockSpec(memory_space=pltpu.VMEM),
            pl.BlockSpec(memory_space=pltpu.VMEM),
        ],
        out_specs=(
            pl.BlockSpec(memory_space=pl.ANY),
            pl.BlockSpec(memory_space=pltpu.VMEM),
        ),
        scratch_shapes=[
            dma,
            dma((4, 4, CHUNKS)),
            dma,
            dma((2, 4, EARLY)),
            dma((2, 4, CHUNKS)),
            dma((4, CHUNKS)),
            dma((2, COMBOS, 4)),
            dma((4, EARLY)),
            dma((COMBOS,)),
            dma((wide * narrow,)),
            dma((wide * narrow,)),
        ],
        compiler_params=pltpu.CompilerParams(
            collective_id=2, has_side_effects=True, vmem_limit_bytes=VMEM_LIMIT
        ),
        name="gather_all",
    )(low, tile)
    return (
        gathered.reshape(wide * narrow * slot_count, BR, D),
        jnp.sum(tiles[:, 0, :NCLASS], axis=0),
    )


def split_small(small):
    freq = small[: NCLASS * D].reshape(NCLASS, D)
    rest = small[NCLASS * D :]
    return (
        freq,
        rest[0:D],
        rest[D : 2 * D],
        rest[2 * D : 3 * D],
        rest[3 * D : 4 * D],
        rest[4 * D : 5 * D],
        rest[5 * D : 5 * D + OUTW],
    )


def prepare(series, pad_mask):
    valid = (1 - pad_mask).astype(jnp.float32)
    count_series = series.shape[0]
    context = (series[:, :CTX] * valid[:, :CTX]).reshape(count_series, NPATCH, PATCH)
    marks = pad_mask[:, :CTX].astype(jnp.float32).reshape(count_series, NPATCH, PATCH)
    feat = jnp.concatenate([context, marks], axis=-1)
    return (feat, horizons(series), horizons(valid))


def horizons(points):
    count_series = points.shape[0]
    pieces = points.reshape(count_series, -1, PATCH)
    return jnp.concatenate(
        [pieces[:, 1 + j : 1 + j + NPATCH] for j in range(HORIZON // PATCH)], axis=-1
    ).reshape(count_series * NPATCH, HORIZON)


def loss_parts(out, target, tmask, onehot, class_weight):
    column = lax.broadcasted_iota(jnp.int32, (HORIZON, OUTW), 1)
    row = lax.broadcasted_iota(jnp.int32, (HORIZON, OUTW), 0)
    spread = (lax.div(column, NQ + 1) == row).astype(jnp.float32)
    wanted = jnp.dot(target, spread, precision=lax.Precision.HIGHEST)
    mask = matmul(tmask.astype(jnp.bfloat16), spread.astype(jnp.bfloat16))
    kind = lax.rem(lax.broadcasted_iota(jnp.int32, (1, OUTW), 1), NQ + 1)
    level = kind.astype(jnp.float32) / (NQ + 1)
    error = out - wanted
    above, below = level * -error, (level - 1.0) * -error
    slope = jnp.where(above > below, -level, jnp.where(above < below, 1.0 - level, 0.5 - level))
    square = jnp.sum(jnp.where(kind == 0, error * error * mask, 0.0), axis=1)
    quant = jnp.sum(jnp.where(kind == 0, 0.0, jnp.maximum(above, below) * mask), axis=1)
    weight = jnp.repeat(jnp.sum(onehot * class_weight[None, :], axis=1), NPATCH)[:, None]
    grad = weight * mask * jnp.where(kind == 0, 2.0 * error, slope / NQ)
    sums = [
        jnp.sum(onehot * jnp.sum(part.reshape(-1, NPATCH), axis=1)[:, None], 0)
        for part in (square, quant)
    ]
    return jnp.stack(sums), grad.astype(jnp.bfloat16)


def layer_forward(state_zero, mats, parts, cosine, sine, causal):
    w_qkv, w_out, w_up, w_down = (mats[2], mats[3], mats[4], mats[5])
    gain_one, gain_two = (parts[3], parts[4])
    count_series = state_zero.shape[0] // NPATCH
    normed_one = rms_norm(state_zero, gain_one).astype(jnp.bfloat16)
    qkv = matmul(normed_one, w_qkv).reshape(count_series, NPATCH, 3, HEADS, HDIM)
    queries = (rotate(qkv[:, :, 0], cosine, sine) * HDIM ** (-0.5)).astype(jnp.bfloat16)
    key_rot = rotate(qkv[:, :, 1], cosine, sine).astype(jnp.bfloat16)
    value_all = qkv[:, :, 2].astype(jnp.bfloat16)
    scores = jnp.einsum("sqhd,skhd->shqk", queries, key_rot, preferred_element_type=jnp.float32)
    scores = jnp.where(causal, scores, -1e30)
    peak = jnp.max(scores, axis=-1, keepdims=True)
    expo = jnp.exp(scores - peak)
    total = jnp.sum(expo, axis=-1, keepdims=True)
    log_total = peak + jnp.log(total)
    attend = (expo / total).astype(jnp.bfloat16)
    mixed = jnp.einsum("shqk,skhd->sqhd", attend, value_all, preferred_element_type=jnp.float32)
    mixed = mixed.astype(jnp.bfloat16).reshape(state_zero.shape[0], D)
    state_one = state_zero + matmul(mixed, w_out)
    normed_two = rms_norm(state_one, gain_two).astype(jnp.bfloat16)
    up_pre = matmul(normed_two, w_up)
    activ = silu(up_pre).astype(jnp.bfloat16)
    state_two = state_one + matmul(activ, w_down)
    return (
        state_two,
        (
            normed_one,
            queries,
            key_rot,
            value_all,
            log_total,
            mixed,
            state_one,
            normed_two,
            up_pre,
            activ,
        ),
    )


def layer_backward(grad_two, state_zero, kept, mats, parts, cosine, sine, causal):
    (
        normed_one,
        queries,
        key_rot,
        value_all,
        log_total,
        mixed,
        state_one,
        normed_two,
        up_pre,
        activ,
    ) = kept
    w_qkv, w_out, w_up, w_down = (mats[2], mats[3], mats[4], mats[5])
    gain_one, gain_two = (parts[3], parts[4])
    tokens = state_zero.shape[0]
    count_series = tokens // NPATCH
    grad_mlp = grad_two.astype(jnp.bfloat16)
    grad_act = backmul(grad_mlp, w_down)
    grad_up_pre = (grad_act * silu_slope(up_pre)).astype(jnp.bfloat16)
    grad_normed = backmul(grad_up_pre, w_up)
    _, pull = jax.vjp(rms_norm, state_one, gain_two)
    grad_norm_in, grad_gain_two = pull(grad_normed)
    grad_one = grad_two + grad_norm_in
    grad_proj = grad_one.astype(jnp.bfloat16)
    grad_mixed = (
        backmul(grad_proj, w_out).astype(jnp.bfloat16).reshape(count_series, NPATCH, HEADS, HDIM)
    )
    scores = jnp.einsum("sqhd,skhd->shqk", queries, key_rot, preferred_element_type=jnp.float32)
    attend = jnp.where(causal, jnp.exp(scores - log_total), 0.0)
    grad_attend = jnp.einsum(
        "sqhd,skhd->shqk", grad_mixed, value_all, preferred_element_type=jnp.float32
    )
    grad_scores = (
        attend * (grad_attend - jnp.sum(grad_attend * attend, axis=-1, keepdims=True))
    ).astype(jnp.bfloat16)
    grad_query = jnp.einsum(
        "shqk,skhd->sqhd", grad_scores, key_rot, preferred_element_type=jnp.float32
    )
    grad_key = jnp.einsum(
        "shqk,sqhd->skhd", grad_scores, queries, preferred_element_type=jnp.float32
    )
    grad_value = jnp.einsum(
        "shqk,sqhd->skhd",
        attend.astype(jnp.bfloat16),
        grad_mixed,
        preferred_element_type=jnp.float32,
    )
    grad_qkv = jnp.stack(
        [
            rotate(grad_query, cosine, -sine) * HDIM ** (-0.5),
            rotate(grad_key, cosine, -sine),
            grad_value,
        ],
        axis=2,
    )
    grad_qkv = grad_qkv.reshape(tokens, 3 * D).astype(jnp.bfloat16)
    grad_normed_one = backmul(grad_qkv, w_qkv)
    _, pull = jax.vjp(rms_norm, state_zero, gain_one)
    grad_zero_in, grad_gain_one = pull(grad_normed_one)
    return (
        grad_one + grad_zero_in,
        (
            (normed_one, grad_qkv),
            (mixed, grad_proj),
            (normed_two, grad_up_pre),
            (activ, grad_mlp),
        ),
        grad_gain_one,
        grad_gain_two,
    )


def adamw(weight, first, second, grad, step):
    power = step[0].astype(jnp.float32)
    first = BETA * first + (1.0 - BETA) * grad
    second = BETA * second + (1.0 - BETA) * grad * grad
    fix_one = 1.0 - jnp.power(BETA, power)
    fix_two = 1.0 - jnp.power(BETA, power)
    new = weight - RATE * (
        first / fix_one / (jnp.sqrt(second / fix_two) + EPSILON) + DECAY * weight
    )
    return (new, first, second)


def on_device(
    series,
    pad_mask,
    freq_class,
    owner,
    step,
    master,
    moment1,
    moment2,
    small_master,
    small_m1,
    small_m2,
):
    slot_count = master.shape[0]
    parts = split_small(small_master)
    freq, bias_one, bias_two, head_bias, out_bias = (
        parts[0],
        parts[1],
        parts[2],
        parts[5],
        parts[6],
    )
    feat, target, tmask = prepare(series, pad_mask)
    count_series = series.shape[0]
    tokens = count_series * NPATCH
    onehot = (freq_class[:, None] == jnp.arange(NCLASS, dtype=jnp.int32)[None, :]).astype(
        jnp.float32
    )
    local_counts = jnp.sum(
        onehot * jnp.sum(tmask.reshape(count_series, -1), axis=1)[:, None], 0
    )
    gathered, counts = gather_all(master.astype(jnp.bfloat16), local_counts)
    mats = unpack(gathered, owner)
    tok_in, tok_out, head_in, head_out = (mats[0], mats[1], mats[6], mats[7])
    class_weight = 1.0 / (counts * NCLASS)
    cosine, sine = tables()
    causal = jnp.arange(NPATCH)[:, None] >= jnp.arange(NPATCH)[None, :]
    patch_in = feat.reshape(tokens, 2 * PATCH).astype(jnp.bfloat16)
    tok_pre = matmul(patch_in, tok_in)
    hidden = silu(tok_pre[:, :D] + bias_one).astype(jnp.bfloat16)
    class_rows = jnp.repeat(jnp.dot(onehot, freq, precision=lax.Precision.HIGHEST), NPATCH, axis=0)
    state_zero = matmul(hidden, tok_out) + bias_two + tok_pre[:, D:] + class_rows
    state_two, _ = layer_forward(state_zero, mats, parts, cosine, sine, causal)
    state_low = state_two.astype(jnp.bfloat16)
    head_pre = matmul(state_low, head_in)
    head_hidden = silu(head_pre[:, :D] + head_bias).astype(jnp.bfloat16)
    out = matmul(head_hidden, head_out) + out_bias + head_pre[:, D:]

    local_sums, grad_out = loss_parts(out, target, tmask, onehot, class_weight)
    grad_out_bias = jnp.sum(grad_out.astype(jnp.float32), axis=0)
    grad_head_first = backmul(grad_out, head_out) * silu_slope(head_pre[:, :D] + head_bias)
    grad_head_bias = jnp.sum(grad_head_first, axis=0)
    grad_head_pre = jnp.concatenate([grad_head_first, grad_out.astype(jnp.float32)], axis=1).astype(
        jnp.bfloat16
    )
    grad_two = backmul(grad_head_pre, head_in)
    _, kept = layer_forward(state_zero, mats, parts, cosine, sine, causal)
    grad_zero, layer_pairs, grad_gain_one, grad_gain_two = layer_backward(
        grad_two, state_zero, kept, mats, parts, cosine, sine, causal
    )
    grad_prod = grad_zero.astype(jnp.bfloat16)
    grad_first = backmul(grad_prod, tok_out) * silu_slope(tok_pre[:, :D] + bias_one)
    grad_tok_pre = jnp.concatenate([grad_first, grad_zero], axis=1).astype(jnp.bfloat16)
    slots = grad_blocks(
        ((patch_in, grad_tok_pre), (hidden, grad_prod))
        + layer_pairs
        + ((state_low, grad_head_pre), (head_hidden, grad_out)),
        owner,
    )
    grad_freq = jnp.dot(
        onehot.T,
        grad_zero.reshape(count_series, NPATCH, D).sum(axis=1),
        precision=lax.Precision.HIGHEST,
    )
    small_local = jnp.concatenate(
        [
            grad_freq.reshape(-1),
            jnp.sum(grad_first, axis=0),
            jnp.sum(grad_zero, axis=0),
            grad_gain_one,
            grad_gain_two,
            grad_head_bias,
            grad_out_bias,
            local_sums.reshape(-1),
        ]
    )
    rank = lax.axis_index("wide") * lax.axis_size("narrow") + lax.axis_index("narrow")
    mine = rank * slot_count + jnp.arange(slot_count, dtype=jnp.int32)
    filled = jnp.any(owner[:, None] == mine[None, :], axis=0)
    owned, square_total, small_total = scatter_sum(slots, filled, small_local)
    small_grad = small_total[: small_master.shape[0]]
    sums = small_total[small_master.shape[0] :].reshape(2, NCLASS)
    grad_norm = jnp.sqrt(square_total + jnp.sum(small_grad * small_grad))
    scale = jnp.minimum(1.0, CLIP / grad_norm)
    loss = jnp.sum((sums[0] + sums[1] / NQ) * class_weight)
    new_master, new_m1, new_m2 = adamw(master, moment1, moment2, owned * scale, step)
    small_new, small_new_m1, small_new_m2 = adamw(
        small_master, small_m1, small_m2, small_grad * scale, step
    )
    return (
        loss,
        grad_norm,
        new_master,
        new_m1,
        new_m2,
        new_master.astype(jnp.bfloat16),
        small_new,
        small_new_m1,
        small_new_m2,
    )


def solution(mesh):
    return jax.shard_map(
        on_device,
        mesh=mesh,
        in_specs=(
            P(("wide", "narrow"), None),
            P(("wide", "narrow"), None),
            P(("wide", "narrow")),
            P(),
            P(),
            P(("wide", "narrow"), None, None),
            P(("wide", "narrow"), None, None),
            P(("wide", "narrow"), None, None),
            P(),
            P(),
            P(),
        ),
        out_specs=(
            P(),
            P(),
            P(("wide", "narrow"), None, None),
            P(("wide", "narrow"), None, None),
            P(("wide", "narrow"), None, None),
            P(("wide", "narrow"), None, None),
            P(),
            P(),
            P(),
        ),
        check_vma=False,
    )
```

```python
import functools

import jax
import jax.numpy as jnp
from jax import lax
from jax.experimental import pallas as pl
from jax.experimental.pallas import tpu as pltpu
from jax.sharding import PartitionSpec as P

D = 1280
HEADS = 16
HDIM = 80
FF = 5120
PATCH = 32
HORIZON = 128
NQ = 9
NPATCH = 16
NCLASS = 3
BR = 64
TOTAL_SLOTS = 512
CTX = 512
OUTW = 1280
ROWS = 20608
NBLK = 322


CLIP = 0.01
RATE = 0.03
DECAY = 0.1
BETA = 0.5
EPSILON = 1e-08


def matmul(left, right):
    return jnp.dot(left, right, preferred_element_type=jnp.float32)


def tmatmul(left, right):
    return lax.dot_general(
        left, right, (((0,), (0,)), ((), ())), preferred_element_type=jnp.float32
    )


def backmul(left, right):
    return lax.dot_general(
        left, right, (((1,), (1,)), ((), ())), preferred_element_type=jnp.float32
    )


def silu(value):
    return value / (1.0 + jnp.exp(-value))


def silu_slope(value):
    sigmoid = 1.0 / (1.0 + jnp.exp(-value))
    return sigmoid * (1.0 + value * (1.0 - sigmoid))


def rms_norm(hidden, gain):
    return hidden * lax.rsqrt(jnp.mean(hidden * hidden, axis=-1, keepdims=True) + 1e-06) * gain


def tables():
    half = HDIM // 2
    inverse = jnp.power(10000.0, -2.0 * jnp.arange(half, dtype=jnp.float32) / HDIM)
    angle = jnp.arange(NPATCH, dtype=jnp.float32)[:, None] * inverse[None, :]
    return (jnp.cos(angle)[None, :, None, :], jnp.sin(angle)[None, :, None, :])


SPAN = 640


def turned(value, cosine, sine):
    half = HDIM // 2
    lane = lax.rem(lax.broadcasted_iota(jnp.int32, value.shape, 1), HDIM)
    other = jnp.where(lane < half, pltpu.roll(value, D - half, 1), pltpu.roll(value, half, 1))
    shape = (value.shape[0] // NPATCH, NPATCH, D)
    return (
        value.reshape(shape) * cosine[None] + other.reshape(shape) * sine[None]
    ).reshape(value.shape)


def attended(queries, keys):
    scores = backmul(queries, keys)
    row = lax.broadcasted_iota(jnp.int32, scores.shape, 0)
    column = lax.broadcasted_iota(jnp.int32, scores.shape, 1)
    seen = jnp.logical_and(column <= row, column >= row - lax.rem(row, NPATCH))
    scores = jnp.where(seen, scores, -1e30)
    expo = jnp.exp(scores - jnp.max(scores, axis=-1, keepdims=True))
    return expo / jnp.sum(expo, axis=-1, keepdims=True)


def head_lanes(h):
    lane = lax.broadcasted_iota(jnp.int32, (1, SPAN), 1)
    inside = jnp.logical_and(lane >= h * HDIM, lane < (h + 1) * HDIM)
    return jnp.where(inside, 1.0, 0.0)


def attend_kernel(qkv_ref, cos_ref, sin_ref, query_ref, key_ref, value_ref, mixed_ref, total_ref):
    cosine, sine = cos_ref[...], sin_ref[...]
    query_ref[...] = (turned(qkv_ref[:, 0:D], cosine, sine) * HDIM ** (-0.5)).astype(jnp.bfloat16)
    key_ref[...] = turned(qkv_ref[:, D : 2 * D], cosine, sine).astype(jnp.bfloat16)
    value_ref[...] = qkv_ref[:, 2 * D : 3 * D].astype(jnp.bfloat16)
    for first in range(0, D, SPAN):
        span = slice(first, first + SPAN)
        total_ref[...] = jnp.zeros_like(total_ref)

        def head(h, carry, span=span):
            lanes = head_lanes(h).astype(jnp.bfloat16)
            attend = attended(query_ref[:, span] * lanes, key_ref[:, span])
            total_ref[...] += matmul(attend.astype(jnp.bfloat16), value_ref[:, span] * lanes)
            return carry

        lax.fori_loop(0, SPAN // HDIM, head, 0)
        mixed_ref[:, span] = total_ref[...].astype(jnp.bfloat16)


def attend_back_kernel(
    query_ref, key_ref, value_ref, grad_ref, cos_ref, sin_ref, out_ref, dq_ref, dk_ref, dv_ref
):
    for first in range(0, D, SPAN):
        span = slice(first, first + SPAN)
        for ref in (dq_ref, dk_ref, dv_ref):
            ref[:, span] = jnp.zeros((ref.shape[0], SPAN), jnp.float32)

        def head(h, carry, span=span):
            lanes = head_lanes(h).astype(jnp.bfloat16)
            queries, keys = query_ref[:, span] * lanes, key_ref[:, span] * lanes
            grad = grad_ref[:, span] * lanes
            attend = attended(queries, keys)
            grad_attend = backmul(grad, value_ref[:, span])
            grad_scores = (
                attend * (grad_attend - jnp.sum(grad_attend * attend, axis=-1, keepdims=True))
            ).astype(jnp.bfloat16)
            dq_ref[:, span] += matmul(grad_scores, keys)
            dk_ref[:, span] += tmatmul(grad_scores, queries)
            dv_ref[:, span] += tmatmul(attend.astype(jnp.bfloat16), grad)
            return carry

        lax.fori_loop(0, SPAN // HDIM, head, 0)
    cosine, sine = cos_ref[...], sin_ref[...]
    out_ref[:, 0:D] = (turned(dq_ref[...], cosine, -sine) * HDIM ** (-0.5)).astype(jnp.bfloat16)
    out_ref[:, D : 2 * D] = turned(dk_ref[...], cosine, -sine).astype(jnp.bfloat16)
    out_ref[:, 2 * D : 3 * D] = dv_ref[...].astype(jnp.bfloat16)


def flat_tables():
    cosine, sine = (table[0, :, 0, :] for table in tables())
    return (
        jnp.tile(jnp.concatenate([cosine, cosine], axis=1), (1, HEADS)),
        jnp.tile(jnp.concatenate([-sine, sine], axis=1), (1, HEADS)),
    )


def attend_call(kernel, operands, widths, scratch, name):
    tokens = operands[0].shape[0]
    return pl.pallas_call(
        kernel,
        out_shape=tuple(jax.ShapeDtypeStruct((tokens, width), jnp.bfloat16) for width in widths),
        scratch_shapes=[pltpu.VMEM((tokens, width), jnp.float32) for width in scratch],
        compiler_params=pltpu.CompilerParams(vmem_limit_bytes=VMEM_LIMIT),
        name=name,
    )(*operands)


MATS = (
    (2 * PATCH, 2, 2),
    (D, 1, 4),
    (D, 3, 6),
    (D, 1, 4),
    (D, FF // D, 8),
    (FF, 1, 8),
    (D, (D + OUTW) // D, 8),
    (D, 1, 4),
)
BASES = tuple(sum(r * g for r, g, _ in MATS[:i]) // BR for i in range(len(MATS)))
LANES = 128
VMEM_LIMIT = 56 * 1024 * 1024
SCATTER_VMEM = 61 * 1024 * 1024


RING = 48


def steps_of(which):
    total, groups, count = MATS[which]
    return total * groups // (count * BR)


def stages(kind):
    return [pltpu.VMEM((2,) + kind(*MATS[which]), jnp.bfloat16) for which in range(len(MATS))]


def unpack_kernel(owner_ref, gathered_ref, *refs):
    outs, held = refs[:8], refs[8:16]
    ring, wide_ref, load_sem, store_sem = refs[16:]

    def load(b):
        at = lax.rem(b, RING)
        return pltpu.make_async_copy(
            gathered_ref.at[owner_ref[b]], ring.at[at], load_sem.at[at]
        )

    def first_load(b, carry):
        load(b).start()
        return carry

    lax.fori_loop(0, RING, first_load, 0)

    def store(which, i):
        total, groups, count = MATS[which]
        rows = count * BR // groups
        at = lax.rem(i, 2)
        return pltpu.make_async_copy(
            held[which].at[at],
            outs[which].at[pl.ds(pl.multiple_of(i * rows, rows), rows)],
            store_sem.at[which, at],
        )

    for which, (total, groups, count) in enumerate(MATS):
        rows = count * BR // groups

        def step(i, carry, which=which, groups=groups, count=count, rows=rows):
            first = BASES[which] + i * count
            at = lax.rem(i, 2)

            @pl.when(i >= 2)
            def _():
                store(which, i - 2).wait()

            for b in range(count):
                load(first + b).wait()
            for b in range(count):
                block = ring.at[lax.rem(first + b, RING)]
                span = slice(b * BR, (b + 1) * BR)
                if groups == 1:
                    held[which][at, span, :] = block[...]
                    continue
                for c in range(D // LANES):
                    wide_ref[c, span, :] = block[:, c * LANES : (c + 1) * LANES].astype(
                        jnp.float32
                    )
            if groups > 1:
                for j in range(groups):
                    for c in range(D // LANES):
                        left = j * D + c * LANES
                        held[which][at, :, left : left + LANES] = wide_ref[
                            c, pl.ds(j, rows, stride=groups), :
                        ].astype(jnp.bfloat16)
            store(which, i).start()
            for b in range(count):

                @pl.when(first + b + RING < NBLK)
                def _(b=b):
                    load(first + b + RING).start()

            return carry

        lax.fori_loop(0, steps_of(which), step, 0)

    for which in range(len(MATS)):
        for i in range(max(steps_of(which) - 2, 0), steps_of(which)):
            store(which, i).wait()


def unpack(gathered, owner):
    dma = pltpu.SemaphoreType.DMA
    return pl.pallas_call(
        unpack_kernel,
        out_shape=tuple(
            jax.ShapeDtypeStruct((total, groups * D), jnp.bfloat16) for total, groups, _ in MATS
        ),
        in_specs=[
            pl.BlockSpec(memory_space=pltpu.SMEM),
            pl.BlockSpec(memory_space=pl.ANY),
        ],
        out_specs=tuple(pl.BlockSpec(memory_space=pl.ANY) for _ in MATS),
        scratch_shapes=stages(lambda total, groups, count: (count * BR // groups, groups * D))
        + [
            pltpu.VMEM((RING, BR, D), jnp.bfloat16),
            pltpu.VMEM((D // LANES, 8 * BR, LANES), jnp.float32),
            dma((RING,)),
            dma((len(MATS), 2)),
        ],
        compiler_params=pltpu.CompilerParams(vmem_limit_bytes=VMEM_LIMIT),
        cost_estimate=pl.CostEstimate(
            flops=0, bytes_accessed=4 * ROWS * D, transcendentals=0
        ),
        name="unpack",
    )(owner, gathered)


def grad_kernel(owner_ref, *refs):
    lefts, rights, out_ref = refs[:8], refs[8:16], refs[16]
    left_in, right_in, held = refs[17:25], refs[25:33], refs[33:41]
    wide_ref, load_sem, store_sem = refs[41:]

    def loads(which):
        return (
            pltpu.make_async_copy(lefts[which], left_in[which], load_sem.at[which, 0]),
            pltpu.make_async_copy(rights[which], right_in[which], load_sem.at[which, 1]),
        )

    def store(which, i, b):
        at = lax.rem(i, 2)
        return pltpu.make_async_copy(
            held[which].at[at, pl.ds(b * BR, BR), :],
            out_ref.at[owner_ref[BASES[which] + i * MATS[which][2] + b]],
            store_sem.at[which, at, b],
        )

    order = tuple(reversed(range(len(MATS))))
    for which in order:
        for copy in loads(which):
            copy.start()
    for which in order:
        total, groups, count = MATS[which]
        rows = count * BR // groups
        for copy in loads(which):
            copy.wait()

        def step(i, carry, which=which, groups=groups, count=count, rows=rows):
            at = lax.rem(i, 2)

            @pl.when(i >= 2)
            def _():
                for b in range(count):
                    store(which, i - 2, b).wait()

            if steps_of(which) == 1:
                left = left_in[which][...]
            else:
                left = left_in[which][:, pl.ds(pl.multiple_of(i * rows, rows), rows)]
            for j in range(groups):
                part = tmatmul(left, right_in[which][:, j * D : (j + 1) * D])
                if groups == 1:
                    held[which][at] = part.astype(jnp.bfloat16)
                    continue
                for c in range(D // LANES):
                    wide_ref[c, pl.ds(j, rows, stride=groups), :] = part[
                        :, c * LANES : (c + 1) * LANES
                    ]
            if groups > 1:
                for c in range(D // LANES):
                    held[which][at, :, c * LANES : (c + 1) * LANES] = wide_ref[
                        c, 0 : count * BR, :
                    ].astype(jnp.bfloat16)
            for b in range(count):
                store(which, i, b).start()
            return carry

        lax.fori_loop(0, steps_of(which), step, 0)
    for which in order:
        for i in range(max(steps_of(which) - 2, 0), steps_of(which)):
            for b in range(MATS[which][2]):
                store(which, i, b).wait()


def grad_blocks(pairs, owner):
    lefts, rights = zip(*pairs)
    dma = pltpu.SemaphoreType.DMA
    tokens = lefts[0].shape[0]
    return pl.pallas_call(
        grad_kernel,
        out_shape=jax.ShapeDtypeStruct((TOTAL_SLOTS, BR, D), jnp.bfloat16),
        in_specs=[pl.BlockSpec(memory_space=pltpu.SMEM)]
        + [pl.BlockSpec(memory_space=pl.ANY)] * (2 * len(MATS)),
        out_specs=pl.BlockSpec(memory_space=pl.ANY),
        scratch_shapes=[pltpu.VMEM(left.shape, jnp.bfloat16) for left in lefts]
        + [pltpu.VMEM(right.shape, jnp.bfloat16) for right in rights]
        + stages(lambda total, groups, count: (count * BR, D))
        + [
            pltpu.VMEM((D // LANES, 8 * BR, LANES), jnp.float32),
            dma((len(MATS), 2)),
            dma((len(MATS), 2, 8)),
        ],
        compiler_params=pltpu.CompilerParams(vmem_limit_bytes=VMEM_LIMIT),
        cost_estimate=pl.CostEstimate(
            flops=2 * tokens * ROWS * D, bytes_accessed=2 * ROWS * D, transcendentals=0
        ),
        name="grad_blocks",
    )(owner, *lefts, *rights)


CHUNKS = 16
LATE = 4
EARLY = CHUNKS - LATE
COMBOS = 4 * LATE
STEPS = COMBOS + 5
MESH = pl.DeviceIdType.MESH


def total_of(*blocks):
    result = blocks[0].astype(jnp.float32)
    for block in blocks[1:]:
        result = result + block.astype(jnp.float32)
    return result


def scatter_kernel(
    slots_ref,
    small_ref,
    filled_ref,
    out_ref,
    small_out,
    square_out,
    small_in,
    own,
    pair_in,
    pair_sum,
    first_in,
    second_in,
    second_out,
    column,
    up_in,
    down_in,
    up_out,
    down_out,
    result,
    late_own,
    late_pair_in,
    late_sum,
    late_up_in,
    late_down_in,
    late_up_out,
    late_down_out,
    late_column,
    late_first_in,
    late_second_in,
    late_second_out,
    late_result,
    own_sem,
    pair_send,
    pair_recv,
    first_send,
    first_recv,
    second_send,
    second_recv,
    up_send,
    up_recv,
    down_send,
    down_recv,
    result_sem,
    late_own_sem,
    late_pair_send,
    late_pair_recv,
    late_up_send,
    late_up_recv,
    late_down_send,
    late_down_recv,
    late_first_send,
    late_first_recv,
    late_second_send,
    late_second_recv,
    late_result_sem,
    share_send,
    share_recv,
    spread_send,
    spread_recv,
    square_send,
    square_recv,
):
    wide, z = lax.axis_index("wide"), lax.axis_index("narrow")
    core, here = lax.rem(wide, 2), lax.div(wide, 2)
    x, y = lax.rem(here, 2), lax.div(here, 2)
    far = 3 - here

    def device(place, level):
        return (place * 2 + core, level)

    partner = (here * 2 + 1 - core, z)

    def near(k, which):
        along_y = lax.rem(k + which, 2)
        return (y + along_y - 2 * y * along_y) * 2 + (x + (1 - along_y) - 2 * x * (1 - along_y))

    places = 8 * 4
    me = wide * 4 + z
    barrier = pltpu.get_barrier_semaphore()

    def each(action):
        def body(i, carry):
            other = lax.rem(me + i, places)
            action(i, other, (lax.div(other, 4), lax.rem(other, 4)))
            return carry

        lax.fori_loop(1, places, body, 0)

    def greet(i, other, to):
        pl.semaphore_signal(barrier, inc=1, device_id=to, device_id_type=MESH)

    def share(i, other, to):
        return pltpu.make_async_remote_copy(
            src_ref=small_ref.at[other],
            dst_ref=small_in.at[me],
            send_sem=share_send.at[i],
            recv_sem=share_recv.at[i],
            device_id=to,
            device_id_type=MESH,
        )

    def tell(ref, send, recv):
        def make(i, other, to):
            return pltpu.make_async_remote_copy(
                src_ref=ref.at[me],
                dst_ref=ref.at[me],
                send_sem=send.at[i],
                recv_sem=recv.at[i],
                device_id=to,
                device_id_type=MESH,
            )

        return make

    spread = tell(small_out, spread_send, spread_recv)
    square = tell(square_out, square_send, square_recv)
    each(greet)
    small_in[me] = small_ref[me]
    square_out[me] = jnp.zeros((8, LANES), jnp.float32)
    pl.semaphore_wait(barrier, places - 1)

    def own_copy(k):
        at = lax.rem(k, 2)
        return pltpu.make_async_copy(slots_ref.at[:, core, :, k], own.at[at], own_sem.at[at])

    def pair_copy(k):
        at = lax.rem(k, 2)
        return pltpu.make_async_remote_copy(
            src_ref=slots_ref.at[:, 1 - core, :, k],
            dst_ref=pair_in.at[at],
            send_sem=pair_send.at[at],
            recv_sem=pair_recv.at[at],
            device_id=partner,
            device_id_type=MESH,
        )

    def first_copy(k, part):
        place = near(k, 0)
        return pltpu.make_async_remote_copy(
            src_ref=pair_sum.at[lax.rem(k, 3), far if part == 0 else place],
            dst_ref=first_in.at[lax.rem(k, 5), part],
            send_sem=first_send.at[lax.rem(k, 3), part],
            recv_sem=first_recv.at[lax.rem(k, 5), part],
            device_id=device(place, z),
            device_id_type=MESH,
        )

    def second_copy(k):
        return pltpu.make_async_remote_copy(
            src_ref=second_out.at[lax.rem(k, 2)],
            dst_ref=second_in.at[lax.rem(k, 4)],
            send_sem=second_send.at[lax.rem(k, 2)],
            recv_sem=second_recv.at[lax.rem(k, 4)],
            device_id=device(near(k, 1), z),
            device_id_type=MESH,
        )

    def line_copy(source, target, send, recv, way):
        base = 1 if way > 0 else 0

        def make(k, level):
            return pltpu.make_async_remote_copy(
                src_ref=source.at[lax.rem(k, 2), level - base],
                dst_ref=target.at[lax.rem(k, 6), level - base],
                send_sem=send.at[lax.rem(k, 2), level - base],
                recv_sem=recv.at[lax.rem(k, 6), level - base],
                device_id=device(here, z + way),
                device_id_type=MESH,
            )

        return make

    def late_own_copy(c):
        at = lax.rem(c, 2)
        return pltpu.make_async_copy(
            slots_ref.at[lax.rem(c, 4), core, :, EARLY + lax.div(c, 4)],
            late_own.at[at],
            late_own_sem.at[at],
        )

    def late_pair_copy(c):
        at = lax.rem(c, 2)
        return pltpu.make_async_remote_copy(
            src_ref=slots_ref.at[lax.rem(c, 4), 1 - core, :, EARLY + lax.div(c, 4)],
            dst_ref=late_pair_in.at[at],
            send_sem=late_pair_send.at[at],
            recv_sem=late_pair_recv.at[at],
            device_id=partner,
            device_id_type=MESH,
        )

    def late_first_copy(slot, part):
        place = near(slot, 0)
        return pltpu.make_async_remote_copy(
            src_ref=late_column.at[slot, far if part == 0 else place],
            dst_ref=late_first_in.at[slot, part],
            send_sem=late_first_send.at[slot, part],
            recv_sem=late_first_recv.at[slot, part],
            device_id=device(place, z),
            device_id_type=MESH,
        )

    def late_second_copy(slot):
        return pltpu.make_async_remote_copy(
            src_ref=late_second_out.at[slot],
            dst_ref=late_second_in.at[slot],
            send_sem=late_second_send.at[slot],
            recv_sem=late_second_recv.at[slot],
            device_id=device(near(slot, 1), z),
            device_id_type=MESH,
        )

    def late_result_copy(slot):
        return pltpu.make_async_copy(late_result, out_ref.at[EARLY + slot], late_result_sem)

    def result_copy(k):
        at = lax.rem(k, 2)
        return pltpu.make_async_copy(result.at[at], out_ref.at[k], result_sem.at[at])

    def valid(k):
        return jnp.logical_and(k >= 0, k < EARLY)

    def valid_late(c):
        return jnp.logical_and(c >= 0, c < COMBOS)

    def keep(ref, k):
        kept = jnp.where(filled_ref[k, 0:1, 0:1] > 0.0, ref[...], 0.0)
        ref[...] = kept
        squares = square_out[me]
        for i in range(BR // 8):
            for j in range(D // LANES):
                part = kept[i * 8 : (i + 1) * 8, j * LANES : (j + 1) * LANES]
                squares = squares + part * part
        square_out[me] = squares

    def flows(lags, known, sums, ring, ins, outs, copies):
        for base, lag, behind, copy, arrived, leaving in zip(
            (1, 0), lags, (z > 0, z < 3), copies, ins, outs
        ):
            k = lag
            for n in range(base, base + 3):
                ahead = n > z if base else n < z

                @pl.when(jnp.logical_and(known(k - 2), ahead))
                def _(n=n, k=k, copy=copy):
                    copy(k - 2, n).wait_send()

                @pl.when(
                    jnp.logical_and(
                        jnp.logical_and(known(k), behind), jnp.logical_or(ahead, n == z)
                    )
                )
                def _(n=n, k=k, copy=copy):
                    copy(k, n).wait_recv()

                moving = jnp.logical_and(known(k), ahead)

                @pl.when(jnp.logical_and(moving, behind))
                def _(n=n, k=k, base=base, arrived=arrived, leaving=leaving):
                    leaving[lax.rem(k, 2), n - base] = total_of(
                        sums[lax.rem(k, ring), n], arrived[lax.rem(k, 6), n - base]
                    ).astype(jnp.bfloat16)

                @pl.when(jnp.logical_and(moving, jnp.logical_not(behind)))
                def _(n=n, k=k, base=base, leaving=leaving):
                    leaving[lax.rem(k, 2), n - base] = sums[lax.rem(k, ring), n]

                @pl.when(moving)
                def _(n=n, k=k, copy=copy):
                    copy(k, n).start()

    copies = (
        line_copy(up_out, up_in, up_send, up_recv, 1),
        line_copy(down_out, down_in, down_send, down_recv, -1),
    )
    late_copies = (
        line_copy(late_up_out, late_up_in, late_up_send, late_up_recv, 1),
        line_copy(late_down_out, late_down_in, late_down_send, late_down_recv, -1),
    )

    own_copy(0).start()
    pair_copy(0).start()
    late_own_copy(0).start()
    late_pair_copy(0).start()
    each(lambda *at: share(*at).start())

    def step(t, carry):
        @pl.when(valid(t - 3))
        def _():
            first_copy(t - 3, 0).wait_send()
            first_copy(t - 3, 1).wait_send()

        @pl.when(valid(t))
        def _():
            own_copy(t).wait()
            pair_copy(t).wait_recv()
            at, ring = lax.rem(t, 2), lax.rem(t, 3)

            def add(i, inner):
                p, n = lax.div(i, 4), lax.rem(i, 4)
                pair_sum[ring, p, n] = total_of(own[at, p, n], pair_in[at, p, n]).astype(
                    jnp.bfloat16
                )
                return inner

            lax.fori_loop(0, 16, add, 0)
            first_copy(t, 0).start()
            first_copy(t, 1).start()

        @pl.when(valid(t - 1))
        def _():
            pair_copy(t - 1).wait_send()

        @pl.when(t + 1 < EARLY)
        def _():
            own_copy(t + 1).start()
            pair_copy(t + 1).start()

        @pl.when(valid_late(t))
        def _():
            late_own_copy(t).wait()
            late_pair_copy(t).wait_recv()

            def add(n, inner):
                late_sum[lax.rem(t, 4), n] = total_of(
                    late_own[lax.rem(t, 2), n], late_pair_in[lax.rem(t, 2), n]
                ).astype(jnp.bfloat16)
                return inner

            lax.fori_loop(0, 4, add, 0)

        @pl.when(valid_late(t - 1))
        def _():
            late_pair_copy(t - 1).wait_send()

        @pl.when(t + 1 < COMBOS)
        def _():
            late_own_copy(t + 1).start()
            late_pair_copy(t + 1).start()

        @pl.when(valid(t - 3))
        def _():
            second_copy(t - 3).wait_send()

        @pl.when(valid(t - 1))
        def _():
            k = t - 1
            first_copy(k, 0).wait_recv()
            place = near(k, 1)

            def add(n, inner):
                second_out[lax.rem(k, 2), n] = total_of(
                    pair_sum[lax.rem(k, 3), place, n], first_in[lax.rem(k, 5), 0, n]
                ).astype(jnp.bfloat16)
                return inner

            lax.fori_loop(0, 4, add, 0)
            second_copy(k).start()

        @pl.when(valid(t - 2))
        def _():
            k = t - 2
            first_copy(k, 1).wait_recv()
            second_copy(k).wait_recv()

            def add(n, inner):
                column[lax.rem(k, 4), n] = total_of(
                    pair_sum[lax.rem(k, 3), here, n],
                    first_in[lax.rem(k, 5), 1, n],
                    second_in[lax.rem(k, 4), n],
                ).astype(jnp.bfloat16)
                return inner

            lax.fori_loop(0, 4, add, 0)

        flows(
            (t - 2 - z, t - 5 + z), valid, column, 4, (up_in, down_in), (up_out, down_out), copies
        )
        flows(
            (t - z, t - 3 + z),
            valid_late,
            late_sum,
            4,
            (late_up_in, late_down_in),
            (late_up_out, late_down_out),
            late_copies,
        )
        c = t - 3

        @pl.when(valid_late(c))
        def _():
            slot, p = lax.div(c, 4), lax.rem(c, 4)
            mine = late_sum.at[lax.rem(c, 4), z]
            below = late_up_in.at[lax.rem(c, 6), jnp.maximum(z - 1, 0)]
            above = late_down_in.at[lax.rem(c, 6), jnp.minimum(z, 2)]

            @pl.when(z == 0)
            def _():
                late_column[slot, p] = total_of(mine[...], above[...]).astype(jnp.bfloat16)

            @pl.when(z == 3)
            def _():
                late_column[slot, p] = total_of(mine[...], below[...]).astype(jnp.bfloat16)

            @pl.when(jnp.logical_and(z > 0, z < 3))
            def _():
                late_column[slot, p] = total_of(mine[...], below[...], above[...]).astype(
                    jnp.bfloat16
                )

        for slot in range(LATE):
            place = near(slot, 1)

            @pl.when(t == 4 * slot + 6)
            def _(slot=slot):
                late_first_copy(slot, 0).start()
                late_first_copy(slot, 1).start()

            @pl.when(t == 4 * slot + 7)
            def _(slot=slot, place=place):
                late_first_copy(slot, 0).wait_recv()
                late_second_out[slot] = total_of(
                    late_column[slot, place], late_first_in[slot, 0]
                ).astype(jnp.bfloat16)
                late_second_copy(slot).start()

            @pl.when(t == 4 * slot + 8)
            def _(slot=slot):
                late_first_copy(slot, 1).wait_recv()
                late_second_copy(slot).wait_recv()
                if slot:
                    late_result_copy(slot - 1).wait()
                late_result[...] = total_of(
                    late_column[slot, here], late_first_in[slot, 1], late_second_in[slot]
                )
                keep(late_result, EARLY + slot)
                late_result_copy(slot).start()

        k = t - 5

        @pl.when(valid(k - 2))
        def _():
            result_copy(k - 2).wait()

        @pl.when(valid(k))
        def _():
            result[lax.rem(k, 2)] = column[lax.rem(k, 4), z].astype(jnp.float32)

            @pl.when(z > 0)
            def _():
                result[lax.rem(k, 2)] += up_in[lax.rem(k, 6), z - 1].astype(jnp.float32)

            @pl.when(z < 3)
            def _():
                result[lax.rem(k, 2)] += down_in[lax.rem(k, 6), z].astype(jnp.float32)

            keep(result.at[lax.rem(k, 2)], k)
            result_copy(k).start()

        @pl.when(t == CHUNKS // 2)
        def _():
            each(lambda *at: share(*at).wait())
            small = small_in[0]
            for i in range(1, places):
                small = small + small_in[i]
            small_out[me] = small
            each(lambda *at: spread(*at).start())

        return carry

    lax.fori_loop(0, STEPS, step, 0)
    each(lambda *at: square(*at).start())
    late_result_copy(LATE - 1).wait()
    for slot in range(LATE):
        late_first_copy(slot, 0).wait_send()
        late_first_copy(slot, 1).wait_send()
        late_second_copy(slot).wait_send()
    each(lambda *at: spread(*at).wait())
    each(lambda *at: square(*at).wait())


def scatter_sum(slots, filled, small):
    slot_count = filled.shape[0]
    wide, narrow = lax.axis_size("wide"), lax.axis_size("narrow")
    if (wide, narrow, slot_count) != (8, 4, CHUNKS):
        part = lax.psum_scatter(slots, "wide", scatter_dimension=0, tiled=True)
        owned = lax.psum_scatter(
            part.astype(jnp.float32), "narrow", scatter_dimension=0, tiled=True
        )
        owned = jnp.where(filled[:, None, None], owned, 0.0)
        square = lax.psum(jnp.sum(owned * owned), ("wide", "narrow"))
        return owned, square, lax.psum(small, ("wide", "narrow"))
    tiles = (wide * narrow, 8, LANES)
    room = wide * narrow * 8 * LANES - small.shape[0]
    assert room >= 0
    low = functools.partial(pltpu.VMEM, dtype=jnp.bfloat16)
    dma = pltpu.SemaphoreType.DMA
    block = (BR, D)
    owned, small_tiles, square_tiles = pl.pallas_call(
        scatter_kernel,
        out_shape=(
            jax.ShapeDtypeStruct((slot_count,) + block, jnp.float32),
            jax.ShapeDtypeStruct(tiles, jnp.float32),
            jax.ShapeDtypeStruct(tiles, jnp.float32),
        ),
        in_specs=[
            pl.BlockSpec(memory_space=pl.ANY),
            pl.BlockSpec(memory_space=pltpu.VMEM),
            pl.BlockSpec(memory_space=pltpu.VMEM),
        ],
        out_specs=(
            pl.BlockSpec(memory_space=pl.ANY),
            pl.BlockSpec(memory_space=pltpu.VMEM),
            pl.BlockSpec(memory_space=pltpu.VMEM),
        ),
        scratch_shapes=[
            pltpu.VMEM(tiles, jnp.float32),
            low((2, 4, 4) + block),
            low((2, 4, 4) + block),
            low((3, 4, 4) + block),
            low((5, 2, 4) + block),
            low((4, 4) + block),
            low((2, 4) + block),
            low((4, 4) + block),
            low((6, 3) + block),
            low((6, 3) + block),
            low((2, 3) + block),
            low((2, 3) + block),
            pltpu.VMEM((2,) + block, jnp.float32),
            low((2, 4) + block),
            low((2, 4) + block),
            low((4, 4) + block),
            low((6, 3) + block),
            low((6, 3) + block),
            low((2, 3) + block),
            low((2, 3) + block),
            low((LATE, 4) + block),
            low((LATE, 2) + block),
            low((LATE,) + block),
            low((LATE,) + block),
            pltpu.VMEM(block, jnp.float32),
            dma((2,)),
            dma((2,)),
            dma((2,)),
            dma((3, 2)),
            dma((5, 2)),
            dma((2,)),
            dma((4,)),
            dma((2, 3)),
            dma((6, 3)),
            dma((2, 3)),
            dma((6, 3)),
            dma((2,)),
            dma((2,)),
            dma((2,)),
            dma((2,)),
            dma((2, 3)),
            dma((6, 3)),
            dma((2, 3)),
            dma((6, 3)),
            dma((LATE, 2)),
            dma((LATE, 2)),
            dma((LATE,)),
            dma((LATE,)),
            dma,
        ]
        + [dma((wide * narrow,))] * 6,
        compiler_params=pltpu.CompilerParams(
            collective_id=1, has_side_effects=True, vmem_limit_bytes=SCATTER_VMEM
        ),
        name="scatter_sum",
    )(
        slots.reshape(4, 2, narrow, slot_count, BR, D),
        jnp.pad(small, (0, room)).reshape(tiles),
        jnp.broadcast_to(
            filled.astype(jnp.float32)[:, None, None], (slot_count, 8, LANES)
        ),
    )
    return owned, jnp.sum(square_tiles), small_tiles.reshape(-1)[: small.shape[0]]


GATHER_STEPS = EARLY + 5


def gather_kernel(
    own_ref,
    count_ref,
    all_ref,
    counts_ref,
    own_sem,
    recv,
    pair_recv,
    line_send,
    plane_send,
    turn_send,
    late_send,
    pair_send,
    late_pair_send,
    count_send,
    count_recv,
):
    wide, z = lax.axis_index("wide"), lax.axis_index("narrow")
    core, here = lax.rem(wide, 2), lax.div(wide, 2)
    x, y = lax.rem(here, 2), lax.div(here, 2)
    side, front, far = y * 2 + 1 - x, (1 - y) * 2 + x, 3 - here
    places = 8 * 4
    me = wide * 4 + z

    barrier = pltpu.get_barrier_semaphore()

    def greet(i, carry):
        other = lax.rem(me + i, places)
        pl.semaphore_signal(
            barrier,
            inc=1,
            device_id=(lax.div(other, 4), lax.rem(other, 4)),
            device_id_type=MESH,
        )
        return carry

    lax.fori_loop(1, places, greet, 0)
    fill = pltpu.make_async_copy(own_ref, all_ref.at[here, core, z], own_sem)
    fill.start()
    counts_ref[me] = count_ref[...]
    pl.semaphore_wait(barrier, places - 1)
    fill.wait()

    def count_copy(i):
        other = lax.rem(me + i, places)
        return pltpu.make_async_remote_copy(
            src_ref=count_ref,
            dst_ref=counts_ref.at[me],
            send_sem=count_send.at[i],
            recv_sem=count_recv.at[i],
            device_id=(lax.div(other, 4), lax.rem(other, 4)),
            device_id_type=MESH,
        )

    def count_start(i, carry):
        count_copy(i).start()
        return carry

    lax.fori_loop(1, places, count_start, 0)

    def piece(p, n, k, send, to):
        return pltpu.make_async_remote_copy(
            src_ref=all_ref.at[p, core, n, k],
            dst_ref=all_ref.at[p, core, n, k],
            send_sem=send,
            recv_sem=recv.at[p, n, k],
            device_id=to,
            device_id_type=MESH,
        )

    up, down = (wide, z + 1), (wide, z - 1)
    to_side, to_front = (side * 2 + core, z), (front * 2 + core, z)

    def line(n, k, step):
        return piece(here, n, k, line_send.at[step, n, k], (up, down)[step])

    def plane(n, k, which):
        return piece(here, n, k, plane_send.at[which, n, k], (to_side, to_front)[which])

    def turn(n, k, which):
        return piece(
            (side, front)[which], n, k, turn_send.at[n, k], (to_front, to_side)[which]
        )

    def late(c, n, step):
        p, k = lax.rem(here + c, 4), EARLY + lax.div(c, 4)
        return piece(p, n, k, late_send.at[step, c, n], (up, down)[step])

    def pair(p, k, send):
        return pltpu.make_async_remote_copy(
            src_ref=all_ref.at[p, core, :, k],
            dst_ref=all_ref.at[p, core, :, k],
            send_sem=send,
            recv_sem=pair_recv,
            device_id=(here * 2 + 1 - core, z),
            device_id_type=MESH,
        )

    def early_pair(p, k):
        return pair(p, k, pair_send.at[p, k])

    def late_pair(c):
        p, k = lax.rem(here + c, 4), EARLY + lax.div(c, 4)
        return pair(p, k, late_pair_send.at[c])

    def both_lines(make, n, j, start):
        @pl.when(jnp.logical_and(start, z < 3))
        def _():
            if j <= 0:
                make(n, 0)

        @pl.when(jnp.logical_and(start, z > 0))
        def _():
            if j >= 0:
                make(n, 1)

    def early(k):
        return jnp.logical_and(k >= 0, k < EARLY)

    def swap(n, k, go):
        even = lax.rem(n + k, 2) == 0

        @pl.when(jnp.logical_and(go, even))
        def _():
            turn(n, k, 0).start()

        @pl.when(jnp.logical_and(go, jnp.logical_not(even)))
        def _():
            turn(n, k, 1).start()

    for k in range(EARLY, CHUNKS):
        plane(z, k, 0).start()
        plane(z, k, 1).start()

    def step(t, carry):
        @pl.when(early(t))
        def _():
            plane(z, t, 0).start()
            plane(z, t, 1).start()

        both_lines(lambda n, way: line(n, t, way).start(), z, 0, early(t))

        for j in (-1, 1, -2, 2, -3, 3):
            n, k = z + j, t - abs(j)
            there = jnp.logical_and(early(k), jnp.logical_and(n >= 0, n < 4))

            @pl.when(there)
            def _(n=n, k=k, j=j):
                piece(here, n, k, plane_send.at[0, n, k], to_side).wait_recv()

            both_lines(lambda n, way, k=k: line(n, k, way).start(), n, j, there)

            @pl.when(there)
            def _(n=n, k=k):
                plane(n, k, 0).start()
                plane(n, k, 1).start()

        @pl.when(t == 1)
        def _():
            for k in range(EARLY, CHUNKS):
                plane_wait(side, z, k)
                plane_wait(front, z, k)
                swap(z, k, True)

        @pl.when(t == 2)
        def _():
            for k in range(EARLY, CHUNKS):
                plane_wait(far, z, k)

        for j in (0, -1, 1, -2, 2, -3, 3):
            m = t - 2 - abs(j)
            n = z + j
            first = m + lax.div(m + 2, 3)
            for c, more in ((first, True), (first + 1, lax.rem(m, 3) == 0)):
                there = jnp.logical_and(
                    jnp.logical_and(m >= 0, c < COMBOS),
                    jnp.logical_and(jnp.logical_and(n >= 0, n < 4), more),
                )
                if j:

                    @pl.when(there)
                    def _(n=n, c=c):
                        plane_wait(lax.rem(here + c, 4), n, EARLY + lax.div(c, 4))

                both_lines(lambda n, way, c=c: late(c, n, way).start(), n, j, there)

        for n in range(4):
            gap = jnp.abs(z - n)
            k = t - 1 - gap

            @pl.when(early(k))
            def _(n=n, k=k):
                plane_wait(side, n, k)
                plane_wait(front, n, k)

            swap(n, k, early(k))
            k = t - 2 - gap

            @pl.when(early(k))
            def _(n=n, k=k):
                plane_wait(far, n, k)

        for lag, sent in ((3, (here,)), (4, (side, front)), (5, (far,))):
            k = t - lag

            @pl.when(early(k))
            def _(k=k, sent=sent):
                for p in sent:
                    early_pair(p, k).start()

        m = t - 5
        first = m + lax.div(m + 2, 3)
        for c, more in ((first, True), (first + 1, lax.rem(m, 3) == 0)):

            @pl.when(jnp.logical_and(jnp.logical_and(m >= 0, c < COMBOS), more))
            def _(c=c):
                late_pair(c).start()

        return carry

    def plane_wait(p, n, k):
        piece(p, n, k, plane_send.at[0, n, k], to_side).wait_recv()

    lax.fori_loop(0, GATHER_STEPS, step, 0)

    def finish(k, carry):
        for n in range(4):
            plane_used = jnp.logical_or(k < EARLY, n == z)

            @pl.when(plane_used)
            def _(n=n):
                plane(n, k, 0).wait_send()
                plane(n, k, 1).wait_send()
                turn(n, k, 0).wait_send()

            @pl.when(jnp.logical_and(k < EARLY, jnp.logical_and(n <= z, z < 3)))
            def _(n=n):
                line(n, k, 0).wait_send()

            @pl.when(jnp.logical_and(k < EARLY, jnp.logical_and(n >= z, z > 0)))
            def _(n=n):
                line(n, k, 1).wait_send()

            @pl.when(jnp.logical_and(n <= z, z < 3))
            def _(n=n):
                late(k, n, 0).wait_send()

            @pl.when(jnp.logical_and(n >= z, z > 0))
            def _(n=n):
                late(k, n, 1).wait_send()

        @pl.when(k < EARLY)
        def _():
            for p in range(4):
                early_pair(p, k).wait_send()

        late_pair(k).wait_send()
        return carry

    lax.fori_loop(0, CHUNKS, finish, 0)

    def count_wait(i, carry):
        count_copy(i).wait()
        return carry

    lax.fori_loop(1, places, count_wait, 0)
    pltpu.make_async_copy(
        all_ref.at[:, 1 - core], all_ref.at[:, 1 - core], pair_recv
    ).wait()


def gather_all(low, local_counts):
    slot_count = low.shape[0]
    wide, narrow = lax.axis_size("wide"), lax.axis_size("narrow")
    if (wide, narrow, slot_count) != (8, 4, CHUNKS):
        return (
            lax.all_gather(low, ("wide", "narrow"), axis=0, tiled=True),
            lax.psum(local_counts, ("wide", "narrow")),
        )
    dma = pltpu.SemaphoreType.DMA
    tile = jnp.zeros((8, LANES), jnp.float32).at[0, :NCLASS].set(local_counts)
    gathered, tiles = pl.pallas_call(
        gather_kernel,
        out_shape=(
            jax.ShapeDtypeStruct((4, 2, narrow, slot_count, BR, D), jnp.bfloat16),
            jax.ShapeDtypeStruct((wide * narrow, 8, LANES), jnp.float32),
        ),
        in_specs=[
            pl.BlockSpec(memory_space=pltpu.VMEM),
            pl.BlockSpec(memory_space=pltpu.VMEM),
        ],
        out_specs=(
            pl.BlockSpec(memory_space=pl.ANY),
            pl.BlockSpec(memory_space=pltpu.VMEM),
        ),
        scratch_shapes=[
            dma,
            dma((4, 4, CHUNKS)),
            dma,
            dma((2, 4, EARLY)),
            dma((2, 4, CHUNKS)),
            dma((4, CHUNKS)),
            dma((2, COMBOS, 4)),
            dma((4, EARLY)),
            dma((COMBOS,)),
            dma((wide * narrow,)),
            dma((wide * narrow,)),
        ],
        compiler_params=pltpu.CompilerParams(
            collective_id=2, has_side_effects=True, vmem_limit_bytes=VMEM_LIMIT
        ),
        name="gather_all",
    )(low, tile)
    return (
        gathered.reshape(wide * narrow * slot_count, BR, D),
        jnp.sum(tiles[:, 0, :NCLASS], axis=0),
    )


def split_small(small):
    freq = small[: NCLASS * D].reshape(NCLASS, D)
    rest = small[NCLASS * D :]
    return (
        freq,
        rest[0:D],
        rest[D : 2 * D],
        rest[2 * D : 3 * D],
        rest[3 * D : 4 * D],
        rest[4 * D : 5 * D],
        rest[5 * D : 5 * D + OUTW],
    )


def prepare(series, pad_mask):
    valid = (1 - pad_mask).astype(jnp.float32)
    count_series = series.shape[0]
    context = (series[:, :CTX] * valid[:, :CTX]).reshape(count_series, NPATCH, PATCH)
    marks = pad_mask[:, :CTX].astype(jnp.float32).reshape(count_series, NPATCH, PATCH)
    feat = jnp.concatenate([context, marks], axis=-1)
    return (feat, horizons(series), horizons(valid))


def horizons(points):
    count_series = points.shape[0]
    pieces = points.reshape(count_series, -1, PATCH)
    return jnp.concatenate(
        [pieces[:, 1 + j : 1 + j + NPATCH] for j in range(HORIZON // PATCH)], axis=-1
    ).reshape(count_series * NPATCH, HORIZON)


def loss_parts(out, target, tmask, onehot, class_weight):
    column = lax.broadcasted_iota(jnp.int32, (HORIZON, OUTW), 1)
    row = lax.broadcasted_iota(jnp.int32, (HORIZON, OUTW), 0)
    spread = (lax.div(column, NQ + 1) == row).astype(jnp.float32)
    wanted = jnp.dot(target, spread, precision=lax.Precision.HIGHEST)
    mask = matmul(tmask.astype(jnp.bfloat16), spread.astype(jnp.bfloat16))
    kind = lax.rem(lax.broadcasted_iota(jnp.int32, (1, OUTW), 1), NQ + 1)
    level = kind.astype(jnp.float32) / (NQ + 1)
    error = out - wanted
    above, below = level * -error, (level - 1.0) * -error
    slope = jnp.where(above > below, -level, jnp.where(above < below, 1.0 - level, 0.5 - level))
    square = jnp.sum(jnp.where(kind == 0, error * error * mask, 0.0), axis=1)
    quant = jnp.sum(jnp.where(kind == 0, 0.0, jnp.maximum(above, below) * mask), axis=1)
    onehot = jnp.repeat(onehot, NPATCH, axis=0)
    weight = jnp.sum(onehot * class_weight[None, :], axis=1, keepdims=True)
    grad = weight * mask * jnp.where(kind == 0, 2.0 * error, slope / NQ)
    sums = jnp.dot(jnp.stack([square, quant]), onehot, precision=lax.Precision.HIGHEST)
    return sums, grad.astype(jnp.bfloat16)


def layer_forward(state_zero, mats, parts, cosine, sine):
    w_qkv, w_out, w_up, w_down = (mats[2], mats[3], mats[4], mats[5])
    gain_one, gain_two = (parts[3], parts[4])
    normed_one = rms_norm(state_zero, gain_one).astype(jnp.bfloat16)
    qkv = matmul(normed_one, w_qkv)
    queries, key_rot, value_all, mixed = attend_call(
        attend_kernel, (qkv, cosine, sine), (D, D, D, D), (SPAN,), "attend"
    )
    state_one = state_zero + matmul(mixed, w_out)
    normed_two = rms_norm(state_one, gain_two).astype(jnp.bfloat16)
    up_pre = matmul(normed_two, w_up)
    activ = silu(up_pre).astype(jnp.bfloat16)
    state_two = state_one + matmul(activ, w_down)
    return (
        state_two,
        (
            normed_one,
            queries,
            key_rot,
            value_all,
            mixed,
            state_one,
            normed_two,
            up_pre,
            activ,
        ),
    )


def layer_backward(grad_two, state_zero, kept, mats, parts, cosine, sine):
    (
        normed_one,
        queries,
        key_rot,
        value_all,
        mixed,
        state_one,
        normed_two,
        up_pre,
        activ,
    ) = kept
    w_qkv, w_out, w_up, w_down = (mats[2], mats[3], mats[4], mats[5])
    gain_one, gain_two = (parts[3], parts[4])
    grad_mlp = grad_two.astype(jnp.bfloat16)
    grad_act = backmul(grad_mlp, w_down)
    grad_up_pre = (grad_act * silu_slope(up_pre)).astype(jnp.bfloat16)
    grad_normed = backmul(grad_up_pre, w_up)
    _, pull = jax.vjp(rms_norm, state_one, gain_two)
    grad_norm_in, grad_gain_two = pull(grad_normed)
    grad_one = grad_two + grad_norm_in
    grad_proj = grad_one.astype(jnp.bfloat16)
    grad_mixed = backmul(grad_proj, w_out).astype(jnp.bfloat16)
    (grad_qkv,) = attend_call(
        attend_back_kernel,
        (queries, key_rot, value_all, grad_mixed, cosine, sine),
        (3 * D,),
        (D, D, D),
        "attend_back",
    )
    grad_normed_one = backmul(grad_qkv, w_qkv)
    _, pull = jax.vjp(rms_norm, state_zero, gain_one)
    grad_zero_in, grad_gain_one = pull(grad_normed_one)
    return (
        grad_one + grad_zero_in,
        (
            (normed_one, grad_qkv),
            (mixed, grad_proj),
            (normed_two, grad_up_pre),
            (activ, grad_mlp),
        ),
        grad_gain_one,
        grad_gain_two,
    )


def adamw(weight, first, second, grad, step):
    power = step[0].astype(jnp.float32)
    first = BETA * first + (1.0 - BETA) * grad
    second = BETA * second + (1.0 - BETA) * grad * grad
    fix_one = 1.0 - jnp.power(BETA, power)
    fix_two = 1.0 - jnp.power(BETA, power)
    new = weight - RATE * (
        first / fix_one / (jnp.sqrt(second / fix_two) + EPSILON) + DECAY * weight
    )
    return (new, first, second)


def on_device(
    series,
    pad_mask,
    freq_class,
    owner,
    step,
    master,
    moment1,
    moment2,
    small_master,
    small_m1,
    small_m2,
):
    slot_count = master.shape[0]
    parts = split_small(small_master)
    freq, bias_one, bias_two, head_bias, out_bias = (
        parts[0],
        parts[1],
        parts[2],
        parts[5],
        parts[6],
    )
    feat, target, tmask = prepare(series, pad_mask)
    count_series = series.shape[0]
    tokens = count_series * NPATCH
    onehot = (freq_class[:, None] == jnp.arange(NCLASS, dtype=jnp.int32)[None, :]).astype(
        jnp.float32
    )
    local_counts = jnp.sum(
        onehot * jnp.sum(tmask.reshape(count_series, -1), axis=1)[:, None], 0
    )
    gathered, counts = gather_all(master.astype(jnp.bfloat16), local_counts)
    mats = unpack(gathered, owner)
    tok_in, tok_out, head_in, head_out = (mats[0], mats[1], mats[6], mats[7])
    class_weight = 1.0 / (counts * NCLASS)
    cosine, sine = flat_tables()
    patch_in = feat.reshape(tokens, 2 * PATCH).astype(jnp.bfloat16)
    tok_pre = matmul(patch_in, tok_in)
    hidden = silu(tok_pre[:, :D] + bias_one).astype(jnp.bfloat16)
    class_rows = jnp.repeat(jnp.dot(onehot, freq, precision=lax.Precision.HIGHEST), NPATCH, axis=0)
    state_zero = matmul(hidden, tok_out) + bias_two + tok_pre[:, D:] + class_rows
    state_two, kept = layer_forward(state_zero, mats, parts, cosine, sine)
    state_low = state_two.astype(jnp.bfloat16)
    head_pre = matmul(state_low, head_in)
    head_hidden = silu(head_pre[:, :D] + head_bias).astype(jnp.bfloat16)
    out = matmul(head_hidden, head_out) + out_bias + head_pre[:, D:]

    local_sums, grad_out = loss_parts(out, target, tmask, onehot, class_weight)
    grad_out_bias = jnp.sum(grad_out.astype(jnp.float32), axis=0)
    grad_head_first = backmul(grad_out, head_out) * silu_slope(head_pre[:, :D] + head_bias)
    grad_head_bias = jnp.sum(grad_head_first, axis=0)
    grad_head_pre = jnp.concatenate([grad_head_first, grad_out.astype(jnp.float32)], axis=1).astype(
        jnp.bfloat16
    )
    grad_two = backmul(grad_head_pre, head_in)
    grad_zero, layer_pairs, grad_gain_one, grad_gain_two = layer_backward(
        grad_two, state_zero, kept, mats, parts, cosine, sine
    )
    grad_prod = grad_zero.astype(jnp.bfloat16)
    grad_first = backmul(grad_prod, tok_out) * silu_slope(tok_pre[:, :D] + bias_one)
    grad_tok_pre = jnp.concatenate([grad_first, grad_zero], axis=1).astype(jnp.bfloat16)
    slots = grad_blocks(
        ((patch_in, grad_tok_pre), (hidden, grad_prod))
        + layer_pairs
        + ((state_low, grad_head_pre), (head_hidden, grad_out)),
        owner,
    )
    grad_freq = jnp.dot(
        onehot.T,
        grad_zero.reshape(count_series, NPATCH, D).sum(axis=1),
        precision=lax.Precision.HIGHEST,
    )
    small_local = jnp.concatenate(
        [
            grad_freq.reshape(-1),
            jnp.sum(grad_first, axis=0),
            jnp.sum(grad_zero, axis=0),
            grad_gain_one,
            grad_gain_two,
            grad_head_bias,
            grad_out_bias,
            local_sums.reshape(-1),
        ]
    )
    rank = lax.axis_index("wide") * lax.axis_size("narrow") + lax.axis_index("narrow")
    mine = rank * slot_count + jnp.arange(slot_count, dtype=jnp.int32)
    filled = jnp.any(owner[:, None] == mine[None, :], axis=0)
    owned, square_total, small_total = scatter_sum(slots, filled, small_local)
    small_grad = small_total[: small_master.shape[0]]
    sums = small_total[small_master.shape[0] :].reshape(2, NCLASS)
    grad_norm = jnp.sqrt(square_total + jnp.sum(small_grad * small_grad))
    scale = jnp.minimum(1.0, CLIP / grad_norm)
    loss = jnp.sum((sums[0] + sums[1] / NQ) * class_weight)
    new_master, new_m1, new_m2 = adamw(master, moment1, moment2, owned * scale, step)
    small_new, small_new_m1, small_new_m2 = adamw(
        small_master, small_m1, small_m2, small_grad * scale, step
    )
    return (
        loss,
        grad_norm,
        new_master,
        new_m1,
        new_m2,
        new_master.astype(jnp.bfloat16),
        small_new,
        small_new_m1,
        small_new_m2,
    )


def solution(mesh):
    return jax.shard_map(
        on_device,
        mesh=mesh,
        in_specs=(
            P(("wide", "narrow"), None),
            P(("wide", "narrow"), None),
            P(("wide", "narrow")),
            P(),
            P(),
            P(("wide", "narrow"), None, None),
            P(("wide", "narrow"), None, None),
            P(("wide", "narrow"), None, None),
            P(),
            P(),
            P(),
        ),
        out_specs=(
            P(),
            P(),
            P(("wide", "narrow"), None, None),
            P(("wide", "narrow"), None, None),
            P(("wide", "narrow"), None, None),
            P(("wide", "narrow"), None, None),
            P(),
            P(),
            P(),
        ),
        check_vma=False,
    )
```

```python
import functools

import jax
import jax.numpy as jnp
from jax import lax
from jax.experimental import pallas as pl
from jax.experimental.pallas import tpu as pltpu
from jax.sharding import PartitionSpec as P

D = 1280
HEADS = 16
HDIM = 80
FF = 5120
PATCH = 32
HORIZON = 128
NQ = 9
NPATCH = 16
NCLASS = 3
BR = 64
TOTAL_SLOTS = 512
CTX = 512
OUTW = 1280
ROWS = 20608
NBLK = 322


CLIP = 0.01
RATE = 0.03
DECAY = 0.1
BETA = 0.5
EPSILON = 1e-08


def matmul(left, right):
    return jnp.dot(left, right, preferred_element_type=jnp.float32)


def tmatmul(left, right):
    return lax.dot_general(
        left, right, (((0,), (0,)), ((), ())), preferred_element_type=jnp.float32
    )


def backmul(left, right):
    return lax.dot_general(
        left, right, (((1,), (1,)), ((), ())), preferred_element_type=jnp.float32
    )


def silu(value):
    return value / (1.0 + jnp.exp(-value))


def silu_slope(value):
    sigmoid = 1.0 / (1.0 + jnp.exp(-value))
    return sigmoid * (1.0 + value * (1.0 - sigmoid))


def rms_norm(hidden, gain):
    return hidden * lax.rsqrt(jnp.mean(hidden * hidden, axis=-1, keepdims=True) + 1e-06) * gain


def tables():
    half = HDIM // 2
    inverse = jnp.power(10000.0, -2.0 * jnp.arange(half, dtype=jnp.float32) / HDIM)
    angle = jnp.arange(NPATCH, dtype=jnp.float32)[:, None] * inverse[None, :]
    return (jnp.cos(angle)[None, :, None, :], jnp.sin(angle)[None, :, None, :])


SPAN = 2 * 128
ROWS_TOGETHER = 256


def turned(value, cosine, sine):
    half = HDIM // 2
    lane = lax.rem(lax.broadcasted_iota(jnp.int32, value.shape, 1), HDIM)
    other = jnp.where(lane < half, pltpu.roll(value, D - half, 1), pltpu.roll(value, half, 1))
    shape = (value.shape[0] // NPATCH, NPATCH, D)
    return (
        value.reshape(shape) * cosine[None] + other.reshape(shape) * sine[None]
    ).reshape(value.shape)


def attended(queries, keys):
    scores = backmul(queries, keys)
    row = lax.broadcasted_iota(jnp.int32, scores.shape, 0)
    column = lax.broadcasted_iota(jnp.int32, scores.shape, 1)
    seen = jnp.logical_and(column <= row, column >= row - lax.rem(row, NPATCH))
    scores = jnp.where(seen, scores, -1e30)
    expo = jnp.exp(scores - jnp.max(scores, axis=-1, keepdims=True))
    return expo * (1.0 / jnp.sum(expo, axis=-1, keepdims=True))


def parts_of(ref):
    step = min(ROWS_TOGETHER, ref.shape[0])
    return [slice(at, at + step) for at in range(0, ref.shape[0], step)]


def head_lanes(h):
    start = jnp.minimum(lax.div(h * HDIM, LANES) * LANES, D - SPAN)
    lane = start + lax.broadcasted_iota(jnp.int32, (1, SPAN), 1)
    inside = jnp.logical_and(lane >= h * HDIM, lane < (h + 1) * HDIM)
    return (
        pl.ds(pl.multiple_of(start, LANES), SPAN),
        jnp.where(inside, 1.0, 0.0).astype(jnp.bfloat16),
    )


def attend_kernel(qkv_ref, cos_ref, sin_ref, query_ref, key_ref, value_ref, mixed_ref, total_ref):
    cosine, sine = cos_ref[...], sin_ref[...]
    query_ref[...] = (turned(qkv_ref[:, 0:D], cosine, sine) * HDIM ** (-0.5)).astype(jnp.bfloat16)
    key_ref[...] = turned(qkv_ref[:, D : 2 * D], cosine, sine).astype(jnp.bfloat16)
    value_ref[...] = qkv_ref[:, 2 * D : 3 * D].astype(jnp.bfloat16)
    total_ref[...] = jnp.zeros_like(total_ref)

    def head(h, carry):
        span, lanes = head_lanes(h)
        for rows in parts_of(query_ref):
            attend = attended(query_ref[rows, span] * lanes, key_ref[rows, span])
            total_ref[rows, span] += matmul(
                attend.astype(jnp.bfloat16), value_ref[rows, span] * lanes
            )
        return carry

    lax.fori_loop(0, HEADS, head, 0, unroll=8)
    mixed_ref[...] = total_ref[...].astype(jnp.bfloat16)


def attend_back_kernel(
    query_ref, key_ref, value_ref, grad_ref, cos_ref, sin_ref, out_ref, dq_ref, dk_ref, dv_ref
):
    for ref in (dq_ref, dk_ref, dv_ref):
        ref[...] = jnp.zeros_like(ref)

    def head(h, carry):
        span, lanes = head_lanes(h)
        for rows in parts_of(query_ref):
            queries, keys = query_ref[rows, span] * lanes, key_ref[rows, span] * lanes
            grad = grad_ref[rows, span] * lanes
            attend = attended(queries, keys)
            grad_attend = backmul(grad, value_ref[rows, span])
            grad_scores = (
                attend * (grad_attend - jnp.sum(grad_attend * attend, axis=-1, keepdims=True))
            ).astype(jnp.bfloat16)
            dq_ref[rows, span] += matmul(grad_scores, keys)
            dk_ref[rows, span] += tmatmul(grad_scores, queries)
            dv_ref[rows, span] += tmatmul(attend.astype(jnp.bfloat16), grad)
        return carry

    lax.fori_loop(0, HEADS, head, 0, unroll=8)
    cosine, sine = cos_ref[...], sin_ref[...]
    out_ref[:, 0:D] = (turned(dq_ref[...], cosine, -sine) * HDIM ** (-0.5)).astype(jnp.bfloat16)
    out_ref[:, D : 2 * D] = turned(dk_ref[...], cosine, -sine).astype(jnp.bfloat16)
    out_ref[:, 2 * D : 3 * D] = dv_ref[...].astype(jnp.bfloat16)


def flat_tables():
    cosine, sine = (table[0, :, 0, :] for table in tables())
    return (
        jnp.tile(jnp.concatenate([cosine, cosine], axis=1), (1, HEADS)),
        jnp.tile(jnp.concatenate([-sine, sine], axis=1), (1, HEADS)),
    )


def attend_call(kernel, operands, widths, scratch, name):
    tokens = operands[0].shape[0]
    return pl.pallas_call(
        kernel,
        out_shape=tuple(jax.ShapeDtypeStruct((tokens, width), jnp.bfloat16) for width in widths),
        scratch_shapes=[pltpu.VMEM((tokens, width), jnp.float32) for width in scratch],
        compiler_params=pltpu.CompilerParams(vmem_limit_bytes=VMEM_LIMIT),
        name=name,
    )(*operands)


MATS = (
    (2 * PATCH, 2, 2),
    (D, 1, 10),
    (D, 3, 6),
    (D, 1, 10),
    (D, FF // D, 8),
    (FF, 1, 8),
    (D, (D + OUTW) // D, 8),
    (D, 1, 10),
)
BASES = tuple(sum(r * g for r, g, _ in MATS[:i]) // BR for i in range(len(MATS)))
LANES = 128
VMEM_LIMIT = 56 * 1024 * 1024
SCATTER_VMEM = 61 * 1024 * 1024


RING = 48


def steps_of(which):
    total, groups, count = MATS[which]
    return total * groups // (count * BR)


def stages(kind):
    return [pltpu.VMEM((2,) + kind(*MATS[which]), jnp.bfloat16) for which in range(len(MATS))]


def unpack_kernel(owner_ref, gathered_ref, *refs):
    outs, held = refs[:8], refs[8:16]
    ring, wide_ref, load_sem, store_sem = refs[16:]

    def load(b):
        at = lax.rem(b, RING)
        return pltpu.make_async_copy(
            gathered_ref.at[owner_ref[b]], ring.at[at], load_sem.at[at]
        )

    def first_load(b, carry):
        load(b).start()
        return carry

    lax.fori_loop(0, RING, first_load, 0)

    def store(which, i):
        total, groups, count = MATS[which]
        rows = count * BR // groups
        at = lax.rem(i, 2)
        return pltpu.make_async_copy(
            held[which].at[at],
            outs[which].at[pl.ds(pl.multiple_of(i * rows, rows), rows)],
            store_sem.at[which, at],
        )

    for which, (total, groups, count) in enumerate(MATS):
        rows = count * BR // groups

        def step(i, carry, which=which, groups=groups, count=count, rows=rows):
            first = BASES[which] + i * count
            at = lax.rem(i, 2)

            @pl.when(i >= 2)
            def _():
                store(which, i - 2).wait()

            for b in range(count):
                load(first + b).wait()
            for b in range(count):
                block = ring.at[lax.rem(first + b, RING)]
                span = slice(b * BR, (b + 1) * BR)
                if groups == 1:
                    held[which][at, span, :] = block[...]
                    continue
                for c in range(D // LANES):
                    wide_ref[c, span, :] = block[:, c * LANES : (c + 1) * LANES].astype(
                        jnp.float32
                    )
            if groups > 1:
                for j in range(groups):
                    for c in range(D // LANES):
                        left = j * D + c * LANES
                        held[which][at, :, left : left + LANES] = wide_ref[
                            c, pl.ds(j, rows, stride=groups), :
                        ].astype(jnp.bfloat16)
            store(which, i).start()
            for b in range(count):

                @pl.when(first + b + RING < NBLK)
                def _(b=b):
                    load(first + b + RING).start()

            return carry

        lax.fori_loop(0, steps_of(which), step, 0)

    for which in range(len(MATS)):
        for i in range(max(steps_of(which) - 2, 0), steps_of(which)):
            store(which, i).wait()


def unpack(gathered, owner):
    dma = pltpu.SemaphoreType.DMA
    return pl.pallas_call(
        unpack_kernel,
        out_shape=tuple(
            jax.ShapeDtypeStruct((total, groups * D), jnp.bfloat16) for total, groups, _ in MATS
        ),
        in_specs=[
            pl.BlockSpec(memory_space=pltpu.SMEM),
            pl.BlockSpec(memory_space=pl.ANY),
        ],
        out_specs=tuple(pl.BlockSpec(memory_space=pl.ANY) for _ in MATS),
        scratch_shapes=stages(lambda total, groups, count: (count * BR // groups, groups * D))
        + [
            pltpu.VMEM((RING, BR, D), jnp.bfloat16),
            pltpu.VMEM((D // LANES, 8 * BR, LANES), jnp.float32),
            dma((RING,)),
            dma((len(MATS), 2)),
        ],
        compiler_params=pltpu.CompilerParams(vmem_limit_bytes=VMEM_LIMIT),
        cost_estimate=pl.CostEstimate(
            flops=0, bytes_accessed=4 * ROWS * D, transcendentals=0
        ),
        name="unpack",
    )(owner, gathered)


def grad_kernel(owner_ref, *refs):
    lefts, rights, out_ref = refs[:8], refs[8:16], refs[16]
    left_in, right_in, held = refs[17:25], refs[25:33], refs[33:41]
    wide_ref, load_sem, store_sem = refs[41:]

    def loads(which):
        return (
            pltpu.make_async_copy(lefts[which], left_in[which], load_sem.at[which, 0]),
            pltpu.make_async_copy(rights[which], right_in[which], load_sem.at[which, 1]),
        )

    def store(which, i, b):
        at = lax.rem(i, 2)
        return pltpu.make_async_copy(
            held[which].at[at, pl.ds(b * BR, BR), :],
            out_ref.at[owner_ref[BASES[which] + i * MATS[which][2] + b]],
            store_sem.at[which, at, b],
        )

    order = tuple(reversed(range(len(MATS))))
    for which in order:
        for copy in loads(which):
            copy.start()
    for which in order:
        total, groups, count = MATS[which]
        rows = count * BR // groups
        for copy in loads(which):
            copy.wait()

        def step(i, carry, which=which, groups=groups, count=count, rows=rows):
            at = lax.rem(i, 2)

            @pl.when(i >= 2)
            def _():
                for b in range(count):
                    store(which, i - 2, b).wait()

            if steps_of(which) == 1:
                left = left_in[which][...]
            else:
                left = left_in[which][:, pl.ds(pl.multiple_of(i * rows, rows), rows)]
            for j in range(groups):
                part = tmatmul(left, right_in[which][:, j * D : (j + 1) * D])
                if groups == 1:
                    held[which][at] = part.astype(jnp.bfloat16)
                    continue
                for c in range(D // LANES):
                    wide_ref[c, pl.ds(j, rows, stride=groups), :] = part[
                        :, c * LANES : (c + 1) * LANES
                    ]
            if groups > 1:
                for c in range(D // LANES):
                    held[which][at, :, c * LANES : (c + 1) * LANES] = wide_ref[
                        c, 0 : count * BR, :
                    ].astype(jnp.bfloat16)
            for b in range(count):
                store(which, i, b).start()
            return carry

        lax.fori_loop(0, steps_of(which), step, 0)
    for which in order:
        for i in range(max(steps_of(which) - 2, 0), steps_of(which)):
            for b in range(MATS[which][2]):
                store(which, i, b).wait()


def grad_blocks(pairs, owner):
    lefts, rights = zip(*pairs)
    dma = pltpu.SemaphoreType.DMA
    tokens = lefts[0].shape[0]
    return pl.pallas_call(
        grad_kernel,
        out_shape=jax.ShapeDtypeStruct((TOTAL_SLOTS, BR, D), jnp.bfloat16),
        in_specs=[pl.BlockSpec(memory_space=pltpu.SMEM)]
        + [pl.BlockSpec(memory_space=pl.ANY)] * (2 * len(MATS)),
        out_specs=pl.BlockSpec(memory_space=pl.ANY),
        scratch_shapes=[pltpu.VMEM(left.shape, jnp.bfloat16) for left in lefts]
        + [pltpu.VMEM(right.shape, jnp.bfloat16) for right in rights]
        + stages(lambda total, groups, count: (count * BR, D))
        + [
            pltpu.VMEM((D // LANES, 8 * BR, LANES), jnp.float32),
            dma((len(MATS), 2)),
            dma((len(MATS), 2, 10)),
        ],
        compiler_params=pltpu.CompilerParams(vmem_limit_bytes=VMEM_LIMIT),
        cost_estimate=pl.CostEstimate(
            flops=2 * tokens * ROWS * D, bytes_accessed=2 * ROWS * D, transcendentals=0
        ),
        name="grad_blocks",
    )(owner, *lefts, *rights)


CHUNKS = 16
LATE = 4
EARLY = CHUNKS - LATE
COMBOS = 4 * LATE
STEPS = COMBOS + 5
MESH = pl.DeviceIdType.MESH


def total_of(*blocks):
    result = blocks[0].astype(jnp.float32)
    for block in blocks[1:]:
        result = result + block.astype(jnp.float32)
    return result


def scatter_kernel(
    slots_ref,
    small_ref,
    filled_ref,
    out_ref,
    small_out,
    square_out,
    small_in,
    own,
    pair_in,
    pair_sum,
    first_in,
    second_in,
    second_out,
    column,
    up_in,
    down_in,
    up_out,
    down_out,
    result,
    late_own,
    late_pair_in,
    late_sum,
    late_up_in,
    late_down_in,
    late_up_out,
    late_down_out,
    late_column,
    late_first_in,
    late_second_in,
    late_second_out,
    late_result,
    own_sem,
    pair_send,
    pair_recv,
    first_send,
    first_recv,
    second_send,
    second_recv,
    up_send,
    up_recv,
    down_send,
    down_recv,
    result_sem,
    late_own_sem,
    late_pair_send,
    late_pair_recv,
    late_up_send,
    late_up_recv,
    late_down_send,
    late_down_recv,
    late_first_send,
    late_first_recv,
    late_second_send,
    late_second_recv,
    late_result_sem,
    share_send,
    share_recv,
    spread_send,
    spread_recv,
    square_send,
    square_recv,
):
    wide, z = lax.axis_index("wide"), lax.axis_index("narrow")
    core, here = lax.rem(wide, 2), lax.div(wide, 2)
    x, y = lax.rem(here, 2), lax.div(here, 2)
    far = 3 - here

    def device(place, level):
        return (place * 2 + core, level)

    partner = (here * 2 + 1 - core, z)

    def near(k, which):
        along_y = lax.rem(k + which, 2)
        return (y + along_y - 2 * y * along_y) * 2 + (x + (1 - along_y) - 2 * x * (1 - along_y))

    places = 8 * 4
    me = wide * 4 + z
    barrier = pltpu.get_barrier_semaphore()

    def each(action):
        def body(i, carry):
            other = lax.rem(me + i, places)
            action(i, other, (lax.div(other, 4), lax.rem(other, 4)))
            return carry

        lax.fori_loop(1, places, body, 0)

    def greet(i, other, to):
        pl.semaphore_signal(barrier, inc=1, device_id=to, device_id_type=MESH)

    def share(i, other, to):
        return pltpu.make_async_remote_copy(
            src_ref=small_ref.at[other],
            dst_ref=small_in.at[me],
            send_sem=share_send.at[i],
            recv_sem=share_recv.at[i],
            device_id=to,
            device_id_type=MESH,
        )

    def tell(ref, send, recv):
        def make(i, other, to):
            return pltpu.make_async_remote_copy(
                src_ref=ref.at[me],
                dst_ref=ref.at[me],
                send_sem=send.at[i],
                recv_sem=recv.at[i],
                device_id=to,
                device_id_type=MESH,
            )

        return make

    spread = tell(small_out, spread_send, spread_recv)
    square = tell(square_out, square_send, square_recv)
    each(greet)
    small_in[me] = small_ref[me]
    square_out[me] = jnp.zeros((8, LANES), jnp.float32)
    pl.semaphore_wait(barrier, places - 1)

    def own_copy(k):
        at = lax.rem(k, 2)
        return pltpu.make_async_copy(slots_ref.at[:, core, :, k], own.at[at], own_sem.at[at])

    def pair_copy(k):
        at = lax.rem(k, 2)
        return pltpu.make_async_remote_copy(
            src_ref=slots_ref.at[:, 1 - core, :, k],
            dst_ref=pair_in.at[at],
            send_sem=pair_send.at[at],
            recv_sem=pair_recv.at[at],
            device_id=partner,
            device_id_type=MESH,
        )

    def first_copy(k, part):
        place = near(k, 0)
        return pltpu.make_async_remote_copy(
            src_ref=pair_sum.at[lax.rem(k, 3), far if part == 0 else place],
            dst_ref=first_in.at[lax.rem(k, 5), part],
            send_sem=first_send.at[lax.rem(k, 3), part],
            recv_sem=first_recv.at[lax.rem(k, 5), part],
            device_id=device(place, z),
            device_id_type=MESH,
        )

    def second_copy(k):
        return pltpu.make_async_remote_copy(
            src_ref=second_out.at[lax.rem(k, 2)],
            dst_ref=second_in.at[lax.rem(k, 4)],
            send_sem=second_send.at[lax.rem(k, 2)],
            recv_sem=second_recv.at[lax.rem(k, 4)],
            device_id=device(near(k, 1), z),
            device_id_type=MESH,
        )

    def line_copy(source, target, send, recv, way):
        base = 1 if way > 0 else 0

        def make(k, level):
            return pltpu.make_async_remote_copy(
                src_ref=source.at[lax.rem(k, 2), level - base],
                dst_ref=target.at[lax.rem(k, 6), level - base],
                send_sem=send.at[lax.rem(k, 2), level - base],
                recv_sem=recv.at[lax.rem(k, 6), level - base],
                device_id=device(here, z + way),
                device_id_type=MESH,
            )

        return make

    def late_own_copy(c):
        at = lax.rem(c, 2)
        return pltpu.make_async_copy(
            slots_ref.at[lax.rem(c, 4), core, :, EARLY + lax.div(c, 4)],
            late_own.at[at],
            late_own_sem.at[at],
        )

    def late_pair_copy(c):
        at = lax.rem(c, 2)
        return pltpu.make_async_remote_copy(
            src_ref=slots_ref.at[lax.rem(c, 4), 1 - core, :, EARLY + lax.div(c, 4)],
            dst_ref=late_pair_in.at[at],
            send_sem=late_pair_send.at[at],
            recv_sem=late_pair_recv.at[at],
            device_id=partner,
            device_id_type=MESH,
        )

    def late_first_copy(slot, part):
        place = near(slot, 0)
        return pltpu.make_async_remote_copy(
            src_ref=late_column.at[slot, far if part == 0 else place],
            dst_ref=late_first_in.at[slot, part],
            send_sem=late_first_send.at[slot, part],
            recv_sem=late_first_recv.at[slot, part],
            device_id=device(place, z),
            device_id_type=MESH,
        )

    def late_second_copy(slot):
        return pltpu.make_async_remote_copy(
            src_ref=late_second_out.at[slot],
            dst_ref=late_second_in.at[slot],
            send_sem=late_second_send.at[slot],
            recv_sem=late_second_recv.at[slot],
            device_id=device(near(slot, 1), z),
            device_id_type=MESH,
        )

    def late_result_copy(slot):
        return pltpu.make_async_copy(late_result, out_ref.at[EARLY + slot], late_result_sem)

    def result_copy(k):
        at = lax.rem(k, 2)
        return pltpu.make_async_copy(result.at[at], out_ref.at[k], result_sem.at[at])

    def valid(k):
        return jnp.logical_and(k >= 0, k < EARLY)

    def valid_late(c):
        return jnp.logical_and(c >= 0, c < COMBOS)

    def keep(ref, k):
        kept = jnp.where(filled_ref[k, 0:1, 0:1] > 0.0, ref[...], 0.0)
        ref[...] = kept
        squares = square_out[me]
        for i in range(BR // 8):
            for j in range(D // LANES):
                part = kept[i * 8 : (i + 1) * 8, j * LANES : (j + 1) * LANES]
                squares = squares + part * part
        square_out[me] = squares

    def flows(lags, known, sums, ring, ins, outs, copies):
        for base, lag, behind, copy, arrived, leaving in zip(
            (1, 0), lags, (z > 0, z < 3), copies, ins, outs
        ):
            k = lag
            for n in range(base, base + 3):
                ahead = n > z if base else n < z

                @pl.when(jnp.logical_and(known(k - 2), ahead))
                def _(n=n, k=k, copy=copy):
                    copy(k - 2, n).wait_send()

                @pl.when(
                    jnp.logical_and(
                        jnp.logical_and(known(k), behind), jnp.logical_or(ahead, n == z)
                    )
                )
                def _(n=n, k=k, copy=copy):
                    copy(k, n).wait_recv()

                moving = jnp.logical_and(known(k), ahead)

                @pl.when(jnp.logical_and(moving, behind))
                def _(n=n, k=k, base=base, arrived=arrived, leaving=leaving):
                    leaving[lax.rem(k, 2), n - base] = total_of(
                        sums[lax.rem(k, ring), n], arrived[lax.rem(k, 6), n - base]
                    ).astype(jnp.bfloat16)

                @pl.when(jnp.logical_and(moving, jnp.logical_not(behind)))
                def _(n=n, k=k, base=base, leaving=leaving):
                    leaving[lax.rem(k, 2), n - base] = sums[lax.rem(k, ring), n]

                @pl.when(moving)
                def _(n=n, k=k, copy=copy):
                    copy(k, n).start()

    copies = (
        line_copy(up_out, up_in, up_send, up_recv, 1),
        line_copy(down_out, down_in, down_send, down_recv, -1),
    )
    late_copies = (
        line_copy(late_up_out, late_up_in, late_up_send, late_up_recv, 1),
        line_copy(late_down_out, late_down_in, late_down_send, late_down_recv, -1),
    )

    own_copy(0).start()
    pair_copy(0).start()
    late_own_copy(0).start()
    late_pair_copy(0).start()
    each(lambda *at: share(*at).start())

    def step(t, carry):
        @pl.when(valid(t - 3))
        def _():
            first_copy(t - 3, 0).wait_send()
            first_copy(t - 3, 1).wait_send()

        @pl.when(valid(t))
        def _():
            own_copy(t).wait()
            pair_copy(t).wait_recv()
            at, ring = lax.rem(t, 2), lax.rem(t, 3)

            def add(i, inner):
                p, n = lax.div(i, 4), lax.rem(i, 4)
                pair_sum[ring, p, n] = total_of(own[at, p, n], pair_in[at, p, n]).astype(
                    jnp.bfloat16
                )
                return inner

            lax.fori_loop(0, 16, add, 0)
            first_copy(t, 0).start()
            first_copy(t, 1).start()

        @pl.when(valid(t - 1))
        def _():
            pair_copy(t - 1).wait_send()

        @pl.when(t + 1 < EARLY)
        def _():
            own_copy(t + 1).start()
            pair_copy(t + 1).start()

        @pl.when(valid_late(t))
        def _():
            late_own_copy(t).wait()
            late_pair_copy(t).wait_recv()

            def add(n, inner):
                late_sum[lax.rem(t, 4), n] = total_of(
                    late_own[lax.rem(t, 2), n], late_pair_in[lax.rem(t, 2), n]
                ).astype(jnp.bfloat16)
                return inner

            lax.fori_loop(0, 4, add, 0)

        @pl.when(valid_late(t - 1))
        def _():
            late_pair_copy(t - 1).wait_send()

        @pl.when(t + 1 < COMBOS)
        def _():
            late_own_copy(t + 1).start()
            late_pair_copy(t + 1).start()

        @pl.when(valid(t - 3))
        def _():
            second_copy(t - 3).wait_send()

        @pl.when(valid(t - 1))
        def _():
            k = t - 1
            first_copy(k, 0).wait_recv()
            place = near(k, 1)

            def add(n, inner):
                second_out[lax.rem(k, 2), n] = total_of(
                    pair_sum[lax.rem(k, 3), place, n], first_in[lax.rem(k, 5), 0, n]
                ).astype(jnp.bfloat16)
                return inner

            lax.fori_loop(0, 4, add, 0)
            second_copy(k).start()

        @pl.when(valid(t - 2))
        def _():
            k = t - 2
            first_copy(k, 1).wait_recv()
            second_copy(k).wait_recv()

            def add(n, inner):
                column[lax.rem(k, 4), n] = total_of(
                    pair_sum[lax.rem(k, 3), here, n],
                    first_in[lax.rem(k, 5), 1, n],
                    second_in[lax.rem(k, 4), n],
                ).astype(jnp.bfloat16)
                return inner

            lax.fori_loop(0, 4, add, 0)

        flows(
            (t - 2 - z, t - 5 + z), valid, column, 4, (up_in, down_in), (up_out, down_out), copies
        )
        flows(
            (t - z, t - 3 + z),
            valid_late,
            late_sum,
            4,
            (late_up_in, late_down_in),
            (late_up_out, late_down_out),
            late_copies,
        )
        c = t - 3

        @pl.when(valid_late(c))
        def _():
            slot, p = lax.div(c, 4), lax.rem(c, 4)
            mine = late_sum.at[lax.rem(c, 4), z]
            below = late_up_in.at[lax.rem(c, 6), jnp.maximum(z - 1, 0)]
            above = late_down_in.at[lax.rem(c, 6), jnp.minimum(z, 2)]

            @pl.when(z == 0)
            def _():
                late_column[slot, p] = total_of(mine[...], above[...]).astype(jnp.bfloat16)

            @pl.when(z == 3)
            def _():
                late_column[slot, p] = total_of(mine[...], below[...]).astype(jnp.bfloat16)

            @pl.when(jnp.logical_and(z > 0, z < 3))
            def _():
                late_column[slot, p] = total_of(mine[...], below[...], above[...]).astype(
                    jnp.bfloat16
                )

        for slot in range(LATE):
            place = near(slot, 1)

            @pl.when(t == 4 * slot + 6)
            def _(slot=slot):
                late_first_copy(slot, 0).start()
                late_first_copy(slot, 1).start()

            @pl.when(t == 4 * slot + 7)
            def _(slot=slot, place=place):
                late_first_copy(slot, 0).wait_recv()
                late_second_out[slot] = total_of(
                    late_column[slot, place], late_first_in[slot, 0]
                ).astype(jnp.bfloat16)
                late_second_copy(slot).start()

            @pl.when(t == 4 * slot + 8)
            def _(slot=slot):
                late_first_copy(slot, 1).wait_recv()
                late_second_copy(slot).wait_recv()
                if slot:
                    late_result_copy(slot - 1).wait()
                late_result[...] = total_of(
                    late_column[slot, here], late_first_in[slot, 1], late_second_in[slot]
                )
                keep(late_result, EARLY + slot)
                late_result_copy(slot).start()

        k = t - 5

        @pl.when(valid(k - 2))
        def _():
            result_copy(k - 2).wait()

        @pl.when(valid(k))
        def _():
            result[lax.rem(k, 2)] = column[lax.rem(k, 4), z].astype(jnp.float32)

            @pl.when(z > 0)
            def _():
                result[lax.rem(k, 2)] += up_in[lax.rem(k, 6), z - 1].astype(jnp.float32)

            @pl.when(z < 3)
            def _():
                result[lax.rem(k, 2)] += down_in[lax.rem(k, 6), z].astype(jnp.float32)

            keep(result.at[lax.rem(k, 2)], k)
            result_copy(k).start()

        @pl.when(t == CHUNKS // 2)
        def _():
            each(lambda *at: share(*at).wait())
            small = small_in[0]
            for i in range(1, places):
                small = small + small_in[i]
            small_out[me] = small
            each(lambda *at: spread(*at).start())

        return carry

    lax.fori_loop(0, STEPS, step, 0)
    each(lambda *at: square(*at).start())
    late_result_copy(LATE - 1).wait()
    for slot in range(LATE):
        late_first_copy(slot, 0).wait_send()
        late_first_copy(slot, 1).wait_send()
        late_second_copy(slot).wait_send()
    each(lambda *at: spread(*at).wait())
    each(lambda *at: square(*at).wait())


def scatter_sum(slots, filled, small):
    slot_count = filled.shape[0]
    wide, narrow = lax.axis_size("wide"), lax.axis_size("narrow")
    if (wide, narrow, slot_count) != (8, 4, CHUNKS):
        part = lax.psum_scatter(slots, "wide", scatter_dimension=0, tiled=True)
        owned = lax.psum_scatter(
            part.astype(jnp.float32), "narrow", scatter_dimension=0, tiled=True
        )
        owned = jnp.where(filled[:, None, None], owned, 0.0)
        square = lax.psum(jnp.sum(owned * owned), ("wide", "narrow"))
        return owned, square, lax.psum(small, ("wide", "narrow"))
    tiles = (wide * narrow, 8, LANES)
    room = wide * narrow * 8 * LANES - small.shape[0]
    assert room >= 0
    low = functools.partial(pltpu.VMEM, dtype=jnp.bfloat16)
    dma = pltpu.SemaphoreType.DMA
    block = (BR, D)
    owned, small_tiles, square_tiles = pl.pallas_call(
        scatter_kernel,
        out_shape=(
            jax.ShapeDtypeStruct((slot_count,) + block, jnp.float32),
            jax.ShapeDtypeStruct(tiles, jnp.float32),
            jax.ShapeDtypeStruct(tiles, jnp.float32),
        ),
        in_specs=[
            pl.BlockSpec(memory_space=pl.ANY),
            pl.BlockSpec(memory_space=pltpu.VMEM),
            pl.BlockSpec(memory_space=pltpu.VMEM),
        ],
        out_specs=(
            pl.BlockSpec(memory_space=pl.ANY),
            pl.BlockSpec(memory_space=pltpu.VMEM),
            pl.BlockSpec(memory_space=pltpu.VMEM),
        ),
        scratch_shapes=[
            pltpu.VMEM(tiles, jnp.float32),
            low((2, 4, 4) + block),
            low((2, 4, 4) + block),
            low((3, 4, 4) + block),
            low((5, 2, 4) + block),
            low((4, 4) + block),
            low((2, 4) + block),
            low((4, 4) + block),
            low((6, 3) + block),
            low((6, 3) + block),
            low((2, 3) + block),
            low((2, 3) + block),
            pltpu.VMEM((2,) + block, jnp.float32),
            low((2, 4) + block),
            low((2, 4) + block),
            low((4, 4) + block),
            low((6, 3) + block),
            low((6, 3) + block),
            low((2, 3) + block),
            low((2, 3) + block),
            low((LATE, 4) + block),
            low((LATE, 2) + block),
            low((LATE,) + block),
            low((LATE,) + block),
            pltpu.VMEM(block, jnp.float32),
            dma((2,)),
            dma((2,)),
            dma((2,)),
            dma((3, 2)),
            dma((5, 2)),
            dma((2,)),
            dma((4,)),
            dma((2, 3)),
            dma((6, 3)),
            dma((2, 3)),
            dma((6, 3)),
            dma((2,)),
            dma((2,)),
            dma((2,)),
            dma((2,)),
            dma((2, 3)),
            dma((6, 3)),
            dma((2, 3)),
            dma((6, 3)),
            dma((LATE, 2)),
            dma((LATE, 2)),
            dma((LATE,)),
            dma((LATE,)),
            dma,
        ]
        + [dma((wide * narrow,))] * 6,
        compiler_params=pltpu.CompilerParams(
            collective_id=1, has_side_effects=True, vmem_limit_bytes=SCATTER_VMEM
        ),
        name="scatter_sum",
    )(
        slots.reshape(4, 2, narrow, slot_count, BR, D),
        jnp.pad(small, (0, room)).reshape(tiles),
        jnp.broadcast_to(
            filled.astype(jnp.float32)[:, None, None], (slot_count, 8, LANES)
        ),
    )
    return owned, jnp.sum(square_tiles), small_tiles.reshape(-1)[: small.shape[0]]


GATHER_STEPS = EARLY + 5


def gather_kernel(
    own_ref,
    count_ref,
    all_ref,
    counts_ref,
    own_sem,
    recv,
    pair_recv,
    line_send,
    plane_send,
    turn_send,
    late_send,
    pair_send,
    late_pair_send,
    count_send,
    count_recv,
):
    wide, z = lax.axis_index("wide"), lax.axis_index("narrow")
    core, here = lax.rem(wide, 2), lax.div(wide, 2)
    x, y = lax.rem(here, 2), lax.div(here, 2)
    side, front, far = y * 2 + 1 - x, (1 - y) * 2 + x, 3 - here
    places = 8 * 4
    me = wide * 4 + z

    barrier = pltpu.get_barrier_semaphore()

    def greet(i, carry):
        other = lax.rem(me + i, places)
        pl.semaphore_signal(
            barrier,
            inc=1,
            device_id=(lax.div(other, 4), lax.rem(other, 4)),
            device_id_type=MESH,
        )
        return carry

    lax.fori_loop(1, places, greet, 0)
    fill = pltpu.make_async_copy(own_ref, all_ref.at[here, core, z], own_sem)
    fill.start()
    counts_ref[me] = count_ref[...]
    pl.semaphore_wait(barrier, places - 1)
    fill.wait()

    def count_copy(i):
        other = lax.rem(me + i, places)
        return pltpu.make_async_remote_copy(
            src_ref=count_ref,
            dst_ref=counts_ref.at[me],
            send_sem=count_send.at[i],
            recv_sem=count_recv.at[i],
            device_id=(lax.div(other, 4), lax.rem(other, 4)),
            device_id_type=MESH,
        )

    def count_start(i, carry):
        count_copy(i).start()
        return carry

    lax.fori_loop(1, places, count_start, 0)

    def piece(p, n, k, send, to):
        return pltpu.make_async_remote_copy(
            src_ref=all_ref.at[p, core, n, k],
            dst_ref=all_ref.at[p, core, n, k],
            send_sem=send,
            recv_sem=recv.at[p, n, k],
            device_id=to,
            device_id_type=MESH,
        )

    up, down = (wide, z + 1), (wide, z - 1)
    to_side, to_front = (side * 2 + core, z), (front * 2 + core, z)

    def line(n, k, step):
        return piece(here, n, k, line_send.at[step, n, k], (up, down)[step])

    def plane(n, k, which):
        return piece(here, n, k, plane_send.at[which, n, k], (to_side, to_front)[which])

    def turn(n, k, which):
        return piece(
            (side, front)[which], n, k, turn_send.at[n, k], (to_front, to_side)[which]
        )

    def late(c, n, step):
        p, k = lax.rem(here + c, 4), EARLY + lax.div(c, 4)
        return piece(p, n, k, late_send.at[step, c, n], (up, down)[step])

    def pair(p, k, send):
        return pltpu.make_async_remote_copy(
            src_ref=all_ref.at[p, core, :, k],
            dst_ref=all_ref.at[p, core, :, k],
            send_sem=send,
            recv_sem=pair_recv,
            device_id=(here * 2 + 1 - core, z),
            device_id_type=MESH,
        )

    def early_pair(p, k):
        return pair(p, k, pair_send.at[p, k])

    def late_pair(c):
        p, k = lax.rem(here + c, 4), EARLY + lax.div(c, 4)
        return pair(p, k, late_pair_send.at[c])

    def both_lines(make, n, j, start):
        @pl.when(jnp.logical_and(start, z < 3))
        def _():
            if j <= 0:
                make(n, 0)

        @pl.when(jnp.logical_and(start, z > 0))
        def _():
            if j >= 0:
                make(n, 1)

    def early(k):
        return jnp.logical_and(k >= 0, k < EARLY)

    def swap(n, k, go):
        even = lax.rem(n + k, 2) == 0

        @pl.when(jnp.logical_and(go, even))
        def _():
            turn(n, k, 0).start()

        @pl.when(jnp.logical_and(go, jnp.logical_not(even)))
        def _():
            turn(n, k, 1).start()

    for k in range(EARLY, CHUNKS):
        plane(z, k, 0).start()
        plane(z, k, 1).start()

    def step(t, carry):
        @pl.when(early(t))
        def _():
            plane(z, t, 0).start()
            plane(z, t, 1).start()

        both_lines(lambda n, way: line(n, t, way).start(), z, 0, early(t))

        for j in (-1, 1, -2, 2, -3, 3):
            n, k = z + j, t - abs(j)
            there = jnp.logical_and(early(k), jnp.logical_and(n >= 0, n < 4))

            @pl.when(there)
            def _(n=n, k=k, j=j):
                piece(here, n, k, plane_send.at[0, n, k], to_side).wait_recv()

            both_lines(lambda n, way, k=k: line(n, k, way).start(), n, j, there)

            @pl.when(there)
            def _(n=n, k=k):
                plane(n, k, 0).start()
                plane(n, k, 1).start()

        @pl.when(t == 1)
        def _():
            for k in range(EARLY, CHUNKS):
                plane_wait(side, z, k)
                plane_wait(front, z, k)
                swap(z, k, True)

        @pl.when(t == 2)
        def _():
            for k in range(EARLY, CHUNKS):
                plane_wait(far, z, k)

        for j in (0, -1, 1, -2, 2, -3, 3):
            m = t - 2 - abs(j)
            n = z + j
            first = m + lax.div(m + 2, 3)
            for c, more in ((first, True), (first + 1, lax.rem(m, 3) == 0)):
                there = jnp.logical_and(
                    jnp.logical_and(m >= 0, c < COMBOS),
                    jnp.logical_and(jnp.logical_and(n >= 0, n < 4), more),
                )
                if j:

                    @pl.when(there)
                    def _(n=n, c=c):
                        plane_wait(lax.rem(here + c, 4), n, EARLY + lax.div(c, 4))

                both_lines(lambda n, way, c=c: late(c, n, way).start(), n, j, there)

        for n in range(4):
            gap = jnp.abs(z - n)
            k = t - 1 - gap

            @pl.when(early(k))
            def _(n=n, k=k):
                plane_wait(side, n, k)
                plane_wait(front, n, k)

            swap(n, k, early(k))
            k = t - 2 - gap

            @pl.when(early(k))
            def _(n=n, k=k):
                plane_wait(far, n, k)

        for lag, sent in ((3, (here,)), (4, (side, front)), (5, (far,))):
            k = t - lag

            @pl.when(early(k))
            def _(k=k, sent=sent):
                for p in sent:
                    early_pair(p, k).start()

        m = t - 5
        first = m + lax.div(m + 2, 3)
        for c, more in ((first, True), (first + 1, lax.rem(m, 3) == 0)):

            @pl.when(jnp.logical_and(jnp.logical_and(m >= 0, c < COMBOS), more))
            def _(c=c):
                late_pair(c).start()

        return carry

    def plane_wait(p, n, k):
        piece(p, n, k, plane_send.at[0, n, k], to_side).wait_recv()

    lax.fori_loop(0, GATHER_STEPS, step, 0)

    def finish(k, carry):
        for n in range(4):
            plane_used = jnp.logical_or(k < EARLY, n == z)

            @pl.when(plane_used)
            def _(n=n):
                plane(n, k, 0).wait_send()
                plane(n, k, 1).wait_send()
                turn(n, k, 0).wait_send()

            @pl.when(jnp.logical_and(k < EARLY, jnp.logical_and(n <= z, z < 3)))
            def _(n=n):
                line(n, k, 0).wait_send()

            @pl.when(jnp.logical_and(k < EARLY, jnp.logical_and(n >= z, z > 0)))
            def _(n=n):
                line(n, k, 1).wait_send()

            @pl.when(jnp.logical_and(n <= z, z < 3))
            def _(n=n):
                late(k, n, 0).wait_send()

            @pl.when(jnp.logical_and(n >= z, z > 0))
            def _(n=n):
                late(k, n, 1).wait_send()

        @pl.when(k < EARLY)
        def _():
            for p in range(4):
                early_pair(p, k).wait_send()

        late_pair(k).wait_send()
        return carry

    lax.fori_loop(0, CHUNKS, finish, 0)

    def count_wait(i, carry):
        count_copy(i).wait()
        return carry

    lax.fori_loop(1, places, count_wait, 0)
    pltpu.make_async_copy(
        all_ref.at[:, 1 - core], all_ref.at[:, 1 - core], pair_recv
    ).wait()


def gather_all(low, local_counts):
    slot_count = low.shape[0]
    wide, narrow = lax.axis_size("wide"), lax.axis_size("narrow")
    if (wide, narrow, slot_count) != (8, 4, CHUNKS):
        return (
            lax.all_gather(low, ("wide", "narrow"), axis=0, tiled=True),
            lax.psum(local_counts, ("wide", "narrow")),
        )
    dma = pltpu.SemaphoreType.DMA
    tile = jnp.zeros((8, LANES), jnp.float32).at[0, :NCLASS].set(local_counts)
    gathered, tiles = pl.pallas_call(
        gather_kernel,
        out_shape=(
            jax.ShapeDtypeStruct((4, 2, narrow, slot_count, BR, D), jnp.bfloat16),
            jax.ShapeDtypeStruct((wide * narrow, 8, LANES), jnp.float32),
        ),
        in_specs=[
            pl.BlockSpec(memory_space=pltpu.VMEM),
            pl.BlockSpec(memory_space=pltpu.VMEM),
        ],
        out_specs=(
            pl.BlockSpec(memory_space=pl.ANY),
            pl.BlockSpec(memory_space=pltpu.VMEM),
        ),
        scratch_shapes=[
            dma,
            dma((4, 4, CHUNKS)),
            dma,
            dma((2, 4, EARLY)),
            dma((2, 4, CHUNKS)),
            dma((4, CHUNKS)),
            dma((2, COMBOS, 4)),
            dma((4, EARLY)),
            dma((COMBOS,)),
            dma((wide * narrow,)),
            dma((wide * narrow,)),
        ],
        compiler_params=pltpu.CompilerParams(
            collective_id=2, has_side_effects=True, vmem_limit_bytes=VMEM_LIMIT
        ),
        name="gather_all",
    )(low, tile)
    return (
        gathered.reshape(wide * narrow * slot_count, BR, D),
        jnp.sum(tiles[:, 0, :NCLASS], axis=0),
    )


def split_small(small):
    freq = small[: NCLASS * D].reshape(NCLASS, D)
    rest = small[NCLASS * D :]
    return (
        freq,
        rest[0:D],
        rest[D : 2 * D],
        rest[2 * D : 3 * D],
        rest[3 * D : 4 * D],
        rest[4 * D : 5 * D],
        rest[5 * D : 5 * D + OUTW],
    )


def prepare(series, pad_mask):
    valid = (1 - pad_mask).astype(jnp.float32)
    count_series = series.shape[0]
    context = (series[:, :CTX] * valid[:, :CTX]).reshape(count_series, NPATCH, PATCH)
    marks = pad_mask[:, :CTX].astype(jnp.float32).reshape(count_series, NPATCH, PATCH)
    feat = jnp.concatenate([context, marks], axis=-1)
    return (feat, horizons(series), horizons(valid))


def horizons(points):
    count_series = points.shape[0]
    pieces = points.reshape(count_series, -1, PATCH)
    return jnp.concatenate(
        [pieces[:, 1 + j : 1 + j + NPATCH] for j in range(HORIZON // PATCH)], axis=-1
    ).reshape(count_series * NPATCH, HORIZON)


def loss_parts(out, target, tmask, onehot, class_weight):
    column = lax.broadcasted_iota(jnp.int32, (HORIZON, OUTW), 1)
    row = lax.broadcasted_iota(jnp.int32, (HORIZON, OUTW), 0)
    spread = (lax.div(column, NQ + 1) == row).astype(jnp.float32)
    wanted = jnp.dot(target, spread, precision=lax.Precision.HIGHEST)
    mask = matmul(tmask.astype(jnp.bfloat16), spread.astype(jnp.bfloat16))
    kind = lax.rem(lax.broadcasted_iota(jnp.int32, (1, OUTW), 1), NQ + 1)
    level = kind.astype(jnp.float32) / (NQ + 1)
    error = out - wanted
    above, below = level * -error, (level - 1.0) * -error
    slope = jnp.where(above > below, -level, jnp.where(above < below, 1.0 - level, 0.5 - level))
    square = jnp.sum(jnp.where(kind == 0, error * error * mask, 0.0), axis=1)
    quant = jnp.sum(jnp.where(kind == 0, 0.0, jnp.maximum(above, below) * mask), axis=1)
    onehot = jnp.repeat(onehot, NPATCH, axis=0)
    weight = jnp.sum(onehot * class_weight[None, :], axis=1, keepdims=True)
    grad = weight * mask * jnp.where(kind == 0, 2.0 * error, slope / NQ)
    sums = jnp.dot(jnp.stack([square, quant]), onehot, precision=lax.Precision.HIGHEST)
    return sums, grad.astype(jnp.bfloat16)


def layer_forward(state_zero, mats, parts, cosine, sine):
    w_qkv, w_out, w_up, w_down = (mats[2], mats[3], mats[4], mats[5])
    gain_one, gain_two = (parts[3], parts[4])
    normed_one = rms_norm(state_zero, gain_one).astype(jnp.bfloat16)
    qkv = matmul(normed_one, w_qkv)
    queries, key_rot, value_all, mixed = attend_call(
        attend_kernel, (qkv, cosine, sine), (D, D, D, D), (D,), "attend"
    )
    state_one = state_zero + matmul(mixed, w_out)
    normed_two = rms_norm(state_one, gain_two).astype(jnp.bfloat16)
    up_pre = matmul(normed_two, w_up)
    activ = silu(up_pre).astype(jnp.bfloat16)
    state_two = state_one + matmul(activ, w_down)
    return (
        state_two,
        (
            normed_one,
            queries,
            key_rot,
            value_all,
            mixed,
            state_one,
            normed_two,
            up_pre,
            activ,
        ),
    )


def layer_backward(grad_two, state_zero, kept, mats, parts, cosine, sine):
    (
        normed_one,
        queries,
        key_rot,
        value_all,
        mixed,
        state_one,
        normed_two,
        up_pre,
        activ,
    ) = kept
    w_qkv, w_out, w_up, w_down = (mats[2], mats[3], mats[4], mats[5])
    gain_one, gain_two = (parts[3], parts[4])
    grad_mlp = grad_two.astype(jnp.bfloat16)
    grad_act = backmul(grad_mlp, w_down)
    grad_up_pre = (grad_act * silu_slope(up_pre)).astype(jnp.bfloat16)
    grad_normed = backmul(grad_up_pre, w_up)
    _, pull = jax.vjp(rms_norm, state_one, gain_two)
    grad_norm_in, grad_gain_two = pull(grad_normed)
    grad_one = grad_two + grad_norm_in
    grad_proj = grad_one.astype(jnp.bfloat16)
    grad_mixed = backmul(grad_proj, w_out).astype(jnp.bfloat16)
    (grad_qkv,) = attend_call(
        attend_back_kernel,
        (queries, key_rot, value_all, grad_mixed, cosine, sine),
        (3 * D,),
        (D, D, D),
        "attend_back",
    )
    grad_normed_one = backmul(grad_qkv, w_qkv)
    _, pull = jax.vjp(rms_norm, state_zero, gain_one)
    grad_zero_in, grad_gain_one = pull(grad_normed_one)
    return (
        grad_one + grad_zero_in,
        (
            (normed_one, grad_qkv),
            (mixed, grad_proj),
            (normed_two, grad_up_pre),
            (activ, grad_mlp),
        ),
        grad_gain_one,
        grad_gain_two,
    )


def adamw(weight, first, second, grad, step):
    power = step[0].astype(jnp.float32)
    first = BETA * first + (1.0 - BETA) * grad
    second = BETA * second + (1.0 - BETA) * grad * grad
    fix_one = 1.0 - jnp.power(BETA, power)
    fix_two = 1.0 - jnp.power(BETA, power)
    new = weight - RATE * (
        first / fix_one / (jnp.sqrt(second / fix_two) + EPSILON) + DECAY * weight
    )
    return (new, first, second)


def on_device(
    series,
    pad_mask,
    freq_class,
    owner,
    step,
    master,
    moment1,
    moment2,
    small_master,
    small_m1,
    small_m2,
):
    slot_count = master.shape[0]
    parts = split_small(small_master)
    freq, bias_one, bias_two, head_bias, out_bias = (
        parts[0],
        parts[1],
        parts[2],
        parts[5],
        parts[6],
    )
    feat, target, tmask = prepare(series, pad_mask)
    count_series = series.shape[0]
    tokens = count_series * NPATCH
    onehot = (freq_class[:, None] == jnp.arange(NCLASS, dtype=jnp.int32)[None, :]).astype(
        jnp.float32
    )
    local_counts = jnp.sum(
        onehot * jnp.sum(tmask.reshape(count_series, -1), axis=1)[:, None], 0
    )
    gathered, counts = gather_all(master.astype(jnp.bfloat16), local_counts)
    mats = unpack(gathered, owner)
    tok_in, tok_out, head_in, head_out = (mats[0], mats[1], mats[6], mats[7])
    class_weight = 1.0 / (counts * NCLASS)
    cosine, sine = flat_tables()
    patch_in = feat.reshape(tokens, 2 * PATCH).astype(jnp.bfloat16)
    tok_pre = matmul(patch_in, tok_in)
    hidden = silu(tok_pre[:, :D] + bias_one).astype(jnp.bfloat16)
    class_rows = jnp.repeat(jnp.dot(onehot, freq, precision=lax.Precision.HIGHEST), NPATCH, axis=0)
    state_zero = matmul(hidden, tok_out) + bias_two + tok_pre[:, D:] + class_rows
    state_two, kept = layer_forward(state_zero, mats, parts, cosine, sine)
    state_low = state_two.astype(jnp.bfloat16)
    head_pre = matmul(state_low, head_in)
    head_hidden = silu(head_pre[:, :D] + head_bias).astype(jnp.bfloat16)
    out = matmul(head_hidden, head_out) + out_bias + head_pre[:, D:]

    local_sums, grad_out = loss_parts(out, target, tmask, onehot, class_weight)
    grad_out_bias = jnp.sum(grad_out.astype(jnp.float32), axis=0)
    grad_head_first = backmul(grad_out, head_out) * silu_slope(head_pre[:, :D] + head_bias)
    grad_head_bias = jnp.sum(grad_head_first, axis=0)
    grad_head_pre = jnp.concatenate([grad_head_first, grad_out.astype(jnp.float32)], axis=1).astype(
        jnp.bfloat16
    )
    grad_two = backmul(grad_head_pre, head_in)
    grad_zero, layer_pairs, grad_gain_one, grad_gain_two = layer_backward(
        grad_two, state_zero, kept, mats, parts, cosine, sine
    )
    grad_prod = grad_zero.astype(jnp.bfloat16)
    grad_first = backmul(grad_prod, tok_out) * silu_slope(tok_pre[:, :D] + bias_one)
    grad_tok_pre = jnp.concatenate([grad_first, grad_zero], axis=1).astype(jnp.bfloat16)
    slots = grad_blocks(
        ((patch_in, grad_tok_pre), (hidden, grad_prod))
        + layer_pairs
        + ((state_low, grad_head_pre), (head_hidden, grad_out)),
        owner,
    )
    grad_freq = jnp.dot(
        onehot.T,
        grad_zero.reshape(count_series, NPATCH, D).sum(axis=1),
        precision=lax.Precision.HIGHEST,
    )
    small_local = jnp.concatenate(
        [
            grad_freq.reshape(-1),
            jnp.sum(grad_first, axis=0),
            jnp.sum(grad_zero, axis=0),
            grad_gain_one,
            grad_gain_two,
            grad_head_bias,
            grad_out_bias,
            local_sums.reshape(-1),
        ]
    )
    rank = lax.axis_index("wide") * lax.axis_size("narrow") + lax.axis_index("narrow")
    mine = rank * slot_count + jnp.arange(slot_count, dtype=jnp.int32)
    filled = jnp.any(owner[:, None] == mine[None, :], axis=0)
    owned, square_total, small_total = scatter_sum(slots, filled, small_local)
    small_grad = small_total[: small_master.shape[0]]
    sums = small_total[small_master.shape[0] :].reshape(2, NCLASS)
    grad_norm = jnp.sqrt(square_total + jnp.sum(small_grad * small_grad))
    scale = jnp.minimum(1.0, CLIP / grad_norm)
    loss = jnp.sum((sums[0] + sums[1] / NQ) * class_weight)
    new_master, new_m1, new_m2 = adamw(master, moment1, moment2, owned * scale, step)
    small_new, small_new_m1, small_new_m2 = adamw(
        small_master, small_m1, small_m2, small_grad * scale, step
    )
    return (
        loss,
        grad_norm,
        new_master,
        new_m1,
        new_m2,
        new_master.astype(jnp.bfloat16),
        small_new,
        small_new_m1,
        small_new_m2,
    )


def solution(mesh):
    return jax.shard_map(
        on_device,
        mesh=mesh,
        in_specs=(
            P(("wide", "narrow"), None),
            P(("wide", "narrow"), None),
            P(("wide", "narrow")),
            P(),
            P(),
            P(("wide", "narrow"), None, None),
            P(("wide", "narrow"), None, None),
            P(("wide", "narrow"), None, None),
            P(),
            P(),
            P(),
        ),
        out_specs=(
            P(),
            P(),
            P(("wide", "narrow"), None, None),
            P(("wide", "narrow"), None, None),
            P(("wide", "narrow"), None, None),
            P(("wide", "narrow"), None, None),
            P(),
            P(),
            P(),
        ),
        check_vma=False,
    )
```

```python
import functools

import jax
import jax.numpy as jnp
from jax import lax
from jax.experimental import pallas as pl
from jax.experimental.pallas import tpu as pltpu
from jax.sharding import PartitionSpec as P

D = 1280
HEADS = 16
HDIM = 80
FF = 5120
PATCH = 32
HORIZON = 128
NQ = 9
NPATCH = 16
NCLASS = 3
BR = 64
TOTAL_SLOTS = 512
CTX = 512
OUTW = 1280
ROWS = 20608
NBLK = 322


CLIP = 0.01
RATE = 0.03
DECAY = 0.1
BETA = 0.5
EPSILON = 1e-08


def matmul(left, right):
    return jnp.dot(left, right, preferred_element_type=jnp.float32)


def tmatmul(left, right):
    return lax.dot_general(
        left, right, (((0,), (0,)), ((), ())), preferred_element_type=jnp.float32
    )


def backmul(left, right):
    return lax.dot_general(
        left, right, (((1,), (1,)), ((), ())), preferred_element_type=jnp.float32
    )


def silu(value):
    return value / (1.0 + jnp.exp(-value))


def silu_slope(value):
    sigmoid = 1.0 / (1.0 + jnp.exp(-value))
    return sigmoid * (1.0 + value * (1.0 - sigmoid))


def rms_norm(hidden, gain):
    return hidden * lax.rsqrt(jnp.mean(hidden * hidden, axis=-1, keepdims=True) + 1e-06) * gain


def tables():
    half = HDIM // 2
    inverse = jnp.power(10000.0, -2.0 * jnp.arange(half, dtype=jnp.float32) / HDIM)
    angle = jnp.arange(NPATCH, dtype=jnp.float32)[:, None] * inverse[None, :]
    return (jnp.cos(angle)[None, :, None, :], jnp.sin(angle)[None, :, None, :])


SPAN = 2 * 128
ROWS_TOGETHER = 256


def turned(value, cosine, sine):
    half = HDIM // 2
    lane = lax.rem(lax.broadcasted_iota(jnp.int32, value.shape, 1), HDIM)
    other = jnp.where(lane < half, pltpu.roll(value, D - half, 1), pltpu.roll(value, half, 1))
    shape = (value.shape[0] // NPATCH, NPATCH, D)
    return (
        value.reshape(shape) * cosine[None] + other.reshape(shape) * sine[None]
    ).reshape(value.shape)


def attended(queries, keys):
    scores = backmul(queries, keys)
    row = lax.broadcasted_iota(jnp.int32, scores.shape, 0)
    column = lax.broadcasted_iota(jnp.int32, scores.shape, 1)
    seen = jnp.logical_and(column <= row, column >= row - lax.rem(row, NPATCH))
    scores = jnp.where(seen, scores, -1e30)
    expo = jnp.exp(scores - jnp.max(scores, axis=-1, keepdims=True))
    return expo * (1.0 / jnp.sum(expo, axis=-1, keepdims=True))


def parts_of(ref):
    step = min(ROWS_TOGETHER, ref.shape[0])
    return [slice(at, at + step) for at in range(0, ref.shape[0], step)]


def head_lanes(h):
    start = jnp.minimum(lax.div(h * HDIM, LANES) * LANES, D - SPAN)
    lane = start + lax.broadcasted_iota(jnp.int32, (1, SPAN), 1)
    inside = jnp.logical_and(lane >= h * HDIM, lane < (h + 1) * HDIM)
    return (
        pl.ds(pl.multiple_of(start, LANES), SPAN),
        jnp.where(inside, 1.0, 0.0).astype(jnp.bfloat16),
    )


def attend_kernel(qkv_ref, cos_ref, sin_ref, query_ref, key_ref, value_ref, mixed_ref, total_ref):
    cosine, sine = cos_ref[...], sin_ref[...]
    query_ref[...] = (turned(qkv_ref[:, 0:D], cosine, sine) * HDIM ** (-0.5)).astype(jnp.bfloat16)
    key_ref[...] = turned(qkv_ref[:, D : 2 * D], cosine, sine).astype(jnp.bfloat16)
    value_ref[...] = qkv_ref[:, 2 * D : 3 * D].astype(jnp.bfloat16)
    total_ref[...] = jnp.zeros_like(total_ref)

    def head(h, carry):
        span, lanes = head_lanes(h)
        for rows in parts_of(query_ref):
            attend = attended(query_ref[rows, span] * lanes, key_ref[rows, span])
            total_ref[rows, span] += matmul(
                attend.astype(jnp.bfloat16), value_ref[rows, span] * lanes
            )
        return carry

    lax.fori_loop(0, HEADS, head, 0, unroll=8)
    mixed_ref[...] = total_ref[...].astype(jnp.bfloat16)


def attend_back_kernel(
    query_ref, key_ref, value_ref, grad_ref, cos_ref, sin_ref, out_ref, dq_ref, dk_ref, dv_ref
):
    for ref in (dq_ref, dk_ref, dv_ref):
        ref[...] = jnp.zeros_like(ref)

    def head(h, carry):
        span, lanes = head_lanes(h)
        for rows in parts_of(query_ref):
            queries, keys = query_ref[rows, span] * lanes, key_ref[rows, span] * lanes
            grad = grad_ref[rows, span] * lanes
            attend = attended(queries, keys)
            grad_attend = backmul(grad, value_ref[rows, span])
            grad_scores = (
                attend * (grad_attend - jnp.sum(grad_attend * attend, axis=-1, keepdims=True))
            ).astype(jnp.bfloat16)
            dq_ref[rows, span] += matmul(grad_scores, keys)
            dk_ref[rows, span] += tmatmul(grad_scores, queries)
            dv_ref[rows, span] += tmatmul(attend.astype(jnp.bfloat16), grad)
        return carry

    lax.fori_loop(0, HEADS, head, 0, unroll=8)
    cosine, sine = cos_ref[...], sin_ref[...]
    out_ref[:, 0:D] = (turned(dq_ref[...], cosine, -sine) * HDIM ** (-0.5)).astype(jnp.bfloat16)
    out_ref[:, D : 2 * D] = turned(dk_ref[...], cosine, -sine).astype(jnp.bfloat16)
    out_ref[:, 2 * D : 3 * D] = dv_ref[...].astype(jnp.bfloat16)


def flat_tables():
    cosine, sine = (table[0, :, 0, :] for table in tables())
    return (
        jnp.tile(jnp.concatenate([cosine, cosine], axis=1), (1, HEADS)),
        jnp.tile(jnp.concatenate([-sine, sine], axis=1), (1, HEADS)),
    )


def attend_call(kernel, operands, widths, scratch, name):
    tokens = operands[0].shape[0]
    return pl.pallas_call(
        kernel,
        out_shape=tuple(jax.ShapeDtypeStruct((tokens, width), jnp.bfloat16) for width in widths),
        scratch_shapes=[pltpu.VMEM((tokens, width), jnp.float32) for width in scratch],
        compiler_params=pltpu.CompilerParams(vmem_limit_bytes=VMEM_LIMIT),
        name=name,
    )(*operands)


MATS = (
    (2 * PATCH, 2, 2),
    (D, 1, 10),
    (D, 3, 6),
    (D, 1, 10),
    (D, FF // D, 8),
    (FF, 1, 8),
    (D, (D + OUTW) // D, 8),
    (D, 1, 10),
)
BASES = tuple(sum(r * g for r, g, _ in MATS[:i]) // BR for i in range(len(MATS)))
LANES = 128
VMEM_LIMIT = 56 * 1024 * 1024
SCATTER_VMEM = 61 * 1024 * 1024


RING = 48


def steps_of(which):
    total, groups, count = MATS[which]
    return total * groups // (count * BR)


def stages(kind):
    return [pltpu.VMEM((2,) + kind(*MATS[which]), jnp.bfloat16) for which in range(len(MATS))]


def unpack_kernel(owner_ref, gathered_ref, *refs):
    outs, held = refs[:8], refs[8:16]
    ring, wide_ref, load_sem, store_sem = refs[16:]

    def load(b):
        at = lax.rem(b, RING)
        return pltpu.make_async_copy(
            gathered_ref.at[owner_ref[b]], ring.at[at], load_sem.at[at]
        )

    def first_load(b, carry):
        load(b).start()
        return carry

    lax.fori_loop(0, RING, first_load, 0)

    def store(which, i):
        total, groups, count = MATS[which]
        rows = count * BR // groups
        at = lax.rem(i, 2)
        return pltpu.make_async_copy(
            held[which].at[at],
            outs[which].at[pl.ds(pl.multiple_of(i * rows, rows), rows)],
            store_sem.at[which, at],
        )

    for which, (total, groups, count) in enumerate(MATS):
        rows = count * BR // groups

        def step(i, carry, which=which, groups=groups, count=count, rows=rows):
            first = BASES[which] + i * count
            at = lax.rem(i, 2)

            @pl.when(i >= 2)
            def _():
                store(which, i - 2).wait()

            for b in range(count):
                load(first + b).wait()
            for b in range(count):
                block = ring.at[lax.rem(first + b, RING)]
                span = slice(b * BR, (b + 1) * BR)
                if groups == 1:
                    held[which][at, span, :] = block[...]
                    continue
                for c in range(D // LANES):
                    wide_ref[c, span, :] = block[:, c * LANES : (c + 1) * LANES].astype(
                        jnp.float32
                    )
            if groups > 1:
                for j in range(groups):
                    for c in range(D // LANES):
                        left = j * D + c * LANES
                        held[which][at, :, left : left + LANES] = wide_ref[
                            c, pl.ds(j, rows, stride=groups), :
                        ].astype(jnp.bfloat16)
            store(which, i).start()
            for b in range(count):

                @pl.when(first + b + RING < NBLK)
                def _(b=b):
                    load(first + b + RING).start()

            return carry

        lax.fori_loop(0, steps_of(which), step, 0)

    for which in range(len(MATS)):
        for i in range(max(steps_of(which) - 2, 0), steps_of(which)):
            store(which, i).wait()


def unpack(gathered, owner):
    dma = pltpu.SemaphoreType.DMA
    return pl.pallas_call(
        unpack_kernel,
        out_shape=tuple(
            jax.ShapeDtypeStruct((total, groups * D), jnp.bfloat16) for total, groups, _ in MATS
        ),
        in_specs=[
            pl.BlockSpec(memory_space=pltpu.SMEM),
            pl.BlockSpec(memory_space=pl.ANY),
        ],
        out_specs=tuple(pl.BlockSpec(memory_space=pl.ANY) for _ in MATS),
        scratch_shapes=stages(lambda total, groups, count: (count * BR // groups, groups * D))
        + [
            pltpu.VMEM((RING, BR, D), jnp.bfloat16),
            pltpu.VMEM((D // LANES, 8 * BR, LANES), jnp.float32),
            dma((RING,)),
            dma((len(MATS), 2)),
        ],
        compiler_params=pltpu.CompilerParams(vmem_limit_bytes=VMEM_LIMIT),
        cost_estimate=pl.CostEstimate(
            flops=0, bytes_accessed=4 * ROWS * D, transcendentals=0
        ),
        name="unpack",
    )(owner, gathered)


def grad_kernel(owner_ref, *refs):
    lefts, rights, out_ref = refs[:8], refs[8:16], refs[16]
    left_in, right_in, held = refs[17:25], refs[25:33], refs[33:41]
    wide_ref, load_sem, store_sem = refs[41:]

    def loads(which):
        return (
            pltpu.make_async_copy(lefts[which], left_in[which], load_sem.at[which, 0]),
            pltpu.make_async_copy(rights[which], right_in[which], load_sem.at[which, 1]),
        )

    def store(which, i, b):
        at = lax.rem(i, 2)
        return pltpu.make_async_copy(
            held[which].at[at, pl.ds(b * BR, BR), :],
            out_ref.at[owner_ref[BASES[which] + i * MATS[which][2] + b]],
            store_sem.at[which, at, b],
        )

    order = tuple(reversed(range(len(MATS))))
    for which in order:
        for copy in loads(which):
            copy.start()
    for which in order:
        total, groups, count = MATS[which]
        rows = count * BR // groups
        for copy in loads(which):
            copy.wait()

        def step(i, carry, which=which, groups=groups, count=count, rows=rows):
            at = lax.rem(i, 2)

            @pl.when(i >= 2)
            def _():
                for b in range(count):
                    store(which, i - 2, b).wait()

            if steps_of(which) == 1:
                left = left_in[which][...]
            else:
                left = left_in[which][:, pl.ds(pl.multiple_of(i * rows, rows), rows)]
            for j in range(groups):
                part = tmatmul(left, right_in[which][:, j * D : (j + 1) * D])
                if groups == 1:
                    held[which][at] = part.astype(jnp.bfloat16)
                    continue
                for c in range(D // LANES):
                    wide_ref[c, pl.ds(j, rows, stride=groups), :] = part[
                        :, c * LANES : (c + 1) * LANES
                    ]
            if groups > 1:
                for c in range(D // LANES):
                    held[which][at, :, c * LANES : (c + 1) * LANES] = wide_ref[
                        c, 0 : count * BR, :
                    ].astype(jnp.bfloat16)
            for b in range(count):
                store(which, i, b).start()
            return carry

        lax.fori_loop(0, steps_of(which), step, 0)
    for which in order:
        for i in range(max(steps_of(which) - 2, 0), steps_of(which)):
            for b in range(MATS[which][2]):
                store(which, i, b).wait()


def grad_blocks(pairs, owner):
    lefts, rights = zip(*pairs)
    dma = pltpu.SemaphoreType.DMA
    tokens = lefts[0].shape[0]
    return pl.pallas_call(
        grad_kernel,
        out_shape=jax.ShapeDtypeStruct((TOTAL_SLOTS, BR, D), jnp.bfloat16),
        in_specs=[pl.BlockSpec(memory_space=pltpu.SMEM)]
        + [pl.BlockSpec(memory_space=pl.ANY)] * (2 * len(MATS)),
        out_specs=pl.BlockSpec(memory_space=pl.ANY),
        scratch_shapes=[pltpu.VMEM(left.shape, jnp.bfloat16) for left in lefts]
        + [pltpu.VMEM(right.shape, jnp.bfloat16) for right in rights]
        + stages(lambda total, groups, count: (count * BR, D))
        + [
            pltpu.VMEM((D // LANES, 8 * BR, LANES), jnp.float32),
            dma((len(MATS), 2)),
            dma((len(MATS), 2, 10)),
        ],
        compiler_params=pltpu.CompilerParams(vmem_limit_bytes=VMEM_LIMIT),
        cost_estimate=pl.CostEstimate(
            flops=2 * tokens * ROWS * D, bytes_accessed=2 * ROWS * D, transcendentals=0
        ),
        name="grad_blocks",
    )(owner, *lefts, *rights)


CHUNKS = 16
LATE = 4
EARLY = CHUNKS - LATE
COMBOS = 4 * LATE
SUM_LATE = 3
SUM_EARLY = CHUNKS - SUM_LATE
SUM_COMBOS = 4 * SUM_LATE
STEPS = SUM_EARLY + 7
MESH = pl.DeviceIdType.MESH


def total_of(*blocks):
    result = blocks[0].astype(jnp.float32)
    for block in blocks[1:]:
        result = result + block.astype(jnp.float32)
    return result


def scatter_kernel(
    slots_ref,
    small_ref,
    filled_ref,
    out_ref,
    small_out,
    square_out,
    small_in,
    own,
    pair_in,
    pair_sum,
    first_in,
    second_in,
    second_out,
    column,
    up_in,
    down_in,
    up_out,
    down_out,
    result,
    late_own,
    late_pair_in,
    late_sum,
    late_up_in,
    late_down_in,
    late_up_out,
    late_down_out,
    late_column,
    late_first_in,
    late_second_in,
    late_second_out,
    late_result,
    own_sem,
    pair_send,
    pair_recv,
    first_send,
    first_recv,
    second_send,
    second_recv,
    up_send,
    up_recv,
    down_send,
    down_recv,
    result_sem,
    late_own_sem,
    late_pair_send,
    late_pair_recv,
    late_up_send,
    late_up_recv,
    late_down_send,
    late_down_recv,
    late_first_send,
    late_first_recv,
    late_second_send,
    late_second_recv,
    late_result_sem,
    share_send,
    share_recv,
    spread_send,
    spread_recv,
    square_send,
    square_recv,
):
    wide, z = lax.axis_index("wide"), lax.axis_index("narrow")
    core, here = lax.rem(wide, 2), lax.div(wide, 2)
    x, y = lax.rem(here, 2), lax.div(here, 2)
    far = 3 - here

    def device(place, level):
        return (place * 2 + core, level)

    partner = (here * 2 + 1 - core, z)

    def near(k, which):
        along_y = lax.rem(k + which, 2)
        return (y + along_y - 2 * y * along_y) * 2 + (x + (1 - along_y) - 2 * x * (1 - along_y))

    places = 8 * 4
    me = wide * 4 + z
    barrier = pltpu.get_barrier_semaphore()

    def each(action):
        def body(i, carry):
            other = lax.rem(me + i, places)
            action(i, other, (lax.div(other, 4), lax.rem(other, 4)))
            return carry

        lax.fori_loop(1, places, body, 0)

    def greet(i, other, to):
        pl.semaphore_signal(barrier, inc=1, device_id=to, device_id_type=MESH)

    def share(i, other, to):
        return pltpu.make_async_remote_copy(
            src_ref=small_ref.at[other],
            dst_ref=small_in.at[me],
            send_sem=share_send.at[i],
            recv_sem=share_recv.at[i],
            device_id=to,
            device_id_type=MESH,
        )

    def tell(ref, send, recv):
        def make(i, other, to):
            return pltpu.make_async_remote_copy(
                src_ref=ref.at[me],
                dst_ref=ref.at[me],
                send_sem=send.at[i],
                recv_sem=recv.at[i],
                device_id=to,
                device_id_type=MESH,
            )

        return make

    spread = tell(small_out, spread_send, spread_recv)
    square = tell(square_out, square_send, square_recv)
    each(greet)
    small_in[me] = small_ref[me]
    square_out[me] = jnp.zeros((8, LANES), jnp.float32)
    pl.semaphore_wait(barrier, places - 1)

    def own_copy(k):
        at = lax.rem(k, 2)
        return pltpu.make_async_copy(slots_ref.at[:, core, :, k], own.at[at], own_sem.at[at])

    def pair_copy(k):
        at = lax.rem(k, 2)
        return pltpu.make_async_remote_copy(
            src_ref=slots_ref.at[:, 1 - core, :, k],
            dst_ref=pair_in.at[at],
            send_sem=pair_send.at[at],
            recv_sem=pair_recv.at[at],
            device_id=partner,
            device_id_type=MESH,
        )

    def first_copy(k, part):
        place = near(k, 0)
        return pltpu.make_async_remote_copy(
            src_ref=pair_sum.at[lax.rem(k, 3), far if part == 0 else place],
            dst_ref=first_in.at[lax.rem(k, 5), part],
            send_sem=first_send.at[lax.rem(k, 3), part],
            recv_sem=first_recv.at[lax.rem(k, 5), part],
            device_id=device(place, z),
            device_id_type=MESH,
        )

    def second_copy(k):
        return pltpu.make_async_remote_copy(
            src_ref=second_out.at[lax.rem(k, 2)],
            dst_ref=second_in.at[lax.rem(k, 4)],
            send_sem=second_send.at[lax.rem(k, 2)],
            recv_sem=second_recv.at[lax.rem(k, 4)],
            device_id=device(near(k, 1), z),
            device_id_type=MESH,
        )

    def line_copy(source, target, send, recv, way):
        base = 1 if way > 0 else 0

        def make(k, level):
            return pltpu.make_async_remote_copy(
                src_ref=source.at[lax.rem(k, 2), level - base],
                dst_ref=target.at[lax.rem(k, 6), level - base],
                send_sem=send.at[lax.rem(k, 2), level - base],
                recv_sem=recv.at[lax.rem(k, 6), level - base],
                device_id=device(here, z + way),
                device_id_type=MESH,
            )

        return make

    def late_own_copy(c):
        at = lax.rem(c, 2)
        return pltpu.make_async_copy(
            slots_ref.at[lax.rem(c, 4), core, :, SUM_EARLY + lax.div(c, 4)],
            late_own.at[at],
            late_own_sem.at[at],
        )

    def late_pair_copy(c):
        at = lax.rem(c, 2)
        return pltpu.make_async_remote_copy(
            src_ref=slots_ref.at[lax.rem(c, 4), 1 - core, :, SUM_EARLY + lax.div(c, 4)],
            dst_ref=late_pair_in.at[at],
            send_sem=late_pair_send.at[at],
            recv_sem=late_pair_recv.at[at],
            device_id=partner,
            device_id_type=MESH,
        )

    def late_first_copy(slot, part):
        place = near(slot, 0)
        return pltpu.make_async_remote_copy(
            src_ref=late_column.at[slot, far if part == 0 else place],
            dst_ref=late_first_in.at[slot, part],
            send_sem=late_first_send.at[slot, part],
            recv_sem=late_first_recv.at[slot, part],
            device_id=device(place, z),
            device_id_type=MESH,
        )

    def late_second_copy(slot):
        return pltpu.make_async_remote_copy(
            src_ref=late_second_out.at[slot],
            dst_ref=late_second_in.at[slot],
            send_sem=late_second_send.at[slot],
            recv_sem=late_second_recv.at[slot],
            device_id=device(near(slot, 1), z),
            device_id_type=MESH,
        )

    def late_result_copy(slot):
        return pltpu.make_async_copy(late_result, out_ref.at[SUM_EARLY + slot], late_result_sem)

    def result_copy(k):
        at = lax.rem(k, 2)
        return pltpu.make_async_copy(result.at[at], out_ref.at[k], result_sem.at[at])

    def valid(k):
        return jnp.logical_and(k >= 0, k < SUM_EARLY)

    def valid_late(c):
        return jnp.logical_and(c >= 0, c < SUM_COMBOS)

    def keep(ref, k):
        kept = jnp.where(filled_ref[k, 0:1, 0:1] > 0.0, ref[...], 0.0)
        ref[...] = kept
        squares = square_out[me]
        for i in range(BR // 8):
            for j in range(D // LANES):
                part = kept[i * 8 : (i + 1) * 8, j * LANES : (j + 1) * LANES]
                squares = squares + part * part
        square_out[me] = squares

    def flows(lags, known, sums, ring, ins, outs, copies):
        for base, lag, behind, copy, arrived, leaving in zip(
            (1, 0), lags, (z > 0, z < 3), copies, ins, outs
        ):
            k = lag
            for n in range(base, base + 3):
                ahead = n > z if base else n < z

                @pl.when(jnp.logical_and(known(k - 2), ahead))
                def _(n=n, k=k, copy=copy):
                    copy(k - 2, n).wait_send()

                @pl.when(
                    jnp.logical_and(
                        jnp.logical_and(known(k), behind), jnp.logical_or(ahead, n == z)
                    )
                )
                def _(n=n, k=k, copy=copy):
                    copy(k, n).wait_recv()

                moving = jnp.logical_and(known(k), ahead)

                @pl.when(jnp.logical_and(moving, behind))
                def _(n=n, k=k, base=base, arrived=arrived, leaving=leaving):
                    leaving[lax.rem(k, 2), n - base] = total_of(
                        sums[lax.rem(k, ring), n], arrived[lax.rem(k, 6), n - base]
                    ).astype(jnp.bfloat16)

                @pl.when(jnp.logical_and(moving, jnp.logical_not(behind)))
                def _(n=n, k=k, base=base, leaving=leaving):
                    leaving[lax.rem(k, 2), n - base] = sums[lax.rem(k, ring), n]

                @pl.when(moving)
                def _(n=n, k=k, copy=copy):
                    copy(k, n).start()

    copies = (
        line_copy(up_out, up_in, up_send, up_recv, 1),
        line_copy(down_out, down_in, down_send, down_recv, -1),
    )
    late_copies = (
        line_copy(late_up_out, late_up_in, late_up_send, late_up_recv, 1),
        line_copy(late_down_out, late_down_in, late_down_send, late_down_recv, -1),
    )

    own_copy(0).start()
    pair_copy(0).start()
    late_own_copy(0).start()
    late_pair_copy(0).start()
    each(lambda *at: share(*at).start())

    def step(t, carry):
        @pl.when(valid(t - 3))
        def _():
            first_copy(t - 3, 0).wait_send()
            first_copy(t - 3, 1).wait_send()

        @pl.when(valid(t))
        def _():
            own_copy(t).wait()
            pair_copy(t).wait_recv()
            at, ring = lax.rem(t, 2), lax.rem(t, 3)

            def add(i, inner):
                p, n = lax.div(i, 4), lax.rem(i, 4)
                pair_sum[ring, p, n] = total_of(own[at, p, n], pair_in[at, p, n]).astype(
                    jnp.bfloat16
                )
                return inner

            lax.fori_loop(0, 16, add, 0)
            first_copy(t, 0).start()
            first_copy(t, 1).start()

        @pl.when(valid(t - 1))
        def _():
            pair_copy(t - 1).wait_send()

        @pl.when(t + 1 < SUM_EARLY)
        def _():
            own_copy(t + 1).start()
            pair_copy(t + 1).start()

        @pl.when(valid_late(t))
        def _():
            late_own_copy(t).wait()
            late_pair_copy(t).wait_recv()

            def add(n, inner):
                late_sum[lax.rem(t, 4), n] = total_of(
                    late_own[lax.rem(t, 2), n], late_pair_in[lax.rem(t, 2), n]
                ).astype(jnp.bfloat16)
                return inner

            lax.fori_loop(0, 4, add, 0)

        @pl.when(valid_late(t - 1))
        def _():
            late_pair_copy(t - 1).wait_send()

        @pl.when(t + 1 < SUM_COMBOS)
        def _():
            late_own_copy(t + 1).start()
            late_pair_copy(t + 1).start()

        @pl.when(valid(t - 3))
        def _():
            second_copy(t - 3).wait_send()

        @pl.when(valid(t - 1))
        def _():
            k = t - 1
            first_copy(k, 0).wait_recv()
            place = near(k, 1)

            def add(n, inner):
                second_out[lax.rem(k, 2), n] = total_of(
                    pair_sum[lax.rem(k, 3), place, n], first_in[lax.rem(k, 5), 0, n]
                ).astype(jnp.bfloat16)
                return inner

            lax.fori_loop(0, 4, add, 0)
            second_copy(k).start()

        @pl.when(valid(t - 2))
        def _():
            k = t - 2
            first_copy(k, 1).wait_recv()
            second_copy(k).wait_recv()

            def add(n, inner):
                column[lax.rem(k, 4), n] = total_of(
                    pair_sum[lax.rem(k, 3), here, n],
                    first_in[lax.rem(k, 5), 1, n],
                    second_in[lax.rem(k, 4), n],
                ).astype(jnp.bfloat16)
                return inner

            lax.fori_loop(0, 4, add, 0)

        flows(
            (t - 2 - z, t - 5 + z), valid, column, 4, (up_in, down_in), (up_out, down_out), copies
        )
        flows(
            (t - z, t - 3 + z),
            valid_late,
            late_sum,
            4,
            (late_up_in, late_down_in),
            (late_up_out, late_down_out),
            late_copies,
        )
        c = t - 3

        @pl.when(valid_late(c))
        def _():
            slot, p = lax.div(c, 4), lax.rem(c, 4)
            mine = late_sum.at[lax.rem(c, 4), z]
            below = late_up_in.at[lax.rem(c, 6), jnp.maximum(z - 1, 0)]
            above = late_down_in.at[lax.rem(c, 6), jnp.minimum(z, 2)]

            @pl.when(z == 0)
            def _():
                late_column[slot, p] = total_of(mine[...], above[...]).astype(jnp.bfloat16)

            @pl.when(z == 3)
            def _():
                late_column[slot, p] = total_of(mine[...], below[...]).astype(jnp.bfloat16)

            @pl.when(jnp.logical_and(z > 0, z < 3))
            def _():
                late_column[slot, p] = total_of(mine[...], below[...], above[...]).astype(
                    jnp.bfloat16
                )

        for slot in range(SUM_LATE):
            place = near(slot, 1)

            @pl.when(t == 4 * slot + 6)
            def _(slot=slot):
                late_first_copy(slot, 0).start()
                late_first_copy(slot, 1).start()

            @pl.when(t == 4 * slot + 7)
            def _(slot=slot, place=place):
                late_first_copy(slot, 0).wait_recv()
                late_second_out[slot] = total_of(
                    late_column[slot, place], late_first_in[slot, 0]
                ).astype(jnp.bfloat16)
                late_second_copy(slot).start()

            @pl.when(t == 4 * slot + 8)
            def _(slot=slot):
                late_first_copy(slot, 1).wait_recv()
                late_second_copy(slot).wait_recv()
                if slot:
                    late_result_copy(slot - 1).wait()
                late_result[...] = total_of(
                    late_column[slot, here], late_first_in[slot, 1], late_second_in[slot]
                )
                keep(late_result, SUM_EARLY + slot)
                late_result_copy(slot).start()

        k = t - 5

        @pl.when(valid(k - 2))
        def _():
            result_copy(k - 2).wait()

        @pl.when(valid(k))
        def _():
            result[lax.rem(k, 2)] = column[lax.rem(k, 4), z].astype(jnp.float32)

            @pl.when(z > 0)
            def _():
                result[lax.rem(k, 2)] += up_in[lax.rem(k, 6), z - 1].astype(jnp.float32)

            @pl.when(z < 3)
            def _():
                result[lax.rem(k, 2)] += down_in[lax.rem(k, 6), z].astype(jnp.float32)

            keep(result.at[lax.rem(k, 2)], k)
            result_copy(k).start()

        @pl.when(t == CHUNKS // 2)
        def _():
            each(lambda *at: share(*at).wait())
            small = small_in[0]
            for i in range(1, places):
                small = small + small_in[i]
            small_out[me] = small
            each(lambda *at: spread(*at).start())

        return carry

    lax.fori_loop(0, STEPS, step, 0)
    each(lambda *at: square(*at).start())
    late_result_copy(SUM_LATE - 1).wait()
    for slot in range(SUM_LATE):
        late_first_copy(slot, 0).wait_send()
        late_first_copy(slot, 1).wait_send()
        late_second_copy(slot).wait_send()
    each(lambda *at: spread(*at).wait())
    each(lambda *at: square(*at).wait())


def scatter_sum(slots, filled, small):
    slot_count = filled.shape[0]
    wide, narrow = lax.axis_size("wide"), lax.axis_size("narrow")
    if (wide, narrow, slot_count) != (8, 4, CHUNKS):
        part = lax.psum_scatter(slots, "wide", scatter_dimension=0, tiled=True)
        owned = lax.psum_scatter(
            part.astype(jnp.float32), "narrow", scatter_dimension=0, tiled=True
        )
        owned = jnp.where(filled[:, None, None], owned, 0.0)
        square = lax.psum(jnp.sum(owned * owned), ("wide", "narrow"))
        return owned, square, lax.psum(small, ("wide", "narrow"))
    tiles = (wide * narrow, 8, LANES)
    room = wide * narrow * 8 * LANES - small.shape[0]
    assert room >= 0
    low = functools.partial(pltpu.VMEM, dtype=jnp.bfloat16)
    dma = pltpu.SemaphoreType.DMA
    block = (BR, D)
    owned, small_tiles, square_tiles = pl.pallas_call(
        scatter_kernel,
        out_shape=(
            jax.ShapeDtypeStruct((slot_count,) + block, jnp.float32),
            jax.ShapeDtypeStruct(tiles, jnp.float32),
            jax.ShapeDtypeStruct(tiles, jnp.float32),
        ),
        in_specs=[
            pl.BlockSpec(memory_space=pl.ANY),
            pl.BlockSpec(memory_space=pltpu.VMEM),
            pl.BlockSpec(memory_space=pltpu.VMEM),
        ],
        out_specs=(
            pl.BlockSpec(memory_space=pl.ANY),
            pl.BlockSpec(memory_space=pltpu.VMEM),
            pl.BlockSpec(memory_space=pltpu.VMEM),
        ),
        scratch_shapes=[
            pltpu.VMEM(tiles, jnp.float32),
            low((2, 4, 4) + block),
            low((2, 4, 4) + block),
            low((3, 4, 4) + block),
            low((5, 2, 4) + block),
            low((4, 4) + block),
            low((2, 4) + block),
            low((4, 4) + block),
            low((6, 3) + block),
            low((6, 3) + block),
            low((2, 3) + block),
            low((2, 3) + block),
            pltpu.VMEM((2,) + block, jnp.float32),
            low((2, 4) + block),
            low((2, 4) + block),
            low((4, 4) + block),
            low((6, 3) + block),
            low((6, 3) + block),
            low((2, 3) + block),
            low((2, 3) + block),
            low((SUM_LATE, 4) + block),
            low((SUM_LATE, 2) + block),
            low((SUM_LATE,) + block),
            low((SUM_LATE,) + block),
            pltpu.VMEM(block, jnp.float32),
            dma((2,)),
            dma((2,)),
            dma((2,)),
            dma((3, 2)),
            dma((5, 2)),
            dma((2,)),
            dma((4,)),
            dma((2, 3)),
            dma((6, 3)),
            dma((2, 3)),
            dma((6, 3)),
            dma((2,)),
            dma((2,)),
            dma((2,)),
            dma((2,)),
            dma((2, 3)),
            dma((6, 3)),
            dma((2, 3)),
            dma((6, 3)),
            dma((SUM_LATE, 2)),
            dma((SUM_LATE, 2)),
            dma((SUM_LATE,)),
            dma((SUM_LATE,)),
            dma,
        ]
        + [dma((wide * narrow,))] * 6,
        compiler_params=pltpu.CompilerParams(
            collective_id=1, has_side_effects=True, vmem_limit_bytes=SCATTER_VMEM
        ),
        name="scatter_sum",
    )(
        slots.reshape(4, 2, narrow, slot_count, BR, D),
        jnp.pad(small, (0, room)).reshape(tiles),
        jnp.broadcast_to(
            filled.astype(jnp.float32)[:, None, None], (slot_count, 8, LANES)
        ),
    )
    return owned, jnp.sum(square_tiles), small_tiles.reshape(-1)[: small.shape[0]]


GATHER_STEPS = EARLY + 5


def gather_kernel(
    own_ref,
    count_ref,
    all_ref,
    counts_ref,
    own_sem,
    recv,
    pair_recv,
    line_send,
    plane_send,
    turn_send,
    late_send,
    pair_send,
    late_pair_send,
    count_send,
    count_recv,
):
    wide, z = lax.axis_index("wide"), lax.axis_index("narrow")
    core, here = lax.rem(wide, 2), lax.div(wide, 2)
    x, y = lax.rem(here, 2), lax.div(here, 2)
    side, front, far = y * 2 + 1 - x, (1 - y) * 2 + x, 3 - here
    places = 8 * 4
    me = wide * 4 + z

    barrier = pltpu.get_barrier_semaphore()

    def greet(i, carry):
        other = lax.rem(me + i, places)
        pl.semaphore_signal(
            barrier,
            inc=1,
            device_id=(lax.div(other, 4), lax.rem(other, 4)),
            device_id_type=MESH,
        )
        return carry

    lax.fori_loop(1, places, greet, 0)
    fill = pltpu.make_async_copy(own_ref, all_ref.at[here, core, z], own_sem)
    fill.start()
    counts_ref[me] = count_ref[...]
    pl.semaphore_wait(barrier, places - 1)
    fill.wait()

    def count_copy(i):
        other = lax.rem(me + i, places)
        return pltpu.make_async_remote_copy(
            src_ref=count_ref,
            dst_ref=counts_ref.at[me],
            send_sem=count_send.at[i],
            recv_sem=count_recv.at[i],
            device_id=(lax.div(other, 4), lax.rem(other, 4)),
            device_id_type=MESH,
        )

    def count_start(i, carry):
        count_copy(i).start()
        return carry

    lax.fori_loop(1, places, count_start, 0)

    def piece(p, n, k, send, to):
        return pltpu.make_async_remote_copy(
            src_ref=all_ref.at[p, core, n, k],
            dst_ref=all_ref.at[p, core, n, k],
            send_sem=send,
            recv_sem=recv.at[p, n, k],
            device_id=to,
            device_id_type=MESH,
        )

    up, down = (wide, z + 1), (wide, z - 1)
    to_side, to_front = (side * 2 + core, z), (front * 2 + core, z)

    def line(n, k, step):
        return piece(here, n, k, line_send.at[step, n, k], (up, down)[step])

    def plane(n, k, which):
        return piece(here, n, k, plane_send.at[which, n, k], (to_side, to_front)[which])

    def turn(n, k, which):
        return piece(
            (side, front)[which], n, k, turn_send.at[n, k], (to_front, to_side)[which]
        )

    def late(c, n, step):
        p, k = lax.rem(here + c, 4), EARLY + lax.div(c, 4)
        return piece(p, n, k, late_send.at[step, c, n], (up, down)[step])

    def pair(p, k, send):
        return pltpu.make_async_remote_copy(
            src_ref=all_ref.at[p, core, :, k],
            dst_ref=all_ref.at[p, core, :, k],
            send_sem=send,
            recv_sem=pair_recv,
            device_id=(here * 2 + 1 - core, z),
            device_id_type=MESH,
        )

    def early_pair(p, k):
        return pair(p, k, pair_send.at[p, k])

    def late_pair(c):
        p, k = lax.rem(here + c, 4), EARLY + lax.div(c, 4)
        return pair(p, k, late_pair_send.at[c])

    def both_lines(make, n, j, start):
        @pl.when(jnp.logical_and(start, z < 3))
        def _():
            if j <= 0:
                make(n, 0)

        @pl.when(jnp.logical_and(start, z > 0))
        def _():
            if j >= 0:
                make(n, 1)

    def early(k):
        return jnp.logical_and(k >= 0, k < EARLY)

    def swap(n, k, go):
        even = lax.rem(n + k, 2) == 0

        @pl.when(jnp.logical_and(go, even))
        def _():
            turn(n, k, 0).start()

        @pl.when(jnp.logical_and(go, jnp.logical_not(even)))
        def _():
            turn(n, k, 1).start()

    for k in range(EARLY, CHUNKS):
        plane(z, k, 0).start()
        plane(z, k, 1).start()

    def step(t, carry):
        @pl.when(early(t))
        def _():
            plane(z, t, 0).start()
            plane(z, t, 1).start()

        both_lines(lambda n, way: line(n, t, way).start(), z, 0, early(t))

        for j in (-1, 1, -2, 2, -3, 3):
            n, k = z + j, t - abs(j)
            there = jnp.logical_and(early(k), jnp.logical_and(n >= 0, n < 4))

            @pl.when(there)
            def _(n=n, k=k, j=j):
                piece(here, n, k, plane_send.at[0, n, k], to_side).wait_recv()

            both_lines(lambda n, way, k=k: line(n, k, way).start(), n, j, there)

            @pl.when(there)
            def _(n=n, k=k):
                plane(n, k, 0).start()
                plane(n, k, 1).start()

        @pl.when(t == 1)
        def _():
            for k in range(EARLY, CHUNKS):
                plane_wait(side, z, k)
                plane_wait(front, z, k)
                swap(z, k, True)

        @pl.when(t == 2)
        def _():
            for k in range(EARLY, CHUNKS):
                plane_wait(far, z, k)

        for j in (0, -1, 1, -2, 2, -3, 3):
            m = t - 2 - abs(j)
            n = z + j
            first = m + lax.div(m + 2, 3)
            for c, more in ((first, True), (first + 1, lax.rem(m, 3) == 0)):
                there = jnp.logical_and(
                    jnp.logical_and(m >= 0, c < COMBOS),
                    jnp.logical_and(jnp.logical_and(n >= 0, n < 4), more),
                )
                if j:

                    @pl.when(there)
                    def _(n=n, c=c):
                        plane_wait(lax.rem(here + c, 4), n, EARLY + lax.div(c, 4))

                both_lines(lambda n, way, c=c: late(c, n, way).start(), n, j, there)

        for n in range(4):
            gap = jnp.abs(z - n)
            k = t - 1 - gap

            @pl.when(early(k))
            def _(n=n, k=k):
                plane_wait(side, n, k)
                plane_wait(front, n, k)

            swap(n, k, early(k))
            k = t - 2 - gap

            @pl.when(early(k))
            def _(n=n, k=k):
                plane_wait(far, n, k)

        for lag, sent in ((3, (here,)), (4, (side, front)), (5, (far,))):
            k = t - lag

            @pl.when(early(k))
            def _(k=k, sent=sent):
                for p in sent:
                    early_pair(p, k).start()

        m = t - 5
        first = m + lax.div(m + 2, 3)
        for c, more in ((first, True), (first + 1, lax.rem(m, 3) == 0)):

            @pl.when(jnp.logical_and(jnp.logical_and(m >= 0, c < COMBOS), more))
            def _(c=c):
                late_pair(c).start()

        return carry

    def plane_wait(p, n, k):
        piece(p, n, k, plane_send.at[0, n, k], to_side).wait_recv()

    lax.fori_loop(0, GATHER_STEPS, step, 0)

    def finish(k, carry):
        for n in range(4):
            plane_used = jnp.logical_or(k < EARLY, n == z)

            @pl.when(plane_used)
            def _(n=n):
                plane(n, k, 0).wait_send()
                plane(n, k, 1).wait_send()
                turn(n, k, 0).wait_send()

            @pl.when(jnp.logical_and(k < EARLY, jnp.logical_and(n <= z, z < 3)))
            def _(n=n):
                line(n, k, 0).wait_send()

            @pl.when(jnp.logical_and(k < EARLY, jnp.logical_and(n >= z, z > 0)))
            def _(n=n):
                line(n, k, 1).wait_send()

            @pl.when(jnp.logical_and(n <= z, z < 3))
            def _(n=n):
                late(k, n, 0).wait_send()

            @pl.when(jnp.logical_and(n >= z, z > 0))
            def _(n=n):
                late(k, n, 1).wait_send()

        @pl.when(k < EARLY)
        def _():
            for p in range(4):
                early_pair(p, k).wait_send()

        late_pair(k).wait_send()
        return carry

    lax.fori_loop(0, CHUNKS, finish, 0)

    def count_wait(i, carry):
        count_copy(i).wait()
        return carry

    lax.fori_loop(1, places, count_wait, 0)
    pltpu.make_async_copy(
        all_ref.at[:, 1 - core], all_ref.at[:, 1 - core], pair_recv
    ).wait()


def gather_all(low, local_counts):
    slot_count = low.shape[0]
    wide, narrow = lax.axis_size("wide"), lax.axis_size("narrow")
    if (wide, narrow, slot_count) != (8, 4, CHUNKS):
        return (
            lax.all_gather(low, ("wide", "narrow"), axis=0, tiled=True),
            lax.psum(local_counts, ("wide", "narrow")),
        )
    dma = pltpu.SemaphoreType.DMA
    tile = jnp.zeros((8, LANES), jnp.float32).at[0, :NCLASS].set(local_counts)
    gathered, tiles = pl.pallas_call(
        gather_kernel,
        out_shape=(
            jax.ShapeDtypeStruct((4, 2, narrow, slot_count, BR, D), jnp.bfloat16),
            jax.ShapeDtypeStruct((wide * narrow, 8, LANES), jnp.float32),
        ),
        in_specs=[
            pl.BlockSpec(memory_space=pltpu.VMEM),
            pl.BlockSpec(memory_space=pltpu.VMEM),
        ],
        out_specs=(
            pl.BlockSpec(memory_space=pl.ANY),
            pl.BlockSpec(memory_space=pltpu.VMEM),
        ),
        scratch_shapes=[
            dma,
            dma((4, 4, CHUNKS)),
            dma,
            dma((2, 4, EARLY)),
            dma((2, 4, CHUNKS)),
            dma((4, CHUNKS)),
            dma((2, COMBOS, 4)),
            dma((4, EARLY)),
            dma((COMBOS,)),
            dma((wide * narrow,)),
            dma((wide * narrow,)),
        ],
        compiler_params=pltpu.CompilerParams(
            collective_id=2, has_side_effects=True, vmem_limit_bytes=VMEM_LIMIT
        ),
        name="gather_all",
    )(low, tile)
    return (
        gathered.reshape(wide * narrow * slot_count, BR, D),
        jnp.sum(tiles[:, 0, :NCLASS], axis=0),
    )


def split_small(small):
    freq = small[: NCLASS * D].reshape(NCLASS, D)
    rest = small[NCLASS * D :]
    return (
        freq,
        rest[0:D],
        rest[D : 2 * D],
        rest[2 * D : 3 * D],
        rest[3 * D : 4 * D],
        rest[4 * D : 5 * D],
        rest[5 * D : 5 * D + OUTW],
    )


def prepare(series, pad_mask):
    valid = (1 - pad_mask).astype(jnp.float32)
    count_series = series.shape[0]
    context = (series[:, :CTX] * valid[:, :CTX]).reshape(count_series, NPATCH, PATCH)
    marks = pad_mask[:, :CTX].astype(jnp.float32).reshape(count_series, NPATCH, PATCH)
    feat = jnp.concatenate([context, marks], axis=-1)
    return (feat, horizons(series), horizons(valid))


def horizons(points):
    count_series = points.shape[0]
    pieces = points.reshape(count_series, -1, PATCH)
    return jnp.concatenate(
        [pieces[:, 1 + j : 1 + j + NPATCH] for j in range(HORIZON // PATCH)], axis=-1
    ).reshape(count_series * NPATCH, HORIZON)


def loss_parts(out, target, tmask, onehot, class_weight):
    column = lax.broadcasted_iota(jnp.int32, (HORIZON, OUTW), 1)
    row = lax.broadcasted_iota(jnp.int32, (HORIZON, OUTW), 0)
    spread = (lax.div(column, NQ + 1) == row).astype(jnp.float32)
    wanted = jnp.dot(target, spread, precision=lax.Precision.HIGHEST)
    mask = matmul(tmask.astype(jnp.bfloat16), spread.astype(jnp.bfloat16))
    kind = lax.rem(lax.broadcasted_iota(jnp.int32, (1, OUTW), 1), NQ + 1)
    level = kind.astype(jnp.float32) / (NQ + 1)
    error = out - wanted
    above, below = level * -error, (level - 1.0) * -error
    slope = jnp.where(above > below, -level, jnp.where(above < below, 1.0 - level, 0.5 - level))
    square = jnp.sum(jnp.where(kind == 0, error * error * mask, 0.0), axis=1)
    quant = jnp.sum(jnp.where(kind == 0, 0.0, jnp.maximum(above, below) * mask), axis=1)
    onehot = jnp.repeat(onehot, NPATCH, axis=0)
    weight = jnp.sum(onehot * class_weight[None, :], axis=1, keepdims=True)
    grad = weight * mask * jnp.where(kind == 0, 2.0 * error, slope / NQ)
    sums = jnp.dot(jnp.stack([square, quant]), onehot, precision=lax.Precision.HIGHEST)
    return sums, grad.astype(jnp.bfloat16)


def layer_forward(state_zero, mats, parts, cosine, sine):
    w_qkv, w_out, w_up, w_down = (mats[2], mats[3], mats[4], mats[5])
    gain_one, gain_two = (parts[3], parts[4])
    normed_one = rms_norm(state_zero, gain_one).astype(jnp.bfloat16)
    qkv = matmul(normed_one, w_qkv)
    queries, key_rot, value_all, mixed = attend_call(
        attend_kernel, (qkv, cosine, sine), (D, D, D, D), (D,), "attend"
    )
    state_one = state_zero + matmul(mixed, w_out)
    normed_two = rms_norm(state_one, gain_two).astype(jnp.bfloat16)
    up_pre = matmul(normed_two, w_up)
    activ = silu(up_pre).astype(jnp.bfloat16)
    state_two = state_one + matmul(activ, w_down)
    return (
        state_two,
        (
            normed_one,
            queries,
            key_rot,
            value_all,
            mixed,
            state_one,
            normed_two,
            up_pre,
            activ,
        ),
    )


def layer_backward(grad_two, state_zero, kept, mats, parts, cosine, sine):
    (
        normed_one,
        queries,
        key_rot,
        value_all,
        mixed,
        state_one,
        normed_two,
        up_pre,
        activ,
    ) = kept
    w_qkv, w_out, w_up, w_down = (mats[2], mats[3], mats[4], mats[5])
    gain_one, gain_two = (parts[3], parts[4])
    grad_mlp = grad_two.astype(jnp.bfloat16)
    grad_act = backmul(grad_mlp, w_down)
    grad_up_pre = (grad_act * silu_slope(up_pre)).astype(jnp.bfloat16)
    grad_normed = backmul(grad_up_pre, w_up)
    _, pull = jax.vjp(rms_norm, state_one, gain_two)
    grad_norm_in, grad_gain_two = pull(grad_normed)
    grad_one = grad_two + grad_norm_in
    grad_proj = grad_one.astype(jnp.bfloat16)
    grad_mixed = backmul(grad_proj, w_out).astype(jnp.bfloat16)
    (grad_qkv,) = attend_call(
        attend_back_kernel,
        (queries, key_rot, value_all, grad_mixed, cosine, sine),
        (3 * D,),
        (D, D, D),
        "attend_back",
    )
    grad_normed_one = backmul(grad_qkv, w_qkv)
    _, pull = jax.vjp(rms_norm, state_zero, gain_one)
    grad_zero_in, grad_gain_one = pull(grad_normed_one)
    return (
        grad_one + grad_zero_in,
        (
            (normed_one, grad_qkv),
            (mixed, grad_proj),
            (normed_two, grad_up_pre),
            (activ, grad_mlp),
        ),
        grad_gain_one,
        grad_gain_two,
    )


def adamw(weight, first, second, grad, step):
    power = step[0].astype(jnp.float32)
    first = BETA * first + (1.0 - BETA) * grad
    second = BETA * second + (1.0 - BETA) * grad * grad
    fix_one = 1.0 - jnp.power(BETA, power)
    fix_two = 1.0 - jnp.power(BETA, power)
    new = weight - RATE * (
        first / fix_one / (jnp.sqrt(second / fix_two) + EPSILON) + DECAY * weight
    )
    return (new, first, second)


def on_device(
    series,
    pad_mask,
    freq_class,
    owner,
    step,
    master,
    moment1,
    moment2,
    small_master,
    small_m1,
    small_m2,
):
    slot_count = master.shape[0]
    parts = split_small(small_master)
    freq, bias_one, bias_two, head_bias, out_bias = (
        parts[0],
        parts[1],
        parts[2],
        parts[5],
        parts[6],
    )
    feat, target, tmask = prepare(series, pad_mask)
    count_series = series.shape[0]
    tokens = count_series * NPATCH
    onehot = (freq_class[:, None] == jnp.arange(NCLASS, dtype=jnp.int32)[None, :]).astype(
        jnp.float32
    )
    local_counts = jnp.sum(
        onehot * jnp.sum(tmask.reshape(count_series, -1), axis=1)[:, None], 0
    )
    gathered, counts = gather_all(master.astype(jnp.bfloat16), local_counts)
    mats = unpack(gathered, owner)
    tok_in, tok_out, head_in, head_out = (mats[0], mats[1], mats[6], mats[7])
    class_weight = 1.0 / (counts * NCLASS)
    cosine, sine = flat_tables()
    patch_in = feat.reshape(tokens, 2 * PATCH).astype(jnp.bfloat16)
    tok_pre = matmul(patch_in, tok_in)
    hidden = silu(tok_pre[:, :D] + bias_one).astype(jnp.bfloat16)
    class_rows = jnp.repeat(jnp.dot(onehot, freq, precision=lax.Precision.HIGHEST), NPATCH, axis=0)
    state_zero = matmul(hidden, tok_out) + bias_two + tok_pre[:, D:] + class_rows
    state_two, kept = layer_forward(state_zero, mats, parts, cosine, sine)
    state_low = state_two.astype(jnp.bfloat16)
    head_pre = matmul(state_low, head_in)
    head_hidden = silu(head_pre[:, :D] + head_bias).astype(jnp.bfloat16)
    out = matmul(head_hidden, head_out) + out_bias + head_pre[:, D:]

    local_sums, grad_out = loss_parts(out, target, tmask, onehot, class_weight)
    grad_out_bias = jnp.sum(grad_out.astype(jnp.float32), axis=0)
    grad_head_first = backmul(grad_out, head_out) * silu_slope(head_pre[:, :D] + head_bias)
    grad_head_bias = jnp.sum(grad_head_first, axis=0)
    grad_head_pre = jnp.concatenate([grad_head_first, grad_out.astype(jnp.float32)], axis=1).astype(
        jnp.bfloat16
    )
    grad_two = backmul(grad_head_pre, head_in)
    grad_zero, layer_pairs, grad_gain_one, grad_gain_two = layer_backward(
        grad_two, state_zero, kept, mats, parts, cosine, sine
    )
    grad_prod = grad_zero.astype(jnp.bfloat16)
    grad_first = backmul(grad_prod, tok_out) * silu_slope(tok_pre[:, :D] + bias_one)
    grad_tok_pre = jnp.concatenate([grad_first, grad_zero], axis=1).astype(jnp.bfloat16)
    slots = grad_blocks(
        ((patch_in, grad_tok_pre), (hidden, grad_prod))
        + layer_pairs
        + ((state_low, grad_head_pre), (head_hidden, grad_out)),
        owner,
    )
    grad_freq = jnp.dot(
        onehot.T,
        grad_zero.reshape(count_series, NPATCH, D).sum(axis=1),
        precision=lax.Precision.HIGHEST,
    )
    small_local = jnp.concatenate(
        [
            grad_freq.reshape(-1),
            jnp.sum(grad_first, axis=0),
            jnp.sum(grad_zero, axis=0),
            grad_gain_one,
            grad_gain_two,
            grad_head_bias,
            grad_out_bias,
            local_sums.reshape(-1),
        ]
    )
    rank = lax.axis_index("wide") * lax.axis_size("narrow") + lax.axis_index("narrow")
    mine = rank * slot_count + jnp.arange(slot_count, dtype=jnp.int32)
    filled = jnp.any(owner[:, None] == mine[None, :], axis=0)
    owned, square_total, small_total = scatter_sum(slots, filled, small_local)
    small_grad = small_total[: small_master.shape[0]]
    sums = small_total[small_master.shape[0] :].reshape(2, NCLASS)
    grad_norm = jnp.sqrt(square_total + jnp.sum(small_grad * small_grad))
    scale = jnp.minimum(1.0, CLIP / grad_norm)
    loss = jnp.sum((sums[0] + sums[1] / NQ) * class_weight)
    new_master, new_m1, new_m2 = adamw(master, moment1, moment2, owned * scale, step)
    small_new, small_new_m1, small_new_m2 = adamw(
        small_master, small_m1, small_m2, small_grad * scale, step
    )
    return (
        loss,
        grad_norm,
        new_master,
        new_m1,
        new_m2,
        new_master.astype(jnp.bfloat16),
        small_new,
        small_new_m1,
        small_new_m2,
    )


def solution(mesh):
    return jax.shard_map(
        on_device,
        mesh=mesh,
        in_specs=(
            P(("wide", "narrow"), None),
            P(("wide", "narrow"), None),
            P(("wide", "narrow")),
            P(),
            P(),
            P(("wide", "narrow"), None, None),
            P(("wide", "narrow"), None, None),
            P(("wide", "narrow"), None, None),
            P(),
            P(),
            P(),
        ),
        out_specs=(
            P(),
            P(),
            P(("wide", "narrow"), None, None),
            P(("wide", "narrow"), None, None),
            P(("wide", "narrow"), None, None),
            P(("wide", "narrow"), None, None),
            P(),
            P(),
            P(),
        ),
        check_vma=False,
    )
```

```python
import functools

import jax
import jax.numpy as jnp
from jax import lax
from jax.experimental import pallas as pl
from jax.experimental.pallas import tpu as pltpu
from jax.sharding import PartitionSpec as P

D = 1280
HEADS = 16
HDIM = 80
FF = 5120
PATCH = 32
HORIZON = 128
NQ = 9
NPATCH = 16
NCLASS = 3
BR = 64
TOTAL_SLOTS = 512
CTX = 512
OUTW = 1280
ROWS = 20608
NBLK = 322


CLIP = 0.01
RATE = 0.03
DECAY = 0.1
BETA = 0.5
EPSILON = 1e-08


def matmul(left, right):
    return jnp.dot(left, right, preferred_element_type=jnp.float32)


def tmatmul(left, right):
    return lax.dot_general(
        left, right, (((0,), (0,)), ((), ())), preferred_element_type=jnp.float32
    )


def backmul(left, right):
    return lax.dot_general(
        left, right, (((1,), (1,)), ((), ())), preferred_element_type=jnp.float32
    )


def silu(value):
    return value / (1.0 + jnp.exp(-value))


def silu_slope(value):
    sigmoid = 1.0 / (1.0 + jnp.exp(-value))
    return sigmoid * (1.0 + value * (1.0 - sigmoid))


def rms_norm(hidden, gain):
    return hidden * lax.rsqrt(jnp.mean(hidden * hidden, axis=-1, keepdims=True) + 1e-06) * gain


def tables():
    half = HDIM // 2
    inverse = jnp.power(10000.0, -2.0 * jnp.arange(half, dtype=jnp.float32) / HDIM)
    angle = jnp.arange(NPATCH, dtype=jnp.float32)[:, None] * inverse[None, :]
    return (jnp.cos(angle)[None, :, None, :], jnp.sin(angle)[None, :, None, :])


SPAN = 2 * 128
ROWS_TOGETHER = 256


def turned(value, cosine, sine):
    half = HDIM // 2
    lane = lax.rem(lax.broadcasted_iota(jnp.int32, value.shape, 1), HDIM)
    other = jnp.where(lane < half, pltpu.roll(value, D - half, 1), pltpu.roll(value, half, 1))
    shape = (value.shape[0] // NPATCH, NPATCH, D)
    return (
        value.reshape(shape) * cosine[None] + other.reshape(shape) * sine[None]
    ).reshape(value.shape)


def attended(queries, keys):
    scores = backmul(queries, keys)
    row = lax.broadcasted_iota(jnp.int32, scores.shape, 0)
    column = lax.broadcasted_iota(jnp.int32, scores.shape, 1)
    seen = jnp.logical_and(column <= row, column >= row - lax.rem(row, NPATCH))
    scores = jnp.where(seen, scores, -1e30)
    expo = jnp.exp(scores - jnp.max(scores, axis=-1, keepdims=True))
    return expo * (1.0 / jnp.sum(expo, axis=-1, keepdims=True))


def parts_of(ref):
    step = min(ROWS_TOGETHER, ref.shape[0])
    return [slice(at, at + step) for at in range(0, ref.shape[0], step)]


def head_lanes(h):
    start = jnp.minimum(lax.div(h * HDIM, LANES) * LANES, D - SPAN)
    lane = start + lax.broadcasted_iota(jnp.int32, (1, SPAN), 1)
    inside = jnp.logical_and(lane >= h * HDIM, lane < (h + 1) * HDIM)
    return (
        pl.ds(pl.multiple_of(start, LANES), SPAN),
        jnp.where(inside, 1.0, 0.0).astype(jnp.bfloat16),
    )


def attend_kernel(qkv_ref, cos_ref, sin_ref, query_ref, key_ref, value_ref, mixed_ref, total_ref):
    cosine, sine = cos_ref[...], sin_ref[...]
    query_ref[...] = (turned(qkv_ref[:, 0:D], cosine, sine) * HDIM ** (-0.5)).astype(jnp.bfloat16)
    key_ref[...] = turned(qkv_ref[:, D : 2 * D], cosine, sine).astype(jnp.bfloat16)
    value_ref[...] = qkv_ref[:, 2 * D : 3 * D].astype(jnp.bfloat16)
    total_ref[...] = jnp.zeros_like(total_ref)

    def head(h, carry):
        span, lanes = head_lanes(h)
        for rows in parts_of(query_ref):
            attend = attended(query_ref[rows, span] * lanes, key_ref[rows, span])
            total_ref[rows, span] += matmul(
                attend.astype(jnp.bfloat16), value_ref[rows, span] * lanes
            )
        return carry

    lax.fori_loop(0, HEADS, head, 0, unroll=8)
    mixed_ref[...] = total_ref[...].astype(jnp.bfloat16)


def attend_back_kernel(
    query_ref, key_ref, value_ref, grad_ref, cos_ref, sin_ref, out_ref, dq_ref, dk_ref, dv_ref
):
    for ref in (dq_ref, dk_ref, dv_ref):
        ref[...] = jnp.zeros_like(ref)

    def head(h, carry):
        span, lanes = head_lanes(h)
        for rows in parts_of(query_ref):
            queries, keys = query_ref[rows, span] * lanes, key_ref[rows, span] * lanes
            grad = grad_ref[rows, span] * lanes
            attend = attended(queries, keys)
            grad_attend = backmul(grad, value_ref[rows, span])
            grad_scores = (
                attend * (grad_attend - jnp.sum(grad_attend * attend, axis=-1, keepdims=True))
            ).astype(jnp.bfloat16)
            dq_ref[rows, span] += matmul(grad_scores, keys)
            dk_ref[rows, span] += tmatmul(grad_scores, queries)
            dv_ref[rows, span] += tmatmul(attend.astype(jnp.bfloat16), grad)
        return carry

    lax.fori_loop(0, HEADS, head, 0, unroll=8)
    cosine, sine = cos_ref[...], sin_ref[...]
    out_ref[:, 0:D] = (turned(dq_ref[...], cosine, -sine) * HDIM ** (-0.5)).astype(jnp.bfloat16)
    out_ref[:, D : 2 * D] = turned(dk_ref[...], cosine, -sine).astype(jnp.bfloat16)
    out_ref[:, 2 * D : 3 * D] = dv_ref[...].astype(jnp.bfloat16)


def flat_tables():
    cosine, sine = (table[0, :, 0, :] for table in tables())
    return (
        jnp.tile(jnp.concatenate([cosine, cosine], axis=1), (1, HEADS)),
        jnp.tile(jnp.concatenate([-sine, sine], axis=1), (1, HEADS)),
    )


def attend_call(kernel, operands, widths, scratch, name):
    tokens = operands[0].shape[0]
    return pl.pallas_call(
        kernel,
        out_shape=tuple(jax.ShapeDtypeStruct((tokens, width), jnp.bfloat16) for width in widths),
        scratch_shapes=[pltpu.VMEM((tokens, width), jnp.float32) for width in scratch],
        compiler_params=pltpu.CompilerParams(vmem_limit_bytes=VMEM_LIMIT),
        name=name,
    )(*operands)


MATS = (
    (2 * PATCH, 2, 2),
    (D, 1, 10),
    (D, 3, 6),
    (D, 1, 10),
    (D, FF // D, 8),
    (FF, 1, 8),
    (D, (D + OUTW) // D, 8),
    (D, 1, 10),
)
BASES = tuple(sum(r * g for r, g, _ in MATS[:i]) // BR for i in range(len(MATS)))
LANES = 128
VMEM_LIMIT = 56 * 1024 * 1024
SCATTER_VMEM = 61 * 1024 * 1024


RING = 48


def steps_of(which):
    total, groups, count = MATS[which]
    return total * groups // (count * BR)


def stages(kind):
    return [pltpu.VMEM((2,) + kind(*MATS[which]), jnp.bfloat16) for which in range(len(MATS))]


def unpack_kernel(owner_ref, gathered_ref, *refs):
    outs, held = refs[:8], refs[8:16]
    ring, wide_ref, load_sem, store_sem = refs[16:]

    def load(b):
        at = lax.rem(b, RING)
        return pltpu.make_async_copy(
            gathered_ref.at[owner_ref[b]], ring.at[at], load_sem.at[at]
        )

    def first_load(b, carry):
        load(b).start()
        return carry

    lax.fori_loop(0, RING, first_load, 0)

    def store(which, i):
        total, groups, count = MATS[which]
        rows = count * BR // groups
        at = lax.rem(i, 2)
        return pltpu.make_async_copy(
            held[which].at[at],
            outs[which].at[pl.ds(pl.multiple_of(i * rows, rows), rows)],
            store_sem.at[which, at],
        )

    for which, (total, groups, count) in enumerate(MATS):
        rows = count * BR // groups

        def step(i, carry, which=which, groups=groups, count=count, rows=rows):
            first = BASES[which] + i * count
            at = lax.rem(i, 2)

            @pl.when(i >= 2)
            def _():
                store(which, i - 2).wait()

            for b in range(count):
                load(first + b).wait()
            for b in range(count):
                block = ring.at[lax.rem(first + b, RING)]
                span = slice(b * BR, (b + 1) * BR)
                if groups == 1:
                    held[which][at, span, :] = block[...]
                    continue
                for c in range(D // LANES):
                    wide_ref[c, span, :] = block[:, c * LANES : (c + 1) * LANES].astype(
                        jnp.float32
                    )
            if groups > 1:
                for j in range(groups):
                    for c in range(D // LANES):
                        left = j * D + c * LANES
                        held[which][at, :, left : left + LANES] = wide_ref[
                            c, pl.ds(j, rows, stride=groups), :
                        ].astype(jnp.bfloat16)
            store(which, i).start()
            for b in range(count):

                @pl.when(first + b + RING < NBLK)
                def _(b=b):
                    load(first + b + RING).start()

            return carry

        lax.fori_loop(0, steps_of(which), step, 0)

    for which in range(len(MATS)):
        for i in range(max(steps_of(which) - 2, 0), steps_of(which)):
            store(which, i).wait()


def unpack(gathered, owner):
    dma = pltpu.SemaphoreType.DMA
    return pl.pallas_call(
        unpack_kernel,
        out_shape=tuple(
            jax.ShapeDtypeStruct((total, groups * D), jnp.bfloat16) for total, groups, _ in MATS
        ),
        in_specs=[
            pl.BlockSpec(memory_space=pltpu.SMEM),
            pl.BlockSpec(memory_space=pl.ANY),
        ],
        out_specs=tuple(pl.BlockSpec(memory_space=pl.ANY) for _ in MATS),
        scratch_shapes=stages(lambda total, groups, count: (count * BR // groups, groups * D))
        + [
            pltpu.VMEM((RING, BR, D), jnp.bfloat16),
            pltpu.VMEM((D // LANES, 8 * BR, LANES), jnp.float32),
            dma((RING,)),
            dma((len(MATS), 2)),
        ],
        compiler_params=pltpu.CompilerParams(vmem_limit_bytes=VMEM_LIMIT),
        cost_estimate=pl.CostEstimate(
            flops=0, bytes_accessed=4 * ROWS * D, transcendentals=0
        ),
        name="unpack",
    )(owner, gathered)


def grad_kernel(owner_ref, *refs):
    lefts, rights, out_ref = refs[:8], refs[8:16], refs[16]
    left_in, right_in, held = refs[17:25], refs[25:33], refs[33:41]
    wide_ref, load_sem, store_sem = refs[41:]

    def loads(which):
        return (
            pltpu.make_async_copy(lefts[which], left_in[which], load_sem.at[which, 0]),
            pltpu.make_async_copy(rights[which], right_in[which], load_sem.at[which, 1]),
        )

    def store(which, i, b):
        at = lax.rem(i, 2)
        return pltpu.make_async_copy(
            held[which].at[at, pl.ds(b * BR, BR), :],
            out_ref.at[owner_ref[BASES[which] + i * MATS[which][2] + b]],
            store_sem.at[which, at, b],
        )

    order = tuple(reversed(range(len(MATS))))
    for which in order:
        for copy in loads(which):
            copy.start()
    for which in order:
        total, groups, count = MATS[which]
        rows = count * BR // groups
        for copy in loads(which):
            copy.wait()

        def step(i, carry, which=which, groups=groups, count=count, rows=rows):
            at = lax.rem(i, 2)

            @pl.when(i >= 2)
            def _():
                for b in range(count):
                    store(which, i - 2, b).wait()

            if steps_of(which) == 1:
                left = left_in[which][...]
            else:
                left = left_in[which][:, pl.ds(pl.multiple_of(i * rows, rows), rows)]
            for j in range(groups):
                part = tmatmul(left, right_in[which][:, j * D : (j + 1) * D])
                if groups == 1:
                    held[which][at] = part.astype(jnp.bfloat16)
                    continue
                for c in range(D // LANES):
                    wide_ref[c, pl.ds(j, rows, stride=groups), :] = part[
                        :, c * LANES : (c + 1) * LANES
                    ]
            if groups > 1:
                for c in range(D // LANES):
                    held[which][at, :, c * LANES : (c + 1) * LANES] = wide_ref[
                        c, 0 : count * BR, :
                    ].astype(jnp.bfloat16)
            for b in range(count):
                store(which, i, b).start()
            return carry

        lax.fori_loop(0, steps_of(which), step, 0)
    for which in order:
        for i in range(max(steps_of(which) - 2, 0), steps_of(which)):
            for b in range(MATS[which][2]):
                store(which, i, b).wait()


def grad_blocks(pairs, owner):
    lefts, rights = zip(*pairs)
    dma = pltpu.SemaphoreType.DMA
    tokens = lefts[0].shape[0]
    return pl.pallas_call(
        grad_kernel,
        out_shape=jax.ShapeDtypeStruct((TOTAL_SLOTS, BR, D), jnp.bfloat16),
        in_specs=[pl.BlockSpec(memory_space=pltpu.SMEM)]
        + [pl.BlockSpec(memory_space=pl.ANY)] * (2 * len(MATS)),
        out_specs=pl.BlockSpec(memory_space=pl.ANY),
        scratch_shapes=[pltpu.VMEM(left.shape, jnp.bfloat16) for left in lefts]
        + [pltpu.VMEM(right.shape, jnp.bfloat16) for right in rights]
        + stages(lambda total, groups, count: (count * BR, D))
        + [
            pltpu.VMEM((D // LANES, 8 * BR, LANES), jnp.float32),
            dma((len(MATS), 2)),
            dma((len(MATS), 2, 10)),
        ],
        compiler_params=pltpu.CompilerParams(vmem_limit_bytes=VMEM_LIMIT),
        cost_estimate=pl.CostEstimate(
            flops=2 * tokens * ROWS * D, bytes_accessed=2 * ROWS * D, transcendentals=0
        ),
        name="grad_blocks",
    )(owner, *lefts, *rights)


CHUNKS = 16
LATE = 3
EARLY = CHUNKS - LATE
COMBOS = 4 * LATE
STEPS = EARLY + 7
MESH = pl.DeviceIdType.MESH


def total_of(*blocks):
    result = blocks[0].astype(jnp.float32)
    for block in blocks[1:]:
        result = result + block.astype(jnp.float32)
    return result


def scatter_kernel(
    slots_ref,
    small_ref,
    filled_ref,
    out_ref,
    small_out,
    square_out,
    small_in,
    own,
    pair_in,
    pair_sum,
    first_in,
    second_in,
    second_out,
    column,
    up_in,
    down_in,
    up_out,
    down_out,
    result,
    late_own,
    late_pair_in,
    late_sum,
    late_up_in,
    late_down_in,
    late_up_out,
    late_down_out,
    late_column,
    late_first_in,
    late_second_in,
    late_second_out,
    late_result,
    own_sem,
    pair_send,
    pair_recv,
    first_send,
    first_recv,
    second_send,
    second_recv,
    up_send,
    up_recv,
    down_send,
    down_recv,
    result_sem,
    late_own_sem,
    late_pair_send,
    late_pair_recv,
    late_up_send,
    late_up_recv,
    late_down_send,
    late_down_recv,
    late_first_send,
    late_first_recv,
    late_second_send,
    late_second_recv,
    late_result_sem,
    share_send,
    share_recv,
    spread_send,
    spread_recv,
    square_send,
    square_recv,
):
    wide, z = lax.axis_index("wide"), lax.axis_index("narrow")
    core, here = lax.rem(wide, 2), lax.div(wide, 2)
    x, y = lax.rem(here, 2), lax.div(here, 2)
    far = 3 - here

    def device(place, level):
        return (place * 2 + core, level)

    partner = (here * 2 + 1 - core, z)

    def near(k, which):
        along_y = lax.rem(k + which, 2)
        return (y + along_y - 2 * y * along_y) * 2 + (x + (1 - along_y) - 2 * x * (1 - along_y))

    places = 8 * 4
    me = wide * 4 + z
    barrier = pltpu.get_barrier_semaphore()

    def each(action):
        def body(i, carry):
            other = lax.rem(me + i, places)
            action(i, other, (lax.div(other, 4), lax.rem(other, 4)))
            return carry

        lax.fori_loop(1, places, body, 0)

    def greet(i, other, to):
        pl.semaphore_signal(barrier, inc=1, device_id=to, device_id_type=MESH)

    def share(i, other, to):
        return pltpu.make_async_remote_copy(
            src_ref=small_ref.at[other],
            dst_ref=small_in.at[me],
            send_sem=share_send.at[i],
            recv_sem=share_recv.at[i],
            device_id=to,
            device_id_type=MESH,
        )

    def tell(ref, send, recv):
        def make(i, other, to):
            return pltpu.make_async_remote_copy(
                src_ref=ref.at[me],
                dst_ref=ref.at[me],
                send_sem=send.at[i],
                recv_sem=recv.at[i],
                device_id=to,
                device_id_type=MESH,
            )

        return make

    spread = tell(small_out, spread_send, spread_recv)
    square = tell(square_out, square_send, square_recv)
    each(greet)
    small_in[me] = small_ref[me]
    square_out[me] = jnp.zeros((8, LANES), jnp.float32)
    pl.semaphore_wait(barrier, places - 1)

    def own_copy(k):
        at = lax.rem(k, 2)
        return pltpu.make_async_copy(slots_ref.at[:, core, :, k], own.at[at], own_sem.at[at])

    def pair_copy(k):
        at = lax.rem(k, 2)
        return pltpu.make_async_remote_copy(
            src_ref=slots_ref.at[:, 1 - core, :, k],
            dst_ref=pair_in.at[at],
            send_sem=pair_send.at[at],
            recv_sem=pair_recv.at[at],
            device_id=partner,
            device_id_type=MESH,
        )

    def first_copy(k, part):
        place = near(k, 0)
        return pltpu.make_async_remote_copy(
            src_ref=pair_sum.at[lax.rem(k, 3), far if part == 0 else place],
            dst_ref=first_in.at[lax.rem(k, 5), part],
            send_sem=first_send.at[lax.rem(k, 3), part],
            recv_sem=first_recv.at[lax.rem(k, 5), part],
            device_id=device(place, z),
            device_id_type=MESH,
        )

    def second_copy(k):
        return pltpu.make_async_remote_copy(
            src_ref=second_out.at[lax.rem(k, 2)],
            dst_ref=second_in.at[lax.rem(k, 4)],
            send_sem=second_send.at[lax.rem(k, 2)],
            recv_sem=second_recv.at[lax.rem(k, 4)],
            device_id=device(near(k, 1), z),
            device_id_type=MESH,
        )

    def line_copy(source, target, send, recv, way):
        base = 1 if way > 0 else 0

        def make(k, level):
            return pltpu.make_async_remote_copy(
                src_ref=source.at[lax.rem(k, 2), level - base],
                dst_ref=target.at[lax.rem(k, 6), level - base],
                send_sem=send.at[lax.rem(k, 2), level - base],
                recv_sem=recv.at[lax.rem(k, 6), level - base],
                device_id=device(here, z + way),
                device_id_type=MESH,
            )

        return make

    def late_own_copy(c):
        at = lax.rem(c, 2)
        return pltpu.make_async_copy(
            slots_ref.at[lax.rem(c, 4), core, :, EARLY + lax.div(c, 4)],
            late_own.at[at],
            late_own_sem.at[at],
        )

    def late_pair_copy(c):
        at = lax.rem(c, 2)
        return pltpu.make_async_remote_copy(
            src_ref=slots_ref.at[lax.rem(c, 4), 1 - core, :, EARLY + lax.div(c, 4)],
            dst_ref=late_pair_in.at[at],
            send_sem=late_pair_send.at[at],
            recv_sem=late_pair_recv.at[at],
            device_id=partner,
            device_id_type=MESH,
        )

    def late_first_copy(slot, part):
        place = near(slot, 0)
        return pltpu.make_async_remote_copy(
            src_ref=late_column.at[slot, far if part == 0 else place],
            dst_ref=late_first_in.at[slot, part],
            send_sem=late_first_send.at[slot, part],
            recv_sem=late_first_recv.at[slot, part],
            device_id=device(place, z),
            device_id_type=MESH,
        )

    def late_second_copy(slot):
        return pltpu.make_async_remote_copy(
            src_ref=late_second_out.at[slot],
            dst_ref=late_second_in.at[slot],
            send_sem=late_second_send.at[slot],
            recv_sem=late_second_recv.at[slot],
            device_id=device(near(slot, 1), z),
            device_id_type=MESH,
        )

    def late_result_copy(slot):
        return pltpu.make_async_copy(late_result, out_ref.at[EARLY + slot], late_result_sem)

    def result_copy(k):
        at = lax.rem(k, 2)
        return pltpu.make_async_copy(result.at[at], out_ref.at[k], result_sem.at[at])

    def valid(k):
        return jnp.logical_and(k >= 0, k < EARLY)

    def valid_late(c):
        return jnp.logical_and(c >= 0, c < COMBOS)

    def keep(ref, k):
        kept = jnp.where(filled_ref[k, 0:1, 0:1] > 0.0, ref[...], 0.0)
        ref[...] = kept
        squares = square_out[me]
        for i in range(BR // 8):
            for j in range(D // LANES):
                part = kept[i * 8 : (i + 1) * 8, j * LANES : (j + 1) * LANES]
                squares = squares + part * part
        square_out[me] = squares

    def flows(lags, known, sums, ring, ins, outs, copies):
        for base, lag, behind, copy, arrived, leaving in zip(
            (1, 0), lags, (z > 0, z < 3), copies, ins, outs
        ):
            k = lag
            for n in range(base, base + 3):
                ahead = n > z if base else n < z

                @pl.when(jnp.logical_and(known(k - 2), ahead))
                def _(n=n, k=k, copy=copy):
                    copy(k - 2, n).wait_send()

                @pl.when(
                    jnp.logical_and(
                        jnp.logical_and(known(k), behind), jnp.logical_or(ahead, n == z)
                    )
                )
                def _(n=n, k=k, copy=copy):
                    copy(k, n).wait_recv()

                moving = jnp.logical_and(known(k), ahead)

                @pl.when(jnp.logical_and(moving, behind))
                def _(n=n, k=k, base=base, arrived=arrived, leaving=leaving):
                    leaving[lax.rem(k, 2), n - base] = total_of(
                        sums[lax.rem(k, ring), n], arrived[lax.rem(k, 6), n - base]
                    ).astype(jnp.bfloat16)

                @pl.when(jnp.logical_and(moving, jnp.logical_not(behind)))
                def _(n=n, k=k, base=base, leaving=leaving):
                    leaving[lax.rem(k, 2), n - base] = sums[lax.rem(k, ring), n]

                @pl.when(moving)
                def _(n=n, k=k, copy=copy):
                    copy(k, n).start()

    copies = (
        line_copy(up_out, up_in, up_send, up_recv, 1),
        line_copy(down_out, down_in, down_send, down_recv, -1),
    )
    late_copies = (
        line_copy(late_up_out, late_up_in, late_up_send, late_up_recv, 1),
        line_copy(late_down_out, late_down_in, late_down_send, late_down_recv, -1),
    )

    own_copy(0).start()
    pair_copy(0).start()
    late_own_copy(0).start()
    late_pair_copy(0).start()
    each(lambda *at: share(*at).start())

    def step(t, carry):
        @pl.when(valid(t - 3))
        def _():
            first_copy(t - 3, 0).wait_send()
            first_copy(t - 3, 1).wait_send()

        @pl.when(valid(t))
        def _():
            own_copy(t).wait()
            pair_copy(t).wait_recv()
            at, ring = lax.rem(t, 2), lax.rem(t, 3)

            def add(i, inner):
                p, n = lax.div(i, 4), lax.rem(i, 4)
                pair_sum[ring, p, n] = total_of(own[at, p, n], pair_in[at, p, n]).astype(
                    jnp.bfloat16
                )
                return inner

            lax.fori_loop(0, 16, add, 0)
            first_copy(t, 0).start()
            first_copy(t, 1).start()

        @pl.when(valid(t - 1))
        def _():
            pair_copy(t - 1).wait_send()

        @pl.when(t + 1 < EARLY)
        def _():
            own_copy(t + 1).start()
            pair_copy(t + 1).start()

        @pl.when(valid_late(t))
        def _():
            late_own_copy(t).wait()
            late_pair_copy(t).wait_recv()

            def add(n, inner):
                late_sum[lax.rem(t, 4), n] = total_of(
                    late_own[lax.rem(t, 2), n], late_pair_in[lax.rem(t, 2), n]
                ).astype(jnp.bfloat16)
                return inner

            lax.fori_loop(0, 4, add, 0)

        @pl.when(valid_late(t - 1))
        def _():
            late_pair_copy(t - 1).wait_send()

        @pl.when(t + 1 < COMBOS)
        def _():
            late_own_copy(t + 1).start()
            late_pair_copy(t + 1).start()

        @pl.when(valid(t - 3))
        def _():
            second_copy(t - 3).wait_send()

        @pl.when(valid(t - 1))
        def _():
            k = t - 1
            first_copy(k, 0).wait_recv()
            place = near(k, 1)

            def add(n, inner):
                second_out[lax.rem(k, 2), n] = total_of(
                    pair_sum[lax.rem(k, 3), place, n], first_in[lax.rem(k, 5), 0, n]
                ).astype(jnp.bfloat16)
                return inner

            lax.fori_loop(0, 4, add, 0)
            second_copy(k).start()

        @pl.when(valid(t - 2))
        def _():
            k = t - 2
            first_copy(k, 1).wait_recv()
            second_copy(k).wait_recv()

            def add(n, inner):
                column[lax.rem(k, 4), n] = total_of(
                    pair_sum[lax.rem(k, 3), here, n],
                    first_in[lax.rem(k, 5), 1, n],
                    second_in[lax.rem(k, 4), n],
                ).astype(jnp.bfloat16)
                return inner

            lax.fori_loop(0, 4, add, 0)

        flows(
            (t - 2 - z, t - 5 + z), valid, column, 4, (up_in, down_in), (up_out, down_out), copies
        )
        flows(
            (t - z, t - 3 + z),
            valid_late,
            late_sum,
            4,
            (late_up_in, late_down_in),
            (late_up_out, late_down_out),
            late_copies,
        )
        c = t - 3

        @pl.when(valid_late(c))
        def _():
            slot, p = lax.div(c, 4), lax.rem(c, 4)
            mine = late_sum.at[lax.rem(c, 4), z]
            below = late_up_in.at[lax.rem(c, 6), jnp.maximum(z - 1, 0)]
            above = late_down_in.at[lax.rem(c, 6), jnp.minimum(z, 2)]

            @pl.when(z == 0)
            def _():
                late_column[slot, p] = total_of(mine[...], above[...]).astype(jnp.bfloat16)

            @pl.when(z == 3)
            def _():
                late_column[slot, p] = total_of(mine[...], below[...]).astype(jnp.bfloat16)

            @pl.when(jnp.logical_and(z > 0, z < 3))
            def _():
                late_column[slot, p] = total_of(mine[...], below[...], above[...]).astype(
                    jnp.bfloat16
                )

        for slot in range(LATE):
            place = near(slot, 1)

            @pl.when(t == 4 * slot + 6)
            def _(slot=slot):
                late_first_copy(slot, 0).start()
                late_first_copy(slot, 1).start()

            @pl.when(t == 4 * slot + 7)
            def _(slot=slot, place=place):
                late_first_copy(slot, 0).wait_recv()
                late_second_out[slot] = total_of(
                    late_column[slot, place], late_first_in[slot, 0]
                ).astype(jnp.bfloat16)
                late_second_copy(slot).start()

            @pl.when(t == 4 * slot + 8)
            def _(slot=slot):
                late_first_copy(slot, 1).wait_recv()
                late_second_copy(slot).wait_recv()
                if slot:
                    late_result_copy(slot - 1).wait()
                late_result[...] = total_of(
                    late_column[slot, here], late_first_in[slot, 1], late_second_in[slot]
                )
                keep(late_result, EARLY + slot)
                late_result_copy(slot).start()

        k = t - 5

        @pl.when(valid(k - 2))
        def _():
            result_copy(k - 2).wait()

        @pl.when(valid(k))
        def _():
            result[lax.rem(k, 2)] = column[lax.rem(k, 4), z].astype(jnp.float32)

            @pl.when(z > 0)
            def _():
                result[lax.rem(k, 2)] += up_in[lax.rem(k, 6), z - 1].astype(jnp.float32)

            @pl.when(z < 3)
            def _():
                result[lax.rem(k, 2)] += down_in[lax.rem(k, 6), z].astype(jnp.float32)

            keep(result.at[lax.rem(k, 2)], k)
            result_copy(k).start()

        @pl.when(t == CHUNKS // 2)
        def _():
            each(lambda *at: share(*at).wait())
            small = small_in[0]
            for i in range(1, places):
                small = small + small_in[i]
            small_out[me] = small
            each(lambda *at: spread(*at).start())

        return carry

    lax.fori_loop(0, STEPS, step, 0)
    each(lambda *at: square(*at).start())
    late_result_copy(LATE - 1).wait()
    for slot in range(LATE):
        late_first_copy(slot, 0).wait_send()
        late_first_copy(slot, 1).wait_send()
        late_second_copy(slot).wait_send()
    each(lambda *at: spread(*at).wait())
    each(lambda *at: square(*at).wait())


def scatter_sum(slots, filled, small):
    slot_count = filled.shape[0]
    wide, narrow = lax.axis_size("wide"), lax.axis_size("narrow")
    if (wide, narrow, slot_count) != (8, 4, CHUNKS):
        part = lax.psum_scatter(slots, "wide", scatter_dimension=0, tiled=True)
        owned = lax.psum_scatter(
            part.astype(jnp.float32), "narrow", scatter_dimension=0, tiled=True
        )
        owned = jnp.where(filled[:, None, None], owned, 0.0)
        square = lax.psum(jnp.sum(owned * owned), ("wide", "narrow"))
        return owned, square, lax.psum(small, ("wide", "narrow"))
    tiles = (wide * narrow, 8, LANES)
    room = wide * narrow * 8 * LANES - small.shape[0]
    assert room >= 0
    low = functools.partial(pltpu.VMEM, dtype=jnp.bfloat16)
    dma = pltpu.SemaphoreType.DMA
    block = (BR, D)
    owned, small_tiles, square_tiles = pl.pallas_call(
        scatter_kernel,
        out_shape=(
            jax.ShapeDtypeStruct((slot_count,) + block, jnp.float32),
            jax.ShapeDtypeStruct(tiles, jnp.float32),
            jax.ShapeDtypeStruct(tiles, jnp.float32),
        ),
        in_specs=[
            pl.BlockSpec(memory_space=pl.ANY),
            pl.BlockSpec(memory_space=pltpu.VMEM),
            pl.BlockSpec(memory_space=pltpu.VMEM),
        ],
        out_specs=(
            pl.BlockSpec(memory_space=pl.ANY),
            pl.BlockSpec(memory_space=pltpu.VMEM),
            pl.BlockSpec(memory_space=pltpu.VMEM),
        ),
        scratch_shapes=[
            pltpu.VMEM(tiles, jnp.float32),
            low((2, 4, 4) + block),
            low((2, 4, 4) + block),
            low((3, 4, 4) + block),
            low((5, 2, 4) + block),
            low((4, 4) + block),
            low((2, 4) + block),
            low((4, 4) + block),
            low((6, 3) + block),
            low((6, 3) + block),
            low((2, 3) + block),
            low((2, 3) + block),
            pltpu.VMEM((2,) + block, jnp.float32),
            low((2, 4) + block),
            low((2, 4) + block),
            low((4, 4) + block),
            low((6, 3) + block),
            low((6, 3) + block),
            low((2, 3) + block),
            low((2, 3) + block),
            low((LATE, 4) + block),
            low((LATE, 2) + block),
            low((LATE,) + block),
            low((LATE,) + block),
            pltpu.VMEM(block, jnp.float32),
            dma((2,)),
            dma((2,)),
            dma((2,)),
            dma((3, 2)),
            dma((5, 2)),
            dma((2,)),
            dma((4,)),
            dma((2, 3)),
            dma((6, 3)),
            dma((2, 3)),
            dma((6, 3)),
            dma((2,)),
            dma((2,)),
            dma((2,)),
            dma((2,)),
            dma((2, 3)),
            dma((6, 3)),
            dma((2, 3)),
            dma((6, 3)),
            dma((LATE, 2)),
            dma((LATE, 2)),
            dma((LATE,)),
            dma((LATE,)),
            dma,
        ]
        + [dma((wide * narrow,))] * 6,
        compiler_params=pltpu.CompilerParams(
            collective_id=1, has_side_effects=True, vmem_limit_bytes=SCATTER_VMEM
        ),
        name="scatter_sum",
    )(
        slots.reshape(4, 2, narrow, slot_count, BR, D),
        jnp.pad(small, (0, room)).reshape(tiles),
        jnp.broadcast_to(
            filled.astype(jnp.float32)[:, None, None], (slot_count, 8, LANES)
        ),
    )
    return owned, jnp.sum(square_tiles), small_tiles.reshape(-1)[: small.shape[0]]


GATHER_STEPS = EARLY + 5


def gather_kernel(
    own_ref,
    count_ref,
    all_ref,
    counts_ref,
    own_sem,
    recv,
    pair_recv,
    line_send,
    plane_send,
    turn_send,
    late_send,
    pair_send,
    late_pair_send,
    count_send,
    count_recv,
):
    wide, z = lax.axis_index("wide"), lax.axis_index("narrow")
    core, here = lax.rem(wide, 2), lax.div(wide, 2)
    x, y = lax.rem(here, 2), lax.div(here, 2)
    side, front, far = y * 2 + 1 - x, (1 - y) * 2 + x, 3 - here
    places = 8 * 4
    me = wide * 4 + z

    barrier = pltpu.get_barrier_semaphore()

    def greet(i, carry):
        other = lax.rem(me + i, places)
        pl.semaphore_signal(
            barrier,
            inc=1,
            device_id=(lax.div(other, 4), lax.rem(other, 4)),
            device_id_type=MESH,
        )
        return carry

    lax.fori_loop(1, places, greet, 0)
    fill = pltpu.make_async_copy(own_ref, all_ref.at[here, core, z], own_sem)
    fill.start()
    counts_ref[me] = count_ref[...]
    pl.semaphore_wait(barrier, places - 1)
    fill.wait()

    def count_copy(i):
        other = lax.rem(me + i, places)
        return pltpu.make_async_remote_copy(
            src_ref=count_ref,
            dst_ref=counts_ref.at[me],
            send_sem=count_send.at[i],
            recv_sem=count_recv.at[i],
            device_id=(lax.div(other, 4), lax.rem(other, 4)),
            device_id_type=MESH,
        )

    def count_start(i, carry):
        count_copy(i).start()
        return carry

    lax.fori_loop(1, places, count_start, 0)

    def piece(p, n, k, send, to):
        return pltpu.make_async_remote_copy(
            src_ref=all_ref.at[p, core, n, k],
            dst_ref=all_ref.at[p, core, n, k],
            send_sem=send,
            recv_sem=recv.at[p, n, k],
            device_id=to,
            device_id_type=MESH,
        )

    up, down = (wide, z + 1), (wide, z - 1)
    to_side, to_front = (side * 2 + core, z), (front * 2 + core, z)

    def line(n, k, step):
        return piece(here, n, k, line_send.at[step, n, k], (up, down)[step])

    def plane(n, k, which):
        return piece(here, n, k, plane_send.at[which, n, k], (to_side, to_front)[which])

    def turn(n, k, which):
        return piece(
            (side, front)[which], n, k, turn_send.at[n, k], (to_front, to_side)[which]
        )

    def late(c, n, step):
        p, k = lax.rem(here + c, 4), EARLY + lax.div(c, 4)
        return piece(p, n, k, late_send.at[step, c, n], (up, down)[step])

    def pair(p, k, send):
        return pltpu.make_async_remote_copy(
            src_ref=all_ref.at[p, core, :, k],
            dst_ref=all_ref.at[p, core, :, k],
            send_sem=send,
            recv_sem=pair_recv,
            device_id=(here * 2 + 1 - core, z),
            device_id_type=MESH,
        )

    def early_pair(p, k):
        return pair(p, k, pair_send.at[p, k])

    def late_pair(c):
        p, k = lax.rem(here + c, 4), EARLY + lax.div(c, 4)
        return pair(p, k, late_pair_send.at[c])

    def both_lines(make, n, j, start):
        @pl.when(jnp.logical_and(start, z < 3))
        def _():
            if j <= 0:
                make(n, 0)

        @pl.when(jnp.logical_and(start, z > 0))
        def _():
            if j >= 0:
                make(n, 1)

    def early(k):
        return jnp.logical_and(k >= 0, k < EARLY)

    def swap(n, k, go):
        even = lax.rem(n + k, 2) == 0

        @pl.when(jnp.logical_and(go, even))
        def _():
            turn(n, k, 0).start()

        @pl.when(jnp.logical_and(go, jnp.logical_not(even)))
        def _():
            turn(n, k, 1).start()

    for k in range(EARLY, CHUNKS):
        plane(z, k, 0).start()
        plane(z, k, 1).start()

    def step(t, carry):
        @pl.when(early(t))
        def _():
            plane(z, t, 0).start()
            plane(z, t, 1).start()

        both_lines(lambda n, way: line(n, t, way).start(), z, 0, early(t))

        for j in (-1, 1, -2, 2, -3, 3):
            n, k = z + j, t - abs(j)
            there = jnp.logical_and(early(k), jnp.logical_and(n >= 0, n < 4))

            @pl.when(there)
            def _(n=n, k=k, j=j):
                piece(here, n, k, plane_send.at[0, n, k], to_side).wait_recv()

            both_lines(lambda n, way, k=k: line(n, k, way).start(), n, j, there)

            @pl.when(there)
            def _(n=n, k=k):
                plane(n, k, 0).start()
                plane(n, k, 1).start()

        @pl.when(t == 1)
        def _():
            for k in range(EARLY, CHUNKS):
                plane_wait(side, z, k)
                plane_wait(front, z, k)
                swap(z, k, True)

        @pl.when(t == 2)
        def _():
            for k in range(EARLY, CHUNKS):
                plane_wait(far, z, k)

        for j in (0, -1, 1, -2, 2, -3, 3):
            c = t - 2 - abs(j)
            n = z + j
            there = jnp.logical_and(
                jnp.logical_and(c >= 0, c < COMBOS), jnp.logical_and(n >= 0, n < 4)
            )
            if j:

                @pl.when(there)
                def _(n=n, c=c):
                    plane_wait(lax.rem(here + c, 4), n, EARLY + lax.div(c, 4))

            both_lines(lambda n, way, c=c: late(c, n, way).start(), n, j, there)

        for n in range(4):
            gap = jnp.abs(z - n)
            k = t - 1 - gap

            @pl.when(early(k))
            def _(n=n, k=k):
                plane_wait(side, n, k)
                plane_wait(front, n, k)

            swap(n, k, early(k))
            k = t - 2 - gap

            @pl.when(early(k))
            def _(n=n, k=k):
                plane_wait(far, n, k)

        for lag, sent in ((3, (here,)), (4, (side, front)), (5, (far,))):
            k = t - lag

            @pl.when(early(k))
            def _(k=k, sent=sent):
                for p in sent:
                    early_pair(p, k).start()

        @pl.when(jnp.logical_and(t >= 5, t < 5 + COMBOS))
        def _():
            late_pair(t - 5).start()

        return carry

    def plane_wait(p, n, k):
        piece(p, n, k, plane_send.at[0, n, k], to_side).wait_recv()

    lax.fori_loop(0, GATHER_STEPS, step, 0)

    def finish(k, carry):
        for n in range(4):
            plane_used = jnp.logical_or(k < EARLY, n == z)

            @pl.when(plane_used)
            def _(n=n):
                plane(n, k, 0).wait_send()
                plane(n, k, 1).wait_send()
                turn(n, k, 0).wait_send()

            @pl.when(jnp.logical_and(k < EARLY, jnp.logical_and(n <= z, z < 3)))
            def _(n=n):
                line(n, k, 0).wait_send()

            @pl.when(jnp.logical_and(k < EARLY, jnp.logical_and(n >= z, z > 0)))
            def _(n=n):
                line(n, k, 1).wait_send()

            @pl.when(jnp.logical_and(k < COMBOS, jnp.logical_and(n <= z, z < 3)))
            def _(n=n):
                late(k, n, 0).wait_send()

            @pl.when(jnp.logical_and(k < COMBOS, jnp.logical_and(n >= z, z > 0)))
            def _(n=n):
                late(k, n, 1).wait_send()

        @pl.when(k < EARLY)
        def _():
            for p in range(4):
                early_pair(p, k).wait_send()

        @pl.when(k < COMBOS)
        def _():
            late_pair(k).wait_send()

        return carry

    lax.fori_loop(0, CHUNKS, finish, 0)

    def count_wait(i, carry):
        count_copy(i).wait()
        return carry

    lax.fori_loop(1, places, count_wait, 0)
    pltpu.make_async_copy(
        all_ref.at[:, 1 - core], all_ref.at[:, 1 - core], pair_recv
    ).wait()


def gather_all(low, local_counts):
    slot_count = low.shape[0]
    wide, narrow = lax.axis_size("wide"), lax.axis_size("narrow")
    if (wide, narrow, slot_count) != (8, 4, CHUNKS):
        return (
            lax.all_gather(low, ("wide", "narrow"), axis=0, tiled=True),
            lax.psum(local_counts, ("wide", "narrow")),
        )
    dma = pltpu.SemaphoreType.DMA
    tile = jnp.zeros((8, LANES), jnp.float32).at[0, :NCLASS].set(local_counts)
    gathered, tiles = pl.pallas_call(
        gather_kernel,
        out_shape=(
            jax.ShapeDtypeStruct((4, 2, narrow, slot_count, BR, D), jnp.bfloat16),
            jax.ShapeDtypeStruct((wide * narrow, 8, LANES), jnp.float32),
        ),
        in_specs=[
            pl.BlockSpec(memory_space=pltpu.VMEM),
            pl.BlockSpec(memory_space=pltpu.VMEM),
        ],
        out_specs=(
            pl.BlockSpec(memory_space=pl.ANY),
            pl.BlockSpec(memory_space=pltpu.VMEM),
        ),
        scratch_shapes=[
            dma,
            dma((4, 4, CHUNKS)),
            dma,
            dma((2, 4, EARLY)),
            dma((2, 4, CHUNKS)),
            dma((4, CHUNKS)),
            dma((2, COMBOS, 4)),
            dma((4, EARLY)),
            dma((COMBOS,)),
            dma((wide * narrow,)),
            dma((wide * narrow,)),
        ],
        compiler_params=pltpu.CompilerParams(
            collective_id=2, has_side_effects=True, vmem_limit_bytes=VMEM_LIMIT
        ),
        name="gather_all",
    )(low, tile)
    return (
        gathered.reshape(wide * narrow * slot_count, BR, D),
        jnp.sum(tiles[:, 0, :NCLASS], axis=0),
    )


def split_small(small):
    freq = small[: NCLASS * D].reshape(NCLASS, D)
    rest = small[NCLASS * D :]
    return (
        freq,
        rest[0:D],
        rest[D : 2 * D],
        rest[2 * D : 3 * D],
        rest[3 * D : 4 * D],
        rest[4 * D : 5 * D],
        rest[5 * D : 5 * D + OUTW],
    )


def prepare(series, pad_mask):
    valid = (1 - pad_mask).astype(jnp.float32)
    count_series = series.shape[0]
    context = (series[:, :CTX] * valid[:, :CTX]).reshape(count_series, NPATCH, PATCH)
    marks = pad_mask[:, :CTX].astype(jnp.float32).reshape(count_series, NPATCH, PATCH)
    feat = jnp.concatenate([context, marks], axis=-1)
    return (feat, horizons(series), horizons(valid))


def horizons(points):
    count_series = points.shape[0]
    pieces = points.reshape(count_series, -1, PATCH)
    return jnp.concatenate(
        [pieces[:, 1 + j : 1 + j + NPATCH] for j in range(HORIZON // PATCH)], axis=-1
    ).reshape(count_series * NPATCH, HORIZON)


def loss_parts(out, target, tmask, onehot, class_weight):
    column = lax.broadcasted_iota(jnp.int32, (HORIZON, OUTW), 1)
    row = lax.broadcasted_iota(jnp.int32, (HORIZON, OUTW), 0)
    spread = (lax.div(column, NQ + 1) == row).astype(jnp.float32)
    wanted = jnp.dot(target, spread, precision=lax.Precision.HIGHEST)
    mask = matmul(tmask.astype(jnp.bfloat16), spread.astype(jnp.bfloat16))
    kind = lax.rem(lax.broadcasted_iota(jnp.int32, (1, OUTW), 1), NQ + 1)
    level = kind.astype(jnp.float32) / (NQ + 1)
    error = out - wanted
    above, below = level * -error, (level - 1.0) * -error
    slope = jnp.where(above > below, -level, jnp.where(above < below, 1.0 - level, 0.5 - level))
    square = jnp.sum(jnp.where(kind == 0, error * error * mask, 0.0), axis=1)
    quant = jnp.sum(jnp.where(kind == 0, 0.0, jnp.maximum(above, below) * mask), axis=1)
    onehot = jnp.repeat(onehot, NPATCH, axis=0)
    weight = jnp.sum(onehot * class_weight[None, :], axis=1, keepdims=True)
    grad = weight * mask * jnp.where(kind == 0, 2.0 * error, slope / NQ)
    sums = jnp.dot(jnp.stack([square, quant]), onehot, precision=lax.Precision.HIGHEST)
    return sums, grad.astype(jnp.bfloat16)


def layer_forward(state_zero, mats, parts, cosine, sine):
    w_qkv, w_out, w_up, w_down = (mats[2], mats[3], mats[4], mats[5])
    gain_one, gain_two = (parts[3], parts[4])
    normed_one = rms_norm(state_zero, gain_one).astype(jnp.bfloat16)
    qkv = matmul(normed_one, w_qkv)
    queries, key_rot, value_all, mixed = attend_call(
        attend_kernel, (qkv, cosine, sine), (D, D, D, D), (D,), "attend"
    )
    state_one = state_zero + matmul(mixed, w_out)
    normed_two = rms_norm(state_one, gain_two).astype(jnp.bfloat16)
    up_pre = matmul(normed_two, w_up)
    activ = silu(up_pre).astype(jnp.bfloat16)
    state_two = state_one + matmul(activ, w_down)
    return (
        state_two,
        (
            normed_one,
            queries,
            key_rot,
            value_all,
            mixed,
            state_one,
            normed_two,
            up_pre,
            activ,
        ),
    )


def layer_backward(grad_two, state_zero, kept, mats, parts, cosine, sine):
    (
        normed_one,
        queries,
        key_rot,
        value_all,
        mixed,
        state_one,
        normed_two,
        up_pre,
        activ,
    ) = kept
    w_qkv, w_out, w_up, w_down = (mats[2], mats[3], mats[4], mats[5])
    gain_one, gain_two = (parts[3], parts[4])
    grad_mlp = grad_two.astype(jnp.bfloat16)
    grad_act = backmul(grad_mlp, w_down)
    grad_up_pre = (grad_act * silu_slope(up_pre)).astype(jnp.bfloat16)
    grad_normed = backmul(grad_up_pre, w_up)
    _, pull = jax.vjp(rms_norm, state_one, gain_two)
    grad_norm_in, grad_gain_two = pull(grad_normed)
    grad_one = grad_two + grad_norm_in
    grad_proj = grad_one.astype(jnp.bfloat16)
    grad_mixed = backmul(grad_proj, w_out).astype(jnp.bfloat16)
    (grad_qkv,) = attend_call(
        attend_back_kernel,
        (queries, key_rot, value_all, grad_mixed, cosine, sine),
        (3 * D,),
        (D, D, D),
        "attend_back",
    )
    grad_normed_one = backmul(grad_qkv, w_qkv)
    _, pull = jax.vjp(rms_norm, state_zero, gain_one)
    grad_zero_in, grad_gain_one = pull(grad_normed_one)
    return (
        grad_one + grad_zero_in,
        (
            (normed_one, grad_qkv),
            (mixed, grad_proj),
            (normed_two, grad_up_pre),
            (activ, grad_mlp),
        ),
        grad_gain_one,
        grad_gain_two,
    )


def adamw(weight, first, second, grad, step):
    power = step[0].astype(jnp.float32)
    first = BETA * first + (1.0 - BETA) * grad
    second = BETA * second + (1.0 - BETA) * grad * grad
    fix_one = 1.0 - jnp.power(BETA, power)
    fix_two = 1.0 - jnp.power(BETA, power)
    new = weight - RATE * (
        first / fix_one / (jnp.sqrt(second / fix_two) + EPSILON) + DECAY * weight
    )
    return (new, first, second)


def on_device(
    series,
    pad_mask,
    freq_class,
    owner,
    step,
    master,
    moment1,
    moment2,
    small_master,
    small_m1,
    small_m2,
):
    slot_count = master.shape[0]
    parts = split_small(small_master)
    freq, bias_one, bias_two, head_bias, out_bias = (
        parts[0],
        parts[1],
        parts[2],
        parts[5],
        parts[6],
    )
    feat, target, tmask = prepare(series, pad_mask)
    count_series = series.shape[0]
    tokens = count_series * NPATCH
    onehot = (freq_class[:, None] == jnp.arange(NCLASS, dtype=jnp.int32)[None, :]).astype(
        jnp.float32
    )
    local_counts = jnp.sum(
        onehot * jnp.sum(tmask.reshape(count_series, -1), axis=1)[:, None], 0
    )
    gathered, counts = gather_all(master.astype(jnp.bfloat16), local_counts)
    mats = unpack(gathered, owner)
    tok_in, tok_out, head_in, head_out = (mats[0], mats[1], mats[6], mats[7])
    class_weight = 1.0 / (counts * NCLASS)
    cosine, sine = flat_tables()
    patch_in = feat.reshape(tokens, 2 * PATCH).astype(jnp.bfloat16)
    tok_pre = matmul(patch_in, tok_in)
    hidden = silu(tok_pre[:, :D] + bias_one).astype(jnp.bfloat16)
    class_rows = jnp.repeat(jnp.dot(onehot, freq, precision=lax.Precision.HIGHEST), NPATCH, axis=0)
    state_zero = matmul(hidden, tok_out) + bias_two + tok_pre[:, D:] + class_rows
    state_two, kept = layer_forward(state_zero, mats, parts, cosine, sine)
    state_low = state_two.astype(jnp.bfloat16)
    head_pre = matmul(state_low, head_in)
    head_hidden = silu(head_pre[:, :D] + head_bias).astype(jnp.bfloat16)
    out = matmul(head_hidden, head_out) + out_bias + head_pre[:, D:]

    local_sums, grad_out = loss_parts(out, target, tmask, onehot, class_weight)
    grad_out_bias = jnp.sum(grad_out.astype(jnp.float32), axis=0)
    grad_head_first = backmul(grad_out, head_out) * silu_slope(head_pre[:, :D] + head_bias)
    grad_head_bias = jnp.sum(grad_head_first, axis=0)
    grad_head_pre = jnp.concatenate([grad_head_first, grad_out.astype(jnp.float32)], axis=1).astype(
        jnp.bfloat16
    )
    grad_two = backmul(grad_head_pre, head_in)
    grad_zero, layer_pairs, grad_gain_one, grad_gain_two = layer_backward(
        grad_two, state_zero, kept, mats, parts, cosine, sine
    )
    grad_prod = grad_zero.astype(jnp.bfloat16)
    grad_first = backmul(grad_prod, tok_out) * silu_slope(tok_pre[:, :D] + bias_one)
    grad_tok_pre = jnp.concatenate([grad_first, grad_zero], axis=1).astype(jnp.bfloat16)
    slots = grad_blocks(
        ((patch_in, grad_tok_pre), (hidden, grad_prod))
        + layer_pairs
        + ((state_low, grad_head_pre), (head_hidden, grad_out)),
        owner,
    )
    grad_freq = jnp.dot(
        onehot.T,
        grad_zero.reshape(count_series, NPATCH, D).sum(axis=1),
        precision=lax.Precision.HIGHEST,
    )
    small_local = jnp.concatenate(
        [
            grad_freq.reshape(-1),
            jnp.sum(grad_first, axis=0),
            jnp.sum(grad_zero, axis=0),
            grad_gain_one,
            grad_gain_two,
            grad_head_bias,
            grad_out_bias,
            local_sums.reshape(-1),
        ]
    )
    rank = lax.axis_index("wide") * lax.axis_size("narrow") + lax.axis_index("narrow")
    mine = rank * slot_count + jnp.arange(slot_count, dtype=jnp.int32)
    filled = jnp.any(owner[:, None] == mine[None, :], axis=0)
    owned, square_total, small_total = scatter_sum(slots, filled, small_local)
    small_grad = small_total[: small_master.shape[0]]
    sums = small_total[small_master.shape[0] :].reshape(2, NCLASS)
    grad_norm = jnp.sqrt(square_total + jnp.sum(small_grad * small_grad))
    scale = jnp.minimum(1.0, CLIP / grad_norm)
    loss = jnp.sum((sums[0] + sums[1] / NQ) * class_weight)
    new_master, new_m1, new_m2 = adamw(master, moment1, moment2, owned * scale, step)
    small_new, small_new_m1, small_new_m2 = adamw(
        small_master, small_m1, small_m2, small_grad * scale, step
    )
    return (
        loss,
        grad_norm,
        new_master,
        new_m1,
        new_m2,
        new_master.astype(jnp.bfloat16),
        small_new,
        small_new_m1,
        small_new_m2,
    )


def solution(mesh):
    return jax.shard_map(
        on_device,
        mesh=mesh,
        in_specs=(
            P(("wide", "narrow"), None),
            P(("wide", "narrow"), None),
            P(("wide", "narrow")),
            P(),
            P(),
            P(("wide", "narrow"), None, None),
            P(("wide", "narrow"), None, None),
            P(("wide", "narrow"), None, None),
            P(),
            P(),
            P(),
        ),
        out_specs=(
            P(),
            P(),
            P(("wide", "narrow"), None, None),
            P(("wide", "narrow"), None, None),
            P(("wide", "narrow"), None, None),
            P(("wide", "narrow"), None, None),
            P(),
            P(),
            P(),
        ),
        check_vma=False,
    )
```
